32 devices in a mesh: dp: 4 (over y, x), ctx: 8 (over z, core).
Axes of the slice: x: 2, y: 2, z: 4, core: 2. Of those that a mesh axis runs over, the one named last changes fastest.
Arguments:
- tokens: bfloat16 [8, 2048, 1024], P('dp', 'ctx'), may hold values from -6 to 6
- positions: int32 [8, 2048], P('dp'), may hold values from 0 to 2047, as said below
- w_query: bfloat16 [1024, 2048], P(('dp', 'ctx')), may hold values from -0.1875 to 0.1875
- w_key: bfloat16 [1024, 1024], P(('dp', 'ctx')), may hold values from -0.1875 to 0.1875
- w_value: bfloat16 [1024, 1024], P(('dp', 'ctx')), may hold values from -0.1875 to 0.1875
- w_out: bfloat16 [2048, 1024], P(('dp', 'ctx')), may hold values from -1 to 1
- w_gate: bfloat16 [1024, 3072], P(('dp', 'ctx')), may hold values from -0.1875 to 0.1875
- w_up: bfloat16 [1024, 3072], P(('dp', 'ctx')), may hold values from -0.1875 to 0.1875
- w_down: bfloat16 [3072, 1024], P(('dp', 'ctx')), may hold values from -0.109375 to 0.109375
- attn_gain: bfloat16 [1024], P(('dp', 'ctx')), may hold values from 0.5 to 1.5
- mlp_gain: bfloat16 [1024], P(('dp', 'ctx')), may hold values from 0.5 to 1.5
- q_gain: bfloat16 [128], P(('dp', 'ctx')), may hold values from 0.5 to 1.5
- k_gain: bfloat16 [128], P(('dp', 'ctx')), may hold values from 0.5 to 1.5
- grad_out: bfloat16 [8, 2048, 1024], P('dp', 'ctx'), may hold values from -6 to 6
Outputs:
- output: bfloat16 [8, 2048, 1024], P('dp', 'ctx')
- input_grad: bfloat16 [8, 2048, 1024], P('dp', 'ctx')
- grad_w_query: float32 [1024, 2048], P(('dp', 'ctx'))
- grad_w_key: float32 [1024, 1024], P(('dp', 'ctx'))
- grad_w_value: float32 [1024, 1024], P(('dp', 'ctx'))
- grad_w_out: float32 [2048, 1024], P(('dp', 'ctx'))
- grad_w_gate: float32 [1024, 3072], P(('dp', 'ctx'))
- grad_w_up: float32 [1024, 3072], P(('dp', 'ctx'))
- grad_w_down: float32 [3072, 1024], P(('dp', 'ctx'))
- grad_attn_gain: float32 [1024], P(('dp', 'ctx'))
- grad_mlp_gain: float32 [1024], P(('dp', 'ctx'))
- grad_q_gain: float32 [128], P(('dp', 'ctx'))
- grad_k_gain: float32 [128], P(('dp', 'ctx'))
The draws below stay inside these ranges and needn't reach their ends.
Inputs may be any that keep to these rules, and one draw needn't show every extreme that they name: Each row is a permutation of 0 to 2047 made of 16 blocks of 128 consecutive positions in rising order; slots j * 2 * 128 to (j + 1) * 2 * 128 - 1 hold block c followed by block 15 - c, c drawn per row and per j.
All inputs are finite; a program needn't handle non-finite values.
Results may differ from the reference program's by a relative error of at most 0.023.
Values may be sent and summed in bfloat16 or wider, within the bound.
A program may use at most 384 MiB of HBM per device.

```python
import jax
import jax.numpy as jnp
from jax import lax

D = 1024
H = 16
KV = 8
HD = 128
FF = 3072
SEQ = 2048
BATCH = 8
SPANS = 16
SPAN_LEN = 128


def draw_positions(key, part):
    row_keys = jax.random.split(key, BATCH)
    offsets = jnp.arange(SPAN_LEN, dtype=jnp.int32)

    def one_row(row_key):
        owner = jax.random.permutation(row_key, SPANS // 2).astype(jnp.int32)
        first_block = owner[:, None] * SPAN_LEN + offsets[None, :]
        mirror_block = (SPANS - 1 - owner)[:, None] * SPAN_LEN + offsets[None, :]
        return jnp.concatenate([first_block, mirror_block], axis=1).reshape(SEQ)
    return jax.vmap(one_row)(row_keys).astype(jnp.int32)


def levels(stream_key, extent, cuts, low, high):
    gain = 1.0
    for dim, blocks in cuts:
        steps = jax.random.uniform(jax.random.fold_in(jax.random.fold_in(stream_key, 6), dim), (blocks,), jnp.float32, low / len(cuts), high / len(cuts))
        gain = gain * jnp.repeat(jnp.exp(steps), extent[dim] // blocks).reshape((-1,) + (1,) * (len(extent) - 1 - dim))
    return gain


def centred(stream_key, dims, spread, most, cuts=(), kind=jnp.bfloat16):
    drawn = jax.random.normal(stream_key, dims, jnp.float32) * spread
    if len(cuts) > 0:
        drawn = levels(stream_key, dims, cuts, -0.22, 0.18) * drawn
    return jnp.clip(drawn, min=-most, max=most).astype(kind)


def setup_inputs(seed: int = 0) -> dict:
    seeds = jax.random.split(jax.random.key(seed), 15)
    tokens = centred(seeds[0], (BATCH, SEQ, D), 1.0, 6.0, ((0, 4), (1, 8)))
    positions = draw_positions(jax.random.fold_in(seeds[14], 71), 0)
    w_query = centred(seeds[2], (D, H * HD), D ** -0.5, 0.1875, ((0, 32),))
    w_key = centred(seeds[3], (D, KV * HD), D ** -0.5, 0.1875, ((0, 32),))
    w_value = centred(seeds[4], (D, KV * HD), D ** -0.5, 0.1875, ((0, 32),))
    w_out = centred(seeds[5], (H * HD, D), (H * HD // 64) ** -0.5, 1.0, ((0, 32),))
    w_gate = centred(seeds[6], (D, FF), D ** -0.5, 0.1875, ((0, 32),))
    w_up = centred(seeds[7], (D, FF), D ** -0.5, 0.1875, ((0, 32),))
    w_down = centred(seeds[8], (FF, D), FF ** -0.5, 0.109375, ((0, 32),))
    attn_gain = jnp.clip(1.0 + 0.1 * jax.random.normal(seeds[9], (D,), jnp.float32), 0.5, 1.5).astype(jnp.bfloat16)
    mlp_gain = jnp.clip(1.0 + 0.1 * jax.random.normal(seeds[10], (D,), jnp.float32), 0.5, 1.5).astype(jnp.bfloat16)
    q_gain = jnp.clip(1.0 + 0.1 * jax.random.normal(seeds[11], (HD,), jnp.float32), 0.5, 1.5).astype(jnp.bfloat16)
    k_gain = jnp.clip(1.0 + 0.1 * jax.random.normal(seeds[12], (HD,), jnp.float32), 0.5, 1.5).astype(jnp.bfloat16)
    grad_out = centred(seeds[13], (BATCH, SEQ, D), 1.0, 6.0, ((0, 4), (1, 8)))
    return {"tokens": tokens, "positions": positions, "w_query": w_query, "w_key": w_key, "w_value": w_value, "w_out": w_out, "w_gate": w_gate, "w_up": w_up, "w_down": w_down, "attn_gain": attn_gain, "mlp_gain": mlp_gain, "q_gain": q_gain, "k_gain": k_gain, "grad_out": grad_out}


EPSILON = 1e-06
THETA = 1000000.0

@jax.custom_vjp
def low(v):
    return lax.optimization_barrier(v.astype(jnp.bfloat16)).astype(jnp.float32)

@jax.custom_vjp
def low_back(v):
    return v

def low_keep(v):
    return (low(v), None)

def low_pass(kept, grad):
    return (grad,)

def back_keep(v):
    return (v, None)

def back_low(kept, grad):
    return (low(grad),)
low.defvjp(low_keep, low_pass)
low_back.defvjp(back_keep, back_low)

def matmul(left, right):
    return jnp.dot(left, right, precision=lax.Precision.HIGHEST)

def normed(values, weights):
    return values * lax.rsqrt(lax.optimization_barrier(jnp.mean(values * values, axis=-1, keepdims=True)) + EPSILON) * weights

def angle_tables(position_ids):
    half_width = HD // 2
    inverse = THETA ** (-(jnp.arange(half_width).astype(jnp.float32) * 2.0 / HD))
    angles = position_ids.astype(jnp.float32)[:, None] * inverse[None, :]
    angles = jnp.concatenate([angles, angles], axis=-1)
    return (jnp.cos(angles), jnp.sin(angles))

def rotated(values, cosine, sine_table):
    half_width = values.shape[-1] // 2
    turned = jnp.concatenate([-values[..., half_width:], values[..., :half_width]], axis=-1)
    return values * cosine + turned * sine_table

def attend(packed):
    queries, keys_in, values_in, position_ids = packed
    grouped = queries.reshape(SEQ, KV, H // KV, HD)
    scores = jnp.einsum('qkgd,skd->kgqs', grouped, keys_in, precision=lax.Precision.HIGHEST) * HD ** (-0.5)
    scores = low_back(scores)
    causal = position_ids[None, :] <= position_ids[:, None]
    scores = jnp.where(causal, scores, -1e+30)
    weights_p = low(jax.nn.softmax(scores, axis=-1))
    mixed_heads = jnp.einsum('kgqs,skd->qkgd', weights_p, values_in, precision=lax.Precision.HIGHEST)
    return mixed_heads.reshape(SEQ, H * HD)

def group_forward(tokens_in, position_ids, params):
    w_query, w_key, w_value, w_out, w_gate, w_up, w_down, attn_gain, mlp_gain, q_gain, k_gain = params
    group_size = tokens_in.shape[0]
    row_count = group_size * SEQ
    flat_rows = tokens_in.reshape(row_count, D)
    hidden = low(normed(flat_rows, attn_gain))
    cosine, sine_table = angle_tables(position_ids.reshape(row_count))
    query_raw = low_back(matmul(hidden, w_query)).reshape(row_count, H, HD)
    key_raw = low_back(matmul(hidden, w_key)).reshape(row_count, KV, HD)
    value_raw = low_back(matmul(hidden, w_value))
    queries = low(rotated(normed(query_raw, q_gain), cosine[:, None], sine_table[:, None]))
    keys_in = low(rotated(normed(key_raw, k_gain), cosine[:, None], sine_table[:, None]))
    values_in = low(value_raw)
    mixed_heads = lax.map(jax.checkpoint(attend), (queries.reshape(group_size, SEQ, H, HD), keys_in.reshape(group_size, SEQ, KV, HD), values_in.reshape(group_size, SEQ, KV, HD), position_ids))
    mixed_heads = low(low_back(mixed_heads.reshape(row_count, H * HD)))
    middle = flat_rows + low_back(matmul(mixed_heads, w_out))
    second = low(normed(middle, mlp_gain))
    gate_proj = low_back(matmul(second, w_gate))
    up_proj = low_back(matmul(second, w_up))
    activated = low(jax.nn.silu(gate_proj) * up_proj)
    return middle + low_back(matmul(activated, w_down))

def reference(tokens, positions, w_query, w_key, w_value, w_out, w_gate, w_up, w_down, attn_gain, mlp_gain, q_gain, k_gain, grad_out):
    params = tuple((weight_item.astype(jnp.float32) for weight_item in (w_query, w_key, w_value, w_out, w_gate, w_up, w_down, attn_gain, mlp_gain, q_gain, k_gain)))
    tokens_grouped = tokens.astype(jnp.float32).reshape(BATCH, 1, SEQ, D)
    positions_grouped = positions.reshape(BATCH, 1, SEQ)
    cotangent_grouped = grad_out.astype(jnp.float32).reshape(BATCH, 1, SEQ, D)

    def one_group(totals, group_items):
        tokens_in, position_ids, cotangent = group_items
        output_rows, pullback = jax.vjp(lambda values, weights: group_forward(values, position_ids, weights), tokens_in, params)
        grad_in, grad_params = pullback(cotangent.reshape(SEQ, D))
        totals = tuple((total_item + grad_item for total_item, grad_item in zip(totals, grad_params)))
        return (totals, (output_rows.reshape(1, SEQ, D).astype(jnp.bfloat16), grad_in.astype(jnp.bfloat16)))
    initial = tuple((jnp.zeros(weight_item.shape, jnp.float32) for weight_item in params))
    totals, (outputs, grads_in) = lax.scan(one_group, initial, (tokens_grouped, positions_grouped, cotangent_grouped))
    return (outputs.reshape(BATCH, SEQ, D), grads_in.reshape(BATCH, SEQ, D), totals[0], totals[1], totals[2], totals[3], totals[4], totals[5], totals[6], totals[7], totals[8], totals[9], totals[10])
```

```python
import functools

import jax
import jax.numpy as jnp
import numpy as np
from jax import lax
from jax.experimental import pallas as pl
from jax.experimental.pallas import tpu as pltpu
from jax.sharding import PartitionSpec as P

H = 16
KV = 8
HD = 128
GROUPS = H // KV
EPSILON = 1e-06
THETA = 1000000.0
LOG2E = 1.4426950408889634
KEY_TILE = 512
VMEM_LIMIT = 48 * 1024 * 1024
MESH = pl.DeviceIdType.MESH
F32 = jnp.float32
BF16 = jnp.bfloat16


def normed(values, weights):
    return values * lax.rsqrt(jnp.mean(values * values, axis=-1, keepdims=True) + EPSILON) * weights


def norm_back(values, weights, grad):
    r = lax.rsqrt(jnp.mean(values * values, axis=-1, keepdims=True) + EPSILON)
    unit = values * r
    u = grad * weights
    return r * (u - unit * jnp.mean(u * unit, axis=-1, keepdims=True)), grad * unit


def rope_tables(seq):
    half = HD // 2
    inverse = (THETA ** (-(np.arange(half, dtype=np.float32) * np.float32(2.0) / np.float32(HD)))).astype(np.float32)
    angles = np.arange(seq, dtype=np.float32)[:, None] * inverse[None, :]
    cosine, sine = np.cos(angles), np.sin(angles)
    return (
        jnp.asarray(np.concatenate([cosine, cosine], axis=-1).astype(np.float32)),
        jnp.asarray(np.concatenate([-sine, sine], axis=-1).astype(np.float32)),
    )


def dot(a, b, dims, out=F32):
    return lax.dot_general(a, b, (dims, ((), ())), preferred_element_type=out)


NN = ((1,), (0,))
NT = ((1,), (1,))
TN = ((0,), (0,))


def sort_norm_kernel(order_ref, x_ref, gain_ref, o_ref):
    x = x_ref[...].astype(F32)
    o_ref[...] = normed(x, gain_ref[...]).astype(o_ref.dtype)


def sort_norm(order, rows, gain, span):
    count, width = rows.shape
    return pl.pallas_call(
        sort_norm_kernel,
        out_shape=jax.ShapeDtypeStruct((count, width), BF16),
        grid_spec=pltpu.PrefetchScalarGridSpec(
            num_scalar_prefetch=1,
            grid=(count // span,),
            in_specs=[
                pl.BlockSpec((span, width), lambda i, order: (order[i], 0)),
                pl.BlockSpec((1, width), lambda i, order: (0, 0)),
            ],
            out_specs=pl.BlockSpec((span, width), lambda i, order: (i, 0)),
        ),
        name="sort_norm",
    )(order, rows, gain)


def pick_kernel(order_ref, x_ref, o_ref):
    o_ref[...] = x_ref[...]


def pick_blocks(order, rows, span):
    count, width = rows.shape
    return pl.pallas_call(
        pick_kernel,
        out_shape=jax.ShapeDtypeStruct((count, width), rows.dtype),
        grid_spec=pltpu.PrefetchScalarGridSpec(
            num_scalar_prefetch=1,
            grid=(count // span,),
            in_specs=[pl.BlockSpec((span, width), lambda i, order: (order[i], 0))],
            out_specs=pl.BlockSpec((span, width), lambda i, order: (i, 0)),
        ),
        name="pick_blocks",
    )(order, rows)


def unit_rows(raw):
    r = lax.rsqrt(jnp.mean(raw * raw, axis=-1, keepdims=True) + EPSILON)
    return raw * r, r


def rope(values, cosine, sine):
    return values * cosine + pltpu.roll(values, HD // 2, 1) * sine


def rope_back(values, cosine, sine):
    return values * cosine - pltpu.roll(values, HD // 2, 1) * sine


def prepare_keys(k_ref, cos_ref, sin_ref, gk_ref, ks_ref):
    step = 256

    def body(i, _):
        rows = pl.ds(pl.multiple_of(i * step, step), step)
        unit, _r = unit_rows(k_ref[rows, :].astype(F32))
        ks_ref[rows, :] = rope(unit * gk_ref[...], cos_ref[rows, :], sin_ref[rows, :]).astype(BF16)
        return 0

    lax.fori_loop(0, k_ref.shape[0] // step, body, 0)


def query_block(q_ref, rows, places, cos_ref, sin_ref, gq_ref):
    units, scales, parts = [], [], []
    for g in range(GROUPS):
        unit, r = unit_rows(q_ref[rows, g * HD : (g + 1) * HD].astype(F32))
        turned = rope(unit * gq_ref[...], cos_ref[places, :], sin_ref[places, :])
        units.append(unit)
        scales.append(r)
        parts.append((turned * (LOG2E * HD**-0.5)).astype(BF16))
    return units, scales, jnp.concatenate(parts, axis=0)


def attend_kernel(span, ids_ref, q_ref, k_ref, v_ref, cos_ref, sin_ref, gq_ref, gk_ref, o_ref, lse_ref, ks_ref, acc_ref, sum_ref):
    prepare_keys(k_ref, cos_ref, sin_ref, gk_ref, ks_ref)
    m = GROUPS * span

    def block(j, _):
        b = ids_ref[j]
        rows = pl.ds(pl.multiple_of(j * span, span), span)
        places = pl.ds(pl.multiple_of(b * span, span), span)
        _u, _s, q2 = query_block(q_ref, rows, places, cos_ref, sin_ref, gq_ref)
        acc_ref[...] = jnp.zeros_like(acc_ref)
        sum_ref[...] = jnp.zeros_like(sum_ref)

        def tile(t, masked):
            keys = pl.ds(pl.multiple_of(t * KEY_TILE, KEY_TILE), KEY_TILE)
            p = jnp.exp2(dot(q2, ks_ref[keys, :], NT))
            if masked:
                at = t * KEY_TILE + lax.broadcasted_iota(jnp.int32, p.shape, 1)
                own = b * span + lax.broadcasted_iota(jnp.int32, p.shape, 0) % span
                p = jnp.where(at <= own, p, 0.0)
            part = p[:, 0:HD]
            for i in range(1, KEY_TILE // HD):
                part = part + p[:, i * HD : (i + 1) * HD]
            sum_ref[...] += part
            acc_ref[...] += dot(p.astype(BF16), v_ref[keys, :], NN)

        last = (b * span) // KEY_TILE
        lax.fori_loop(0, last, lambda t, _: (tile(t, False), 0)[1], 0)
        tile(last, True)
        total = jnp.sum(sum_ref[...], axis=-1, keepdims=True)
        mixed = acc_ref[...] * (1.0 / total)
        for g in range(GROUPS):
            o_ref[rows, g * HD : (g + 1) * HD] = mixed[g * span : (g + 1) * span].astype(BF16)
        wide = jnp.broadcast_to(jnp.log2(total), (m, HD))
        lse_ref[0, j] = jnp.transpose(wide)[0:1, :]
        return 0

    lax.fori_loop(0, q_ref.shape[0] // span, block, 0)


def attend(ids, q_raw, kv_raw, cosine, sine, gq, gk, span):
    rows = q_raw.shape[0]
    seq = kv_raw.shape[0]
    heads = q_raw.shape[1] // (GROUPS * HD)
    blocks, m = rows // span, GROUPS * span
    whole = lambda k, ids: (0, 0)
    return pl.pallas_call(
        functools.partial(attend_kernel, span),
        out_shape=[
            jax.ShapeDtypeStruct((rows, heads * GROUPS * HD), BF16),
            jax.ShapeDtypeStruct((heads, blocks, 1, m), F32),
        ],
        grid_spec=pltpu.PrefetchScalarGridSpec(
            num_scalar_prefetch=1,
            grid=(heads,),
            in_specs=[
                pl.BlockSpec((rows, GROUPS * HD), lambda k, ids: (0, k)),
                pl.BlockSpec((seq, HD), lambda k, ids: (0, k)),
                pl.BlockSpec((seq, HD), lambda k, ids: (0, heads + k)),
                pl.BlockSpec((seq, HD), whole),
                pl.BlockSpec((seq, HD), whole),
                pl.BlockSpec((1, HD), whole),
                pl.BlockSpec((1, HD), whole),
            ],
            out_specs=[
                pl.BlockSpec((rows, GROUPS * HD), lambda k, ids: (0, k)),
                pl.BlockSpec((1, blocks, 1, m), lambda k, ids: (k, 0, 0, 0)),
            ],
            scratch_shapes=[
                pltpu.VMEM((seq, HD), BF16),
                pltpu.VMEM((m, HD), F32),
                pltpu.VMEM((m, HD), F32),
            ],
        ),
        compiler_params=pltpu.CompilerParams(vmem_limit_bytes=VMEM_LIMIT),
        cost_estimate=pl.CostEstimate(
            flops=2 * 2 * rows * seq * heads * GROUPS * HD,
            bytes_accessed=2 * (2 * rows * heads * GROUPS * HD + 2 * seq * heads * HD),
            transcendentals=rows * seq * heads * GROUPS // 2,
        ),
        name="attend",
    )(ids, q_raw, kv_raw, kv_raw, cosine, sine, gq, gk)


def attend_back_kernel(
    span, ids_ref, q_ref, k_ref, v_ref, do_ref, o_ref, lse_ref, cos_ref, sin_ref, gq_ref, gk_ref,
    dq_ref, dk_ref, dv_ref, dgq_ref, dgk_ref, ks_ref, dka_ref, dva_ref, dqa_ref,
):
    prepare_keys(k_ref, cos_ref, sin_ref, gk_ref, ks_ref)
    dka_ref[...] = jnp.zeros_like(dka_ref)
    dva_ref[...] = jnp.zeros_like(dva_ref)

    @pl.when(pl.program_id(0) == 0)
    def _():
        dgq_ref[...] = jnp.zeros_like(dgq_ref)
        dgk_ref[...] = jnp.zeros_like(dgk_ref)

    def block(j, _):
        b = ids_ref[j]
        rows = pl.ds(pl.multiple_of(j * span, span), span)
        places = pl.ds(pl.multiple_of(b * span, span), span)
        units, scales, q2 = query_block(q_ref, rows, places, cos_ref, sin_ref, gq_ref)
        do2 = jnp.concatenate([do_ref[rows, g * HD : (g + 1) * HD] for g in range(GROUPS)], axis=0)
        o2 = jnp.concatenate([o_ref[rows, g * HD : (g + 1) * HD] for g in range(GROUPS)], axis=0)
        delta = jnp.sum(jnp.transpose(do2.astype(F32) * o2.astype(F32)), axis=0, keepdims=True)
        lse = lse_ref[0, j]
        dqa_ref[...] = jnp.zeros_like(dqa_ref)

        def tile(t, masked):
            keys = pl.ds(pl.multiple_of(t * KEY_TILE, KEY_TILE), KEY_TILE)
            kt = ks_ref[keys, :]
            p = jnp.exp2(dot(kt, q2, NT) - lse)
            if masked:
                at = t * KEY_TILE + lax.broadcasted_iota(jnp.int32, p.shape, 0)
                own = b * span + lax.broadcasted_iota(jnp.int32, p.shape, 1) % span
                p = jnp.where(at <= own, p, 0.0)
            ds = (p * (dot(v_ref[keys, :], do2, NT) - delta)).astype(BF16)
            dva_ref[keys, :] += dot(p.astype(BF16), do2, NN)
            dka_ref[keys, :] += dot(ds, q2, NN)
            dqa_ref[...] += dot(ds, kt, TN)

        last = (b * span) // KEY_TILE
        lax.fori_loop(0, last, lambda t, _: (tile(t, False), 0)[1], 0)
        tile(last, True)
        dq = dqa_ref[...] * HD**-0.5
        for g in range(GROUPS):
            grad = rope_back(dq[g * span : (g + 1) * span], cos_ref[places, :], sin_ref[places, :])
            dgq_ref[...] += jnp.sum(grad * units[g], axis=0, keepdims=True)
            u = grad * gq_ref[...]
            back = scales[g] * (u - units[g] * jnp.mean(u * units[g], axis=-1, keepdims=True))
            dq_ref[rows, g * HD : (g + 1) * HD] = back.astype(BF16)
        return 0

    lax.fori_loop(0, q_ref.shape[0] // span, block, 0)
    step = 256

    def finish(i, _):
        rows = pl.ds(pl.multiple_of(i * step, step), step)
        unit, r = unit_rows(k_ref[rows, :].astype(F32))
        grad = rope_back(dka_ref[rows, :] * (1.0 / LOG2E), cos_ref[rows, :], sin_ref[rows, :])
        dgk_ref[...] += jnp.sum(grad * unit, axis=0, keepdims=True)
        u = grad * gk_ref[...]
        back = r * (u - unit * jnp.mean(u * unit, axis=-1, keepdims=True))
        dk_ref[rows, :] = back.astype(BF16)
        dv_ref[rows, :] = dva_ref[rows, :].astype(BF16)
        return 0

    lax.fori_loop(0, k_ref.shape[0] // step, finish, 0)


def attend_back(ids, q_raw, kv_raw, grad_mixed, mixed, lse, cosine, sine, gq, gk, span):
    rows = q_raw.shape[0]
    seq = kv_raw.shape[0]
    heads = q_raw.shape[1] // (GROUPS * HD)
    blocks, m = rows // span, GROUPS * span
    whole = lambda k, ids: (0, 0)
    per_query = pl.BlockSpec((rows, GROUPS * HD), lambda k, ids: (0, k))
    per_key = pl.BlockSpec((seq, HD), lambda k, ids: (0, k))
    gain = pl.BlockSpec((1, HD), whole)
    return pl.pallas_call(
        functools.partial(attend_back_kernel, span),
        out_shape=[
            jax.ShapeDtypeStruct((rows, heads * GROUPS * HD), BF16),
            jax.ShapeDtypeStruct((seq, heads * HD), BF16),
            jax.ShapeDtypeStruct((seq, heads * HD), BF16),
            jax.ShapeDtypeStruct((1, HD), F32),
            jax.ShapeDtypeStruct((1, HD), F32),
        ],
        grid_spec=pltpu.PrefetchScalarGridSpec(
            num_scalar_prefetch=1,
            grid=(heads,),
            in_specs=[
                per_query,
                per_key,
                pl.BlockSpec((seq, HD), lambda k, ids: (0, heads + k)),
                per_query,
                per_query,
                pl.BlockSpec((1, blocks, 1, m), lambda k, ids: (k, 0, 0, 0)),
                pl.BlockSpec((seq, HD), whole),
                pl.BlockSpec((seq, HD), whole),
                gain,
                gain,
            ],
            out_specs=[per_query, per_key, per_key, gain, gain],
            scratch_shapes=[
                pltpu.VMEM((seq, HD), BF16),
                pltpu.VMEM((seq, HD), F32),
                pltpu.VMEM((seq, HD), F32),
                pltpu.VMEM((m, HD), F32),
            ],
        ),
        compiler_params=pltpu.CompilerParams(vmem_limit_bytes=VMEM_LIMIT),
        cost_estimate=pl.CostEstimate(
            flops=5 * 2 * rows * seq * heads * GROUPS * HD // 2,
            bytes_accessed=2 * (4 * rows * heads * GROUPS * HD + 4 * seq * heads * HD),
            transcendentals=rows * seq * heads * GROUPS // 2,
        ),
        name="attend_back",
    )(ids, q_raw, kv_raw, kv_raw, grad_mixed, mixed, lse, cosine, sine, gq, gk)


def peers():
    dp, ctx = lax.axis_index("dp"), lax.axis_index("ctx")
    to = lambda d, k: (jnp.bitwise_xor(dp, d), jnp.bitwise_xor(ctx, k))
    return dp, ctx, to


def greet(devices):
    barrier = pltpu.get_barrier_semaphore()
    for device in devices:
        pl.semaphore_signal(barrier, inc=1, device_id=device, device_id_type=MESH)
    pl.semaphore_wait(barrier, len(devices))


def sender(send_sem, recv_sem):
    made = []

    def send(src, dst, device):
        i = len(made)
        copy = pltpu.make_async_remote_copy(
            src_ref=src, dst_ref=dst, send_sem=send_sem.at[i], recv_sem=recv_sem.at[i],
            device_id=device, device_id_type=MESH,
        )
        copy.start()
        made.append(copy)
        return copy

    return send, made


def gather_kernel(pk_ref, wo_ref, tok_ref, w_ref, x_ref, send_sem, recv_sem, local_sem):
    dp, ctx, to = peers()
    c, z = ctx % 2, ctx // 2
    which = ctx // 4
    greet([to(0, 1), to(0, 2), to(0, 4), to(0, 6), to(1, 0), to(2, 0)])
    send, made = sender(send_sem, recv_sem)
    sib, nbr, far, xn, yn = to(0, 1), to(0, 2), to(0, 4), to(1, 0), to(2, 0)
    rows = pk_ref.shape[1]
    cols = pk_ref.shape[2]
    slots = tok_ref.shape[1]

    me = ctx % 4
    local = [
        pltpu.make_async_copy(tok_ref.at[which], x_ref.at[me, 0], local_sem.at[0]),
        pltpu.make_async_copy(pk_ref.at[c], w_ref.at[dp, z, pl.ds(c * rows, rows), pl.ds(0, cols)], local_sem.at[1]),
        pltpu.make_async_copy(wo_ref, w_ref.at[dp, z, :, pl.ds(cols, wo_ref.shape[1])], local_sem.at[2]),
    ]
    for copy in local:
        copy.start()
    swap = send(tok_ref.at[1 - which], x_ref.at[me, 1], far)
    mine_sib = send(tok_ref.at[which], x_ref.at[me, 0], sib)
    mine_nbr = send(tok_ref.at[which], x_ref.at[me, 0], nbr)
    cross = send(pk_ref.at[1 - c], w_ref.at[dp, z, pl.ds(c * rows, rows), pl.ds(0, cols)], sib)
    for copy in local:
        copy.wait()
    cross.wait_recv()

    def block(q, zz, part=None):
        if part is None:
            return w_ref.at[q, zz]
        return w_ref.at[q, zz, pl.ds(part * rows, rows)]

    own = block(dp, z)
    arrive = [send(own, own, to(0, 2 * k)) for k in (1, 2, 3)]
    first_y, first_x, last = [], [], []

    def spread(zz):
        first_y.append(send(block(dp, zz, 0), block(dp, zz, 0), yn))
        first_x.append(send(block(dp, zz, 1), block(dp, zz, 1), xn))
        last.append(send(block(dp, zz, 0), block(dp, zz, 0), xn))
        last.append(send(block(dp, zz, 1), block(dp, zz, 1), yn))

    spread(z)
    swap.wait_recv()
    swap_sib = send(x_ref.at[me, 1], x_ref.at[me, 1], sib)
    swap_nbr = send(x_ref.at[me, 1], x_ref.at[me, 1], nbr)
    order = [z] + [jnp.bitwise_xor(z, k) for k in (1, 2, 3)]
    other = jnp.bitwise_xor(me, 2)
    for k in (1, 2, 3):
        arrive[k - 1].wait_recv()
        spread(order[k])
        if k == 2:
            mine_nbr.wait_recv()
            last.append(send(x_ref.at[other, 0], x_ref.at[other, 0], sib))
    swap_nbr.wait_recv()
    last.append(send(x_ref.at[other, 1], x_ref.at[other, 1], sib))
    for k in range(4):
        zz = order[k]
        first_y[k].wait_recv()
        from_y = block(jnp.bitwise_xor(dp, 2), zz, 0)
        last.append(send(from_y, from_y, xn))
        first_x[k].wait_recv()
        from_x = block(jnp.bitwise_xor(dp, 1), zz, 1)
        last.append(send(from_x, from_x, yn))
    for copy in last + [mine_sib, swap_sib]:
        copy.wait_recv()
    for copy in made:
        copy.wait_send()


def gather(packed, w_out, tokens):
    rows, cols = 2 * packed.shape[1], packed.shape[2] + w_out.shape[1]
    copies = 45
    anywhere = pl.BlockSpec(memory_space=pl.ANY)
    w, x = pl.pallas_call(
        gather_kernel,
        out_shape=[
            jax.ShapeDtypeStruct((4, 4, rows, cols), BF16),
            jax.ShapeDtypeStruct((4, 2) + tokens.shape[1:], BF16),
        ],
        in_specs=[anywhere] * 3,
        out_specs=[anywhere] * 2,
        scratch_shapes=[
            pltpu.SemaphoreType.DMA((copies,)),
            pltpu.SemaphoreType.DMA((copies,)),
            pltpu.SemaphoreType.DMA((3,)),
        ],
        compiler_params=pltpu.CompilerParams(collective_id=0, has_side_effects=True),
        name="gather",
    )(packed, w_out, tokens)
    return w.reshape(16 * rows, cols), x.reshape(-1, tokens.shape[2])


def reduce_kernel(n_in, *refs):
    g_refs, o_ref = refs[:n_in], refs[n_in]
    g_ref, in_a, in_b, mid_a, mid_b, got_a, got_b, out3, in3, send_sem, recv_sem, local_sem = refs[n_in + 1 :]
    dp, ctx, to = peers()
    z = ctx // 2
    x, y = dp % 2, dp // 2
    greet([to(0, 2), to(0, 4), to(0, 6), to(1, 0), to(2, 0)])
    send, made = sender(send_sem, recv_sem)
    xn, yn = to(1, 0), to(2, 0)
    hr = g_ref.shape[3] // 2
    at, local = 0, []
    for i, ref in enumerate(g_refs):
        width = ref.shape[-1]
        local.append(pltpu.make_async_copy(ref, g_ref.at[:, :, :, :, pl.ds(at, width)], local_sem.at[i]))
        at += width
    for copy in local:
        copy.start()
    for copy in local:
        copy.wait()
    low, high = pl.ds(0, hr), pl.ds(hr, hr)
    order = [jnp.bitwise_xor(z, k) for k in (2, 3, 1, 0)]
    a_in, b_in = [], []
    for k, zz in enumerate(order):
        a_in.append(send(g_ref.at[:, 1 - x, zz, low], in_a.at[k], xn))
        b_in.append(send(g_ref.at[1 - y, :, zz, high], in_b.at[k], yn))
    add = lambda p, q: (p.astype(F32) + q.astype(F32)).astype(BF16)
    a_mid, b_mid = [], []
    for k, zz in enumerate(order):
        a_in[k].wait_recv()
        mid_a[k] = add(g_ref[1 - y, x, zz, 0:hr], in_a[k, 1 - y])
        a_mid.append(send(mid_a.at[k], got_a.at[k], yn))
        b_in[k].wait_recv()
        mid_b[k] = add(g_ref[y, 1 - x, zz, hr:], in_b[k, 1 - x])
        b_mid.append(send(mid_b.at[k], got_b.at[k], xn))
    final = []
    for k, zz in enumerate(order):
        a_mid[k].wait_recv()
        out3[k, 0:hr] = (
            g_ref[y, x, zz, 0:hr].astype(F32) + in_a[k, y].astype(F32) + got_a[k].astype(F32)
        ).astype(BF16)
        b_mid[k].wait_recv()
        out3[k, hr:] = (
            g_ref[y, x, zz, hr:].astype(F32) + in_b[k, x].astype(F32) + got_b[k].astype(F32)
        ).astype(BF16)
        if k < 3:
            final.append(send(out3.at[k], in3.at[k], to(0, 2 * (2, 3, 1)[k])))
    for copy in final:
        copy.wait_recv()
    o_ref[...] = (
        out3[3].astype(F32) + in3[0].astype(F32) + in3[1].astype(F32) + in3[2].astype(F32)
    ).astype(BF16)
    for copy in made:
        copy.wait_send()


def reduce(grads):
    rows = grads[0].shape[0] // 16
    cols = sum(g.shape[1] for g in grads)
    grads = [g.reshape(2, 2, 4, rows, g.shape[1]) for g in grads]
    copies = 19
    return pl.pallas_call(
        functools.partial(reduce_kernel, len(grads)),
        out_shape=jax.ShapeDtypeStruct((rows, cols), BF16),
        in_specs=[pl.BlockSpec(memory_space=pl.ANY)] * len(grads),
        out_specs=pl.BlockSpec(memory_space=pltpu.VMEM),
        scratch_shapes=[
            pltpu.VMEM((2, 2, 4, rows, cols), BF16),
            pltpu.VMEM((4, 2, rows // 2, cols), BF16),
            pltpu.VMEM((4, 2, rows // 2, cols), BF16),
        ]
        + [pltpu.VMEM((4, rows // 2, cols), BF16)] * 4
        + [
            pltpu.VMEM((4, rows, cols), BF16),
            pltpu.VMEM((3, rows, cols), BF16),
            pltpu.SemaphoreType.DMA((copies,)),
            pltpu.SemaphoreType.DMA((copies,)),
            pltpu.SemaphoreType.DMA((len(grads),)),
        ],
        compiler_params=pltpu.CompilerParams(
            collective_id=1, has_side_effects=True, vmem_limit_bytes=VMEM_LIMIT
        ),
        name="reduce",
    )(*grads)


def by_core(c, own, other):
    return jnp.where(c == 0, jnp.stack([own, other]), jnp.stack([other, own]))


def layer(
    n_dp, n, tokens, positions, w_query, w_key, w_value, w_out, w_gate, w_up, w_down,
    attn_gain, mlp_gain, q_gain, k_gain, grad_out,
):
    axes = ("dp", "ctx")
    slots, width = tokens.shape[1:]
    seq = positions.shape[1]
    span = slots // 2
    half = n // 2
    chips = n_dp * half
    ctx = lax.axis_index("ctx")
    c = ctx % 2
    which = ctx // half
    r_in, r_out, r_down = w_query.shape[0], w_out.shape[0], w_down.shape[0]
    ff = w_gate.shape[1]
    ff_c = ff // 2
    q_c, kv_c = H * HD // 2, KV * HD // 2

    to_sibling = [(i, i ^ 1) for i in range(n)]
    to_partner = [(i, (i + half) % n) for i in range(n)]
    halves = [list(range(half)), list(range(half, n))]
    same_core = [list(range(0, n, 2)), list(range(1, n, 2))]
    sibling = lambda v: lax.ppermute(v, "ctx", to_sibling)
    partner = lambda v: lax.ppermute(v, "ctx", to_partner)

    def placed(values):
        mine = lax.dynamic_index_in_dim(values, which, 0, False)
        other = lax.dynamic_index_in_dim(values, 1 - which, 0, False)
        return jnp.concatenate([mine, partner(other)], axis=0)

    gains = jnp.concatenate(
        [
            attn_gain[:, None],
            mlp_gain[:, None],
            jnp.pad(q_gain, (0, r_in - q_gain.shape[0]))[:, None],
            jnp.pad(k_gain, (0, r_in - k_gain.shape[0]))[:, None],
            jnp.zeros((r_in, 124), BF16),
        ],
        axis=1,
    )
    tall = (n_dp, n) == (4, 8)
    qkv_halves = [
        jnp.concatenate(
            [
                w_query[:, i * q_c : (i + 1) * q_c],
                w_key[:, i * kv_c : (i + 1) * kv_c],
                w_value[:, i * kv_c : (i + 1) * kv_c],
            ],
            axis=1,
        )
        for i in range(2)
    ]

    def ff_order(shard):
        return shard.reshape(r_in, chips, 2, r_down).transpose(2, 0, 1, 3).reshape(2, r_in, ff_c)

    gate_order, up_order = ff_order(w_gate), ff_order(w_up)
    qkv_c = q_c + 2 * kv_c
    packed = jnp.stack(
        [
            jnp.concatenate([qkv_halves[i], gains, gate_order[i], up_order[i]], axis=1)
            for i in range(2)
        ]
    )
    if tall:
        w_all, x_all = gather(packed, w_out, tokens)
        x_own = lax.dynamic_slice_in_dim(x_all, (ctx % half) * 2 * slots, 2 * slots, 0)
        w_qkv = w_all[:, :qkv_c]
        g_cols = w_all[:, qkv_c : qkv_c + HD].astype(F32)
        w_gu = w_all[:, qkv_c + HD : qkv_c + HD + 2 * ff_c]
        out_rows = w_all[:, qkv_c + HD + 2 * ff_c :].reshape(2, -1, r_out, width)
        out_keep = lax.dynamic_index_in_dim(out_rows, c, 0, False)
        out_give = lax.dynamic_index_in_dim(out_rows, 1 - c, 0, False)
        w_out_c = by_core(c, out_keep, sibling(out_give)).transpose(1, 0, 2, 3).reshape(q_c, width)
        w_down, w_all = lax.optimization_barrier((w_down, w_all))
    else:
        both = lax.all_gather(packed, axes, axis=1, tiled=True)
        w_all = lax.dynamic_index_in_dim(both, c, 0, False)
        out_all = lax.all_gather(w_out, axes, axis=0, tiled=True)
        x_own = placed(tokens)
        x_all = lax.all_gather(x_own, "ctx", axis=0, tiled=True, axis_index_groups=halves)
        w_qkv = w_all[:, :qkv_c]
        g_cols = w_all[:, qkv_c : qkv_c + HD].astype(F32)
        w_gu = w_all[:, qkv_c + HD :]
        w_out_c = lax.dynamic_slice_in_dim(out_all, c * q_c, q_c, 0)
    down_all = lax.all_gather(w_down, axes, axis=0, tiled=True)
    w_down_c = lax.dynamic_index_in_dim(down_all.reshape(chips, 2, r_down, width), c, 1, False).reshape(ff_c, width)
    gain_attn = g_cols[:, 0][None]
    gain_mlp = g_cols[:, 1][None]
    per_head = g_cols.reshape(n_dp * n, r_in, HD)[:, : q_gain.shape[0]].reshape(HD, HD)
    gain_q = per_head[:, 2][None]
    gain_k = per_head[:, 3][None]

    chip = (ctx % half) // 2
    chip_rows = 4 * slots
    x_chip = lax.dynamic_slice_in_dim(x_all, chip * chip_rows, chip_rows, 0)
    go_own = placed(grad_out)
    go_chip = by_core(c, go_own, sibling(go_own)).reshape(chip_rows, width)
    slot_ids = lax.dynamic_index_in_dim(positions, which, 0, False).reshape(2 * n, span)[:, 0] // span
    places = np.stack(
        [
            [s for d in side for k in (d, (d + half) % n) for s in (2 * k, 2 * k + 1)]
            for side in halves
        ]
    ).astype(np.int32)
    ids_all = slot_ids[lax.dynamic_index_in_dim(jnp.asarray(places), which, 0, False)]
    steps = jnp.arange(2 * n, dtype=jnp.int32)
    order = jnp.sum(jnp.where(ids_all[None, :] == steps[:, None], steps[None, :], 0), axis=1).astype(jnp.int32)
    ids = lax.dynamic_slice_in_dim(ids_all, chip * 8, 8, 0)
    cosine, sine = rope_tables(seq)

    hidden_all = sort_norm(order, x_all, gain_attn, span)
    x_chip32 = x_chip.astype(F32)
    hidden = normed(x_chip32, gain_attn).astype(BF16)
    q_raw = dot(hidden, w_qkv[:, :q_c], NN, BF16)
    kv_raw = dot(hidden_all, w_qkv[:, q_c:], NN, BF16)
    mixed, lse = attend(ids, q_raw, kv_raw, cosine, sine, gain_q, gain_k, span)
    proj = dot(mixed, w_out_c, NN, BF16)
    middle = x_chip32 + (proj.astype(F32) + sibling(proj).astype(F32))
    second = normed(middle, gain_mlp).astype(BF16)
    gate = dot(second, w_gu[:, :ff_c], NN, BF16).astype(F32)
    up = dot(second, w_gu[:, ff_c:], NN, BF16).astype(F32)
    sig = jax.nn.sigmoid(gate)
    silu = gate * sig
    activated = (silu * up).astype(BF16)
    down = dot(activated, w_down_c, NN, BF16).reshape(2, 2 * slots, width)
    down_own = lax.dynamic_index_in_dim(down, c, 0, False)
    down_other = sibling(lax.dynamic_index_in_dim(down, 1 - c, 0, False))
    own_rows = lambda v: lax.dynamic_slice_in_dim(v, c * 2 * slots, 2 * slots, 0)
    result = (own_rows(middle) + (down_own.astype(F32) + down_other.astype(F32))).astype(BF16)

    def returned(rows):
        mine, back = rows[:slots], partner(rows[slots:])
        return jnp.where(which == 0, jnp.stack([mine, back]), jnp.stack([back, mine]))

    output = returned(result)

    grad_act = dot(go_chip, w_down_c, NT)
    grad_gate = (grad_act * up * sig * (1.0 + gate * (1.0 - sig))).astype(BF16)
    grad_up = (grad_act * silu).astype(BF16)
    grad_down_w = dot(activated, go_chip, TN, BF16)
    grad_gate_w = dot(second, grad_gate, TN, BF16)
    grad_up_w = dot(second, grad_up, TN, BF16)
    grad_second_part = (dot(grad_gate, w_gu[:, :ff_c], NT) + dot(grad_up, w_gu[:, ff_c:], NT)).astype(BF16)
    grad_second = grad_second_part.astype(F32) + sibling(grad_second_part).astype(F32)
    back, gain_terms = norm_back(middle, gain_mlp, grad_second)
    grad_mlp_gain = jnp.where(c == 0, jnp.sum(gain_terms, axis=0), 0.0)
    grad_middle = go_chip.astype(F32) + back
    grad_attn = grad_middle.astype(BF16)

    def reduced(grad):
        part = lax.psum_scatter(grad, "dp", scatter_dimension=0, tiled=True)
        return lax.psum_scatter(part, "ctx", scatter_dimension=0, tiled=True, axis_index_groups=same_core)

    sum_gu = reduced(jnp.concatenate([grad_gate_w, grad_up_w], axis=1))
    sum_down = reduced(grad_down_w)

    grad_mixed = dot(grad_attn, w_out_c, NT, BF16)
    grad_out_w = dot(mixed, grad_attn, TN, BF16)
    dq, dk, dv, dgq, dgk = attend_back(
        ids, q_raw, kv_raw, grad_mixed, mixed, lse, cosine, sine, gain_q, gain_k, span
    )
    dkv = jnp.concatenate([dk, dv], axis=1)
    grad_q_w = dot(hidden, dq, TN, BF16)
    grad_kv_w = dot(hidden_all, dkv, TN, BF16)
    out_w = grad_out_w.reshape(-1, 2, r_out, width)
    out_mine = lax.dynamic_index_in_dim(out_w, c, 1, False)
    out_recv = sibling(lax.dynamic_index_in_dim(out_w, 1 - c, 1, False))
    grad_out_w = by_core(c, out_mine, out_recv).reshape(chips * r_out, width)

    part_all = pick_blocks(ids_all, dot(dkv, w_qkv[:, q_c:], NT, BF16), span)
    part_q = dot(dq, w_qkv[:, :q_c], NT)
    part_chip = lax.dynamic_slice_in_dim(part_all, chip * chip_rows, chip_rows, 0).astype(F32) + part_q
    part_all = lax.dynamic_update_slice_in_dim(part_all, part_chip.astype(BF16), chip * chip_rows, 0)
    grad_hidden = lax.psum_scatter(
        part_all, "ctx", scatter_dimension=0, tiled=True, axis_index_groups=halves
    ).astype(F32)
    x_own32 = x_own.astype(F32)
    back, _terms = norm_back(x_own32, gain_attn, grad_hidden)
    grad_attn_gain = jnp.sum(part_all.astype(F32) * normed(x_all.astype(F32), 1.0), axis=0)
    input_grad = returned((own_rows(grad_middle) + back).astype(BF16))

    apart = width // HD
    spaced = lambda v: jnp.pad(v.reshape(HD, 1), ((0, 0), (0, apart - 1))).reshape(width, 1)
    gain_cols = jnp.concatenate(
        [grad_attn_gain[:, None], grad_mlp_gain[:, None], spaced(dgq), spaced(dgk), jnp.zeros((width, HD - 4), F32)],
        axis=1,
    ).astype(BF16)
    grads = [grad_q_w, grad_kv_w, gain_cols, grad_out_w]
    if tall:
        sums = reduce(grads)
    else:
        sums = jnp.concatenate([reduced(g) for g in grads], axis=1)
    sum_out = sums[:, qkv_c + HD :]
    def columns(sums):
        rows = sums.reshape(2, r_in, -1)
        mine = lax.dynamic_index_in_dim(rows, c, 0, False)
        other = sibling(lax.dynamic_index_in_dim(rows, 1 - c, 0, False))
        return by_core(c, mine, other).astype(F32)

    qkv_own = columns(sums[:, : qkv_c + HD])
    gain_own = jnp.sum(qkv_own[:, :, qkv_c : qkv_c + 4], axis=0)
    gu_own = columns(sum_gu)
    beside = lambda v: v.transpose(1, 0, 2).reshape(r_in, -1)
    ff_back = lambda v: v.reshape(2, r_in, chips, r_down).transpose(1, 2, 0, 3).reshape(r_in, ff)
    return (
        output,
        input_grad,
        beside(qkv_own[:, :, :q_c]),
        beside(qkv_own[:, :, q_c : q_c + kv_c]),
        beside(qkv_own[:, :, q_c + kv_c : qkv_c]),
        sum_out.astype(F32),
        ff_back(gu_own[:, :, :ff_c]),
        ff_back(gu_own[:, :, ff_c:]),
        sum_down.astype(F32),
        gain_own[:, 0],
        gain_own[:, 1],
        gain_own[::apart, 2],
        gain_own[::apart, 3],
    )


def solution(mesh):
    rows = P(("dp", "ctx"), None)
    gain = P(("dp", "ctx"))
    acts = P("dp", "ctx", None)
    return jax.shard_map(
        functools.partial(layer, mesh.shape["dp"], mesh.shape["ctx"]),
        mesh=mesh,
        in_specs=(acts, P("dp", None)) + (rows,) * 7 + (gain,) * 4 + (acts,),
        out_specs=(acts, acts) + (rows,) * 7 + (gain,) * 4,
        check_vma=False,
    )
```

```python
import functools

import jax
import jax.numpy as jnp
import numpy as np
from jax import lax
from jax.experimental import pallas as pl
from jax.experimental.pallas import tpu as pltpu
from jax.sharding import PartitionSpec as P

H = 16
KV = 8
HD = 128
GROUPS = H // KV
EPSILON = 1e-06
THETA = 1000000.0
LOG2E = 1.4426950408889634
KEY_TILE = 512
ROW_TILE = 256
FF_TILE = 512
FWD_HEADS = 4
BACK_HEADS = 4
VMEM_LIMIT = 48 * 1024 * 1024
MESH = pl.DeviceIdType.MESH
F32 = jnp.float32
BF16 = jnp.bfloat16


def normed(values, weights):
    return values * lax.rsqrt(jnp.mean(values * values, axis=-1, keepdims=True) + EPSILON) * weights


def norm_back(values, weights, grad):
    r = lax.rsqrt(jnp.mean(values * values, axis=-1, keepdims=True) + EPSILON)
    unit = values * r
    u = grad * weights
    return r * (u - unit * jnp.mean(u * unit, axis=-1, keepdims=True)), grad * unit


def rope_tables(seq):
    half = HD // 2
    inverse = (THETA ** (-(np.arange(half, dtype=np.float32) * np.float32(2.0) / np.float32(HD)))).astype(np.float32)
    angles = np.arange(seq, dtype=np.float32)[:, None] * inverse[None, :]
    cosine, sine = np.cos(angles), np.sin(angles)
    return (
        jnp.asarray(np.concatenate([cosine, cosine], axis=-1).astype(np.float32)),
        jnp.asarray(np.concatenate([-sine, sine], axis=-1).astype(np.float32)),
    )


def dot(a, b, dims, out=F32):
    return lax.dot_general(a, b, (dims, ((), ())), preferred_element_type=out)


NN = ((1,), (0,))
NT = ((1,), (1,))
TN = ((0,), (0,))


def row_mean(values):
    return dot(values.astype(BF16), jnp.full((HD, HD), 1.0 / HD, BF16), NN)


def unit_rows(raw):
    r = lax.rsqrt(row_mean(raw * raw) + EPSILON)
    return raw * r, r


def rope(values, cosine, sine):
    return values * cosine + pltpu.roll(values, HD // 2, 1) * sine


def rope_back(values, cosine, sine):
    return values * cosine - pltpu.roll(values, HD // 2, 1) * sine


def lanes(head, width=HD):
    return slice(head * width, (head + 1) * width)


def prepare_keys(span, order_ref, k_ref, v_ref, cos_ref, sin_ref, gk_ref, ks_ref, vs_ref):
    def body(i, _):
        rows = pl.ds(pl.multiple_of(i * span, span), span)
        source = pl.ds(pl.multiple_of(order_ref[i] * span, span), span)
        for p in range(k_ref.shape[1] // HD):
            unit, _r = unit_rows(k_ref[source, lanes(p)].astype(F32))
            ks_ref[rows, lanes(p)] = rope(unit * gk_ref[...], cos_ref[rows, :], sin_ref[rows, :]).astype(BF16)
        vs_ref[rows, :] = v_ref[source, :]
        return 0

    lax.fori_loop(0, k_ref.shape[0] // span, body, 0)


def query_block(q_ref, p, rows, places, cos_ref, sin_ref, gq_ref):
    units, scales, parts = [], [], []
    for g in range(GROUPS):
        unit, r = unit_rows(q_ref[rows, lanes(p * GROUPS + g)].astype(F32))
        turned = rope(unit * gq_ref[...], cos_ref[places, :], sin_ref[places, :])
        units.append(unit)
        scales.append(r)
        parts.append((turned * (LOG2E * HD**-0.5)).astype(BF16))
    return units, scales, jnp.concatenate(parts, axis=0)


def seen(shape, t, b, span, key_axis):
    at = t * KEY_TILE + lax.broadcasted_iota(jnp.int32, shape, key_axis)
    own = b * span + lax.broadcasted_iota(jnp.int32, shape, 1 - key_axis) % span
    return at <= own


def attend_kernel(
    span, ids_ref, order_ref, q_ref, k_ref, v_ref, cos_ref, sin_ref, gq_ref, gk_ref,
    o_ref, lse_ref, ks_ref, vs_ref, acc_ref, sum_ref,
):
    prepare_keys(span, order_ref, k_ref, v_ref, cos_ref, sin_ref, gk_ref, ks_ref, vs_ref)
    m = GROUPS * span
    heads = range(FWD_HEADS)

    def block(j, _):
        b = ids_ref[j]
        rows = pl.ds(pl.multiple_of(j * span, span), span)
        places = pl.ds(pl.multiple_of(b * span, span), span)
        q2 = [query_block(q_ref, p, rows, places, cos_ref, sin_ref, gq_ref)[2] for p in heads]
        acc_ref[...] = jnp.zeros_like(acc_ref)
        sum_ref[...] = jnp.zeros_like(sum_ref)

        def tile(t, masked):
            keys = pl.ds(pl.multiple_of(t * KEY_TILE, KEY_TILE), KEY_TILE)
            scores = [dot(q2[p], ks_ref[keys, lanes(p)], NT) for p in heads]
            keep = seen(scores[0].shape, t, b, span, 1) if masked else None
            for p in heads:
                e = jnp.exp2(scores[p])
                if masked:
                    e = jnp.where(keep, e, 0.0)
                part = e[:, 0:HD]
                for i in range(1, KEY_TILE // HD):
                    part = part + e[:, lanes(i)]
                sum_ref[p] += part
                acc_ref[p] += dot(e.astype(BF16), vs_ref[keys, lanes(p)], NN)

        last = (b * span) // KEY_TILE
        lax.fori_loop(0, last, lambda t, _: (tile(t, False), 0)[1], 0)
        tile(last, True)
        for p in heads:
            total = jnp.sum(sum_ref[p], axis=-1, keepdims=True)
            mixed = acc_ref[p] * (1.0 / total)
            for g in range(GROUPS):
                o_ref[rows, lanes(p * GROUPS + g)] = mixed[g * span : (g + 1) * span].astype(BF16)
            wide = jnp.broadcast_to(jnp.log2(total), (m, HD))
            lse_ref[p, j] = jnp.transpose(wide)[0:1, :]
        return 0

    lax.fori_loop(0, q_ref.shape[0] // span, block, 0)


def attend(ids, order, q_raw, kv_raw, cosine, sine, gq, gk, span):
    rows = q_raw.shape[0]
    seq = kv_raw.shape[0]
    heads = q_raw.shape[1] // (GROUPS * HD)
    blocks, m = rows // span, GROUPS * span
    hp = FWD_HEADS
    whole = lambda k, ids, order: (0, 0)
    per_query = pl.BlockSpec((rows, hp * GROUPS * HD), lambda k, ids, order: (0, k))
    once = pl.Buffered(1)
    return pl.pallas_call(
        functools.partial(attend_kernel, span),
        out_shape=[
            jax.ShapeDtypeStruct((rows, heads * GROUPS * HD), BF16),
            jax.ShapeDtypeStruct((heads, blocks, 1, m), F32),
        ],
        grid_spec=pltpu.PrefetchScalarGridSpec(
            num_scalar_prefetch=2,
            grid=(heads // hp,),
            in_specs=[
                per_query,
                pl.BlockSpec((seq, hp * HD), lambda k, ids, order: (0, k)),
                pl.BlockSpec((seq, hp * HD), lambda k, ids, order: (0, heads // hp + k)),
                pl.BlockSpec((seq, HD), whole, pipeline_mode=once),
                pl.BlockSpec((seq, HD), whole, pipeline_mode=once),
                pl.BlockSpec((1, HD), whole),
                pl.BlockSpec((1, HD), whole),
            ],
            out_specs=[
                per_query,
                pl.BlockSpec((hp, blocks, 1, m), lambda k, ids, order: (k, 0, 0, 0)),
            ],
            scratch_shapes=[
                pltpu.VMEM((seq, hp * HD), BF16),
                pltpu.VMEM((seq, hp * HD), BF16),
                pltpu.VMEM((hp, m, HD), F32),
                pltpu.VMEM((hp, m, HD), F32),
            ],
        ),
        compiler_params=pltpu.CompilerParams(vmem_limit_bytes=VMEM_LIMIT),
        cost_estimate=pl.CostEstimate(
            flops=2 * 2 * rows * seq * heads * GROUPS * HD,
            bytes_accessed=2 * (2 * rows * heads * GROUPS * HD + 2 * seq * heads * HD),
            transcendentals=rows * seq * heads * GROUPS // 2,
        ),
        name="attend",
    )(ids, order, q_raw, kv_raw, kv_raw, cosine, sine, gq, gk)


def attend_back_kernel(
    span, ids_ref, order_ref, q_ref, k_ref, v_ref, do_ref, o_ref, lse_ref, cos_ref, sin_ref, gq_ref, gk_ref,
    dq_ref, dk_ref, dv_ref, dgq_ref, dgk_ref, ks_ref, vs_ref, dka_ref, dva_ref, dqa_ref,
):
    prepare_keys(span, order_ref, k_ref, v_ref, cos_ref, sin_ref, gk_ref, ks_ref, vs_ref)
    dka_ref[...] = jnp.zeros_like(dka_ref)
    dva_ref[...] = jnp.zeros_like(dva_ref)
    heads = range(BACK_HEADS)

    @pl.when(pl.program_id(0) == 0)
    def _():
        dgq_ref[...] = jnp.zeros_like(dgq_ref)
        dgk_ref[...] = jnp.zeros_like(dgk_ref)

    def block(j, _):
        b = ids_ref[j]
        rows = pl.ds(pl.multiple_of(j * span, span), span)
        places = pl.ds(pl.multiple_of(b * span, span), span)
        q2, do2, delta, lse = [], [], [], []
        for p in heads:
            q2.append(query_block(q_ref, p, rows, places, cos_ref, sin_ref, gq_ref)[2])
            pick = lambda ref: jnp.concatenate([ref[rows, lanes(p * GROUPS + g)] for g in range(GROUPS)], axis=0)
            do2.append(pick(do_ref))
            delta.append(
                jnp.sum(jnp.transpose(do2[p].astype(F32) * pick(o_ref).astype(F32)), axis=0, keepdims=True)
            )
            lse.append(lse_ref[p, j])
        dqa_ref[...] = jnp.zeros_like(dqa_ref)

        def tile(t, masked):
            keys = pl.ds(pl.multiple_of(t * KEY_TILE, KEY_TILE), KEY_TILE)
            kt = [ks_ref[keys, lanes(p)] for p in heads]
            scores = [dot(kt[p], q2[p], NT) for p in heads]
            slopes = [dot(vs_ref[keys, lanes(p)], do2[p], NT) for p in heads]
            keep = seen(scores[0].shape, t, b, span, 0) if masked else None
            for p in heads:
                e = jnp.exp2(scores[p] - lse[p])
                if masked:
                    e = jnp.where(keep, e, 0.0)
                ds = (e * (slopes[p] - delta[p])).astype(BF16)
                dva_ref[keys, lanes(p)] += dot(e.astype(BF16), do2[p], NN)
                dka_ref[keys, lanes(p)] += dot(ds, q2[p], NN)
                dqa_ref[p] += dot(ds, kt[p], TN)

        last = (b * span) // KEY_TILE
        lax.fori_loop(0, last, lambda t, _: (tile(t, False), 0)[1], 0)
        tile(last, True)
        for p in heads:
            units, scales, _q = query_block(q_ref, p, rows, places, cos_ref, sin_ref, gq_ref)
            dq = dqa_ref[p] * HD**-0.5
            for g in range(GROUPS):
                grad = rope_back(dq[g * span : (g + 1) * span], cos_ref[places, :], sin_ref[places, :])
                dgq_ref[...] += jnp.sum(grad * units[g], axis=0, keepdims=True)
                u = grad * gq_ref[...]
                back = scales[g] * (u - units[g] * row_mean(u * units[g]))
                dq_ref[rows, lanes(p * GROUPS + g)] = back.astype(BF16)
        return 0

    lax.fori_loop(0, q_ref.shape[0] // span, block, 0)

    def finish(i, _):
        rows = pl.ds(pl.multiple_of(i * span, span), span)
        source = pl.ds(pl.multiple_of(order_ref[i] * span, span), span)
        for p in heads:
            unit, r = unit_rows(k_ref[source, lanes(p)].astype(F32))
            grad = rope_back(dka_ref[rows, lanes(p)] * (1.0 / LOG2E), cos_ref[rows, :], sin_ref[rows, :])
            dgk_ref[...] += jnp.sum(grad * unit, axis=0, keepdims=True)
            u = grad * gk_ref[...]
            back = r * (u - unit * row_mean(u * unit))
            dk_ref[source, lanes(p)] = back.astype(BF16)
        dv_ref[source, :] = dva_ref[rows, :].astype(BF16)
        return 0

    lax.fori_loop(0, k_ref.shape[0] // span, finish, 0)


def attend_back(ids, order, q_raw, kv_raw, grad_mixed, mixed, lse, cosine, sine, gq, gk, span):
    rows = q_raw.shape[0]
    seq = kv_raw.shape[0]
    heads = q_raw.shape[1] // (GROUPS * HD)
    blocks, m = rows // span, GROUPS * span
    hp = BACK_HEADS
    whole = lambda k, ids, order: (0, 0)
    per_query = pl.BlockSpec((rows, hp * GROUPS * HD), lambda k, ids, order: (0, k))
    per_key = pl.BlockSpec((seq, hp * HD), lambda k, ids, order: (0, k))
    gain = pl.BlockSpec((1, HD), whole)
    once = pl.Buffered(1)
    return pl.pallas_call(
        functools.partial(attend_back_kernel, span),
        out_shape=[
            jax.ShapeDtypeStruct((rows, heads * GROUPS * HD), BF16),
            jax.ShapeDtypeStruct((seq, heads * HD), BF16),
            jax.ShapeDtypeStruct((seq, heads * HD), BF16),
            jax.ShapeDtypeStruct((1, HD), F32),
            jax.ShapeDtypeStruct((1, HD), F32),
        ],
        grid_spec=pltpu.PrefetchScalarGridSpec(
            num_scalar_prefetch=2,
            grid=(heads // hp,),
            in_specs=[
                per_query,
                per_key,
                pl.BlockSpec((seq, hp * HD), lambda k, ids, order: (0, heads // hp + k)),
                per_query,
                per_query,
                pl.BlockSpec((hp, blocks, 1, m), lambda k, ids, order: (k, 0, 0, 0)),
                pl.BlockSpec((seq, HD), whole, pipeline_mode=once),
                pl.BlockSpec((seq, HD), whole, pipeline_mode=once),
                gain,
                gain,
            ],
            out_specs=[per_query, per_key, per_key, gain, gain],
            scratch_shapes=[
                pltpu.VMEM((seq, hp * HD), BF16),
                pltpu.VMEM((seq, hp * HD), BF16),
                pltpu.VMEM((seq, hp * HD), F32),
                pltpu.VMEM((seq, hp * HD), F32),
                pltpu.VMEM((hp, m, HD), F32),
            ],
        ),
        compiler_params=pltpu.CompilerParams(vmem_limit_bytes=VMEM_LIMIT),
        cost_estimate=pl.CostEstimate(
            flops=5 * 2 * rows * seq * heads * GROUPS * HD // 2,
            bytes_accessed=2 * (4 * rows * heads * GROUPS * HD + 4 * seq * heads * HD),
            transcendentals=rows * seq * heads * GROUPS // 2,
        ),
        name="attend_back",
    )(ids, order, q_raw, kv_raw, kv_raw, grad_mixed, mixed, lse, cosine, sine, gq, gk)


def project_kernel(own, chip_ref, x_ref, gain_ref, wq_ref, wkv_ref, h_ref, q_ref, kv_ref):
    hidden = normed(x_ref[...].astype(F32), gain_ref[...]).astype(BF16)
    h_ref[...] = hidden
    kv_ref[...] = dot(hidden, wkv_ref[...], NN).astype(BF16)

    @pl.when(pl.program_id(0) < own)
    def _():
        q_ref[...] = dot(hidden, wq_ref[...], NN).astype(BF16)


def project(chip, x_all, gain, w_all, chip_rows):
    seq, width = x_all.shape
    size = min(ROW_TILE, chip_rows)
    own, tiles = chip_rows // size, seq // size
    at = lambda i, chip: ((i + chip[0] * own) % tiles, 0)
    weight = lambda col: pl.BlockSpec((width, width), lambda i, chip: (0, col), pipeline_mode=pl.Buffered(1))
    return pl.pallas_call(
        functools.partial(project_kernel, own),
        out_shape=[
            jax.ShapeDtypeStruct((seq, width), BF16),
            jax.ShapeDtypeStruct((chip_rows, width), BF16),
            jax.ShapeDtypeStruct((seq, width), BF16),
        ],
        grid_spec=pltpu.PrefetchScalarGridSpec(
            num_scalar_prefetch=1,
            grid=(tiles,),
            in_specs=[
                pl.BlockSpec((size, width), at),
                pl.BlockSpec((1, width), lambda i, chip: (0, 0)),
                weight(0),
                weight(1),
            ],
            out_specs=[
                pl.BlockSpec((size, width), at),
                pl.BlockSpec((size, width), lambda i, chip: (jnp.minimum(i, own - 1), 0)),
                pl.BlockSpec((size, width), at),
            ],
        ),
        compiler_params=pltpu.CompilerParams(vmem_limit_bytes=VMEM_LIMIT),
        name="project",
    )(chip, x_all, gain, w_all, w_all)


def project_back_kernel(own, chip_ref, dq_ref, dk_ref, dv_ref, x_ref, wq_ref, wk_ref, wv_ref, p_ref, g_ref, acc_ref):
    i = pl.program_id(0)
    acc_ref[...] = dot(dk_ref[...], wk_ref[...], NT) + dot(dv_ref[...], wv_ref[...], NT)

    @pl.when(i < own)
    def _():
        acc_ref[...] += dot(dq_ref[...], wq_ref[...], NT)

    @pl.when(i == 0)
    def _():
        g_ref[...] = jnp.zeros_like(g_ref)

    part = acc_ref[...]
    p_ref[...] = part.astype(BF16)
    g_ref[...] += jnp.sum(part * normed(x_ref[...].astype(F32), 1.0), axis=0, keepdims=True)


def project_back(chip, dq, dk, dv, x_all, w_all):
    seq, width = x_all.shape
    chip_rows, kv = dq.shape[0], dk.shape[1]
    size = min(ROW_TILE, chip_rows)
    own, tiles = chip_rows // size, seq // size
    at = lambda i, chip: ((i + chip[0] * own) % tiles, 0)
    weight = lambda cols, col: pl.BlockSpec((width, cols), lambda i, chip: (0, col), pipeline_mode=pl.Buffered(1))
    return pl.pallas_call(
        functools.partial(project_back_kernel, own),
        out_shape=[jax.ShapeDtypeStruct((seq, width), BF16), jax.ShapeDtypeStruct((1, width), F32)],
        grid_spec=pltpu.PrefetchScalarGridSpec(
            num_scalar_prefetch=1,
            grid=(tiles,),
            in_specs=[
                pl.BlockSpec((size, width), lambda i, chip: (jnp.minimum(i, own - 1), 0)),
                pl.BlockSpec((size, kv), at),
                pl.BlockSpec((size, kv), at),
                pl.BlockSpec((size, width), at),
                weight(width, 0),
                weight(kv, width // kv),
                weight(kv, width // kv + 1),
            ],
            out_specs=[
                pl.BlockSpec((size, width), at),
                pl.BlockSpec((1, width), lambda i, chip: (0, 0)),
            ],
            scratch_shapes=[pltpu.VMEM((size, width), F32)],
        ),
        compiler_params=pltpu.CompilerParams(vmem_limit_bytes=VMEM_LIMIT),
        name="project_back",
    )(chip, dq, dk, dv, x_all, w_all, w_all, w_all)


def feed_kernel(x_ref, p0_ref, p1_ref, gain_ref, go_ref, w_ref, d_ref, mid_ref, sec_ref, act_ref, gg_ref):
    count = x_ref.shape[0]
    size = min(ROW_TILE, count)
    tile = lambda i: pl.ds(pl.multiple_of(i * size, size), size)

    @pl.when(pl.program_id(0) == 0)
    def _():
        def start(i, _):
            rows = tile(i)
            middle = x_ref[rows, :].astype(F32) + (p0_ref[rows, :].astype(F32) + p1_ref[rows, :].astype(F32))
            mid_ref[rows, :] = middle
            sec_ref[rows, :] = normed(middle, gain_ref[...]).astype(BF16)
            return 0

        lax.fori_loop(0, count // size, start, 0)

    def body(i, _):
        rows = tile(i)
        both = dot(sec_ref[rows, :], w_ref[...], NN)
        grad = dot(go_ref[rows, :], d_ref[...], NT)
        gate, up = both[:, :FF_TILE], both[:, FF_TILE:]
        sig = jax.nn.sigmoid(gate)
        silu = gate * sig
        act_ref[rows, :] = (silu * up).astype(BF16)
        gg_ref[rows, :FF_TILE] = (grad * up * sig * (1.0 + gate * (1.0 - sig))).astype(BF16)
        gg_ref[rows, FF_TILE:] = (grad * silu).astype(BF16)
        return 0

    lax.fori_loop(0, count // size, body, 0)


def feed(x, p0, p1, gain, go, w_all, at, w_down):
    rows, width = x.shape
    ff = w_down.shape[0]
    whole = lambda: pl.BlockSpec((rows, width), lambda j: (0, 0), pipeline_mode=pl.Buffered(1))
    return pl.pallas_call(
        feed_kernel,
        out_shape=[
            jax.ShapeDtypeStruct((rows, width), F32),
            jax.ShapeDtypeStruct((rows, width), BF16),
            jax.ShapeDtypeStruct((rows, ff), BF16),
            jax.ShapeDtypeStruct((rows, 2 * ff), BF16),
        ],
        grid=(ff // FF_TILE,),
        in_specs=[
            whole(), whole(), whole(),
            pl.BlockSpec((1, width), lambda j: (0, 0)),
            whole(),
            pl.BlockSpec((width, 2 * FF_TILE), lambda j: (0, at // (2 * FF_TILE) + j)),
            pl.BlockSpec((FF_TILE, width), lambda j: (j, 0)),
        ],
        out_specs=[
            pl.BlockSpec((rows, width), lambda j: (0, 0)),
            pl.BlockSpec((rows, width), lambda j: (0, 0)),
            pl.BlockSpec((rows, FF_TILE), lambda j: (0, j)),
            pl.BlockSpec((rows, 2 * FF_TILE), lambda j: (0, j)),
        ],
        compiler_params=pltpu.CompilerParams(vmem_limit_bytes=VMEM_LIMIT),
        name="feed",
    )(x, p0, p1, gain, go, w_all, w_down)


def middle_back_kernel(mid_ref, s0_ref, s1_ref, go_ref, gain_ref, wo_ref, ga_ref, gm_ref, g_ref):
    back, terms = norm_back(mid_ref[...], gain_ref[...], s0_ref[...].astype(F32) + s1_ref[...].astype(F32))
    grad = (go_ref[...].astype(F32) + back).astype(BF16)
    ga_ref[...] = grad
    gm_ref[...] = dot(grad, wo_ref[...], NT).astype(BF16)

    @pl.when(pl.program_id(0) == 0)
    def _():
        g_ref[...] = jnp.zeros_like(g_ref)

    g_ref[...] += jnp.sum(terms, axis=0, keepdims=True)


def middle_back(middle, s0, s1, go, gain, w_out):
    rows, width = middle.shape
    size = min(ROW_TILE, rows)
    row = pl.BlockSpec((size, width), lambda i: (i, 0))
    line = pl.BlockSpec((1, width), lambda i: (0, 0))
    return pl.pallas_call(
        middle_back_kernel,
        out_shape=[
            jax.ShapeDtypeStruct((rows, width), BF16),
            jax.ShapeDtypeStruct((rows, w_out.shape[0]), BF16),
            jax.ShapeDtypeStruct((1, width), F32),
        ],
        grid=(rows // size,),
        in_specs=[row, row, row, row, line, pl.BlockSpec(w_out.shape, lambda i: (0, 0), pipeline_mode=pl.Buffered(1))],
        out_specs=[row, pl.BlockSpec((size, w_out.shape[0]), lambda i: (i, 0)), line],
        compiler_params=pltpu.CompilerParams(vmem_limit_bytes=VMEM_LIMIT),
        name="middle_back",
    )(middle, s0, s1, go, gain, w_out)


def peers():
    dp, ctx = lax.axis_index("dp"), lax.axis_index("ctx")
    to = lambda d, k: (jnp.bitwise_xor(dp, d), jnp.bitwise_xor(ctx, k))
    return dp, ctx, to


def greet(devices):
    barrier = pltpu.get_barrier_semaphore()
    for device in devices:
        pl.semaphore_signal(barrier, inc=1, device_id=device, device_id_type=MESH)
    pl.semaphore_wait(barrier, len(devices))


def sender(send_sem, recv_sem):
    made = []

    def send(src, dst, device):
        i = len(made)
        copy = pltpu.make_async_remote_copy(
            src_ref=src, dst_ref=dst, send_sem=send_sem.at[i], recv_sem=recv_sem.at[i],
            device_id=device, device_id_type=MESH,
        )
        copy.start()
        made.append(copy)
        return copy

    return send, made


def gather_kernel(pk_ref, wo_ref, tok_ref, go_ref, w_ref, x_ref, g_ref, send_sem, recv_sem, local_sem):
    dp, ctx, to = peers()
    c, z = ctx % 2, ctx // 2
    which, me = ctx // 4, ctx % 4
    inner = jnp.logical_or(z == 1, z == 2)
    greet([to(0, 1), to(0, 2), to(0, 4), to(0, 6), to(1, 0), to(2, 0)])
    send, made = sender(send_sem, recv_sem)
    sib, nbr, far, across, xn, yn = to(0, 1), to(0, 2), to(0, 4), to(0, 6), to(1, 0), to(2, 0)
    rows, cols = pk_ref.shape[1:]

    place = w_ref.at[dp, z, pl.ds(c * rows, rows), pl.ds(0, cols)]
    local = [
        pltpu.make_async_copy(pk_ref.at[c], place, local_sem.at[0]),
        pltpu.make_async_copy(wo_ref, w_ref.at[dp, z, :, pl.ds(cols, wo_ref.shape[1])], local_sem.at[1]),
        pltpu.make_async_copy(tok_ref.at[which], x_ref.at[me, 0], local_sem.at[2]),
        pltpu.make_async_copy(go_ref.at[which], g_ref.at[c, 0], local_sem.at[3]),
    ]
    for copy in local:
        copy.start()
    cross = send(pk_ref.at[1 - c], place, sib)
    for copy in local:
        copy.wait()
    cross.wait_recv()
    done = []

    def half(h, q, zz):
        return w_ref.at[q, zz, pl.ds(h * rows, rows)]

    first = []

    def spread(zz):
        low, high = half(0, dp, zz), half(1, dp, zz)
        first.append((send(low, low, yn), low, half(0, jnp.bitwise_xor(dp, 2), zz), xn))
        first.append((send(high, high, xn), high, half(1, jnp.bitwise_xor(dp, 1), zz), yn))

    def pass_on():
        for copy, own, part, device in first[:2]:
            done.append(send(own, own, device))
            copy.wait_recv()
            done.append(send(part, part, device))
        del first[:2]

    z_one = jnp.bitwise_xor(z, 1)
    z_near = jnp.bitwise_xor(z, jnp.where(inner, 3, 2))
    z_far = jnp.bitwise_xor(z, jnp.where(inner, 2, 3))
    relayed = []

    def relay(slot, source, device):
        copy = pltpu.make_async_remote_copy(
            src_ref=w_ref.at[dp, source], dst_ref=w_ref.at[dp, source],
            send_sem=send_sem.at[send_sem.shape[0] - 4 + len(relayed)],
            recv_sem=recv_sem.at[send_sem.shape[0] - 2 + slot],
            device_id=device, device_id_type=MESH,
        )
        relayed.append(copy)
        pl.when(inner)(copy.start)
        return copy

    step = send(w_ref.at[dp, z], w_ref.at[dp, z], nbr)
    near = relay(0, z, across)
    spread(z)
    pass_on()
    step.wait_recv()
    far_block = relay(1, z_one, across)
    spread(z_one)
    near.wait_recv()
    relay(0, z_near, nbr)
    spread(z_near)
    pass_on()
    far_block.wait_recv()
    relay(1, z_far, nbr)
    spread(z_far)
    swap = send(tok_ref.at[1 - which], x_ref.at[me, 1], far)
    mine_nbr = send(tok_ref.at[which], x_ref.at[me, 0], nbr)
    done += [send(tok_ref.at[which], x_ref.at[me, 0], sib), send(go_ref.at[which], g_ref.at[c, 0], sib)]
    pass_on()
    swap.wait_recv()
    done.append(send(x_ref.at[me, 1], x_ref.at[me, 1], sib))
    swap_nbr = send(x_ref.at[me, 1], x_ref.at[me, 1], nbr)
    go_swap = send(go_ref.at[1 - which], g_ref.at[c, 1], far)
    pass_on()
    other = jnp.bitwise_xor(me, 2)
    mine_nbr.wait_recv()
    done.append(send(x_ref.at[other, 0], x_ref.at[other, 0], sib))
    swap_nbr.wait_recv()
    done.append(send(x_ref.at[other, 1], x_ref.at[other, 1], sib))
    go_swap.wait_recv()
    done.append(send(g_ref.at[c, 1], g_ref.at[c, 1], sib))
    for copy in done:
        copy.wait_recv()
    for copy in made:
        copy.wait_send()

    @pl.when(inner)
    def _():
        for copy in relayed:
            copy.wait_send()


def gather(packed, w_out, tokens, grad_out):
    rows, cols = 2 * packed.shape[1], packed.shape[2] + w_out.shape[1]
    slots, width = tokens.shape[1:]
    copies = 36 + 4
    anywhere = pl.BlockSpec(memory_space=pl.ANY)
    near = pl.BlockSpec(memory_space=pltpu.VMEM)
    w, x, g = pl.pallas_call(
        gather_kernel,
        out_shape=[
            jax.ShapeDtypeStruct((4, 4, rows, cols), BF16),
            jax.ShapeDtypeStruct((4, 2, slots, width), BF16),
            jax.ShapeDtypeStruct((2, 2, slots, width), BF16),
        ],
        in_specs=[near] * 4,
        out_specs=[anywhere] * 3,
        scratch_shapes=[
            pltpu.SemaphoreType.DMA((copies,)),
            pltpu.SemaphoreType.DMA((copies,)),
            pltpu.SemaphoreType.DMA((4,)),
        ],
        compiler_params=pltpu.CompilerParams(
            collective_id=0, has_side_effects=True, vmem_limit_bytes=VMEM_LIMIT
        ),
        name="gather",
    )(packed, w_out, tokens, grad_out)
    return w.reshape(16 * rows, cols), x.reshape(-1, width), g.reshape(-1, width)


def reduce_kernel(n_in, *refs):
    g_refs, (part_ref, x_ref, ga_ref, gain_ref) = refs[:n_in], refs[n_in : n_in + 4]
    o_ref, s_ref, ig_ref = refs[n_in + 4 : n_in + 7]
    (
        g_ref, in_a, in_b, mid_a, mid_b, got_a, got_b, out3, in3,
        mine_ref, sib_ref, give_ref, nbr_ref, back_ref, send_sem, recv_sem, local_sem,
    ) = refs[n_in + 7 :]
    dp, ctx, to = peers()
    c, z = ctx % 2, ctx // 2
    which, chip = ctx // 4, z % 2
    x, y = dp % 2, dp // 2
    greet([to(0, 1), to(0, 2), to(0, 4), to(0, 6), to(1, 0), to(2, 0)])
    send, made = sender(send_sem, recv_sem)
    sib, nbr, far, xn, yn = to(0, 1), to(0, 2), to(0, 4), to(1, 0), to(2, 0)
    hr = g_ref.shape[3] // 2
    at, local = 0, []
    for i, ref in enumerate(g_refs):
        width = ref.shape[-1]
        local.append(pltpu.make_async_copy(ref, g_ref.at[:, :, :, :, pl.ds(at, width)], local_sem.at[i]))
        at += width
    local.append(pltpu.make_async_copy(part_ref.at[:, c], mine_ref, local_sem.at[n_in]))
    for copy in local:
        copy.start()
    cross = send(part_ref.at[:, 1 - c], sib_ref, sib)
    for copy in local:
        copy.wait()
    low, high = pl.ds(0, hr), pl.ds(hr, hr)
    order = [jnp.bitwise_xor(z, k) for k in (2, 3, 1, 0)]
    a_in, b_in, a_mid, b_mid, last = [], [], [], [], []
    size = 64
    tile = lambda i: pl.ds(pl.multiple_of(i * size, size), size)
    count = mine_ref.shape[1]

    def enter(k):
        a_in.append(send(g_ref.at[:, 1 - x, order[k], low], in_a.at[k], xn))
        b_in.append(send(g_ref.at[1 - y, :, order[k], high], in_b.at[k], yn))

    def middle(k):
        add = lambda p, q: (p.astype(F32) + q.astype(F32)).astype(BF16)
        a_in[k].wait_recv()
        mid_a[k] = add(g_ref[1 - y, x, order[k], 0:hr], in_a[k, 1 - y])
        a_mid.append(send(mid_a.at[k], got_a.at[k], yn))
        b_in[k].wait_recv()
        mid_b[k] = add(g_ref[y, 1 - x, order[k], hr:], in_b[k, 1 - x])
        b_mid.append(send(mid_b.at[k], got_b.at[k], xn))

    def leave(k):
        add = lambda p, q, r: (p.astype(F32) + q.astype(F32) + r.astype(F32)).astype(BF16)
        a_mid[k].wait_recv()
        out3[k, 0:hr] = add(g_ref[y, x, order[k], 0:hr], in_a[k, y], got_a[k])
        b_mid[k].wait_recv()
        out3[k, hr:] = add(g_ref[y, x, order[k], hr:], in_b[k, x], got_b[k])
        if k < 3:
            last.append(send(out3.at[k], in3.at[k], to(0, 2 * (2, 3, 1)[k])))

    enter(0)
    enter(1)
    cross.wait_recv()

    def give(i, _):
        rows = tile(i)
        give_ref[rows] = (mine_ref[1 - chip, rows].astype(F32) + sib_ref[1 - chip, rows].astype(F32)).astype(BF16)
        return 0

    lax.fori_loop(0, count // size, give, 0)
    swap = send(give_ref, nbr_ref, nbr)
    middle(0)
    enter(2)
    middle(1)
    enter(3)
    leave(0)
    middle(2)
    leave(1)
    swap.wait_recv()

    def back(i, _):
        rows = tile(i)
        grad = mine_ref[chip, rows].astype(F32) + sib_ref[chip, rows].astype(F32) + nbr_ref[rows].astype(F32)
        through, _terms = norm_back(x_ref[rows, :].astype(F32), gain_ref[...], grad)
        back_ref[rows] = (ga_ref[rows, :].astype(F32) + through).astype(BF16)
        return 0

    lax.fori_loop(0, count // size, back, 0)
    slots = ig_ref.shape[1]
    home = send(back_ref.at[pl.ds(slots, slots)], ig_ref.at[which], far)
    keep = pltpu.make_async_copy(back_ref.at[pl.ds(0, slots)], ig_ref.at[which], local_sem.at[0])
    keep.start()
    middle(3)
    leave(2)
    leave(3)
    for copy in last:
        copy.wait_recv()
    o_ref[...] = (
        out3[3].astype(F32) + in3[0].astype(F32) + in3[1].astype(F32) + in3[2].astype(F32)
    ).astype(BF16)
    other = send(o_ref.at[pl.ds((1 - c) * hr, hr), pl.ds(0, s_ref.shape[1])], s_ref, sib)
    keep.wait()
    other.wait_recv()
    home.wait_recv()
    for copy in made:
        copy.wait_send()


def reduce(grads, near_cols, part, x, grad_middle, gain):
    rows = grads[0].shape[0] // 16
    cols = sum(g.shape[1] for g in grads)
    grads = [g.reshape(2, 2, 4, rows, g.shape[1]) for g in grads]
    count, width = x.shape
    copies = 23
    anywhere = pl.BlockSpec(memory_space=pl.ANY)
    near = pl.BlockSpec(memory_space=pltpu.VMEM)
    return pl.pallas_call(
        functools.partial(reduce_kernel, len(grads)),
        out_shape=[
            jax.ShapeDtypeStruct((rows, cols), BF16),
            jax.ShapeDtypeStruct((rows // 2, near_cols), BF16),
            jax.ShapeDtypeStruct((2, count // 2, width), BF16),
        ],
        in_specs=[anywhere] * (len(grads) + 1) + [near] * 3,
        out_specs=[near, anywhere, anywhere],
        scratch_shapes=[
            pltpu.VMEM((2, 2, 4, rows, cols), BF16),
            pltpu.VMEM((4, 2, rows // 2, cols), BF16),
            pltpu.VMEM((4, 2, rows // 2, cols), BF16),
        ]
        + [pltpu.VMEM((4, rows // 2, cols), BF16)] * 4
        + [
            pltpu.VMEM((4, rows, cols), BF16),
            pltpu.VMEM((3, rows, cols), BF16),
            pltpu.VMEM((2, count, width), BF16),
            pltpu.VMEM((2, count, width), BF16),
            pltpu.VMEM((count, width), BF16),
            pltpu.VMEM((count, width), BF16),
            pltpu.VMEM((count, width), BF16),
            pltpu.SemaphoreType.DMA((copies,)),
            pltpu.SemaphoreType.DMA((copies,)),
            pltpu.SemaphoreType.DMA((len(grads) + 1,)),
        ],
        compiler_params=pltpu.CompilerParams(
            collective_id=1, has_side_effects=True, vmem_limit_bytes=VMEM_LIMIT
        ),
        name="reduce",
    )(*grads, part.reshape(2, 2, count, width), x, grad_middle, gain)


def by_core(c, own, other):
    return jnp.where(c == 0, jnp.stack([own, other]), jnp.stack([other, own]))


def layer(
    n_dp, n, tokens, positions, w_query, w_key, w_value, w_out, w_gate, w_up, w_down,
    attn_gain, mlp_gain, q_gain, k_gain, grad_out,
):
    axes = ("dp", "ctx")
    slots, width = tokens.shape[1:]
    seq = positions.shape[1]
    span = slots // 2
    half = n // 2
    chips = n_dp * half
    ctx = lax.axis_index("ctx")
    c = ctx % 2
    which = ctx // half
    r_in, r_out, r_down = w_query.shape[0], w_out.shape[0], w_down.shape[0]
    ff = w_gate.shape[1]
    ff_c = ff // 2
    q_c, kv_c = H * HD // 2, KV * HD // 2

    to_sibling = [(i, i ^ 1) for i in range(n)]
    to_partner = [(i, (i + half) % n) for i in range(n)]
    halves = [list(range(half)), list(range(half, n))]
    same_core = [list(range(0, n, 2)), list(range(1, n, 2))]
    sibling = lambda v: lax.ppermute(v, "ctx", to_sibling)
    partner = lambda v: lax.ppermute(v, "ctx", to_partner)

    def placed(values):
        mine = lax.dynamic_index_in_dim(values, which, 0, False)
        other = lax.dynamic_index_in_dim(values, 1 - which, 0, False)
        return jnp.concatenate([mine, partner(other)], axis=0)

    gains = jnp.concatenate(
        [
            attn_gain[:, None],
            mlp_gain[:, None],
            jnp.pad(q_gain, (0, r_in - q_gain.shape[0]))[:, None],
            jnp.pad(k_gain, (0, r_in - k_gain.shape[0]))[:, None],
            jnp.zeros((r_in, 124), BF16),
        ],
        axis=1,
    )
    tall = (n_dp, n) == (4, 8)
    qkv_halves = [
        jnp.concatenate(
            [
                w_query[:, i * q_c : (i + 1) * q_c],
                w_key[:, i * kv_c : (i + 1) * kv_c],
                w_value[:, i * kv_c : (i + 1) * kv_c],
            ],
            axis=1,
        )
        for i in range(2)
    ]

    def ff_order(shard):
        return shard.reshape(r_in, chips, 2, r_down).transpose(2, 0, 1, 3).reshape(2, r_in, ff_c)

    gate_order, up_order = ff_order(w_gate), ff_order(w_up)
    qkv_c = q_c + 2 * kv_c
    all_c = qkv_c + 2 * ff_c
    by_tile = lambda v: v.reshape(2, r_in, ff_c // FF_TILE, FF_TILE)
    gu_shard = jnp.stack([by_tile(gate_order), by_tile(up_order)], axis=3).reshape(2, r_in, 2 * ff_c)
    packed = jnp.stack([jnp.concatenate([qkv_halves[i], gu_shard[i], gains], axis=1) for i in range(2)])
    if tall:
        w_all, x_all, go_chip = gather(packed, w_out, tokens, grad_out)
        x_own = lax.dynamic_slice_in_dim(x_all, (ctx % half) * 2 * slots, 2 * slots, 0)
        out_rows = w_all[:, all_c + HD :].reshape(2, -1, r_out, width)
        out_keep = lax.dynamic_index_in_dim(out_rows, c, 0, False)
        out_give = lax.dynamic_index_in_dim(out_rows, 1 - c, 0, False)
        w_out_c = by_core(c, out_keep, sibling(out_give)).transpose(1, 0, 2, 3).reshape(q_c, width)
        w_down, w_all = lax.optimization_barrier((w_down, w_all))
    else:
        both = lax.all_gather(packed, axes, axis=1, tiled=True)
        w_all = lax.dynamic_index_in_dim(both, c, 0, False)
        out_all = lax.all_gather(w_out, axes, axis=0, tiled=True)
        w_out_c = lax.dynamic_slice_in_dim(out_all, c * q_c, q_c, 0)
        x_own = placed(tokens)
        x_all = lax.all_gather(x_own, "ctx", axis=0, tiled=True, axis_index_groups=halves)
        go_own = placed(grad_out)
        go_chip = by_core(c, go_own, sibling(go_own)).reshape(4 * slots, width)
    down_all = lax.all_gather(w_down, axes, axis=0, tiled=True).reshape(chips, 2, r_down, width)
    w_down_c = lax.dynamic_index_in_dim(down_all, c, 1, False).reshape(ff_c, width)
    g_cols = w_all[:, all_c : all_c + HD].astype(F32)
    gain_attn = g_cols[:, 0][None]
    gain_mlp = g_cols[:, 1][None]
    per_head = g_cols.reshape(n_dp * n, r_in, HD)[:, : q_gain.shape[0]].reshape(HD, HD)
    gain_q = per_head[:, 2][None]
    gain_k = per_head[:, 3][None]

    chip = (ctx % half) // 2
    chip_rows = 4 * slots
    x_chip = lax.dynamic_slice_in_dim(x_all, chip * chip_rows, chip_rows, 0)
    slot_ids = lax.dynamic_index_in_dim(positions, which, 0, False).reshape(2 * n, span)[:, 0] // span
    places = np.stack(
        [
            [s for d in side for k in (d, (d + half) % n) for s in (2 * k, 2 * k + 1)]
            for side in halves
        ]
    ).astype(np.int32)
    ids_all = slot_ids[lax.dynamic_index_in_dim(jnp.asarray(places), which, 0, False)]
    steps = jnp.arange(2 * n, dtype=jnp.int32)
    order = jnp.sum(jnp.where(ids_all[None, :] == steps[:, None], steps[None, :], 0), axis=1).astype(jnp.int32)
    ids = lax.dynamic_slice_in_dim(ids_all, chip * 8, 8, 0)
    cosine, sine = rope_tables(seq)

    chip_at = chip.astype(jnp.int32).reshape(1)
    hidden_all, q_raw, kv_raw = project(chip_at, x_all, gain_attn, w_all, chip_rows)
    hidden = lax.dynamic_slice_in_dim(hidden_all, chip * chip_rows, chip_rows, 0)
    mixed, lse = attend(ids, order, q_raw, kv_raw, cosine, sine, gain_q, gain_k, span)
    proj = dot(mixed, w_out_c, NN, BF16)
    middle, second, activated, grad_gu = feed(
        x_chip, proj, sibling(proj), gain_mlp, go_chip, w_all, qkv_c, w_down_c
    )
    down = dot(activated, w_down_c, NN, BF16).reshape(2, 2 * slots, width)
    down_own = lax.dynamic_index_in_dim(down, c, 0, False)
    down_other = sibling(lax.dynamic_index_in_dim(down, 1 - c, 0, False))
    own_rows = lambda v: lax.dynamic_slice_in_dim(v, c * 2 * slots, 2 * slots, 0)
    result = (own_rows(middle) + (down_own.astype(F32) + down_other.astype(F32))).astype(BF16)

    def returned(rows):
        mine, back = rows[:slots], partner(rows[slots:])
        return jnp.where(which == 0, jnp.stack([mine, back]), jnp.stack([back, mine]))


    second_part = dot(grad_gu, w_all[:, qkv_c:all_c], NT, BF16)
    grad_gu_w = dot(second, grad_gu, TN, BF16)
    grad_down_w = dot(activated, go_chip, TN, BF16)
    grad_attn, grad_mixed, mlp_gain_sum = middle_back(
        middle, second_part, sibling(second_part), go_chip, gain_mlp, w_out_c
    )
    grad_mlp_gain = jnp.where(c == 0, mlp_gain_sum[0], 0.0)

    def reduced(grad):
        part = lax.psum_scatter(grad, "dp", scatter_dimension=0, tiled=True)
        return lax.psum_scatter(part, "ctx", scatter_dimension=0, tiled=True, axis_index_groups=same_core)

    sum_gu = reduced(grad_gu_w)
    sum_down = reduced(grad_down_w)

    grad_out_w = dot(mixed, grad_attn, TN, BF16)
    result, grad_mixed = lax.optimization_barrier((result, grad_mixed))
    output = returned(result)
    dq, dk, dv, dgq, dgk = attend_back(
        ids, order, q_raw, kv_raw, grad_mixed, mixed, lse, cosine, sine, gain_q, gain_k, span
    )
    output, dq = lax.optimization_barrier((output, dq))
    part_all, attn_gain_sum = project_back(chip_at, dq, dk, dv, x_all, w_all)
    grad_q_w = dot(hidden, dq, TN, BF16)
    grad_k_w = dot(hidden_all, dk, TN, BF16)
    grad_v_w = dot(hidden_all, dv, TN, BF16)
    out_w = grad_out_w.reshape(-1, 2, r_out, width)
    out_mine = lax.dynamic_index_in_dim(out_w, c, 1, False)
    out_recv = sibling(lax.dynamic_index_in_dim(out_w, 1 - c, 1, False))
    grad_out_w = by_core(c, out_mine, out_recv).reshape(chips * r_out, width)

    apart = width // HD
    spaced = lambda v: jnp.pad(v.reshape(HD, 1), ((0, 0), (0, apart - 1))).reshape(width, 1)
    gain_cols = jnp.concatenate(
        [attn_gain_sum.T, grad_mlp_gain[:, None], spaced(dgq), spaced(dgk), jnp.zeros((width, HD - 4), F32)],
        axis=1,
    ).astype(BF16)
    grads = [grad_q_w, grad_k_w, grad_v_w, gain_cols, grad_out_w]
    near_c = qkv_c + HD
    own_grad = own_rows(grad_attn)
    by_rows = lambda v: lax.dynamic_index_in_dim(v.reshape(2, r_in, -1), c, 0, False)

    def columns(sums):
        other = lax.dynamic_index_in_dim(sums.reshape(2, r_in, -1), 1 - c, 0, False)
        return by_core(c, by_rows(sums), sibling(other)).astype(F32)

    if tall:
        sums, near_sums, input_grad = reduce(grads, near_c, part_all, x_own, own_grad, gain_attn)
        qkv_own = by_core(c, by_rows(sums[:, :near_c]), near_sums).astype(F32)
    else:
        sums = jnp.concatenate([reduced(g) for g in grads], axis=1)
        qkv_own = columns(sums[:, :near_c])
        grad_hidden = lax.psum_scatter(
            part_all, "ctx", scatter_dimension=0, tiled=True, axis_index_groups=halves
        ).astype(F32)
        back, _terms = norm_back(x_own.astype(F32), gain_attn, grad_hidden)
        input_grad = returned((own_grad.astype(F32) + back).astype(BF16))
    sum_out = sums[:, near_c:]
    gain_own = jnp.sum(qkv_own[:, :, qkv_c : qkv_c + 4], axis=0)
    gu_own = columns(sum_gu).reshape(2, r_in, ff_c // FF_TILE, 2, FF_TILE)
    beside = lambda v: v.transpose(1, 0, 2).reshape(r_in, -1)
    ff_back = lambda v: v.reshape(2, r_in, chips, r_down).transpose(1, 2, 0, 3).reshape(r_in, ff)
    return (
        output,
        input_grad,
        beside(qkv_own[:, :, :q_c]),
        beside(qkv_own[:, :, q_c : q_c + kv_c]),
        beside(qkv_own[:, :, q_c + kv_c : qkv_c]),
        sum_out.astype(F32),
        ff_back(gu_own[:, :, :, 0]),
        ff_back(gu_own[:, :, :, 1]),
        sum_down.astype(F32),
        gain_own[:, 0],
        gain_own[:, 1],
        gain_own[::apart, 2],
        gain_own[::apart, 3],
    )


def solution(mesh):
    rows = P(("dp", "ctx"), None)
    gain = P(("dp", "ctx"))
    acts = P("dp", "ctx", None)
    return jax.shard_map(
        functools.partial(layer, mesh.shape["dp"], mesh.shape["ctx"]),
        mesh=mesh,
        in_specs=(acts, P("dp", None)) + (rows,) * 7 + (gain,) * 4 + (acts,),
        out_specs=(acts, acts) + (rows,) * 7 + (gain,) * 4,
        check_vma=False,
    )
```

```python
import functools

import jax
import jax.numpy as jnp
import numpy as np
from jax import lax
from jax.experimental import pallas as pl
from jax.experimental.pallas import tpu as pltpu
from jax.sharding import PartitionSpec as P

H = 16
KV = 8
HD = 128
GROUPS = H // KV
EPSILON = 1e-06
THETA = 1000000.0
LOG2E = 1.4426950408889634
KEY_TILE = 512
ROW_TILE = 256
FF_TILE = 512
FWD_HEADS = 4
BACK_HEADS = 4
VMEM_LIMIT = 48 * 1024 * 1024
MESH = pl.DeviceIdType.MESH
F32 = jnp.float32
BF16 = jnp.bfloat16


def normed(values, weights):
    return values * lax.rsqrt(jnp.mean(values * values, axis=-1, keepdims=True) + EPSILON) * weights


def norm_back(values, weights, grad):
    r = lax.rsqrt(jnp.mean(values * values, axis=-1, keepdims=True) + EPSILON)
    unit = values * r
    u = grad * weights
    return r * (u - unit * jnp.mean(u * unit, axis=-1, keepdims=True)), grad * unit


def rope_tables(seq):
    half = HD // 2
    inverse = (THETA ** (-(np.arange(half, dtype=np.float32) * np.float32(2.0) / np.float32(HD)))).astype(np.float32)
    angles = np.arange(seq, dtype=np.float32)[:, None] * inverse[None, :]
    cosine, sine = np.cos(angles), np.sin(angles)
    return (
        jnp.asarray(np.concatenate([cosine, cosine], axis=-1).astype(np.float32)),
        jnp.asarray(np.concatenate([-sine, sine], axis=-1).astype(np.float32)),
    )


def dot(a, b, dims, out=F32):
    return lax.dot_general(a, b, (dims, ((), ())), preferred_element_type=out)


NN = ((1,), (0,))
NT = ((1,), (1,))
TN = ((0,), (0,))


def row_mean(values):
    return dot(values.astype(BF16), jnp.full((HD, HD), 1.0 / HD, BF16), NN)


def unit_rows(raw):
    r = lax.rsqrt(row_mean(raw * raw) + EPSILON)
    return raw * r, r


def rope(values, cosine, sine):
    return values * cosine + pltpu.roll(values, HD // 2, 1) * sine


def rope_back(values, cosine, sine):
    return values * cosine - pltpu.roll(values, HD // 2, 1) * sine


def lanes(head, width=HD):
    return slice(head * width, (head + 1) * width)


def prepare_keys(span, order_ref, k_ref, v_ref, cos_ref, sin_ref, gk_ref, ks_ref, vs_ref):
    def body(i, _):
        rows = pl.ds(pl.multiple_of(i * span, span), span)
        source = pl.ds(pl.multiple_of(order_ref[i] * span, span), span)
        for p in range(k_ref.shape[1] // HD):
            unit, _r = unit_rows(k_ref[source, lanes(p)].astype(F32))
            ks_ref[rows, lanes(p)] = rope(unit * gk_ref[...], cos_ref[rows, :], sin_ref[rows, :]).astype(BF16)
        vs_ref[rows, :] = v_ref[source, :]
        return 0

    lax.fori_loop(0, k_ref.shape[0] // span, body, 0)


def query_block(q_ref, p, rows, places, cos_ref, sin_ref, gq_ref):
    units, scales, parts = [], [], []
    for g in range(GROUPS):
        unit, r = unit_rows(q_ref[rows, lanes(p * GROUPS + g)].astype(F32))
        turned = rope(unit * gq_ref[...], cos_ref[places, :], sin_ref[places, :])
        units.append(unit)
        scales.append(r)
        parts.append((turned * (LOG2E * HD**-0.5)).astype(BF16))
    return units, scales, jnp.concatenate(parts, axis=0)


def seen(shape, t, b, span, key_axis):
    at = t * KEY_TILE + lax.broadcasted_iota(jnp.int32, shape, key_axis)
    own = b * span + lax.broadcasted_iota(jnp.int32, shape, 1 - key_axis) % span
    return at <= own


def attend_kernel(
    span, ids_ref, order_ref, q_ref, k_ref, v_ref, cos_ref, sin_ref, gq_ref, gk_ref,
    o_ref, lse_ref, ks_ref, vs_ref, acc_ref, sum_ref,
):
    prepare_keys(span, order_ref, k_ref, v_ref, cos_ref, sin_ref, gk_ref, ks_ref, vs_ref)
    m = GROUPS * span
    heads = range(FWD_HEADS)

    def block(j, _):
        b = ids_ref[j]
        rows = pl.ds(pl.multiple_of(j * span, span), span)
        places = pl.ds(pl.multiple_of(b * span, span), span)
        q2 = [query_block(q_ref, p, rows, places, cos_ref, sin_ref, gq_ref)[2] for p in heads]
        acc_ref[...] = jnp.zeros_like(acc_ref)
        sum_ref[...] = jnp.zeros_like(sum_ref)

        def tile(t, masked):
            keys = pl.ds(pl.multiple_of(t * KEY_TILE, KEY_TILE), KEY_TILE)
            scores = [dot(q2[p], ks_ref[keys, lanes(p)], NT) for p in heads]
            keep = seen(scores[0].shape, t, b, span, 1) if masked else None
            for p in heads:
                e = jnp.exp2(scores[p])
                if masked:
                    e = jnp.where(keep, e, 0.0)
                part = e[:, 0:HD]
                for i in range(1, KEY_TILE // HD):
                    part = part + e[:, lanes(i)]
                sum_ref[p] += part
                acc_ref[p] += dot(e.astype(BF16), vs_ref[keys, lanes(p)], NN)

        last = (b * span) // KEY_TILE
        lax.fori_loop(0, last, lambda t, _: (tile(t, False), 0)[1], 0)
        tile(last, True)
        for p in heads:
            total = jnp.sum(sum_ref[p], axis=-1, keepdims=True)
            mixed = acc_ref[p] * (1.0 / total)
            for g in range(GROUPS):
                o_ref[rows, lanes(p * GROUPS + g)] = mixed[g * span : (g + 1) * span].astype(BF16)
            wide = jnp.broadcast_to(jnp.log2(total), (m, HD))
            lse_ref[p, j] = jnp.transpose(wide)[0:1, :]
        return 0

    lax.fori_loop(0, q_ref.shape[0] // span, block, 0)


def attend(ids, order, q_raw, kv_raw, cosine, sine, gq, gk, span):
    rows = q_raw.shape[0]
    seq = kv_raw.shape[0]
    heads = q_raw.shape[1] // (GROUPS * HD)
    blocks, m = rows // span, GROUPS * span
    hp = FWD_HEADS
    whole = lambda k, ids, order: (0, 0)
    per_query = pl.BlockSpec((rows, hp * GROUPS * HD), lambda k, ids, order: (0, k))
    once = pl.Buffered(1)
    return pl.pallas_call(
        functools.partial(attend_kernel, span),
        out_shape=[
            jax.ShapeDtypeStruct((rows, heads * GROUPS * HD), BF16),
            jax.ShapeDtypeStruct((heads, blocks, 1, m), F32),
        ],
        grid_spec=pltpu.PrefetchScalarGridSpec(
            num_scalar_prefetch=2,
            grid=(heads // hp,),
            in_specs=[
                per_query,
                pl.BlockSpec((seq, hp * HD), lambda k, ids, order: (0, k)),
                pl.BlockSpec((seq, hp * HD), lambda k, ids, order: (0, heads // hp + k)),
                pl.BlockSpec((seq, HD), whole, pipeline_mode=once),
                pl.BlockSpec((seq, HD), whole, pipeline_mode=once),
                pl.BlockSpec((1, HD), whole),
                pl.BlockSpec((1, HD), whole),
            ],
            out_specs=[
                per_query,
                pl.BlockSpec((hp, blocks, 1, m), lambda k, ids, order: (k, 0, 0, 0)),
            ],
            scratch_shapes=[
                pltpu.VMEM((seq, hp * HD), BF16),
                pltpu.VMEM((seq, hp * HD), BF16),
                pltpu.VMEM((hp, m, HD), F32),
                pltpu.VMEM((hp, m, HD), F32),
            ],
        ),
        compiler_params=pltpu.CompilerParams(vmem_limit_bytes=VMEM_LIMIT),
        cost_estimate=pl.CostEstimate(
            flops=2 * 2 * rows * seq * heads * GROUPS * HD,
            bytes_accessed=2 * (2 * rows * heads * GROUPS * HD + 2 * seq * heads * HD),
            transcendentals=rows * seq * heads * GROUPS // 2,
        ),
        name="attend",
    )(ids, order, q_raw, kv_raw, kv_raw, cosine, sine, gq, gk)


def attend_back_kernel(
    span, ids_ref, order_ref, q_ref, k_ref, v_ref, do_ref, o_ref, lse_ref, cos_ref, sin_ref, gq_ref, gk_ref,
    dq_ref, dk_ref, dv_ref, dgq_ref, dgk_ref, ks_ref, vs_ref, dka_ref, dva_ref, dqa_ref,
):
    prepare_keys(span, order_ref, k_ref, v_ref, cos_ref, sin_ref, gk_ref, ks_ref, vs_ref)
    dka_ref[...] = jnp.zeros_like(dka_ref)
    dva_ref[...] = jnp.zeros_like(dva_ref)
    heads = range(BACK_HEADS)

    @pl.when(pl.program_id(0) == 0)
    def _():
        dgq_ref[...] = jnp.zeros_like(dgq_ref)
        dgk_ref[...] = jnp.zeros_like(dgk_ref)

    def block(j, _):
        b = ids_ref[j]
        rows = pl.ds(pl.multiple_of(j * span, span), span)
        places = pl.ds(pl.multiple_of(b * span, span), span)
        q2, do2, delta, lse = [], [], [], []
        for p in heads:
            q2.append(query_block(q_ref, p, rows, places, cos_ref, sin_ref, gq_ref)[2])
            pick = lambda ref: jnp.concatenate([ref[rows, lanes(p * GROUPS + g)] for g in range(GROUPS)], axis=0)
            do2.append(pick(do_ref))
            delta.append(
                jnp.sum(jnp.transpose(do2[p].astype(F32) * pick(o_ref).astype(F32)), axis=0, keepdims=True)
            )
            lse.append(lse_ref[p, j])
        dqa_ref[...] = jnp.zeros_like(dqa_ref)

        def tile(t, masked):
            keys = pl.ds(pl.multiple_of(t * KEY_TILE, KEY_TILE), KEY_TILE)
            kt = [ks_ref[keys, lanes(p)] for p in heads]
            scores = [dot(kt[p], q2[p], NT) for p in heads]
            slopes = [dot(vs_ref[keys, lanes(p)], do2[p], NT) for p in heads]
            keep = seen(scores[0].shape, t, b, span, 0) if masked else None
            for p in heads:
                e = jnp.exp2(scores[p] - lse[p])
                if masked:
                    e = jnp.where(keep, e, 0.0)
                ds = (e * (slopes[p] - delta[p])).astype(BF16)
                dva_ref[keys, lanes(p)] += dot(e.astype(BF16), do2[p], NN)
                dka_ref[keys, lanes(p)] += dot(ds, q2[p], NN)
                dqa_ref[p] += dot(ds, kt[p], TN)

        last = (b * span) // KEY_TILE
        lax.fori_loop(0, last, lambda t, _: (tile(t, False), 0)[1], 0)
        tile(last, True)
        for p in heads:
            units, scales, _q = query_block(q_ref, p, rows, places, cos_ref, sin_ref, gq_ref)
            dq = dqa_ref[p] * HD**-0.5
            for g in range(GROUPS):
                grad = rope_back(dq[g * span : (g + 1) * span], cos_ref[places, :], sin_ref[places, :])
                dgq_ref[...] += jnp.sum(grad * units[g], axis=0, keepdims=True)
                u = grad * gq_ref[...]
                back = scales[g] * (u - units[g] * row_mean(u * units[g]))
                dq_ref[rows, lanes(p * GROUPS + g)] = back.astype(BF16)
        return 0

    lax.fori_loop(0, q_ref.shape[0] // span, block, 0)

    def finish(i, _):
        rows = pl.ds(pl.multiple_of(i * span, span), span)
        source = pl.ds(pl.multiple_of(order_ref[i] * span, span), span)
        for p in heads:
            unit, r = unit_rows(k_ref[source, lanes(p)].astype(F32))
            grad = rope_back(dka_ref[rows, lanes(p)] * (1.0 / LOG2E), cos_ref[rows, :], sin_ref[rows, :])
            dgk_ref[...] += jnp.sum(grad * unit, axis=0, keepdims=True)
            u = grad * gk_ref[...]
            back = r * (u - unit * row_mean(u * unit))
            dk_ref[source, lanes(p)] = back.astype(BF16)
        dv_ref[source, :] = dva_ref[rows, :].astype(BF16)
        return 0

    lax.fori_loop(0, k_ref.shape[0] // span, finish, 0)


def attend_back(ids, order, q_raw, kv_raw, grad_mixed, mixed, lse, cosine, sine, gq, gk, span):
    rows = q_raw.shape[0]
    seq = kv_raw.shape[0]
    heads = q_raw.shape[1] // (GROUPS * HD)
    blocks, m = rows // span, GROUPS * span
    hp = BACK_HEADS
    whole = lambda k, ids, order: (0, 0)
    per_query = pl.BlockSpec((rows, hp * GROUPS * HD), lambda k, ids, order: (0, k))
    per_key = pl.BlockSpec((seq, hp * HD), lambda k, ids, order: (0, k))
    gain = pl.BlockSpec((1, HD), whole)
    once = pl.Buffered(1)
    return pl.pallas_call(
        functools.partial(attend_back_kernel, span),
        out_shape=[
            jax.ShapeDtypeStruct((rows, heads * GROUPS * HD), BF16),
            jax.ShapeDtypeStruct((seq, heads * HD), BF16),
            jax.ShapeDtypeStruct((seq, heads * HD), BF16),
            jax.ShapeDtypeStruct((1, HD), F32),
            jax.ShapeDtypeStruct((1, HD), F32),
        ],
        grid_spec=pltpu.PrefetchScalarGridSpec(
            num_scalar_prefetch=2,
            grid=(heads // hp,),
            in_specs=[
                per_query,
                per_key,
                pl.BlockSpec((seq, hp * HD), lambda k, ids, order: (0, heads // hp + k)),
                per_query,
                per_query,
                pl.BlockSpec((hp, blocks, 1, m), lambda k, ids, order: (k, 0, 0, 0)),
                pl.BlockSpec((seq, HD), whole, pipeline_mode=once),
                pl.BlockSpec((seq, HD), whole, pipeline_mode=once),
                gain,
                gain,
            ],
            out_specs=[per_query, per_key, per_key, gain, gain],
            scratch_shapes=[
                pltpu.VMEM((seq, hp * HD), BF16),
                pltpu.VMEM((seq, hp * HD), BF16),
                pltpu.VMEM((seq, hp * HD), F32),
                pltpu.VMEM((seq, hp * HD), F32),
                pltpu.VMEM((hp, m, HD), F32),
            ],
        ),
        compiler_params=pltpu.CompilerParams(vmem_limit_bytes=VMEM_LIMIT),
        cost_estimate=pl.CostEstimate(
            flops=5 * 2 * rows * seq * heads * GROUPS * HD // 2,
            bytes_accessed=2 * (4 * rows * heads * GROUPS * HD + 4 * seq * heads * HD),
            transcendentals=rows * seq * heads * GROUPS // 2,
        ),
        name="attend_back",
    )(ids, order, q_raw, kv_raw, kv_raw, grad_mixed, mixed, lse, cosine, sine, gq, gk)


def project_kernel(own, chip_ref, x_ref, gain_ref, wq_ref, wkv_ref, h_ref, q_ref, kv_ref):
    hidden = normed(x_ref[...].astype(F32), gain_ref[...]).astype(BF16)
    h_ref[...] = hidden
    kv_ref[...] = dot(hidden, wkv_ref[...], NN).astype(BF16)

    @pl.when(pl.program_id(0) < own)
    def _():
        q_ref[...] = dot(hidden, wq_ref[...], NN).astype(BF16)


def project(chip, x_all, gain, w_all, chip_rows):
    seq, width = x_all.shape
    size = min(ROW_TILE, chip_rows)
    own, tiles = chip_rows // size, seq // size
    at = lambda i, chip: ((i + chip[0] * own) % tiles, 0)
    weight = lambda col: pl.BlockSpec((width, width), lambda i, chip: (0, col), pipeline_mode=pl.Buffered(1))
    return pl.pallas_call(
        functools.partial(project_kernel, own),
        out_shape=[
            jax.ShapeDtypeStruct((seq, width), BF16),
            jax.ShapeDtypeStruct((chip_rows, width), BF16),
            jax.ShapeDtypeStruct((seq, width), BF16),
        ],
        grid_spec=pltpu.PrefetchScalarGridSpec(
            num_scalar_prefetch=1,
            grid=(tiles,),
            in_specs=[
                pl.BlockSpec((size, width), at),
                pl.BlockSpec((1, width), lambda i, chip: (0, 0)),
                weight(0),
                weight(1),
            ],
            out_specs=[
                pl.BlockSpec((size, width), at),
                pl.BlockSpec((size, width), lambda i, chip: (jnp.minimum(i, own - 1), 0)),
                pl.BlockSpec((size, width), at),
            ],
        ),
        compiler_params=pltpu.CompilerParams(vmem_limit_bytes=VMEM_LIMIT),
        name="project",
    )(chip, x_all, gain, w_all, w_all)


def project_back_kernel(own, chip_ref, dq_ref, dk_ref, dv_ref, x_ref, wq_ref, wk_ref, wv_ref, p_ref, g_ref, acc_ref):
    i = pl.program_id(0)
    acc_ref[...] = dot(dk_ref[...], wk_ref[...], NT) + dot(dv_ref[...], wv_ref[...], NT)

    @pl.when(i < own)
    def _():
        acc_ref[...] += dot(dq_ref[...], wq_ref[...], NT)

    @pl.when(i == 0)
    def _():
        g_ref[...] = jnp.zeros_like(g_ref)

    part = acc_ref[...]
    p_ref[...] = part.astype(BF16)
    g_ref[...] += jnp.sum(part * normed(x_ref[...].astype(F32), 1.0), axis=0, keepdims=True)


def project_back(chip, dq, dk, dv, x_all, w_all):
    seq, width = x_all.shape
    chip_rows, kv = dq.shape[0], dk.shape[1]
    size = min(ROW_TILE, chip_rows)
    own, tiles = chip_rows // size, seq // size
    at = lambda i, chip: ((i + chip[0] * own) % tiles, 0)
    weight = lambda cols, col: pl.BlockSpec((width, cols), lambda i, chip: (0, col), pipeline_mode=pl.Buffered(1))
    return pl.pallas_call(
        functools.partial(project_back_kernel, own),
        out_shape=[jax.ShapeDtypeStruct((seq, width), BF16), jax.ShapeDtypeStruct((1, width), F32)],
        grid_spec=pltpu.PrefetchScalarGridSpec(
            num_scalar_prefetch=1,
            grid=(tiles,),
            in_specs=[
                pl.BlockSpec((size, width), lambda i, chip: (jnp.minimum(i, own - 1), 0)),
                pl.BlockSpec((size, kv), at),
                pl.BlockSpec((size, kv), at),
                pl.BlockSpec((size, width), at),
                weight(width, 0),
                weight(kv, width // kv),
                weight(kv, width // kv + 1),
            ],
            out_specs=[
                pl.BlockSpec((size, width), at),
                pl.BlockSpec((1, width), lambda i, chip: (0, 0)),
            ],
            scratch_shapes=[pltpu.VMEM((size, width), F32)],
        ),
        compiler_params=pltpu.CompilerParams(vmem_limit_bytes=VMEM_LIMIT),
        name="project_back",
    )(chip, dq, dk, dv, x_all, w_all, w_all, w_all)


def feed_kernel(chip_ref, x_ref, p0_ref, p1_ref, gain_ref, go_ref, w_ref, d_ref, mid_ref, sec_ref, act_ref, gg_ref):
    count = x_ref.shape[0]
    size = min(ROW_TILE, count)
    tile = lambda i: pl.ds(pl.multiple_of(i * size, size), size)

    @pl.when(pl.program_id(0) == 0)
    def _():
        def start(i, _):
            rows = tile(i)
            middle = x_ref[rows, :].astype(F32) + (p0_ref[rows, :].astype(F32) + p1_ref[rows, :].astype(F32))
            mid_ref[rows, :] = middle
            sec_ref[rows, :] = normed(middle, gain_ref[...]).astype(BF16)
            return 0

        lax.fori_loop(0, count // size, start, 0)

    def body(i, _):
        rows = tile(i)
        both = dot(sec_ref[rows, :], w_ref[...], NN)
        grad = dot(go_ref[rows, :], d_ref[...], NT)
        gate, up = both[:, :FF_TILE], both[:, FF_TILE:]
        sig = jax.nn.sigmoid(gate)
        silu = gate * sig
        act_ref[rows, :] = (silu * up).astype(BF16)
        gg_ref[rows, :FF_TILE] = (grad * up * sig * (1.0 + gate * (1.0 - sig))).astype(BF16)
        gg_ref[rows, FF_TILE:] = (grad * silu).astype(BF16)
        return 0

    lax.fori_loop(0, count // size, body, 0)


def feed(chip, x_all, p0, p1, gain, go, w_all, at, w_down):
    rows, width = go.shape
    ff = w_down.shape[0]
    once = pl.Buffered(1)
    whole = lambda: pl.BlockSpec((rows, width), lambda j, chip: (0, 0), pipeline_mode=once)
    return pl.pallas_call(
        feed_kernel,
        out_shape=[
            jax.ShapeDtypeStruct((rows, width), F32),
            jax.ShapeDtypeStruct((rows, width), BF16),
            jax.ShapeDtypeStruct((rows, ff), BF16),
            jax.ShapeDtypeStruct((rows, 2 * ff), BF16),
        ],
        grid_spec=pltpu.PrefetchScalarGridSpec(
            num_scalar_prefetch=1,
            grid=(ff // FF_TILE,),
            in_specs=[
                pl.BlockSpec((rows, width), lambda j, chip: (chip[0], 0), pipeline_mode=once),
                whole(), whole(),
                pl.BlockSpec((1, width), lambda j, chip: (0, 0)),
                whole(),
                pl.BlockSpec((width, 2 * FF_TILE), lambda j, chip: (0, at // (2 * FF_TILE) + j)),
                pl.BlockSpec((FF_TILE, width), lambda j, chip: (j, 0)),
            ],
            out_specs=[
                pl.BlockSpec((rows, width), lambda j, chip: (0, 0)),
                pl.BlockSpec((rows, width), lambda j, chip: (0, 0)),
                pl.BlockSpec((rows, FF_TILE), lambda j, chip: (0, j)),
                pl.BlockSpec((rows, 2 * FF_TILE), lambda j, chip: (0, j)),
            ],
        ),
        compiler_params=pltpu.CompilerParams(vmem_limit_bytes=VMEM_LIMIT),
        name="feed",
    )(chip, x_all, p0, p1, gain, go, w_all, w_down)


def middle_back_kernel(mid_ref, s0_ref, s1_ref, go_ref, gain_ref, wo_ref, ga_ref, gm_ref, g_ref):
    back, terms = norm_back(mid_ref[...], gain_ref[...], s0_ref[...].astype(F32) + s1_ref[...].astype(F32))
    grad = (go_ref[...].astype(F32) + back).astype(BF16)
    ga_ref[...] = grad
    gm_ref[...] = dot(grad, wo_ref[...], NT).astype(BF16)

    @pl.when(pl.program_id(0) == 0)
    def _():
        g_ref[...] = jnp.zeros_like(g_ref)

    g_ref[...] += jnp.sum(terms, axis=0, keepdims=True)


def middle_back(middle, s0, s1, go, gain, w_out):
    rows, width = middle.shape
    size = min(ROW_TILE, rows)
    row = pl.BlockSpec((size, width), lambda i: (i, 0))
    line = pl.BlockSpec((1, width), lambda i: (0, 0))
    return pl.pallas_call(
        middle_back_kernel,
        out_shape=[
            jax.ShapeDtypeStruct((rows, width), BF16),
            jax.ShapeDtypeStruct((rows, w_out.shape[0]), BF16),
            jax.ShapeDtypeStruct((1, width), F32),
        ],
        grid=(rows // size,),
        in_specs=[row, row, row, row, line, pl.BlockSpec(w_out.shape, lambda i: (0, 0), pipeline_mode=pl.Buffered(1))],
        out_specs=[row, pl.BlockSpec((size, w_out.shape[0]), lambda i: (i, 0)), line],
        compiler_params=pltpu.CompilerParams(vmem_limit_bytes=VMEM_LIMIT),
        name="middle_back",
    )(middle, s0, s1, go, gain, w_out)


LINK_TIME = pl.CostEstimate(flops=0, bytes_accessed=300_000_000, transcendentals=0)


def peers():
    dp, ctx = lax.axis_index("dp"), lax.axis_index("ctx")
    to = lambda d, k: (jnp.bitwise_xor(dp, d), jnp.bitwise_xor(ctx, k))
    return dp, ctx, to


def greet(devices):
    barrier = pltpu.get_barrier_semaphore()
    for device in devices:
        pl.semaphore_signal(barrier, inc=1, device_id=device, device_id_type=MESH)
    pl.semaphore_wait(barrier, len(devices))


def sender(send_sem, recv_sem):
    made = []

    def send(src, dst, device):
        i = len(made)
        copy = pltpu.make_async_remote_copy(
            src_ref=src, dst_ref=dst, send_sem=send_sem.at[i], recv_sem=recv_sem.at[i],
            device_id=device, device_id_type=MESH,
        )
        copy.start()
        made.append(copy)
        return copy

    return send, made


def gather_kernel(
    pk_ref, wd_ref, tok_ref, go_ref, w_ref, d_ref, x_ref, g_ref, send_sem, recv_sem, local_sem
):
    dp, ctx, to = peers()
    c, z = ctx % 2, ctx // 2
    which, me = ctx // 4, ctx % 4
    inner = jnp.logical_or(z == 1, z == 2)
    greet([to(0, 1), to(0, 2), to(0, 4), to(0, 6), to(1, 0), to(2, 0)])
    send, made = sender(send_sem, recv_sem)
    sib, nbr, far, across, xn, yn = to(0, 1), to(0, 2), to(0, 4), to(0, 6), to(1, 0), to(2, 0)
    rows = pk_ref.shape[1]

    place = w_ref.at[dp, z, pl.ds(c * rows, rows)]
    local = [
        pltpu.make_async_copy(pk_ref.at[c], place, local_sem.at[0]),
        pltpu.make_async_copy(wd_ref, d_ref.at[dp, z], local_sem.at[1]),
        pltpu.make_async_copy(tok_ref.at[which], x_ref.at[me, 0], local_sem.at[2]),
        pltpu.make_async_copy(go_ref.at[which], g_ref.at[c, 0], local_sem.at[3]),
    ]
    for copy in local:
        copy.start()
    cross = send(pk_ref.at[1 - c], place, sib)
    for copy in local:
        copy.wait()
    cross.wait_recv()
    done = []

    refs = [w_ref, d_ref]

    def half(ref, h, q, zz):
        size = ref.shape[2] // 2
        return ref.at[q, zz, pl.ds(h * size, size)]

    first = []

    def spread(zz):
        for ref in refs:
            low, high = half(ref, 0, dp, zz), half(ref, 1, dp, zz)
            first.append((send(low, low, yn), low, half(ref, 0, jnp.bitwise_xor(dp, 2), zz), xn))
            first.append((send(high, high, xn), high, half(ref, 1, jnp.bitwise_xor(dp, 1), zz), yn))

    def pass_on():
        for copy, own, part, device in first[:4]:
            done.append(send(own, own, device))
            copy.wait_recv()
            done.append(send(part, part, device))
        del first[:4]

    z_one = jnp.bitwise_xor(z, 1)
    z_near = jnp.bitwise_xor(z, jnp.where(inner, 3, 2))
    z_far = jnp.bitwise_xor(z, jnp.where(inner, 2, 3))
    relayed = []

    def relay(slot, source, device):
        for i, ref in enumerate(refs):
            copy = pltpu.make_async_remote_copy(
                src_ref=ref.at[dp, source], dst_ref=ref.at[dp, source],
                send_sem=send_sem.at[send_sem.shape[0] - 8 + len(relayed)],
                recv_sem=recv_sem.at[send_sem.shape[0] - 4 + 2 * slot + i],
                device_id=device, device_id_type=MESH,
            )
            relayed.append(copy)
            pl.when(inner)(copy.start)
        return relayed[-2:]

    def arrived(copies):
        for copy in copies:
            copy.wait_recv()

    step = [send(ref.at[dp, z], ref.at[dp, z], nbr) for ref in refs]
    near = relay(0, z, across)
    spread(z)
    pass_on()
    arrived(step)
    far_block = relay(1, z_one, across)
    spread(z_one)
    arrived(near)
    relay(0, z_near, nbr)
    spread(z_near)
    pass_on()
    arrived(far_block)
    relay(1, z_far, nbr)
    spread(z_far)
    swap = send(tok_ref.at[1 - which], x_ref.at[me, 1], far)
    mine_nbr = send(tok_ref.at[which], x_ref.at[me, 0], nbr)
    done += [send(tok_ref.at[which], x_ref.at[me, 0], sib), send(go_ref.at[which], g_ref.at[c, 0], sib)]
    pass_on()
    swap.wait_recv()
    done.append(send(x_ref.at[me, 1], x_ref.at[me, 1], sib))
    swap_nbr = send(x_ref.at[me, 1], x_ref.at[me, 1], nbr)
    go_swap = send(go_ref.at[1 - which], g_ref.at[c, 1], far)
    pass_on()
    other = jnp.bitwise_xor(me, 2)
    mine_nbr.wait_recv()
    done.append(send(x_ref.at[other, 0], x_ref.at[other, 0], sib))
    swap_nbr.wait_recv()
    done.append(send(x_ref.at[other, 1], x_ref.at[other, 1], sib))
    go_swap.wait_recv()
    done.append(send(g_ref.at[c, 1], g_ref.at[c, 1], sib))
    for copy in done:
        copy.wait_recv()
    for copy in made:
        copy.wait_send()

    @pl.when(inner)
    def _():
        for copy in relayed:
            copy.wait_send()


def gather(packed, w_down, tokens, grad_out):
    rows, cols = 2 * packed.shape[1], packed.shape[2]
    slots, width = tokens.shape[1:]
    copies = 61 + 8
    anywhere = pl.BlockSpec(memory_space=pl.ANY)
    near = pl.BlockSpec(memory_space=pltpu.VMEM)
    w, d, x, g = pl.pallas_call(
        gather_kernel,
        out_shape=[
            jax.ShapeDtypeStruct((4, 4, rows, cols), BF16),
            jax.ShapeDtypeStruct((4, 4) + w_down.shape, BF16),
            jax.ShapeDtypeStruct((4, 2, slots, width), BF16),
            jax.ShapeDtypeStruct((2, 2, slots, width), BF16),
        ],
        in_specs=[near] * 4,
        out_specs=[anywhere] * 4,
        scratch_shapes=[
            pltpu.SemaphoreType.DMA((copies,)),
            pltpu.SemaphoreType.DMA((copies,)),
            pltpu.SemaphoreType.DMA((4,)),
        ],
        compiler_params=pltpu.CompilerParams(
            collective_id=0, has_side_effects=True, vmem_limit_bytes=VMEM_LIMIT
        ),
        cost_estimate=LINK_TIME,
        name="gather",
    )(packed, w_down, tokens, grad_out)
    return w.reshape(16 * rows, cols), d.reshape(-1, width), x.reshape(-1, width), g.reshape(-1, width)


def reduce_kernel(n_in, *refs):
    g_refs, (ow_ref, or_ref, part_ref, xa_ref, gm_ref, gain_ref) = refs[:n_in], refs[n_in : n_in + 6]
    gq_ref, gk_ref, gv_ref, gg_ref, go_ref, ig_ref = refs[n_in + 6 : n_in + 12]
    (
        g_ref, in_a, in_b, mid_a, mid_b, got_a, got_b, out3, in3,
        mine_ref, sib_ref, give_ref, nbr_ref, back_ref, x_ref, ga_ref, o_ref, s_ref, send_sem, recv_sem, local_sem,
    ) = refs[n_in + 12 :]
    dp, ctx, to = peers()
    c, z = ctx % 2, ctx // 2
    which, chip = ctx // 4, z % 2
    x, y = dp % 2, dp // 2
    hr = g_ref.shape[3] // 2
    at, local = 0, []
    for i, ref in enumerate(g_refs):
        width = ref.shape[-1]
        local.append(pltpu.make_async_copy(ref, g_ref.at[:, :, :, :, pl.ds(at, width)], local_sem.at[i]))
        at += width
    wide = pl.ds(at, ow_ref.shape[-1])
    count = mine_ref.shape[1]
    local += [
        pltpu.make_async_copy(ow_ref.at[:, :, c], g_ref.at[c, :, :, :, wide], local_sem.at[n_in]),
        pltpu.make_async_copy(or_ref, g_ref.at[1 - c, :, :, :, wide], local_sem.at[n_in + 1]),
        pltpu.make_async_copy(part_ref.at[:, c], mine_ref, local_sem.at[n_in + 2]),
        pltpu.make_async_copy(xa_ref.at[ctx % 4], x_ref, local_sem.at[n_in + 3]),
        pltpu.make_async_copy(gm_ref.at[c], ga_ref, local_sem.at[n_in + 4]),
    ]
    for copy in local:
        copy.start()
    greet([to(0, 1), to(0, 2), to(0, 4), to(0, 6), to(1, 0), to(2, 0)])
    send, made = sender(send_sem, recv_sem)
    sib, nbr, far, across = to(0, 1), to(0, 2), to(0, 4), to(0, 6)
    xn, yn = to(1, 0), to(2, 0)
    cross = send(part_ref.at[:, 1 - c], sib_ref, sib)
    for copy in local:
        copy.wait()
    low, high = pl.ds(0, hr), pl.ds(hr, hr)
    inner = jnp.logical_or(z == 1, z == 2)
    outer = jnp.logical_not(inner)
    order = [jnp.bitwise_xor(z, jnp.where(inner, 3, 2)), jnp.bitwise_xor(z, jnp.where(inner, 2, 3)), jnp.bitwise_xor(z, 1), z]
    passed = []

    def pass_z(kind, slot, source, part, device, role):
        copy = pltpu.make_async_remote_copy(
            src_ref=out3.at[source, :, parts[part]], dst_ref=in3.at[slot, :, parts[part]],
            send_sem=send_sem.at[40 + 2 * kind + part], recv_sem=recv_sem.at[40 + 2 * slot + part],
            device_id=device, device_id_type=MESH,
        )
        pl.when(role)(copy.start)
        passed.append((role, copy))

    def from_z(slot, part):
        return pltpu.make_async_remote_copy(
            src_ref=out3.at[0, :, parts[part]], dst_ref=in3.at[slot, :, parts[part]],
            send_sem=send_sem.at[40 + part], recv_sem=recv_sem.at[40 + 2 * slot + part],
            device_id=nbr, device_id_type=MESH,
        )

    def add_z(block, slot, part):
        p = parts[part]
        out3[block, :, p] = (out3[block, :, p].astype(F32) + in3[slot, :, p].astype(F32)).astype(BF16)

    def inward(i):
        k, part = i // 2, i % 2

        @pl.when(inner)
        def _():
            from_z(k, part).wait_recv()
            add_z(k, k, part)

        pass_z(3 + k, 3 + k, k, part, across, inner)

    def outward(part):
        @pl.when(inner)
        def _():
            from_z(4, part).wait_recv()
            add_z(2, 4, part)

        pass_z(5, 2, 2, part, nbr, inner)

    a_in, b_in, a_mid, b_mid = [], [], [], []
    size = 64
    tile = lambda i: pl.ds(pl.multiple_of(i * size, size), size)
    cut = g_ref.shape[4] // 2 // HD * HD
    parts = (pl.ds(0, cut), pl.ds(cut, g_ref.shape[4] - cut))

    def enter(i):
        k, p = i // 2, parts[i % 2]
        a_in.append(send(g_ref.at[:, 1 - x, order[k], low, p], in_a.at[k, :, :, p], xn))
        b_in.append(send(g_ref.at[1 - y, :, order[k], high, p], in_b.at[k, :, :, p], yn))

    def middle(i):
        k, p = i // 2, parts[i % 2]
        add = lambda p, q: (p.astype(F32) + q.astype(F32)).astype(BF16)
        a_in[i].wait_recv()
        mid_a[k, :, p] = add(g_ref[1 - y, x, order[k], 0:hr, p], in_a[k, 1 - y, :, p])
        a_mid.append(send(mid_a.at[k, :, p], got_a.at[k, :, p], yn))
        b_in[i].wait_recv()
        mid_b[k, :, p] = add(g_ref[y, 1 - x, order[k], hr:, p], in_b[k, 1 - x, :, p])
        b_mid.append(send(mid_b.at[k, :, p], got_b.at[k, :, p], xn))

    def leave(i):
        k, p = i // 2, parts[i % 2]
        add = lambda p, q, r: (p.astype(F32) + q.astype(F32) + r.astype(F32)).astype(BF16)
        a_mid[i].wait_recv()
        out3[k, 0:hr, p] = add(g_ref[y, x, order[k], 0:hr, p], in_a[k, y, :, p], got_a[k, :, p])
        b_mid[i].wait_recv()
        out3[k, hr:, p] = add(g_ref[y, x, order[k], hr:, p], in_b[k, x, :, p], got_b[k, :, p])
        if k < 3:
            pass_z(k, k, k, i % 2, nbr, outer)

    enter(0)
    enter(1)
    enter(2)
    cross.wait_recv()
    slots = ig_ref.shape[1]

    def give(i, _):
        rows = tile(i)
        give_ref[rows] = (mine_ref[1 - chip, rows].astype(F32) + sib_ref[1 - chip, rows].astype(F32)).astype(BF16)
        return 0

    def back(i, _):
        rows = tile(i)
        grad = mine_ref[chip, rows].astype(F32) + sib_ref[chip, rows].astype(F32) + nbr_ref[rows].astype(F32)
        through, _terms = norm_back(x_ref[rows, :].astype(F32), gain_ref[...], grad)
        back_ref[rows] = (ga_ref[rows, :].astype(F32) + through).astype(BF16)
        return 0

    swaps = []
    for first in (slots, 0):
        lax.fori_loop(first // size, (first + slots) // size, give, 0)
        rows = pl.ds(first, slots)
        swaps.append(send(give_ref.at[rows], nbr_ref.at[rows], nbr))
    middle(0)
    enter(3)
    middle(1)
    enter(4)
    swaps[0].wait_recv()
    lax.fori_loop(slots // size, 2 * slots // size, back, 0)
    home = send(back_ref.at[pl.ds(slots, slots)], ig_ref.at[which], far)
    leave(0)
    middle(2)
    enter(5)
    leave(1)
    middle(3)
    enter(6)
    leave(2)
    inward(0)
    middle(4)
    enter(7)
    leave(3)
    inward(1)
    swaps[1].wait_recv()
    lax.fori_loop(0, slots // size, back, 0)
    keep = pltpu.make_async_copy(back_ref.at[pl.ds(0, slots)], ig_ref.at[which], local_sem.at[0])
    keep.start()
    middle(5)
    leave(4)
    inward(2)
    middle(6)
    leave(5)
    inward(3)
    outward(0)
    middle(7)
    leave(6)
    outward(1)
    leave(7)
    for part in range(2):
        from_z(2, part).wait_recv()

    @pl.when(inner)
    def _():
        for part in range(2):
            from_z(3, part).wait_recv()
            add_z(3, 3, part)

    total = out3[3].astype(F32) + in3[2].astype(F32)
    near = s_ref.shape[1]
    o_ref[...] = total[:, :near].astype(BF16)
    other = send(o_ref.at[pl.ds(pl.multiple_of((1 - c) * hr, hr), hr)], s_ref, sib)
    go_ref[...] = total[:, near:]
    own = o_ref.at[pl.ds(pl.multiple_of(c * hr, hr), hr)]

    def place(source, core):
        col = 0
        for ref in (gq_ref, gk_ref, gv_ref):
            size = ref.shape[1] // 2
            ref[:, pl.ds(pl.multiple_of(core * size, size), size)] = source[:, col : col + size].astype(F32)
            col += size

    place(own, c)
    other.wait_recv()
    place(s_ref, 1 - c)
    gains = near - HD
    gg_ref[...] = own[:, gains:].astype(F32) + s_ref[:, gains:].astype(F32)
    keep.wait()
    home.wait_recv()
    for copy in made:
        copy.wait_send()
    for role, copy in passed:
        pl.when(role)(copy.wait_send)


def reduce(grads, out_own, out_sib, part, x_all, grad_middle, gain):
    rows = grads[0].shape[0] // 16
    width = x_all.shape[1]
    near_cols = sum(g.shape[1] for g in grads)
    cols = near_cols + width
    count = part.shape[0] // 4
    split = lambda v: v.reshape(2, 2, 4, rows, v.shape[1])
    copies = 52
    anywhere = pl.BlockSpec(memory_space=pl.ANY)
    near = pl.BlockSpec(memory_space=pltpu.VMEM)
    return pl.pallas_call(
        functools.partial(reduce_kernel, len(grads)),
        out_shape=[
            *[jax.ShapeDtypeStruct((rows // 2, 2 * g.shape[-1]), F32) for g in grads[:3]],
            jax.ShapeDtypeStruct((rows // 2, HD), F32),
            jax.ShapeDtypeStruct((rows, width), F32),
            jax.ShapeDtypeStruct((2, count // 2, width), BF16),
        ],
        in_specs=[anywhere] * (len(grads) + 5) + [near],
        out_specs=[near] * 5 + [anywhere],
        scratch_shapes=[
            pltpu.VMEM((2, 2, 4, rows, cols), BF16),
            pltpu.VMEM((4, 2, rows // 2, cols), BF16),
            pltpu.VMEM((4, 2, rows // 2, cols), BF16),
        ]
        + [pltpu.VMEM((4, rows // 2, cols), BF16)] * 4
        + [
            pltpu.VMEM((4, rows, cols), BF16),
            pltpu.VMEM((5, rows, cols), BF16),
            pltpu.VMEM((2, count, width), BF16),
            pltpu.VMEM((2, count, width), BF16),
        ]
        + [pltpu.VMEM((count, width), BF16)] * 5
        + [
            pltpu.VMEM((rows, near_cols), BF16),
            pltpu.VMEM((rows // 2, near_cols), BF16),
            pltpu.SemaphoreType.DMA((copies,)),
            pltpu.SemaphoreType.DMA((copies,)),
            pltpu.SemaphoreType.DMA((len(grads) + 5,)),
        ],
        compiler_params=pltpu.CompilerParams(
            collective_id=1, has_side_effects=True, vmem_limit_bytes=VMEM_LIMIT
        ),
        cost_estimate=LINK_TIME,
        name="reduce",
    )(
        *[split(g) for g in grads],
        out_own.reshape(2, 4, 2, rows, width),
        out_sib.reshape(2, 4, rows, width),
        part.reshape(2, 2, count, width),
        x_all.reshape(4, count, width),
        grad_middle.reshape(2, count, width),
        gain,
    )


def by_core(c, own, other):
    return jnp.where(c == 0, jnp.stack([own, other]), jnp.stack([other, own]))


def layer(
    n_dp, n, tokens, positions, w_query, w_key, w_value, w_out, w_gate, w_up, w_down,
    attn_gain, mlp_gain, q_gain, k_gain, grad_out,
):
    axes = ("dp", "ctx")
    slots, width = tokens.shape[1:]
    seq = positions.shape[1]
    span = slots // 2
    half = n // 2
    chips = n_dp * half
    ctx = lax.axis_index("ctx")
    c = ctx % 2
    which = ctx // half
    r_in, r_out, r_down = w_query.shape[0], w_out.shape[0], w_down.shape[0]
    ff = w_gate.shape[1]
    ff_c = ff // 2
    q_c, kv_c = H * HD // 2, KV * HD // 2

    to_sibling = [(i, i ^ 1) for i in range(n)]
    to_partner = [(i, (i + half) % n) for i in range(n)]
    halves = [list(range(half)), list(range(half, n))]
    same_core = [list(range(0, n, 2)), list(range(1, n, 2))]
    sibling = lambda v: lax.ppermute(v, "ctx", to_sibling)
    partner = lambda v: lax.ppermute(v, "ctx", to_partner)

    def placed(values):
        mine = lax.dynamic_index_in_dim(values, which, 0, False)
        other = lax.dynamic_index_in_dim(values, 1 - which, 0, False)
        return jnp.concatenate([mine, partner(other)], axis=0)

    gains = jnp.concatenate(
        [
            attn_gain[:, None],
            mlp_gain[:, None],
            jnp.pad(q_gain, (0, r_in - q_gain.shape[0]))[:, None],
            jnp.pad(k_gain, (0, r_in - k_gain.shape[0]))[:, None],
            jnp.zeros((r_in, 124), BF16),
        ],
        axis=1,
    )
    tall = (n_dp, n) == (4, 8)
    qkv_halves = [
        jnp.concatenate(
            [
                w_query[:, i * q_c : (i + 1) * q_c],
                w_key[:, i * kv_c : (i + 1) * kv_c],
                w_value[:, i * kv_c : (i + 1) * kv_c],
            ],
            axis=1,
        )
        for i in range(2)
    ]

    def ff_order(shard):
        return shard.reshape(r_in, chips, 2, r_down).transpose(2, 0, 1, 3).reshape(2, r_in, ff_c)

    gate_order, up_order = ff_order(w_gate), ff_order(w_up)
    qkv_c = q_c + 2 * kv_c
    all_c = qkv_c + 2 * ff_c
    by_tile = lambda v: v.reshape(2, r_in, ff_c // FF_TILE, FF_TILE)
    gu_shard = jnp.stack([by_tile(gate_order), by_tile(up_order)], axis=3).reshape(2, r_in, 2 * ff_c)
    packed = jnp.stack([jnp.concatenate([qkv_halves[i], gu_shard[i], gains], axis=1) for i in range(2)])
    if tall:
        w_all, w_down_c, x_all, go_chip = gather(packed, w_down, tokens, grad_out)
        w_out, w_all = lax.optimization_barrier((w_out, w_all))
    else:
        both = lax.all_gather(packed, axes, axis=1, tiled=True)
        w_all = lax.dynamic_index_in_dim(both, c, 0, False)
        down_all = lax.all_gather(w_down, axes, axis=0, tiled=True).reshape(chips, 2, r_down, width)
        w_down_c = lax.dynamic_index_in_dim(down_all, c, 1, False).reshape(ff_c, width)
        x_own = placed(tokens)
        x_all = lax.all_gather(x_own, "ctx", axis=0, tiled=True, axis_index_groups=halves)
        go_own = placed(grad_out)
        go_chip = by_core(c, go_own, sibling(go_own)).reshape(4 * slots, width)
    out_all = lax.all_gather(w_out, axes, axis=0, tiled=True)
    w_out_c = lax.dynamic_slice_in_dim(out_all, c * q_c, q_c, 0)
    g_cols = w_all[:, all_c : all_c + HD].astype(F32)
    gain_attn = g_cols[:, 0][None]
    gain_mlp = g_cols[:, 1][None]
    per_head = g_cols.reshape(n_dp * n, r_in, HD)[:, : q_gain.shape[0]].reshape(HD, HD)
    gain_q = per_head[:, 2][None]
    gain_k = per_head[:, 3][None]

    chip = (ctx % half) // 2
    chip_rows = 4 * slots
    slot_ids = lax.dynamic_index_in_dim(positions, which, 0, False).reshape(2 * n, span)[:, 0] // span
    places = np.stack(
        [
            [s for d in side for k in (d, (d + half) % n) for s in (2 * k, 2 * k + 1)]
            for side in halves
        ]
    ).astype(np.int32)
    ids_all = slot_ids[lax.dynamic_index_in_dim(jnp.asarray(places), which, 0, False)]
    steps = jnp.arange(2 * n, dtype=jnp.int32)
    order = jnp.sum(jnp.where(ids_all[None, :] == steps[:, None], steps[None, :], 0), axis=1).astype(jnp.int32)
    ids = lax.dynamic_slice_in_dim(ids_all, chip * 8, 8, 0)
    cosine, sine = rope_tables(seq)

    chip_at = chip.astype(jnp.int32).reshape(1)
    hidden_all, q_raw, kv_raw = project(chip_at, x_all, gain_attn, w_all, chip_rows)
    hidden = lax.dynamic_slice_in_dim(hidden_all, chip * chip_rows, chip_rows, 0)
    mixed, lse = attend(ids, order, q_raw, kv_raw, cosine, sine, gain_q, gain_k, span)
    proj = dot(mixed, w_out_c, NN, BF16)
    middle, second, activated, grad_gu = feed(
        chip_at, x_all, proj, sibling(proj), gain_mlp, go_chip, w_all, qkv_c, w_down_c
    )
    down = dot(activated, w_down_c, NN, BF16).reshape(2, 2 * slots, width)
    down_own = lax.dynamic_index_in_dim(down, c, 0, False)
    down_other = sibling(lax.dynamic_index_in_dim(down, 1 - c, 0, False))
    own_rows = lambda v: lax.dynamic_slice_in_dim(v, c * 2 * slots, 2 * slots, 0)
    result = (own_rows(middle) + (down_own.astype(F32) + down_other.astype(F32))).astype(BF16)

    def returned(rows):
        mine, back = rows[:slots], partner(rows[slots:])
        return jnp.where(which == 0, jnp.stack([mine, back]), jnp.stack([back, mine]))


    second_part = dot(grad_gu, w_all[:, qkv_c:all_c], NT, BF16)
    grad_gu_w = dot(second, grad_gu, TN, BF16)
    grad_down_w = dot(activated, go_chip, TN, BF16)
    grad_attn, grad_mixed, mlp_gain_sum = middle_back(
        middle, second_part, sibling(second_part), go_chip, gain_mlp, w_out_c
    )
    grad_mlp_gain = jnp.where(c == 0, mlp_gain_sum[0], 0.0)

    over_dp = lambda grad: lax.psum_scatter(grad, "dp", scatter_dimension=0, tiled=True)
    over_ctx = lambda part: lax.psum_scatter(
        part, "ctx", scatter_dimension=0, tiled=True, axis_index_groups=same_core
    )
    part_gu = over_dp(grad_gu_w)
    part_down = over_dp(grad_down_w)

    out_w = dot(mixed, grad_attn, TN, BF16).reshape(-1, 2, r_out, width)
    out_recv = sibling(lax.dynamic_index_in_dim(out_w, 1 - c, 1, False))
    out_recv, grad_mixed = lax.optimization_barrier((out_recv, grad_mixed))
    result, grad_mixed = lax.optimization_barrier((result, grad_mixed))
    output = returned(result)
    dq, dk, dv, dgq, dgk = attend_back(
        ids, order, q_raw, kv_raw, grad_mixed, mixed, lse, cosine, sine, gain_q, gain_k, span
    )
    output, dq, dk, dv, part_gu, part_down = lax.optimization_barrier((output, dq, dk, dv, part_gu, part_down))
    rows2, extra = 2 * r_in, r_down - 2 * r_in
    part_down = part_down.reshape(half, r_down, width)
    rest = part_down[:, rows2:]
    fold = rows2 // extra
    folded = [rest[:, :, i * width // fold : (i + 1) * width // fold] for i in range(fold)]
    pieces = [part_gu.reshape(half, rows2, -1), part_down[:, :rows2], jnp.concatenate(folded, axis=1)]
    sum_ff = over_ctx(jnp.concatenate(pieces, axis=2).reshape(half * rows2, -1))
    sum_gu = sum_ff[:, : 2 * ff_c]
    tail = sum_ff[:, 2 * ff_c + width :].reshape(fold, extra, -1)
    sum_down = jnp.concatenate(
        [sum_ff[:, 2 * ff_c : 2 * ff_c + width], jnp.concatenate([tail[i] for i in range(fold)], axis=1)], axis=0
    )
    part_all, attn_gain_sum = project_back(chip_at, dq, dk, dv, x_all, w_all)
    grad_q_w = dot(hidden, dq, TN, BF16)
    grad_k_w = dot(hidden_all, dk, TN, BF16)
    grad_v_w = dot(hidden_all, dv, TN, BF16)
    lot = lambda v: v.reshape(n_dp * n, -1)
    entries = jnp.concatenate([lot(attn_gain_sum), lot(grad_mlp_gain), lot(dgq), lot(dgk)], axis=1)
    entries = jnp.pad(entries[:, None], ((0, 0), (0, r_in - 1), (0, HD - entries.shape[1])))
    grads = [grad_q_w, grad_k_w, grad_v_w, entries.reshape(width, HD).astype(BF16)]
    near_c = qkv_c + HD
    beside = lambda v: v.transpose(1, 0, 2).reshape(r_in, -1)
    by_rows = lambda v: lax.dynamic_index_in_dim(v.reshape(2, r_in, -1), c, 0, False)

    def columns(sums):
        other = lax.dynamic_index_in_dim(sums.reshape(2, r_in, -1), 1 - c, 0, False)
        return by_core(c, by_rows(sums), sibling(other)).astype(F32)

    if tall:
        grad_q, grad_k, grad_v, gain_own, sum_out, input_grad = reduce(
            grads, out_w, out_recv, part_all, x_all, grad_attn, gain_attn
        )
    else:
        qkv_own = columns(over_ctx(over_dp(jnp.concatenate(grads, axis=1))))
        out_mine = lax.dynamic_index_in_dim(out_w, c, 1, False)
        sum_out = over_ctx(over_dp(by_core(c, out_mine, out_recv).reshape(chips * r_out, width))).astype(F32)
        grad_q = beside(qkv_own[:, :, :q_c])
        grad_k = beside(qkv_own[:, :, q_c : q_c + kv_c])
        grad_v = beside(qkv_own[:, :, q_c + kv_c : qkv_c])
        gain_own = jnp.sum(qkv_own[:, :, qkv_c:], axis=0)
        grad_hidden = lax.psum_scatter(
            part_all, "ctx", scatter_dimension=0, tiled=True, axis_index_groups=halves
        ).astype(F32)
        back, _terms = norm_back(x_own.astype(F32), gain_attn, grad_hidden)
        input_grad = returned((own_rows(grad_attn).astype(F32) + back).astype(BF16))
    gain_row, r_head = gain_own[0], q_gain.shape[0]
    gu_own = columns(sum_gu).reshape(2, r_in, ff_c // FF_TILE, 2, FF_TILE)
    ff_back = lambda v: v.reshape(2, r_in, chips, r_down).transpose(1, 2, 0, 3).reshape(r_in, ff)
    return (
        output,
        input_grad,
        grad_q,
        grad_k,
        grad_v,
        sum_out,
        ff_back(gu_own[:, :, :, 0]),
        ff_back(gu_own[:, :, :, 1]),
        sum_down.astype(F32),
        gain_row[:r_in],
        gain_row[r_in : 2 * r_in],
        gain_row[2 * r_in : 2 * r_in + r_head],
        gain_row[2 * r_in + r_head : 2 * r_in + 2 * r_head],
    )


def solution(mesh):
    rows = P(("dp", "ctx"), None)
    gain = P(("dp", "ctx"))
    acts = P("dp", "ctx", None)
    return jax.shard_map(
        functools.partial(layer, mesh.shape["dp"], mesh.shape["ctx"]),
        mesh=mesh,
        in_specs=(acts, P("dp", None)) + (rows,) * 7 + (gain,) * 4 + (acts,),
        out_specs=(acts, acts) + (rows,) * 7 + (gain,) * 4,
        check_vma=False,
    )
```

```python
import functools

import jax
import jax.numpy as jnp
import numpy as np
from jax import lax
from jax.experimental import pallas as pl
from jax.experimental.pallas import tpu as pltpu
from jax.sharding import PartitionSpec as P

H = 16
KV = 8
HD = 128
GROUPS = H // KV
EPSILON = 1e-06
THETA = 1000000.0
LOG2E = 1.4426950408889634
KEY_TILE = 512
ROW_TILE = 256
FF_TILE = 384
VMEM_LIMIT = 48 * 1024 * 1024
MESH = pl.DeviceIdType.MESH
F32 = jnp.float32
BF16 = jnp.bfloat16


def normed(values, weights):
    return values * lax.rsqrt(jnp.mean(values * values, axis=-1, keepdims=True) + EPSILON) * weights


def norm_back(values, weights, grad):
    r = lax.rsqrt(jnp.mean(values * values, axis=-1, keepdims=True) + EPSILON)
    unit = values * r
    u = grad * weights
    return r * (u - unit * jnp.mean(u * unit, axis=-1, keepdims=True)), grad * unit


def rope_tables(seq):
    half = HD // 2
    inverse = (THETA ** (-(np.arange(half, dtype=np.float32) * np.float32(2.0) / np.float32(HD)))).astype(np.float32)
    angles = np.arange(seq, dtype=np.float32)[:, None] * inverse[None, :]
    cosine, sine = np.cos(angles), np.sin(angles)
    return (
        jnp.asarray(np.concatenate([cosine, cosine], axis=-1).astype(np.float32)),
        jnp.asarray(np.concatenate([-sine, sine], axis=-1).astype(np.float32)),
    )


def dot(a, b, dims, out=F32):
    return lax.dot_general(a, b, (dims, ((), ())), preferred_element_type=out)


NN = ((1,), (0,))
NT = ((1,), (1,))
TN = ((0,), (0,))


def row_mean(values):
    return dot(values.astype(BF16), jnp.full((HD, HD), 1.0 / HD, BF16), NN)


def unit_rows(raw):
    r = lax.rsqrt(row_mean(raw * raw) + EPSILON)
    return raw * r, r


def rope(values, cosine, sine):
    return values * cosine + pltpu.roll(values, HD // 2, 1) * sine


def rope_back(values, cosine, sine):
    return values * cosine - pltpu.roll(values, HD // 2, 1) * sine


def lanes(head, width=HD):
    return slice(head * width, (head + 1) * width)


def prepare_keys(span, order_ref, k_ref, v_ref, cos_ref, sin_ref, gk_ref, ks_ref, vs_ref):
    def body(i, _):
        rows = pl.ds(pl.multiple_of(i * span, span), span)
        source = pl.ds(pl.multiple_of(order_ref[i] * span, span), span)
        for p in range(k_ref.shape[1] // HD):
            unit, _r = unit_rows(k_ref[source, lanes(p)].astype(F32))
            ks_ref[rows, lanes(p)] = rope(unit * gk_ref[...], cos_ref[rows, :], sin_ref[rows, :]).astype(BF16)
        vs_ref[rows, :] = v_ref[source, :]
        return 0

    lax.fori_loop(0, k_ref.shape[0] // span, body, 0)


def query_block(q_ref, p, rows, places, cos_ref, sin_ref, gq_ref):
    units, scales, parts = [], [], []
    for g in range(GROUPS):
        unit, r = unit_rows(q_ref[rows, lanes(p * GROUPS + g)].astype(F32))
        turned = rope(unit * gq_ref[...], cos_ref[places, :], sin_ref[places, :])
        units.append(unit)
        scales.append(r)
        parts.append((turned * (LOG2E * HD**-0.5)).astype(BF16))
    return units, scales, jnp.concatenate(parts, axis=0)


def seen(shape, t, b, span, key_axis):
    at = t * KEY_TILE + lax.broadcasted_iota(jnp.int32, shape, key_axis)
    own = b * span + lax.broadcasted_iota(jnp.int32, shape, 1 - key_axis) % span
    return at <= own


def attend_kernel(
    span, ids_ref, order_ref, q_ref, k_ref, v_ref, cos_ref, sin_ref, gq_ref, gk_ref,
    o_ref, lse_ref, ks_ref, vs_ref, acc_ref, sum_ref,
):
    @pl.when(pl.program_id(0) == 0)
    def _():
        prepare_keys(span, order_ref, k_ref, v_ref, cos_ref, sin_ref, gk_ref, ks_ref, vs_ref)

    m = GROUPS * span
    heads = range(k_ref.shape[1] // HD)
    b = ids_ref[pl.program_id(0)]
    rows = slice(None)
    places = pl.ds(pl.multiple_of(b * span, span), span)
    q2 = [query_block(q_ref, p, rows, places, cos_ref, sin_ref, gq_ref)[2] for p in heads]
    acc_ref[...] = jnp.zeros_like(acc_ref)
    sum_ref[...] = jnp.zeros_like(sum_ref)

    def tile(t, masked):
        keys = pl.ds(pl.multiple_of(t * KEY_TILE, KEY_TILE), KEY_TILE)
        scores = [dot(q2[p], ks_ref[keys, lanes(p)], NT) for p in heads]
        keep = seen(scores[0].shape, t, b, span, 1) if masked else None
        for p in heads:
            e = jnp.exp2(scores[p])
            if masked:
                e = jnp.where(keep, e, 0.0)
            part = e[:, 0:HD]
            for i in range(1, KEY_TILE // HD):
                part = part + e[:, lanes(i)]
            sum_ref[p] += part
            acc_ref[p] += dot(e.astype(BF16), vs_ref[keys, lanes(p)], NN)

    last = (b * span) // KEY_TILE
    lax.fori_loop(0, last, lambda t, _: (tile(t, False), 0)[1], 0)
    tile(last, True)
    for p in heads:
        total = jnp.sum(sum_ref[p], axis=-1, keepdims=True)
        mixed = acc_ref[p] * (1.0 / total)
        for g in range(GROUPS):
            o_ref[rows, lanes(p * GROUPS + g)] = mixed[g * span : (g + 1) * span].astype(BF16)
        wide = jnp.broadcast_to(jnp.log2(total), (m, HD))
        lse_ref[p, 0] = jnp.transpose(wide)[0:1, :]


def attend(ids, order, q_raw, kv_raw, cosine, sine, gq, gk, span):
    rows = q_raw.shape[0]
    seq = kv_raw.shape[0]
    heads = q_raw.shape[1] // (GROUPS * HD)
    blocks, m = rows // span, GROUPS * span
    hp = heads
    whole = lambda k, ids, order: (0, 0)
    per_query = pl.BlockSpec((span, hp * GROUPS * HD), lambda j, ids, order: (j, 0))
    once = pl.Buffered(1)
    return pl.pallas_call(
        functools.partial(attend_kernel, span),
        out_shape=[
            jax.ShapeDtypeStruct((rows, heads * GROUPS * HD), BF16),
            jax.ShapeDtypeStruct((heads, blocks, 1, m), F32),
        ],
        grid_spec=pltpu.PrefetchScalarGridSpec(
            num_scalar_prefetch=2,
            grid=(blocks,),
            in_specs=[
                per_query,
                pl.BlockSpec((seq, hp * HD), whole, pipeline_mode=once),
                pl.BlockSpec((seq, hp * HD), lambda j, ids, order: (0, 1), pipeline_mode=once),
                pl.BlockSpec((seq, HD), whole, pipeline_mode=once),
                pl.BlockSpec((seq, HD), whole, pipeline_mode=once),
                pl.BlockSpec((1, HD), whole),
                pl.BlockSpec((1, HD), whole),
            ],
            out_specs=[
                per_query,
                pl.BlockSpec((hp, 1, 1, m), lambda j, ids, order: (0, j, 0, 0)),
            ],
            scratch_shapes=[
                pltpu.VMEM((seq, hp * HD), BF16),
                pltpu.VMEM((seq, hp * HD), BF16),
                pltpu.VMEM((hp, m, HD), F32),
                pltpu.VMEM((hp, m, HD), F32),
            ],
        ),
        compiler_params=pltpu.CompilerParams(vmem_limit_bytes=VMEM_LIMIT),
        cost_estimate=pl.CostEstimate(
            flops=2 * 2 * rows * seq * heads * GROUPS * HD,
            bytes_accessed=2 * (2 * rows * heads * GROUPS * HD + 2 * seq * heads * HD),
            transcendentals=rows * seq * heads * GROUPS // 2,
        ),
        name="attend",
    )(ids, order, q_raw, kv_raw, kv_raw, cosine, sine, gq, gk)


def attend_back_kernel(
    span, ids_ref, order_ref, q_ref, k_ref, v_ref, do_ref, o_ref, lse_ref, cos_ref, sin_ref, gq_ref, gk_ref,
    dq_ref, dk_ref, dv_ref, dgq_ref, dgk_ref, ks_ref, vs_ref, dka_ref, dva_ref, dqa_ref,
):
    heads = range(k_ref.shape[1] // HD)

    @pl.when(pl.program_id(0) == 0)
    def _():
        prepare_keys(span, order_ref, k_ref, v_ref, cos_ref, sin_ref, gk_ref, ks_ref, vs_ref)
        dka_ref[...] = jnp.zeros_like(dka_ref)
        dva_ref[...] = jnp.zeros_like(dva_ref)
        dgq_ref[...] = jnp.zeros_like(dgq_ref)
        dgk_ref[...] = jnp.zeros_like(dgk_ref)

    b = ids_ref[pl.program_id(0)]
    rows = slice(None)
    places = pl.ds(pl.multiple_of(b * span, span), span)
    q2, do2, delta, lse = [], [], [], []
    for p in heads:
        q2.append(query_block(q_ref, p, rows, places, cos_ref, sin_ref, gq_ref)[2])
        pick = lambda ref: jnp.concatenate([ref[rows, lanes(p * GROUPS + g)] for g in range(GROUPS)], axis=0)
        do2.append(pick(do_ref))
        delta.append(
            jnp.sum(jnp.transpose(do2[p].astype(F32) * pick(o_ref).astype(F32)), axis=0, keepdims=True)
        )
        lse.append(lse_ref[p, 0])
    dqa_ref[...] = jnp.zeros_like(dqa_ref)

    def tile(t, masked):
        keys = pl.ds(pl.multiple_of(t * KEY_TILE, KEY_TILE), KEY_TILE)
        kt = [ks_ref[keys, lanes(p)] for p in heads]
        scores = [dot(kt[p], q2[p], NT) for p in heads]
        slopes = [dot(vs_ref[keys, lanes(p)], do2[p], NT) for p in heads]
        keep = seen(scores[0].shape, t, b, span, 0) if masked else None
        for p in heads:
            e = jnp.exp2(scores[p] - lse[p])
            if masked:
                e = jnp.where(keep, e, 0.0)
            ds = (e * (slopes[p] - delta[p])).astype(BF16)
            dva_ref[keys, lanes(p)] += dot(e.astype(BF16), do2[p], NN)
            dka_ref[keys, lanes(p)] += dot(ds, q2[p], NN)
            dqa_ref[p] += dot(ds, kt[p], TN)

    last = (b * span) // KEY_TILE
    lax.fori_loop(0, last, lambda t, _: (tile(t, False), 0)[1], 0)
    tile(last, True)
    for p in heads:
        units, scales, _q = query_block(q_ref, p, rows, places, cos_ref, sin_ref, gq_ref)
        dq = dqa_ref[p] * HD**-0.5
        for g in range(GROUPS):
            grad = rope_back(dq[g * span : (g + 1) * span], cos_ref[places, :], sin_ref[places, :])
            dgq_ref[...] += jnp.sum(grad * units[g], axis=0, keepdims=True)
            u = grad * gq_ref[...]
            back = scales[g] * (u - units[g] * row_mean(u * units[g]))
            dq_ref[rows, lanes(p * GROUPS + g)] = back.astype(BF16)

    def finish(i, _):
        rows = pl.ds(pl.multiple_of(i * span, span), span)
        source = pl.ds(pl.multiple_of(order_ref[i] * span, span), span)
        for p in heads:
            unit, r = unit_rows(k_ref[source, lanes(p)].astype(F32))
            grad = rope_back(dka_ref[rows, lanes(p)] * (1.0 / LOG2E), cos_ref[rows, :], sin_ref[rows, :])
            dgk_ref[...] += jnp.sum(grad * unit, axis=0, keepdims=True)
            u = grad * gk_ref[...]
            back = r * (u - unit * row_mean(u * unit))
            dk_ref[source, lanes(p)] = back.astype(BF16)
        dv_ref[source, :] = dva_ref[rows, :].astype(BF16)
        return 0

    @pl.when(pl.program_id(0) == pl.num_programs(0) - 1)
    def _():
        lax.fori_loop(0, k_ref.shape[0] // span, finish, 0)


def attend_back(ids, order, q_raw, kv_raw, grad_mixed, mixed, lse, cosine, sine, gq, gk, span):
    rows = q_raw.shape[0]
    seq = kv_raw.shape[0]
    heads = q_raw.shape[1] // (GROUPS * HD)
    blocks, m = rows // span, GROUPS * span
    hp = heads
    whole = lambda k, ids, order: (0, 0)
    once = pl.Buffered(1)
    per_query = pl.BlockSpec((span, hp * GROUPS * HD), lambda j, ids, order: (j, 0))
    per_key = pl.BlockSpec((seq, hp * HD), whole, pipeline_mode=once)
    gain = pl.BlockSpec((1, HD), whole)
    return pl.pallas_call(
        functools.partial(attend_back_kernel, span),
        out_shape=[
            jax.ShapeDtypeStruct((rows, heads * GROUPS * HD), BF16),
            jax.ShapeDtypeStruct((seq, heads * HD), BF16),
            jax.ShapeDtypeStruct((seq, heads * HD), BF16),
            jax.ShapeDtypeStruct((1, HD), F32),
            jax.ShapeDtypeStruct((1, HD), F32),
        ],
        grid_spec=pltpu.PrefetchScalarGridSpec(
            num_scalar_prefetch=2,
            grid=(blocks,),
            in_specs=[
                per_query,
                per_key,
                pl.BlockSpec((seq, hp * HD), lambda j, ids, order: (0, 1), pipeline_mode=once),
                per_query,
                per_query,
                pl.BlockSpec((hp, 1, 1, m), lambda j, ids, order: (0, j, 0, 0)),
                pl.BlockSpec((seq, HD), whole, pipeline_mode=once),
                pl.BlockSpec((seq, HD), whole, pipeline_mode=once),
                gain,
                gain,
            ],
            out_specs=[per_query] + [pl.BlockSpec((seq, hp * HD), whole)] * 2 + [gain, gain],
            scratch_shapes=[
                pltpu.VMEM((seq, hp * HD), BF16),
                pltpu.VMEM((seq, hp * HD), BF16),
                pltpu.VMEM((seq, hp * HD), F32),
                pltpu.VMEM((seq, hp * HD), F32),
                pltpu.VMEM((hp, m, HD), F32),
            ],
        ),
        compiler_params=pltpu.CompilerParams(vmem_limit_bytes=VMEM_LIMIT),
        cost_estimate=pl.CostEstimate(
            flops=5 * 2 * rows * seq * heads * GROUPS * HD // 2,
            bytes_accessed=2 * (4 * rows * heads * GROUPS * HD + 4 * seq * heads * HD),
            transcendentals=rows * seq * heads * GROUPS // 2,
        ),
        name="attend_back",
    )(ids, order, q_raw, kv_raw, kv_raw, grad_mixed, mixed, lse, cosine, sine, gq, gk)


def project_kernel(own, chip_ref, x_ref, gain_ref, wq_ref, wkv_ref, h_ref, q_ref, kv_ref):
    hidden = normed(x_ref[...].astype(F32), gain_ref[...]).astype(BF16)
    h_ref[...] = hidden
    kv_ref[...] = dot(hidden, wkv_ref[...], NN).astype(BF16)

    @pl.when(pl.program_id(0) < own)
    def _():
        q_ref[...] = dot(hidden, wq_ref[...], NN).astype(BF16)


def project(chip, x_all, gain, w_all, first, chip_rows):
    seq, width = x_all.shape
    size = min(ROW_TILE, chip_rows)
    own, tiles = chip_rows // size, seq // size
    at = lambda i, chip: ((i + chip[0] * own) % tiles, 0)
    weight = lambda col: pl.BlockSpec((width, width), lambda i, chip: (0, col), pipeline_mode=pl.Buffered(1))
    return pl.pallas_call(
        functools.partial(project_kernel, own),
        out_shape=[
            jax.ShapeDtypeStruct((seq, width), BF16),
            jax.ShapeDtypeStruct((chip_rows, width), BF16),
            jax.ShapeDtypeStruct((seq, width), BF16),
        ],
        grid_spec=pltpu.PrefetchScalarGridSpec(
            num_scalar_prefetch=1,
            grid=(tiles,),
            in_specs=[
                pl.BlockSpec((size, width), at),
                pl.BlockSpec((1, width), lambda i, chip: (0, 0)),
                weight(first // width),
                weight(first // width + 1),
            ],
            out_specs=[
                pl.BlockSpec((size, width), at),
                pl.BlockSpec((size, width), lambda i, chip: (jnp.minimum(i, own - 1), 0)),
                pl.BlockSpec((size, width), at),
            ],
        ),
        compiler_params=pltpu.CompilerParams(vmem_limit_bytes=VMEM_LIMIT),
        name="project",
    )(chip, x_all, gain, w_all, w_all)


def project_back_kernel(own, chip_ref, dq_ref, dk_ref, dv_ref, x_ref, wq_ref, wk_ref, wv_ref, p_ref, g_ref, acc_ref):
    i = pl.program_id(0)
    acc_ref[...] = dot(dk_ref[...], wk_ref[...], NT) + dot(dv_ref[...], wv_ref[...], NT)

    @pl.when(i < own)
    def _():
        acc_ref[...] += dot(dq_ref[...], wq_ref[...], NT)

    @pl.when(i == 0)
    def _():
        g_ref[...] = jnp.zeros_like(g_ref)

    part = acc_ref[...]
    p_ref[...] = part.astype(BF16)
    g_ref[...] += jnp.sum(part * normed(x_ref[...].astype(F32), 1.0), axis=0, keepdims=True)


def project_back(chip, dq, dk, dv, x_all, w_all, first):
    seq, width = x_all.shape
    chip_rows, kv = dq.shape[0], dk.shape[1]
    size = min(ROW_TILE, chip_rows)
    own, tiles = chip_rows // size, seq // size
    at = lambda i, chip: ((i + chip[0] * own) % tiles, 0)
    weight = lambda cols, col: pl.BlockSpec((width, cols), lambda i, chip: (0, col), pipeline_mode=pl.Buffered(1))
    return pl.pallas_call(
        functools.partial(project_back_kernel, own),
        out_shape=[jax.ShapeDtypeStruct((seq, width), BF16), jax.ShapeDtypeStruct((1, width), F32)],
        grid_spec=pltpu.PrefetchScalarGridSpec(
            num_scalar_prefetch=1,
            grid=(tiles,),
            in_specs=[
                pl.BlockSpec((size, width), lambda i, chip: (jnp.minimum(i, own - 1), 0)),
                pl.BlockSpec((size, kv), at),
                pl.BlockSpec((size, kv), at),
                pl.BlockSpec((size, width), at),
                weight(width, first // width),
                weight(kv, (first + width) // kv),
                weight(kv, (first + width) // kv + 1),
            ],
            out_specs=[
                pl.BlockSpec((size, width), at),
                pl.BlockSpec((1, width), lambda i, chip: (0, 0)),
            ],
            scratch_shapes=[pltpu.VMEM((size, width), F32)],
        ),
        compiler_params=pltpu.CompilerParams(vmem_limit_bytes=VMEM_LIMIT),
        name="project_back",
    )(chip, dq, dk, dv, x_all, w_all, w_all, w_all)


def feed_kernel(chip_ref, x_ref, p0_ref, p1_ref, gain_ref, w_ref, mid_ref, sec_ref, act_ref, gu_ref):
    count = x_ref.shape[0]
    size = min(ROW_TILE, count)
    tile = lambda i: pl.ds(pl.multiple_of(i * size, size), size)

    @pl.when(pl.program_id(0) == 0)
    def _():
        def start(i, _):
            rows = tile(i)
            middle = x_ref[rows, :].astype(F32) + (p0_ref[rows, :].astype(F32) + p1_ref[rows, :].astype(F32))
            mid_ref[rows, :] = middle
            sec_ref[rows, :] = normed(middle, gain_ref[...]).astype(BF16)
            return 0

        lax.fori_loop(0, count // size, start, 0)

    def body(i, _):
        rows = tile(i)
        both = dot(sec_ref[rows, :], w_ref[...], NN)
        gate, up = both[:, :FF_TILE], both[:, FF_TILE:]
        act_ref[rows, :] = (gate * jax.nn.sigmoid(gate) * up).astype(BF16)
        gu_ref[rows, :] = both.astype(BF16)
        return 0

    lax.fori_loop(0, count // size, body, 0)


def feed(chip, x_all, p0, p1, gain, w_all, ff):
    rows, width = p0.shape
    once = pl.Buffered(1)
    whole = lambda: pl.BlockSpec((rows, width), lambda j, chip: (0, 0), pipeline_mode=once)
    return pl.pallas_call(
        feed_kernel,
        out_shape=[
            jax.ShapeDtypeStruct((rows, width), F32),
            jax.ShapeDtypeStruct((rows, width), BF16),
            jax.ShapeDtypeStruct((rows, ff), BF16),
            jax.ShapeDtypeStruct((rows, 2 * ff), BF16),
        ],
        grid_spec=pltpu.PrefetchScalarGridSpec(
            num_scalar_prefetch=1,
            grid=(ff // FF_TILE,),
            in_specs=[
                pl.BlockSpec((rows, width), lambda j, chip: (chip[0], 0), pipeline_mode=once),
                whole(), whole(),
                pl.BlockSpec((1, width), lambda j, chip: (0, 0)),
                pl.BlockSpec((width, 2 * FF_TILE), lambda j, chip: (0, j)),
            ],
            out_specs=[
                pl.BlockSpec((rows, width), lambda j, chip: (0, 0)),
                pl.BlockSpec((rows, width), lambda j, chip: (0, 0)),
                pl.BlockSpec((rows, FF_TILE), lambda j, chip: (0, j)),
                pl.BlockSpec((rows, 2 * FF_TILE), lambda j, chip: (0, j)),
            ],
        ),
        compiler_params=pltpu.CompilerParams(vmem_limit_bytes=VMEM_LIMIT),
        name="feed",
    )(chip, x_all, p0, p1, gain, w_all)


def feed_back_kernel(core_ref, gu_ref, go_ref, wd_ref, gg_ref, d_ref):
    count = gu_ref.shape[0]
    size = min(ROW_TILE, count)
    unit = wd_ref.shape[2]
    for u in range(FF_TILE // unit):
        d_ref[u * unit : (u + 1) * unit, :] = wd_ref[u, 0]

    def body(i, _):
        rows = pl.ds(pl.multiple_of(i * size, size), size)
        grad = dot(go_ref[rows, :], d_ref[...], NT)
        gate, up = gu_ref[rows, :FF_TILE].astype(F32), gu_ref[rows, FF_TILE:].astype(F32)
        sig = jax.nn.sigmoid(gate)
        gg_ref[rows, :FF_TILE] = (grad * up * sig * (1.0 + gate * (1.0 - sig))).astype(BF16)
        gg_ref[rows, FF_TILE:] = (grad * (gate * sig)).astype(BF16)
        return 0

    lax.fori_loop(0, count // size, body, 0)


def feed_back(core, gate_up, go, w_down):
    rows, width = go.shape
    chips, _, unit, _ = w_down.shape
    ff = chips * unit
    return pl.pallas_call(
        feed_back_kernel,
        out_shape=[jax.ShapeDtypeStruct((rows, 2 * ff), BF16), jax.ShapeDtypeStruct((ff, width), BF16)],
        grid_spec=pltpu.PrefetchScalarGridSpec(
            num_scalar_prefetch=1,
            grid=(ff // FF_TILE,),
            in_specs=[
                pl.BlockSpec((rows, 2 * FF_TILE), lambda j, core: (0, j)),
                pl.BlockSpec((rows, width), lambda j, core: (0, 0), pipeline_mode=pl.Buffered(1)),
                pl.BlockSpec((FF_TILE // unit, 1, unit, width), lambda j, core: (j, core[0], 0, 0)),
            ],
            out_specs=[
                pl.BlockSpec((rows, 2 * FF_TILE), lambda j, core: (0, j)),
                pl.BlockSpec((FF_TILE, width), lambda j, core: (j, 0)),
            ],
        ),
        compiler_params=pltpu.CompilerParams(vmem_limit_bytes=VMEM_LIMIT),
        name="feed_back",
    )(core, gate_up, go, w_down)


def middle_back_kernel(mid_ref, s0_ref, s1_ref, go_ref, gain_ref, wo_ref, ga_ref, gm_ref, g_ref):
    back, terms = norm_back(mid_ref[...], gain_ref[...], s0_ref[...].astype(F32) + s1_ref[...].astype(F32))
    grad = (go_ref[...].astype(F32) + back).astype(BF16)
    ga_ref[...] = grad
    gm_ref[...] = dot(grad, wo_ref[...], NT).astype(BF16)

    @pl.when(pl.program_id(0) == 0)
    def _():
        g_ref[...] = jnp.zeros_like(g_ref)

    g_ref[...] += jnp.sum(terms, axis=0, keepdims=True)


def middle_back(middle, s0, s1, go, gain, w_out):
    rows, width = middle.shape
    size = min(ROW_TILE, rows)
    row = pl.BlockSpec((size, width), lambda i: (i, 0))
    line = pl.BlockSpec((1, width), lambda i: (0, 0))
    return pl.pallas_call(
        middle_back_kernel,
        out_shape=[
            jax.ShapeDtypeStruct((rows, width), BF16),
            jax.ShapeDtypeStruct((rows, w_out.shape[0]), BF16),
            jax.ShapeDtypeStruct((1, width), F32),
        ],
        grid=(rows // size,),
        in_specs=[row, row, row, row, line, pl.BlockSpec(w_out.shape, lambda i: (0, 0), pipeline_mode=pl.Buffered(1))],
        out_specs=[row, pl.BlockSpec((size, w_out.shape[0]), lambda i: (i, 0)), line],
        compiler_params=pltpu.CompilerParams(vmem_limit_bytes=VMEM_LIMIT),
        name="middle_back",
    )(middle, s0, s1, go, gain, w_out)


LINK_TIME = pl.CostEstimate(flops=0, bytes_accessed=300_000_000, transcendentals=0)


def peers():
    dp, ctx = lax.axis_index("dp"), lax.axis_index("ctx")
    to = lambda d, k: (jnp.bitwise_xor(dp, d), jnp.bitwise_xor(ctx, k))
    return dp, ctx, to


def greet(devices):
    barrier = pltpu.get_barrier_semaphore()
    for device in devices:
        pl.semaphore_signal(barrier, inc=1, device_id=device, device_id_type=MESH)
    pl.semaphore_wait(barrier, len(devices))


def sender(send_sem, recv_sem):
    made = []

    def send(src, dst, device):
        i = len(made)
        copy = pltpu.make_async_remote_copy(
            src_ref=src, dst_ref=dst, send_sem=send_sem.at[i], recv_sem=recv_sem.at[i],
            device_id=device, device_id_type=MESH,
        )
        copy.start()
        made.append(copy)
        return copy

    return send, made


def gather_kernel(pk_ref, wo_ref, tok_ref, go_ref, w_ref, x_ref, g_ref, send_sem, recv_sem, local_sem):
    dp, ctx, to = peers()
    c, z = ctx % 2, ctx // 2
    which, me = ctx // 4, ctx % 4
    inner = jnp.logical_or(z == 1, z == 2)
    greet([to(0, 1), to(0, 2), to(0, 4), to(0, 6), to(1, 0), to(2, 0)])
    send, made = sender(send_sem, recv_sem)
    sib, nbr, far, across, xn, yn = to(0, 1), to(0, 2), to(0, 4), to(0, 6), to(1, 0), to(2, 0)
    rows, cols = pk_ref.shape[1:]

    place = w_ref.at[dp, z, pl.ds(c * rows, rows), pl.ds(0, cols)]
    local = [
        pltpu.make_async_copy(pk_ref.at[c], place, local_sem.at[0]),
        pltpu.make_async_copy(wo_ref, w_ref.at[dp, z, :, pl.ds(cols, wo_ref.shape[1])], local_sem.at[1]),
        pltpu.make_async_copy(tok_ref.at[which], x_ref.at[me, 0], local_sem.at[2]),
        pltpu.make_async_copy(go_ref.at[which], g_ref.at[c, 0], local_sem.at[3]),
    ]
    for copy in local:
        copy.start()
    cross = send(pk_ref.at[1 - c], place, sib)
    for copy in local:
        copy.wait()
    cross.wait_recv()
    done = []

    def half(h, q, zz):
        return w_ref.at[q, zz, pl.ds(h * rows, rows)]

    first = []

    def spread(zz):
        low, high = half(0, dp, zz), half(1, dp, zz)
        first.append((send(low, low, yn), low, half(0, jnp.bitwise_xor(dp, 2), zz), xn))
        first.append((send(high, high, xn), high, half(1, jnp.bitwise_xor(dp, 1), zz), yn))

    def pass_on():
        for copy, own, part, device in first[:2]:
            done.append(send(own, own, device))
            copy.wait_recv()
            done.append(send(part, part, device))
        del first[:2]

    z_one = jnp.bitwise_xor(z, 1)
    z_near = jnp.bitwise_xor(z, jnp.where(inner, 3, 2))
    z_far = jnp.bitwise_xor(z, jnp.where(inner, 2, 3))
    relayed = []

    def relay(slot, source, device):
        copy = pltpu.make_async_remote_copy(
            src_ref=w_ref.at[dp, source], dst_ref=w_ref.at[dp, source],
            send_sem=send_sem.at[send_sem.shape[0] - 4 + len(relayed)],
            recv_sem=recv_sem.at[send_sem.shape[0] - 2 + slot],
            device_id=device, device_id_type=MESH,
        )
        relayed.append(copy)
        pl.when(inner)(copy.start)
        return copy

    step = send(w_ref.at[dp, z], w_ref.at[dp, z], nbr)
    near = relay(0, z, across)
    spread(z)
    pass_on()
    step.wait_recv()
    far_block = relay(1, z_one, across)
    spread(z_one)
    near.wait_recv()
    relay(0, z_near, nbr)
    spread(z_near)
    pass_on()
    far_block.wait_recv()
    relay(1, z_far, nbr)
    spread(z_far)
    swap = send(tok_ref.at[1 - which], x_ref.at[me, 1], far)
    mine_nbr = send(tok_ref.at[which], x_ref.at[me, 0], nbr)
    done += [send(tok_ref.at[which], x_ref.at[me, 0], sib), send(go_ref.at[which], g_ref.at[c, 0], sib)]
    pass_on()
    swap.wait_recv()
    done.append(send(x_ref.at[me, 1], x_ref.at[me, 1], sib))
    swap_nbr = send(x_ref.at[me, 1], x_ref.at[me, 1], nbr)
    go_swap = send(go_ref.at[1 - which], g_ref.at[c, 1], far)
    pass_on()
    other = jnp.bitwise_xor(me, 2)
    mine_nbr.wait_recv()
    done.append(send(x_ref.at[other, 0], x_ref.at[other, 0], sib))
    swap_nbr.wait_recv()
    done.append(send(x_ref.at[other, 1], x_ref.at[other, 1], sib))
    go_swap.wait_recv()
    done.append(send(g_ref.at[c, 1], g_ref.at[c, 1], sib))
    for copy in done:
        copy.wait_recv()
    for copy in made:
        copy.wait_send()

    @pl.when(inner)
    def _():
        for copy in relayed:
            copy.wait_send()


def gather(packed, w_out, tokens, grad_out):
    rows, cols = 2 * packed.shape[1], packed.shape[2] + w_out.shape[1]
    slots, width = tokens.shape[1:]
    copies = 36 + 4
    anywhere = pl.BlockSpec(memory_space=pl.ANY)
    near = pl.BlockSpec(memory_space=pltpu.VMEM)
    w, x, g = pl.pallas_call(
        gather_kernel,
        out_shape=[
            jax.ShapeDtypeStruct((4, 4, rows, cols), BF16),
            jax.ShapeDtypeStruct((4, 2, slots, width), BF16),
            jax.ShapeDtypeStruct((2, 2, slots, width), BF16),
        ],
        in_specs=[near] * 4,
        out_specs=[anywhere] * 3,
        scratch_shapes=[
            pltpu.SemaphoreType.DMA((copies,)),
            pltpu.SemaphoreType.DMA((copies,)),
            pltpu.SemaphoreType.DMA((4,)),
        ],
        compiler_params=pltpu.CompilerParams(
            collective_id=0, has_side_effects=True, vmem_limit_bytes=VMEM_LIMIT
        ),
        cost_estimate=LINK_TIME,
        name="gather",
    )(packed, w_out, tokens, grad_out)
    return w.reshape(16 * rows, cols), x.reshape(-1, width), g.reshape(-1, width)


def reduce_kernel(
    h_hbm, dq_hbm, dk_hbm, dv_hbm, e_hbm, ow_hbm, or_hbm, part_ref, xa_hbm, gm_hbm, gain_ref,
    a_ref, go_ref, ig_ref,
    g_ref, in_a, in_b, mid_a, mid_b, got_a, got_b, out3, in3, mine_ref, sib_ref, give_ref, nbr_ref, back_ref,
    x_ref, ga_ref, h_ref, dq_ref, dk_ref, dv_ref, o_ref, s_ref, send_sem, recv_sem, local_sem,
):
    dp, ctx, to = peers()
    c, z = ctx % 2, ctx // 2
    which, chip = ctx // 4, z % 2
    x, y = dp % 2, dp // 2
    hr = g_ref.shape[3] // 2
    count = mine_ref.shape[1]
    q_cols, kv_cols = dq_ref.shape[1], dk_ref.shape[1]
    near = s_ref.shape[1]
    first_col, width = near - HD, ow_hbm.shape[-1]
    local = []

    def fetch(src, dst):
        copy = pltpu.make_async_copy(src, dst, local_sem.at[len(local)])
        copy.start()
        local.append(copy)

    fetch(ow_hbm.at[:, :, c], g_ref.at[c, :, :, :, pl.ds(near, width)])
    fetch(or_hbm, g_ref.at[1 - c, :, :, :, pl.ds(near, width)])
    fetch(e_hbm, g_ref.at[:, :, :, :, pl.ds(first_col, HD)])
    fetch(part_ref.at[:, c], mine_ref)
    fetch(dq_hbm, dq_ref)
    fetch(h_hbm, h_ref)
    fetch(dk_hbm, dk_ref)
    fetch(dv_hbm, dv_ref)
    fetch(xa_hbm.at[ctx % 4], x_ref)
    fetch(gm_hbm.at[c], ga_ref)
    greet([to(0, 1), to(0, 2), to(0, 4), to(0, 6), to(1, 0), to(2, 0)])
    send, made = sender(send_sem, recv_sem)
    sib, nbr, far, across = to(0, 1), to(0, 2), to(0, 4), to(0, 6)
    xn, yn = to(1, 0), to(2, 0)
    cross = send(part_ref.at[:, 1 - c], sib_ref, sib)

    def ready(count):
        for copy in local[:count]:
            copy.wait()
        del local[:count]

    def weigh(rows, grad_ref, at):
        def body(i, _):
            some = h_ref[rows, pl.ds(pl.multiple_of(i * 4 * 2 * hr, 128), 4 * 2 * hr)]
            part = dot(some, grad_ref[...], TN).astype(BF16)
            g_ref[i // 2, i % 2, :, :, at : at + grad_ref.shape[1]] = part.reshape(4, 2 * hr, grad_ref.shape[1])
            return 0

        lax.fori_loop(0, 4, body, 0)

    low, high = pl.ds(0, hr), pl.ds(hr, hr)
    inner = jnp.logical_or(z == 1, z == 2)
    outer = jnp.logical_not(inner)
    order = [jnp.bitwise_xor(z, jnp.where(inner, 3, 2)), jnp.bitwise_xor(z, jnp.where(inner, 2, 3)), jnp.bitwise_xor(z, 1), z]
    passed = []

    def pass_z(kind, slot, source, part, device, role):
        copy = pltpu.make_async_remote_copy(
            src_ref=out3.at[source, :, parts[part]], dst_ref=in3.at[slot, :, parts[part]],
            send_sem=send_sem.at[40 + 2 * kind + part], recv_sem=recv_sem.at[40 + 2 * slot + part],
            device_id=device, device_id_type=MESH,
        )
        pl.when(role)(copy.start)
        passed.append((role, copy))

    def from_z(slot, part):
        return pltpu.make_async_remote_copy(
            src_ref=out3.at[0, :, parts[part]], dst_ref=in3.at[slot, :, parts[part]],
            send_sem=send_sem.at[40 + part], recv_sem=recv_sem.at[40 + 2 * slot + part],
            device_id=nbr, device_id_type=MESH,
        )

    def add_z(block, slot, part):
        p = parts[part]
        out3[block, :, p] = (out3[block, :, p].astype(F32) + in3[slot, :, p].astype(F32)).astype(BF16)

    def inward(i):
        k, part = i % 4, i // 4

        @pl.when(inner)
        def _():
            from_z(k, part).wait_recv()
            add_z(k, k, part)

        pass_z(3 + k, 3 + k, k, part, across, inner)

    def outward(part):
        @pl.when(inner)
        def _():
            from_z(4, part).wait_recv()
            add_z(2, 4, part)

        pass_z(5, 2, 2, part, nbr, inner)

    a_in, b_in, a_mid, b_mid = [], [], [], []
    size = 64
    tile = lambda i: pl.ds(pl.multiple_of(i * size, size), size)
    parts = (pl.ds(first_col, HD + width), pl.ds(0, first_col))

    def enter(i):
        k, p = i % 4, parts[i // 4]
        a_in.append(send(g_ref.at[:, 1 - x, order[k], low, p], in_a.at[k, :, :, p], xn))
        b_in.append(send(g_ref.at[1 - y, :, order[k], high, p], in_b.at[k, :, :, p], yn))

    def middle(i):
        k, p = i % 4, parts[i // 4]
        add = lambda p, q: (p.astype(F32) + q.astype(F32)).astype(BF16)
        a_in[i].wait_recv()
        mid_a[k, :, p] = add(g_ref[1 - y, x, order[k], 0:hr, p], in_a[k, 1 - y, :, p])
        a_mid.append(send(mid_a.at[k, :, p], got_a.at[k, :, p], yn))
        b_in[i].wait_recv()
        mid_b[k, :, p] = add(g_ref[y, 1 - x, order[k], hr:, p], in_b[k, 1 - x, :, p])
        b_mid.append(send(mid_b.at[k, :, p], got_b.at[k, :, p], xn))

    def leave(i):
        k, p = i % 4, parts[i // 4]
        add = lambda p, q, r: (p.astype(F32) + q.astype(F32) + r.astype(F32)).astype(BF16)
        a_mid[i].wait_recv()
        out3[k, 0:hr, p] = add(g_ref[y, x, order[k], 0:hr, p], in_a[k, y, :, p], got_a[k, :, p])
        b_mid[i].wait_recv()
        out3[k, hr:, p] = add(g_ref[y, x, order[k], hr:, p], in_b[k, x, :, p], got_b[k, :, p])
        if k < 3:
            pass_z(k, k, k, i // 4, nbr, outer)

    ready(3)
    enter(0)
    enter(1)
    enter(2)
    ready(1)
    cross.wait_recv()
    slots = ig_ref.shape[1]

    def give(i, _):
        rows = tile(i)
        give_ref[rows] = (mine_ref[1 - chip, rows].astype(F32) + sib_ref[1 - chip, rows].astype(F32)).astype(BF16)
        return 0

    def back(i, _):
        rows = tile(i)
        grad = mine_ref[chip, rows].astype(F32) + sib_ref[chip, rows].astype(F32) + nbr_ref[rows].astype(F32)
        through, _terms = norm_back(x_ref[rows, :].astype(F32), gain_ref[...], grad)
        back_ref[rows] = (ga_ref[rows, :].astype(F32) + through).astype(BF16)
        return 0

    swaps = []
    for first in (slots, 0):
        lax.fori_loop(first // size, (first + slots) // size, give, 0)
        rows = pl.ds(first, slots)
        swaps.append(send(give_ref.at[rows], nbr_ref.at[rows], nbr))
    ready(2)
    weigh(pl.ds(pl.multiple_of(chip * dq_ref.shape[0], dq_ref.shape[0]), dq_ref.shape[0]), dq_ref, 0)
    middle(0)
    enter(3)
    middle(1)
    middle(2)
    ready(2)
    weigh(slice(None), dk_ref, q_cols)
    weigh(slice(None), dv_ref, q_cols + kv_cols)
    enter(4)
    enter(5)
    leave(0)
    leave(1)
    middle(3)
    ready(2)
    swaps[0].wait_recv()
    lax.fori_loop(slots // size, 2 * slots // size, back, 0)
    home = send(back_ref.at[pl.ds(slots, slots)], ig_ref.at[which], far)
    leave(2)
    inward(0)
    inward(1)
    middle(4)
    enter(6)
    leave(3)
    middle(5)
    enter(7)
    leave(4)
    outward(0)
    swaps[1].wait_recv()
    lax.fori_loop(0, slots // size, back, 0)
    keep = pltpu.make_async_copy(back_ref.at[pl.ds(0, slots)], ig_ref.at[which], local_sem.at[0])
    keep.start()
    middle(6)
    leave(5)
    inward(4)
    middle(7)
    leave(6)
    inward(5)
    leave(7)
    outward(1)
    for part in range(2):
        from_z(2, part).wait_recv()

    @pl.when(inner)
    def _():
        for part in range(2):
            from_z(3, part).wait_recv()
            add_z(3, 3, part)

    total = out3[3].astype(F32) + in3[2].astype(F32)
    o_ref[...] = total[:, :near].astype(BF16)
    other = send(o_ref.at[pl.ds(pl.multiple_of((1 - c) * hr, hr), hr)], s_ref, sib)
    go_ref[...] = total[:, near:].astype(BF16)
    own = o_ref.at[pl.ds(pl.multiple_of(c * hr, hr), hr)]

    def place(source, core):
        at = 0
        for size in (q_cols, kv_cols, kv_cols):
            a_ref[:, pl.ds(pl.multiple_of(2 * at + core * size, HD), size)] = source[:, at : at + size]
            at += size

    place(own, c)
    other.wait_recv()
    place(s_ref, 1 - c)
    both = own[:, first_col:].astype(F32) + s_ref[:, first_col:].astype(F32)
    a_ref[:, 2 * first_col :] = both.astype(BF16)
    keep.wait()
    home.wait_recv()
    for copy in made:
        copy.wait_send()
    for role, copy in passed:
        pl.when(role)(copy.wait_send)


def reduce(hidden, dq, dk, dv, entries, out_own, out_sib, part, x_all, grad_middle, gain):
    seq, width = x_all.shape
    rows = width // 16
    near_cols = dq.shape[1] + dk.shape[1] + dv.shape[1] + HD
    cols = near_cols + width
    count = part.shape[0] // 4
    copies = 52
    anywhere = pl.BlockSpec(memory_space=pl.ANY)
    near = pl.BlockSpec(memory_space=pltpu.VMEM)
    return pl.pallas_call(
        reduce_kernel,
        out_shape=[
            jax.ShapeDtypeStruct((rows // 2, 2 * (near_cols - HD) + HD), BF16),
            jax.ShapeDtypeStruct((rows, width), BF16),
            jax.ShapeDtypeStruct((2, count // 2, width), BF16),
        ],
        in_specs=[anywhere] * 10 + [near],
        out_specs=[near] * 2 + [anywhere],
        scratch_shapes=[
            pltpu.VMEM((2, 2, 4, rows, cols), BF16),
            pltpu.VMEM((4, 2, rows // 2, cols), BF16),
            pltpu.VMEM((4, 2, rows // 2, cols), BF16),
        ]
        + [pltpu.VMEM((4, rows // 2, cols), BF16)] * 4
        + [
            pltpu.VMEM((4, rows, cols), BF16),
            pltpu.VMEM((5, rows, cols), BF16),
            pltpu.VMEM((2, count, width), BF16),
            pltpu.VMEM((2, count, width), BF16),
        ]
        + [pltpu.VMEM((count, width), BF16)] * 5
        + [pltpu.VMEM(v.shape, BF16) for v in (hidden, dq, dk, dv)]
        + [
            pltpu.VMEM((rows, near_cols), BF16),
            pltpu.VMEM((rows // 2, near_cols), BF16),
            pltpu.SemaphoreType.DMA((copies,)),
            pltpu.SemaphoreType.DMA((copies,)),
            pltpu.SemaphoreType.DMA((10,)),
        ],
        compiler_params=pltpu.CompilerParams(
            collective_id=1, has_side_effects=True, vmem_limit_bytes=VMEM_LIMIT
        ),
        cost_estimate=LINK_TIME,
        name="reduce",
    )(
        hidden, dq, dk, dv,
        entries.reshape(2, 2, 4, rows, HD),
        out_own.reshape(2, 4, 2, rows, width),
        out_sib.reshape(2, 4, rows, width),
        part.reshape(2, 2, count, width),
        x_all.reshape(4, count, width),
        grad_middle.reshape(2, count, width),
        gain,
    )


def by_core(c, own, other):
    return jnp.where(c == 0, jnp.stack([own, other]), jnp.stack([other, own]))


def layer(
    n_dp, n, tokens, positions, w_query, w_key, w_value, w_out, w_gate, w_up, w_down,
    attn_gain, mlp_gain, q_gain, k_gain, grad_out,
):
    axes = ("dp", "ctx")
    slots, width = tokens.shape[1:]
    seq = positions.shape[1]
    span = slots // 2
    half = n // 2
    chips = n_dp * half
    ctx = lax.axis_index("ctx")
    c = ctx % 2
    which = ctx // half
    r_in, r_out, r_down = w_query.shape[0], w_out.shape[0], w_down.shape[0]
    ff = w_gate.shape[1]
    ff_c = ff // 2
    q_c, kv_c = H * HD // 2, KV * HD // 2

    to_sibling = [(i, i ^ 1) for i in range(n)]
    to_partner = [(i, (i + half) % n) for i in range(n)]
    halves = [list(range(half)), list(range(half, n))]
    same_core = [list(range(0, n, 2)), list(range(1, n, 2))]
    sibling = lambda v: lax.ppermute(v, "ctx", to_sibling)
    partner = lambda v: lax.ppermute(v, "ctx", to_partner)

    def placed(values):
        mine = lax.dynamic_index_in_dim(values, which, 0, False)
        other = lax.dynamic_index_in_dim(values, 1 - which, 0, False)
        return jnp.concatenate([mine, partner(other)], axis=0)

    gains = jnp.concatenate(
        [
            attn_gain[:, None],
            mlp_gain[:, None],
            jnp.pad(q_gain, (0, r_in - q_gain.shape[0]))[:, None],
            jnp.pad(k_gain, (0, r_in - k_gain.shape[0]))[:, None],
            jnp.zeros((r_in, 124), BF16),
        ],
        axis=1,
    )
    tall = (n_dp, n) == (4, 8)
    qkv_halves = [
        jnp.concatenate(
            [
                w_query[:, i * q_c : (i + 1) * q_c],
                w_key[:, i * kv_c : (i + 1) * kv_c],
                w_value[:, i * kv_c : (i + 1) * kv_c],
            ],
            axis=1,
        )
        for i in range(2)
    ]

    def ff_order(shard):
        return shard.reshape(r_in, chips, 2, r_down).transpose(2, 0, 1, 3).reshape(2, r_in, ff_c)

    gate_order, up_order = ff_order(w_gate), ff_order(w_up)
    qkv_c = q_c + 2 * kv_c
    gu_c = 2 * ff_c
    all_c = gu_c + qkv_c
    by_tile = lambda v: v.reshape(2, r_in, ff_c // FF_TILE, FF_TILE)
    gu_shard = jnp.stack([by_tile(gate_order), by_tile(up_order)], axis=3).reshape(2, r_in, 2 * ff_c)
    packed = jnp.stack([jnp.concatenate([gu_shard[i], qkv_halves[i], gains], axis=1) for i in range(2)])
    if tall:
        w_all, x_all, go_chip = gather(packed, w_out, tokens, grad_out)
        out_rows = w_all[:, all_c + HD :].reshape(2, -1, r_out, width)
        out_keep = lax.dynamic_index_in_dim(out_rows, c, 0, False)
        out_give = lax.dynamic_index_in_dim(out_rows, 1 - c, 0, False)
        w_out_c = by_core(c, out_keep, sibling(out_give)).transpose(1, 0, 2, 3).reshape(q_c, width)
        w_down, w_all = lax.optimization_barrier((w_down, w_all))
    else:
        both = lax.all_gather(packed, axes, axis=1, tiled=True)
        w_all = lax.dynamic_index_in_dim(both, c, 0, False)
        out_all = lax.all_gather(w_out, axes, axis=0, tiled=True)
        w_out_c = lax.dynamic_slice_in_dim(out_all, c * q_c, q_c, 0)
        x_own = placed(tokens)
        x_all = lax.all_gather(x_own, "ctx", axis=0, tiled=True, axis_index_groups=halves)
        go_own = placed(grad_out)
        go_chip = by_core(c, go_own, sibling(go_own)).reshape(4 * slots, width)
    down_all = lax.all_gather(w_down, axes, axis=0, tiled=True).reshape(chips, 2, r_down, width)
    g_cols = w_all[:, all_c : all_c + HD].astype(F32)
    gain_attn = g_cols[:, 0][None]
    gain_mlp = g_cols[:, 1][None]
    per_head = g_cols.reshape(n_dp * n, r_in, HD)[:, : q_gain.shape[0]].reshape(HD, HD)
    gain_q = per_head[:, 2][None]
    gain_k = per_head[:, 3][None]

    chip = (ctx % half) // 2
    chip_rows = 4 * slots
    slot_ids = lax.dynamic_index_in_dim(positions, which, 0, False).reshape(2 * n, span)[:, 0] // span
    places = np.stack(
        [
            [s for d in side for k in (d, (d + half) % n) for s in (2 * k, 2 * k + 1)]
            for side in halves
        ]
    ).astype(np.int32)
    ids_all = slot_ids[lax.dynamic_index_in_dim(jnp.asarray(places), which, 0, False)]
    steps = jnp.arange(2 * n, dtype=jnp.int32)
    order = jnp.sum(jnp.where(ids_all[None, :] == steps[:, None], steps[None, :], 0), axis=1).astype(jnp.int32)
    ids = lax.dynamic_slice_in_dim(ids_all, chip * 8, 8, 0)
    cosine, sine = rope_tables(seq)

    chip_at = chip.astype(jnp.int32).reshape(1)
    hidden_all, q_raw, kv_raw = project(chip_at, x_all, gain_attn, w_all, gu_c, chip_rows)
    mixed, lse = attend(ids, order, q_raw, kv_raw, cosine, sine, gain_q, gain_k, span)
    proj = dot(mixed, w_out_c, NN, BF16)
    middle, second, activated, gate_up = feed(chip_at, x_all, proj, sibling(proj), gain_mlp, w_all, ff_c)
    grad_gu, w_down_c = feed_back(c.astype(jnp.int32).reshape(1), gate_up, go_chip, down_all)
    down = dot(activated, w_down_c, NN, BF16).reshape(2, 2 * slots, width)
    down_own = lax.dynamic_index_in_dim(down, c, 0, False)
    down_other = sibling(lax.dynamic_index_in_dim(down, 1 - c, 0, False))
    own_rows = lambda v: lax.dynamic_slice_in_dim(v, c * 2 * slots, 2 * slots, 0)
    result = (own_rows(middle) + (down_own.astype(F32) + down_other.astype(F32))).astype(BF16)

    def returned(rows):
        mine, back = rows[:slots], partner(rows[slots:])
        return jnp.where(which == 0, jnp.stack([mine, back]), jnp.stack([back, mine]))


    second_part = dot(grad_gu, w_all[:, :gu_c], NT, BF16)
    grad_gu_w = dot(second, grad_gu, TN, BF16)
    grad_down_w = dot(activated, go_chip, TN, BF16)
    grad_attn, grad_mixed, mlp_gain_sum = middle_back(
        middle, second_part, sibling(second_part), go_chip, gain_mlp, w_out_c
    )
    grad_mlp_gain = jnp.where(c == 0, mlp_gain_sum[0], 0.0)

    over_dp = lambda grad: lax.psum_scatter(grad, "dp", scatter_dimension=0, tiled=True)
    over_ctx = lambda part: lax.psum_scatter(
        part, "ctx", scatter_dimension=0, tiled=True, axis_index_groups=same_core
    )
    part_gu = over_dp(grad_gu_w)
    part_down = over_dp(grad_down_w)

    out_w = dot(mixed, grad_attn, TN, BF16).reshape(-1, 2, r_out, width)
    out_recv = sibling(lax.dynamic_index_in_dim(out_w, 1 - c, 1, False))
    out_recv, grad_mixed = lax.optimization_barrier((out_recv, grad_mixed))
    result, grad_mixed, part_down = lax.optimization_barrier((result, grad_mixed, part_down))
    if tall:
        pieces = part_down.reshape(half, r_down, width)
        place = ctx // 2
        down_own = lax.dynamic_index_in_dim(pieces, place, 0, False).astype(F32)
        down_got = [
            lax.ppermute(
                lax.dynamic_index_in_dim(pieces, jnp.bitwise_xor(place, k), 0, False),
                "ctx",
                [(i, i ^ (2 * k)) for i in range(n)],
            )
            for k in range(1, half)
        ]
    else:
        down_own, down_got = over_ctx(part_down).astype(F32), []
    output = returned(result)
    dq, dk, dv, dgq, dgk = attend_back(
        ids, order, q_raw, kv_raw, grad_mixed, mixed, lse, cosine, sine, gain_q, gain_k, span
    )
    output, dq, dk, dv, part_gu, down_got = lax.optimization_barrier((output, dq, dk, dv, part_gu, down_got))
    sum_gu = over_ctx(part_gu)
    sum_down = down_own
    for piece in down_got:
        sum_down = sum_down + piece.astype(F32)
    part_all, attn_gain_sum = project_back(chip_at, dq, dk, dv, x_all, w_all, gu_c)
    lot = lambda v: v.reshape(n_dp * n, -1)
    entries = jnp.concatenate([lot(attn_gain_sum), lot(grad_mlp_gain), lot(dgq), lot(dgk)], axis=1)
    entries = jnp.pad(entries[:, None], ((0, 0), (0, r_in - 1), (0, HD - entries.shape[1])))
    entries = entries.reshape(width, HD).astype(BF16)
    near_c = qkv_c + HD
    beside = lambda v: v.transpose(1, 0, 2).reshape(r_in, -1)
    by_rows = lambda v: lax.dynamic_index_in_dim(v.reshape(2, r_in, -1), c, 0, False)

    def columns(sums):
        other = lax.dynamic_index_in_dim(sums.reshape(2, r_in, -1), 1 - c, 0, False)
        return by_core(c, by_rows(sums), sibling(other)).astype(F32)

    if tall:
        sums, sum_out, input_grad = reduce(
            hidden_all, dq, dk, dv, entries, out_w, out_recv, part_all, x_all, grad_attn, gain_attn
        )
        grad_q, grad_k, grad_v = (
            sums[:, i:j].astype(F32) for i, j in ((0, 2 * q_c), (2 * q_c, 2 * q_c + 2 * kv_c), (2 * q_c + 2 * kv_c, 2 * qkv_c))
        )
        sum_out, gain_own = sum_out.astype(F32), sums[:, 2 * qkv_c :].astype(F32)
    else:
        hidden = lax.dynamic_slice_in_dim(hidden_all, chip * chip_rows, chip_rows, 0)
        grads = [dot(hidden, dq, TN, BF16), dot(hidden_all, dk, TN, BF16), dot(hidden_all, dv, TN, BF16), entries]
        qkv_own = columns(over_ctx(over_dp(jnp.concatenate(grads, axis=1))))
        out_mine = lax.dynamic_index_in_dim(out_w, c, 1, False)
        sum_out = over_ctx(over_dp(by_core(c, out_mine, out_recv).reshape(chips * r_out, width))).astype(F32)
        grad_q = beside(qkv_own[:, :, :q_c])
        grad_k = beside(qkv_own[:, :, q_c : q_c + kv_c])
        grad_v = beside(qkv_own[:, :, q_c + kv_c : qkv_c])
        gain_own = jnp.sum(qkv_own[:, :, qkv_c:], axis=0)
        grad_hidden = lax.psum_scatter(
            part_all, "ctx", scatter_dimension=0, tiled=True, axis_index_groups=halves
        ).astype(F32)
        back, _terms = norm_back(x_own.astype(F32), gain_attn, grad_hidden)
        input_grad = returned((own_rows(grad_attn).astype(F32) + back).astype(BF16))
    sum_gu, gain_own = lax.optimization_barrier((sum_gu, gain_own))
    gain_row, r_head = gain_own[0], q_gain.shape[0]
    gu_own = columns(sum_gu).reshape(2, r_in, ff_c // FF_TILE, 2, FF_TILE)
    ff_back = lambda v: v.reshape(2, r_in, chips, r_down).transpose(1, 2, 0, 3).reshape(r_in, ff)
    return (
        output,
        input_grad,
        grad_q,
        grad_k,
        grad_v,
        sum_out,
        ff_back(gu_own[:, :, :, 0]),
        ff_back(gu_own[:, :, :, 1]),
        sum_down,
        gain_row[:r_in],
        gain_row[r_in : 2 * r_in],
        gain_row[2 * r_in : 2 * r_in + r_head],
        gain_row[2 * r_in + r_head : 2 * r_in + 2 * r_head],
    )


def solution(mesh):
    rows = P(("dp", "ctx"), None)
    gain = P(("dp", "ctx"))
    acts = P("dp", "ctx", None)
    return jax.shard_map(
        functools.partial(layer, mesh.shape["dp"], mesh.shape["ctx"]),
        mesh=mesh,
        in_specs=(acts, P("dp", None)) + (rows,) * 7 + (gain,) * 4 + (acts,),
        out_specs=(acts, acts) + (rows,) * 7 + (gain,) * 4,
        check_vma=False,
    )
```

```python
import functools

import jax
import jax.numpy as jnp
import numpy as np
from jax import lax
from jax.experimental import pallas as pl
from jax.experimental.pallas import tpu as pltpu
from jax.sharding import PartitionSpec as P

H = 16
KV = 8
HD = 128
GROUPS = H // KV
EPSILON = 1e-06
THETA = 1000000.0
LOG2E = 1.4426950408889634
KEY_TILE = 512
ROW_TILE = 256
FF_TILE = 384
MIB = 1024 * 1024
MESH = pl.DeviceIdType.MESH
F32 = jnp.float32
BF16 = jnp.bfloat16


def normed(values, weights):
    return values * lax.rsqrt(jnp.mean(values * values, axis=-1, keepdims=True) + EPSILON) * weights


def norm_back(values, weights, grad):
    r = lax.rsqrt(jnp.mean(values * values, axis=-1, keepdims=True) + EPSILON)
    unit = values * r
    u = grad * weights
    return r * (u - unit * jnp.mean(u * unit, axis=-1, keepdims=True)), grad * unit


def rope_tables(seq):
    half = HD // 2
    inverse = (THETA ** (-(np.arange(half, dtype=np.float32) * np.float32(2.0) / np.float32(HD)))).astype(np.float32)
    angles = np.arange(seq, dtype=np.float32)[:, None] * inverse[None, :]
    cosine, sine = np.cos(angles), np.sin(angles)
    return (
        jnp.asarray(np.concatenate([cosine, cosine], axis=-1).astype(np.float32)),
        jnp.asarray(np.concatenate([-sine, sine], axis=-1).astype(np.float32)),
    )


def dot(a, b, dims, out=F32):
    return lax.dot_general(a, b, (dims, ((), ())), preferred_element_type=out)


NN = ((1,), (0,))
NT = ((1,), (1,))
TN = ((0,), (0,))


def row_mean(values):
    return dot(values.astype(BF16), jnp.full((HD, HD), 1.0 / HD, BF16), NN)


def unit_rows(raw):
    r = lax.rsqrt(row_mean(raw * raw) + EPSILON)
    return raw * r, r


def rope(values, cosine, sine):
    return values * cosine + pltpu.roll(values, HD // 2, 1) * sine


def rope_back(values, cosine, sine):
    return values * cosine - pltpu.roll(values, HD // 2, 1) * sine


def lanes(head, width=HD):
    return slice(head * width, (head + 1) * width)


def prepare_keys(span, order_ref, k_ref, v_ref, cos_ref, sin_ref, gk_ref, ks_ref, vs_ref):
    def body(i, _):
        rows = pl.ds(pl.multiple_of(i * span, span), span)
        source = pl.ds(pl.multiple_of(order_ref[i] * span, span), span)
        for p in range(k_ref.shape[1] // HD):
            unit, _r = unit_rows(k_ref[source, lanes(p)].astype(F32))
            ks_ref[rows, lanes(p)] = rope(unit * gk_ref[...], cos_ref[rows, :], sin_ref[rows, :]).astype(BF16)
        vs_ref[rows, :] = v_ref[source, :]
        return 0

    lax.fori_loop(0, k_ref.shape[0] // span, body, 0)


def query_block(q_ref, p, rows, places, cos_ref, sin_ref, gq_ref):
    units, scales, parts = [], [], []
    for g in range(GROUPS):
        unit, r = unit_rows(q_ref[rows, lanes(p * GROUPS + g)].astype(F32))
        turned = rope(unit * gq_ref[...], cos_ref[places, :], sin_ref[places, :])
        units.append(unit)
        scales.append(r)
        parts.append((turned * (LOG2E * HD**-0.5)).astype(BF16))
    return units, scales, jnp.concatenate(parts, axis=0)


def seen(shape, t, b, span, key_axis):
    at = t * KEY_TILE + lax.broadcasted_iota(jnp.int32, shape, key_axis)
    own = b * span + lax.broadcasted_iota(jnp.int32, shape, 1 - key_axis) % span
    return at <= own


def attend_kernel(
    span, ids_ref, order_ref, q_ref, k_ref, v_ref, cos_ref, sin_ref, gq_ref, gk_ref,
    o_ref, lse_ref, ks_ref, vs_ref, acc_ref, sum_ref,
):
    @pl.when(pl.program_id(0) == 0)
    def _():
        prepare_keys(span, order_ref, k_ref, v_ref, cos_ref, sin_ref, gk_ref, ks_ref, vs_ref)

    m = GROUPS * span
    heads = range(k_ref.shape[1] // HD)
    b = ids_ref[pl.program_id(0)]
    rows = slice(None)
    places = pl.ds(pl.multiple_of(b * span, span), span)
    q2 = [query_block(q_ref, p, rows, places, cos_ref, sin_ref, gq_ref)[2] for p in heads]
    acc_ref[...] = jnp.zeros_like(acc_ref)
    sum_ref[...] = jnp.zeros_like(sum_ref)

    def tile(t, masked):
        keys = pl.ds(pl.multiple_of(t * KEY_TILE, KEY_TILE), KEY_TILE)
        scores = [dot(q2[p], ks_ref[keys, lanes(p)], NT) for p in heads]
        keep = seen(scores[0].shape, t, b, span, 1) if masked else None
        for p in heads:
            e = jnp.exp2(scores[p])
            if masked:
                e = jnp.where(keep, e, 0.0)
            part = e[:, 0:HD]
            for i in range(1, KEY_TILE // HD):
                part = part + e[:, lanes(i)]
            sum_ref[p] += part
            acc_ref[p] += dot(e.astype(BF16), vs_ref[keys, lanes(p)], NN)

    last = (b * span) // KEY_TILE
    lax.fori_loop(0, last, lambda t, _: (tile(t, False), 0)[1], 0)
    tile(last, True)
    for p in heads:
        total = jnp.sum(sum_ref[p], axis=-1, keepdims=True)
        mixed = acc_ref[p] * (1.0 / total)
        for g in range(GROUPS):
            o_ref[rows, lanes(p * GROUPS + g)] = mixed[g * span : (g + 1) * span].astype(BF16)
        wide = jnp.broadcast_to(jnp.log2(total), (m, HD))
        lse_ref[p, 0] = jnp.transpose(wide)[0:1, :]


def attend(ids, order, q_raw, kv_raw, cosine, sine, gq, gk, span):
    rows = q_raw.shape[0]
    seq = kv_raw.shape[0]
    heads = q_raw.shape[1] // (GROUPS * HD)
    blocks, m = rows // span, GROUPS * span
    hp = heads
    whole = lambda k, ids, order: (0, 0)
    per_query = pl.BlockSpec((span, hp * GROUPS * HD), lambda j, ids, order: (j, 0))
    once = pl.Buffered(1)
    return pl.pallas_call(
        functools.partial(attend_kernel, span),
        out_shape=[
            jax.ShapeDtypeStruct((rows, heads * GROUPS * HD), BF16),
            jax.ShapeDtypeStruct((heads, blocks, 1, m), F32),
        ],
        grid_spec=pltpu.PrefetchScalarGridSpec(
            num_scalar_prefetch=2,
            grid=(blocks,),
            in_specs=[
                per_query,
                pl.BlockSpec((seq, hp * HD), whole, pipeline_mode=once),
                pl.BlockSpec((seq, hp * HD), lambda j, ids, order: (0, 1), pipeline_mode=once),
                pl.BlockSpec((seq, HD), whole, pipeline_mode=once),
                pl.BlockSpec((seq, HD), whole, pipeline_mode=once),
                pl.BlockSpec((1, HD), whole),
                pl.BlockSpec((1, HD), whole),
            ],
            out_specs=[
                per_query,
                pl.BlockSpec((hp, 1, 1, m), lambda j, ids, order: (0, j, 0, 0)),
            ],
            scratch_shapes=[
                pltpu.VMEM((seq, hp * HD), BF16),
                pltpu.VMEM((seq, hp * HD), BF16),
                pltpu.VMEM((hp, m, HD), F32),
                pltpu.VMEM((hp, m, HD), F32),
            ],
        ),
        compiler_params=pltpu.CompilerParams(vmem_limit_bytes=48 * MIB),
        cost_estimate=pl.CostEstimate(
            flops=2 * 2 * rows * seq * heads * GROUPS * HD,
            bytes_accessed=2 * (2 * rows * heads * GROUPS * HD + 2 * seq * heads * HD),
            transcendentals=rows * seq * heads * GROUPS // 2,
        ),
        name="attend",
    )(ids, order, q_raw, kv_raw, kv_raw, cosine, sine, gq, gk)


def attend_back_kernel(
    span, ids_ref, order_ref, q_ref, k_ref, v_ref, do_ref, o_ref, lse_ref, cos_ref, sin_ref, gq_ref, gk_ref,
    dq_ref, dk_ref, dv_ref, dgq_ref, dgk_ref, ks_ref, vs_ref, dka_ref, dva_ref, dqa_ref,
):
    heads = range(k_ref.shape[1] // HD)

    @pl.when(pl.program_id(0) == 0)
    def _():
        prepare_keys(span, order_ref, k_ref, v_ref, cos_ref, sin_ref, gk_ref, ks_ref, vs_ref)
        dka_ref[...] = jnp.zeros_like(dka_ref)
        dva_ref[...] = jnp.zeros_like(dva_ref)
        dgq_ref[...] = jnp.zeros_like(dgq_ref)
        dgk_ref[...] = jnp.zeros_like(dgk_ref)

    b = ids_ref[pl.program_id(0)]
    rows = slice(None)
    places = pl.ds(pl.multiple_of(b * span, span), span)
    q2, do2, delta, lse = [], [], [], []
    for p in heads:
        q2.append(query_block(q_ref, p, rows, places, cos_ref, sin_ref, gq_ref)[2])
        pick = lambda ref: jnp.concatenate([ref[rows, lanes(p * GROUPS + g)] for g in range(GROUPS)], axis=0)
        do2.append(pick(do_ref))
        delta.append(
            jnp.sum(jnp.transpose(do2[p].astype(F32) * pick(o_ref).astype(F32)), axis=0, keepdims=True)
        )
        lse.append(lse_ref[p, 0])
    dqa_ref[...] = jnp.zeros_like(dqa_ref)

    def tile(t, masked):
        keys = pl.ds(pl.multiple_of(t * KEY_TILE, KEY_TILE), KEY_TILE)
        kt = [ks_ref[keys, lanes(p)] for p in heads]
        scores = [dot(kt[p], q2[p], NT) for p in heads]
        slopes = [dot(vs_ref[keys, lanes(p)], do2[p], NT) for p in heads]
        keep = seen(scores[0].shape, t, b, span, 0) if masked else None
        for p in heads:
            e = jnp.exp2(scores[p] - lse[p])
            if masked:
                e = jnp.where(keep, e, 0.0)
            ds = (e * (slopes[p] - delta[p])).astype(BF16)
            dva_ref[keys, lanes(p)] += dot(e.astype(BF16), do2[p], NN)
            dka_ref[keys, lanes(p)] += dot(ds, q2[p], NN)
            dqa_ref[p] += dot(ds, kt[p], TN)

    last = (b * span) // KEY_TILE
    lax.fori_loop(0, last, lambda t, _: (tile(t, False), 0)[1], 0)
    tile(last, True)
    for p in heads:
        units, scales, _q = query_block(q_ref, p, rows, places, cos_ref, sin_ref, gq_ref)
        dq = dqa_ref[p] * HD**-0.5
        for g in range(GROUPS):
            grad = rope_back(dq[g * span : (g + 1) * span], cos_ref[places, :], sin_ref[places, :])
            dgq_ref[...] += jnp.sum(grad * units[g], axis=0, keepdims=True)
            u = grad * gq_ref[...]
            back = scales[g] * (u - units[g] * row_mean(u * units[g]))
            dq_ref[rows, lanes(p * GROUPS + g)] = back.astype(BF16)

    def finish(i, _):
        rows = pl.ds(pl.multiple_of(i * span, span), span)
        source = pl.ds(pl.multiple_of(order_ref[i] * span, span), span)
        for p in heads:
            unit, r = unit_rows(k_ref[source, lanes(p)].astype(F32))
            grad = rope_back(dka_ref[rows, lanes(p)] * (1.0 / LOG2E), cos_ref[rows, :], sin_ref[rows, :])
            dgk_ref[...] += jnp.sum(grad * unit, axis=0, keepdims=True)
            u = grad * gk_ref[...]
            back = r * (u - unit * row_mean(u * unit))
            dk_ref[source, lanes(p)] = back.astype(BF16)
        dv_ref[source, :] = dva_ref[rows, :].astype(BF16)
        return 0

    @pl.when(pl.program_id(0) == pl.num_programs(0) - 1)
    def _():
        lax.fori_loop(0, k_ref.shape[0] // span, finish, 0)


def attend_back(ids, order, q_raw, kv_raw, grad_mixed, mixed, lse, cosine, sine, gq, gk, span):
    rows = q_raw.shape[0]
    seq = kv_raw.shape[0]
    heads = q_raw.shape[1] // (GROUPS * HD)
    blocks, m = rows // span, GROUPS * span
    hp = heads
    whole = lambda k, ids, order: (0, 0)
    once = pl.Buffered(1)
    per_query = pl.BlockSpec((span, hp * GROUPS * HD), lambda j, ids, order: (j, 0))
    per_key = pl.BlockSpec((seq, hp * HD), whole, pipeline_mode=once)
    gain = pl.BlockSpec((1, HD), whole)
    return pl.pallas_call(
        functools.partial(attend_back_kernel, span),
        out_shape=[
            jax.ShapeDtypeStruct((rows, heads * GROUPS * HD), BF16),
            jax.ShapeDtypeStruct((seq, heads * HD), BF16),
            jax.ShapeDtypeStruct((seq, heads * HD), BF16),
            jax.ShapeDtypeStruct((1, HD), F32),
            jax.ShapeDtypeStruct((1, HD), F32),
        ],
        grid_spec=pltpu.PrefetchScalarGridSpec(
            num_scalar_prefetch=2,
            grid=(blocks,),
            in_specs=[
                per_query,
                per_key,
                pl.BlockSpec((seq, hp * HD), lambda j, ids, order: (0, 1), pipeline_mode=once),
                per_query,
                per_query,
                pl.BlockSpec((hp, 1, 1, m), lambda j, ids, order: (0, j, 0, 0)),
                pl.BlockSpec((seq, HD), whole, pipeline_mode=once),
                pl.BlockSpec((seq, HD), whole, pipeline_mode=once),
                gain,
                gain,
            ],
            out_specs=[per_query] + [pl.BlockSpec((seq, hp * HD), whole)] * 2 + [gain, gain],
            scratch_shapes=[
                pltpu.VMEM((seq, hp * HD), BF16),
                pltpu.VMEM((seq, hp * HD), BF16),
                pltpu.VMEM((seq, hp * HD), F32),
                pltpu.VMEM((seq, hp * HD), F32),
                pltpu.VMEM((hp, m, HD), F32),
            ],
        ),
        compiler_params=pltpu.CompilerParams(vmem_limit_bytes=46 * MIB),
        cost_estimate=pl.CostEstimate(
            flops=5 * 2 * rows * seq * heads * GROUPS * HD // 2,
            bytes_accessed=2 * (4 * rows * heads * GROUPS * HD + 4 * seq * heads * HD),
            transcendentals=rows * seq * heads * GROUPS // 2,
        ),
        name="attend_back",
    )(ids, order, q_raw, kv_raw, kv_raw, grad_mixed, mixed, lse, cosine, sine, gq, gk)


def project_kernel(own, chip_ref, x_ref, gain_ref, wq_ref, wkv_ref, h_ref, q_ref, kv_ref):
    hidden = normed(x_ref[...].astype(F32), gain_ref[...]).astype(BF16)
    h_ref[...] = hidden
    kv_ref[...] = dot(hidden, wkv_ref[...], NN).astype(BF16)

    @pl.when(pl.program_id(0) < own)
    def _():
        q_ref[...] = dot(hidden, wq_ref[...], NN).astype(BF16)


def project(chip, x_all, gain, w_all, first, chip_rows):
    seq, width = x_all.shape
    size = min(ROW_TILE, chip_rows)
    own, tiles = chip_rows // size, seq // size
    at = lambda i, chip: ((i + chip[0] * own) % tiles, 0)
    weight = lambda col: pl.BlockSpec((width, width), lambda i, chip: (0, col), pipeline_mode=pl.Buffered(1))
    return pl.pallas_call(
        functools.partial(project_kernel, own),
        out_shape=[
            jax.ShapeDtypeStruct((seq, width), BF16),
            jax.ShapeDtypeStruct((chip_rows, width), BF16),
            jax.ShapeDtypeStruct((seq, width), BF16),
        ],
        grid_spec=pltpu.PrefetchScalarGridSpec(
            num_scalar_prefetch=1,
            grid=(tiles,),
            in_specs=[
                pl.BlockSpec((size, width), at),
                pl.BlockSpec((1, width), lambda i, chip: (0, 0)),
                weight(first // width),
                weight(first // width + 1),
            ],
            out_specs=[
                pl.BlockSpec((size, width), at),
                pl.BlockSpec((size, width), lambda i, chip: (jnp.minimum(i, own - 1), 0)),
                pl.BlockSpec((size, width), at),
            ],
        ),
        compiler_params=pltpu.CompilerParams(vmem_limit_bytes=48 * MIB),
        name="project",
    )(chip, x_all, gain, w_all, w_all)


def project_back_kernel(own, chip_ref, dq_ref, dk_ref, dv_ref, x_ref, wq_ref, wk_ref, wv_ref, p_ref, g_ref, acc_ref):
    i = pl.program_id(0)
    acc_ref[...] = dot(dk_ref[...], wk_ref[...], NT) + dot(dv_ref[...], wv_ref[...], NT)

    @pl.when(i < own)
    def _():
        acc_ref[...] += dot(dq_ref[...], wq_ref[...], NT)

    @pl.when(i == 0)
    def _():
        g_ref[...] = jnp.zeros_like(g_ref)

    part = acc_ref[...]
    p_ref[...] = part.astype(BF16)
    g_ref[...] += jnp.sum(part * normed(x_ref[...].astype(F32), 1.0), axis=0, keepdims=True)


def project_back(chip, dq, dk, dv, x_all, w_all, first):
    seq, width = x_all.shape
    chip_rows, kv = dq.shape[0], dk.shape[1]
    size = min(ROW_TILE, chip_rows)
    own, tiles = chip_rows // size, seq // size
    at = lambda i, chip: ((i + chip[0] * own) % tiles, 0)
    weight = lambda cols, col: pl.BlockSpec((width, cols), lambda i, chip: (0, col), pipeline_mode=pl.Buffered(1))
    return pl.pallas_call(
        functools.partial(project_back_kernel, own),
        out_shape=[jax.ShapeDtypeStruct((seq, width), BF16), jax.ShapeDtypeStruct((1, width), F32)],
        grid_spec=pltpu.PrefetchScalarGridSpec(
            num_scalar_prefetch=1,
            grid=(tiles,),
            in_specs=[
                pl.BlockSpec((size, width), lambda i, chip: (jnp.minimum(i, own - 1), 0)),
                pl.BlockSpec((size, kv), at),
                pl.BlockSpec((size, kv), at),
                pl.BlockSpec((size, width), at),
                weight(width, first // width),
                weight(kv, (first + width) // kv),
                weight(kv, (first + width) // kv + 1),
            ],
            out_specs=[
                pl.BlockSpec((size, width), at),
                pl.BlockSpec((1, width), lambda i, chip: (0, 0)),
            ],
            scratch_shapes=[pltpu.VMEM((size, width), F32)],
        ),
        compiler_params=pltpu.CompilerParams(vmem_limit_bytes=48 * MIB),
        name="project_back",
    )(chip, dq, dk, dv, x_all, w_all, w_all, w_all)


def feed_kernel(chip_ref, x_ref, p0_ref, p1_ref, gain_ref, w_ref, mid_ref, sec_ref, act_ref, gu_ref):
    count = x_ref.shape[0]
    size = min(ROW_TILE, count)
    tile = lambda i: pl.ds(pl.multiple_of(i * size, size), size)

    @pl.when(pl.program_id(0) == 0)
    def _():
        def start(i, _):
            rows = tile(i)
            middle = x_ref[rows, :].astype(F32) + (p0_ref[rows, :].astype(F32) + p1_ref[rows, :].astype(F32))
            mid_ref[rows, :] = middle
            sec_ref[rows, :] = normed(middle, gain_ref[...]).astype(BF16)
            return 0

        lax.fori_loop(0, count // size, start, 0)

    def body(i, _):
        rows = tile(i)
        both = dot(sec_ref[rows, :], w_ref[...], NN)
        gate, up = both[:, :FF_TILE], both[:, FF_TILE:]
        act_ref[rows, :] = (gate * jax.nn.sigmoid(gate) * up).astype(BF16)
        gu_ref[rows, :] = both.astype(BF16)
        return 0

    lax.fori_loop(0, count // size, body, 0)


def feed(chip, x_all, p0, p1, gain, w_all, ff):
    rows, width = p0.shape
    once = pl.Buffered(1)
    whole = lambda: pl.BlockSpec((rows, width), lambda j, chip: (0, 0), pipeline_mode=once)
    return pl.pallas_call(
        feed_kernel,
        out_shape=[
            jax.ShapeDtypeStruct((rows, width), F32),
            jax.ShapeDtypeStruct((rows, width), BF16),
            jax.ShapeDtypeStruct((rows, ff), BF16),
            jax.ShapeDtypeStruct((rows, 2 * ff), BF16),
        ],
        grid_spec=pltpu.PrefetchScalarGridSpec(
            num_scalar_prefetch=1,
            grid=(ff // FF_TILE,),
            in_specs=[
                pl.BlockSpec((rows, width), lambda j, chip: (chip[0], 0), pipeline_mode=once),
                whole(), whole(),
                pl.BlockSpec((1, width), lambda j, chip: (0, 0)),
                pl.BlockSpec((width, 2 * FF_TILE), lambda j, chip: (0, j)),
            ],
            out_specs=[
                pl.BlockSpec((rows, width), lambda j, chip: (0, 0)),
                pl.BlockSpec((rows, width), lambda j, chip: (0, 0)),
                pl.BlockSpec((rows, FF_TILE), lambda j, chip: (0, j)),
                pl.BlockSpec((rows, 2 * FF_TILE), lambda j, chip: (0, j)),
            ],
        ),
        compiler_params=pltpu.CompilerParams(vmem_limit_bytes=38 * MIB),
        name="feed",
    )(chip, x_all, p0, p1, gain, w_all)


def feed_back_kernel(core_ref, gu_ref, go_ref, wd_ref, gg_ref, d_ref):
    count = gu_ref.shape[0]
    size = min(ROW_TILE, count)
    unit = wd_ref.shape[2]
    for u in range(FF_TILE // unit):
        d_ref[u * unit : (u + 1) * unit, :] = wd_ref[u, 0]

    def body(i, _):
        rows = pl.ds(pl.multiple_of(i * size, size), size)
        grad = dot(go_ref[rows, :], d_ref[...], NT)
        gate, up = gu_ref[rows, :FF_TILE].astype(F32), gu_ref[rows, FF_TILE:].astype(F32)
        sig = jax.nn.sigmoid(gate)
        gg_ref[rows, :FF_TILE] = (grad * up * sig * (1.0 + gate * (1.0 - sig))).astype(BF16)
        gg_ref[rows, FF_TILE:] = (grad * (gate * sig)).astype(BF16)
        return 0

    lax.fori_loop(0, count // size, body, 0)


def feed_back(core, gate_up, go, w_down):
    rows, width = go.shape
    chips, _, unit, _ = w_down.shape
    ff = chips * unit
    return pl.pallas_call(
        feed_back_kernel,
        out_shape=[jax.ShapeDtypeStruct((rows, 2 * ff), BF16), jax.ShapeDtypeStruct((ff, width), BF16)],
        grid_spec=pltpu.PrefetchScalarGridSpec(
            num_scalar_prefetch=1,
            grid=(ff // FF_TILE,),
            in_specs=[
                pl.BlockSpec((rows, 2 * FF_TILE), lambda j, core: (0, j)),
                pl.BlockSpec((rows, width), lambda j, core: (0, 0), pipeline_mode=pl.Buffered(1)),
                pl.BlockSpec((FF_TILE // unit, 1, unit, width), lambda j, core: (j, core[0], 0, 0)),
            ],
            out_specs=[
                pl.BlockSpec((rows, 2 * FF_TILE), lambda j, core: (0, j)),
                pl.BlockSpec((FF_TILE, width), lambda j, core: (j, 0)),
            ],
        ),
        compiler_params=pltpu.CompilerParams(vmem_limit_bytes=48 * MIB),
        name="feed_back",
    )(core, gate_up, go, w_down)


def middle_back_kernel(mid_ref, s0_ref, s1_ref, go_ref, gain_ref, wo_ref, ga_ref, gm_ref, g_ref):
    back, terms = norm_back(mid_ref[...], gain_ref[...], s0_ref[...].astype(F32) + s1_ref[...].astype(F32))
    grad = (go_ref[...].astype(F32) + back).astype(BF16)
    ga_ref[...] = grad
    gm_ref[...] = dot(grad, wo_ref[...], NT).astype(BF16)

    @pl.when(pl.program_id(0) == 0)
    def _():
        g_ref[...] = jnp.zeros_like(g_ref)

    g_ref[...] += jnp.sum(terms, axis=0, keepdims=True)


def middle_back(middle, s0, s1, go, gain, w_out):
    rows, width = middle.shape
    size = min(ROW_TILE, rows)
    row = pl.BlockSpec((size, width), lambda i: (i, 0))
    line = pl.BlockSpec((1, width), lambda i: (0, 0))
    return pl.pallas_call(
        middle_back_kernel,
        out_shape=[
            jax.ShapeDtypeStruct((rows, width), BF16),
            jax.ShapeDtypeStruct((rows, w_out.shape[0]), BF16),
            jax.ShapeDtypeStruct((1, width), F32),
        ],
        grid=(rows // size,),
        in_specs=[row, row, row, row, line, pl.BlockSpec(w_out.shape, lambda i: (0, 0), pipeline_mode=pl.Buffered(1))],
        out_specs=[row, pl.BlockSpec((size, w_out.shape[0]), lambda i: (i, 0)), line],
        compiler_params=pltpu.CompilerParams(vmem_limit_bytes=22 * MIB),
        name="middle_back",
    )(middle, s0, s1, go, gain, w_out)


LINK_TIME = pl.CostEstimate(flops=0, bytes_accessed=300_000_000, transcendentals=0)


def peers():
    dp, ctx = lax.axis_index("dp"), lax.axis_index("ctx")
    to = lambda d, k: (jnp.bitwise_xor(dp, d), jnp.bitwise_xor(ctx, k))
    return dp, ctx, to


def greet(devices):
    barrier = pltpu.get_barrier_semaphore()
    for device in devices:
        pl.semaphore_signal(barrier, inc=1, device_id=device, device_id_type=MESH)
    pl.semaphore_wait(barrier, len(devices))


def sender(send_sem, recv_sem):
    made = []

    def send(src, dst, device):
        i = len(made)
        copy = pltpu.make_async_remote_copy(
            src_ref=src, dst_ref=dst, send_sem=send_sem.at[i], recv_sem=recv_sem.at[i],
            device_id=device, device_id_type=MESH,
        )
        copy.start()
        made.append(copy)
        return copy

    return send, made


def gather_kernel(pk_ref, wo_ref, tok_ref, go_ref, w_ref, x_ref, g_ref, send_sem, recv_sem, local_sem):
    dp, ctx, to = peers()
    c, z = ctx % 2, ctx // 2
    which, me = ctx // 4, ctx % 4
    inner = jnp.logical_or(z == 1, z == 2)
    greet([to(0, 1), to(0, 2), to(0, 4), to(0, 6), to(1, 0), to(2, 0)])
    send, made = sender(send_sem, recv_sem)
    sib, nbr, far, across, xn, yn = to(0, 1), to(0, 2), to(0, 4), to(0, 6), to(1, 0), to(2, 0)
    rows, cols = pk_ref.shape[1:]

    place = w_ref.at[dp, z, pl.ds(c * rows, rows), pl.ds(0, cols)]
    local = [
        pltpu.make_async_copy(pk_ref.at[c], place, local_sem.at[0]),
        pltpu.make_async_copy(wo_ref, w_ref.at[dp, z, :, pl.ds(cols, wo_ref.shape[1])], local_sem.at[1]),
        pltpu.make_async_copy(tok_ref.at[which], x_ref.at[me, 0], local_sem.at[2]),
        pltpu.make_async_copy(go_ref.at[which], g_ref.at[c, 0], local_sem.at[3]),
    ]
    for copy in local:
        copy.start()
    cross = send(pk_ref.at[1 - c], place, sib)
    for copy in local:
        copy.wait()
    cross.wait_recv()
    done = []

    def half(h, q, zz):
        return w_ref.at[q, zz, pl.ds(h * rows, rows)]

    first = []

    def spread(zz):
        low, high = half(0, dp, zz), half(1, dp, zz)
        first.append((send(low, low, yn), low, half(0, jnp.bitwise_xor(dp, 2), zz), xn))
        first.append((send(high, high, xn), high, half(1, jnp.bitwise_xor(dp, 1), zz), yn))

    def pass_on():
        for copy, own, part, device in first[:2]:
            done.append(send(own, own, device))
            copy.wait_recv()
            done.append(send(part, part, device))
        del first[:2]

    z_one = jnp.bitwise_xor(z, 1)
    z_near = jnp.bitwise_xor(z, jnp.where(inner, 3, 2))
    z_far = jnp.bitwise_xor(z, jnp.where(inner, 2, 3))
    relayed = []

    def relay(slot, source, device):
        copy = pltpu.make_async_remote_copy(
            src_ref=w_ref.at[dp, source], dst_ref=w_ref.at[dp, source],
            send_sem=send_sem.at[send_sem.shape[0] - 4 + len(relayed)],
            recv_sem=recv_sem.at[send_sem.shape[0] - 2 + slot],
            device_id=device, device_id_type=MESH,
        )
        relayed.append(copy)
        pl.when(inner)(copy.start)
        return copy

    step = send(w_ref.at[dp, z], w_ref.at[dp, z], nbr)
    near = relay(0, z, across)
    spread(z)
    pass_on()
    step.wait_recv()
    far_block = relay(1, z_one, across)
    spread(z_one)
    near.wait_recv()
    relay(0, z_near, nbr)
    spread(z_near)
    pass_on()
    far_block.wait_recv()
    relay(1, z_far, nbr)
    spread(z_far)
    swap = send(tok_ref.at[1 - which], x_ref.at[me, 1], far)
    mine_nbr = send(tok_ref.at[which], x_ref.at[me, 0], nbr)
    done += [send(tok_ref.at[which], x_ref.at[me, 0], sib), send(go_ref.at[which], g_ref.at[c, 0], sib)]
    pass_on()
    swap.wait_recv()
    done.append(send(x_ref.at[me, 1], x_ref.at[me, 1], sib))
    swap_nbr = send(x_ref.at[me, 1], x_ref.at[me, 1], nbr)
    go_swap = send(go_ref.at[1 - which], g_ref.at[c, 1], far)
    pass_on()
    other = jnp.bitwise_xor(me, 2)
    mine_nbr.wait_recv()
    done.append(send(x_ref.at[other, 0], x_ref.at[other, 0], sib))
    swap_nbr.wait_recv()
    done.append(send(x_ref.at[other, 1], x_ref.at[other, 1], sib))
    go_swap.wait_recv()
    done.append(send(g_ref.at[c, 1], g_ref.at[c, 1], sib))
    for copy in done:
        copy.wait_recv()
    for copy in made:
        copy.wait_send()

    @pl.when(inner)
    def _():
        for copy in relayed:
            copy.wait_send()


def gather(packed, w_out, tokens, grad_out):
    rows, cols = 2 * packed.shape[1], packed.shape[2] + w_out.shape[1]
    slots, width = tokens.shape[1:]
    copies = 36 + 4
    anywhere = pl.BlockSpec(memory_space=pl.ANY)
    near = pl.BlockSpec(memory_space=pltpu.VMEM)
    w, x, g = pl.pallas_call(
        gather_kernel,
        out_shape=[
            jax.ShapeDtypeStruct((4, 4, rows, cols), BF16),
            jax.ShapeDtypeStruct((4, 2, slots, width), BF16),
            jax.ShapeDtypeStruct((2, 2, slots, width), BF16),
        ],
        in_specs=[near] * 4,
        out_specs=[anywhere] * 3,
        scratch_shapes=[
            pltpu.SemaphoreType.DMA((copies,)),
            pltpu.SemaphoreType.DMA((copies,)),
            pltpu.SemaphoreType.DMA((4,)),
        ],
        compiler_params=pltpu.CompilerParams(
            collective_id=0, has_side_effects=True, vmem_limit_bytes=48 * MIB
        ),
        cost_estimate=LINK_TIME,
        name="gather",
    )(packed, w_out, tokens, grad_out)
    return w.reshape(16 * rows, cols), x.reshape(-1, width), g.reshape(-1, width)


def reduce_kernel(
    h_hbm, dq_hbm, dk_hbm, dv_hbm, e_hbm, ow_hbm, or_hbm, part_ref, xa_hbm, gm_hbm, gain_ref,
    a_ref, go_ref, ig_ref,
    g_ref, in_a, in_b, mid_a, mid_b, got_a, got_b, out3, in3, mine_ref, sib_ref, give_ref, nbr_ref, back_ref,
    x_ref, ga_ref, h_ref, dq_ref, dk_ref, dv_ref, o_ref, s_ref, send_sem, recv_sem, local_sem,
):
    dp, ctx, to = peers()
    c, z = ctx % 2, ctx // 2
    which, chip = ctx // 4, z % 2
    x, y = dp % 2, dp // 2
    hr = g_ref.shape[3] // 2
    count = mine_ref.shape[1]
    q_cols, kv_cols = dq_ref.shape[1], dk_ref.shape[1]
    near = s_ref.shape[1]
    first_col, width = near - HD, ow_hbm.shape[-1]
    local = []

    def fetch(src, dst):
        copy = pltpu.make_async_copy(src, dst, local_sem.at[len(local)])
        copy.start()
        local.append(copy)

    fetch(ow_hbm.at[:, :, c], g_ref.at[c, :, :, :, pl.ds(near, width)])
    fetch(or_hbm, g_ref.at[1 - c, :, :, :, pl.ds(near, width)])
    fetch(e_hbm, g_ref.at[:, :, :, :, pl.ds(first_col, HD)])
    fetch(part_ref.at[:, c], mine_ref)
    fetch(dq_hbm, dq_ref)
    fetch(h_hbm, h_ref)
    fetch(dk_hbm, dk_ref)
    fetch(dv_hbm, dv_ref)
    fetch(xa_hbm.at[ctx % 4], x_ref)
    fetch(gm_hbm.at[c], ga_ref)
    greet([to(0, 1), to(0, 2), to(0, 4), to(0, 6), to(1, 0), to(2, 0)])
    send, made = sender(send_sem, recv_sem)
    sib, nbr, far, across = to(0, 1), to(0, 2), to(0, 4), to(0, 6)
    xn, yn = to(1, 0), to(2, 0)
    cross = send(part_ref.at[:, 1 - c], sib_ref, sib)

    def ready(count):
        for copy in local[:count]:
            copy.wait()
        del local[:count]

    def weigh(rows, grad_ref, at):
        def body(i, _):
            some = h_ref[rows, pl.ds(pl.multiple_of(i * 4 * 2 * hr, 128), 4 * 2 * hr)]
            part = dot(some, grad_ref[...], TN).astype(BF16)
            g_ref[i // 2, i % 2, :, :, at : at + grad_ref.shape[1]] = part.reshape(4, 2 * hr, grad_ref.shape[1])
            return 0

        lax.fori_loop(0, 4, body, 0)

    low, high = pl.ds(0, hr), pl.ds(hr, hr)
    inner = jnp.logical_or(z == 1, z == 2)
    outer = jnp.logical_not(inner)
    order = [jnp.bitwise_xor(z, jnp.where(inner, 3, 2)), jnp.bitwise_xor(z, jnp.where(inner, 2, 3)), jnp.bitwise_xor(z, 1), z]
    passed = []

    def pass_z(kind, slot, source, part, device, role):
        copy = pltpu.make_async_remote_copy(
            src_ref=out3.at[source, :, parts[part]], dst_ref=in3.at[slot, :, parts[part]],
            send_sem=send_sem.at[40 + 2 * kind + part], recv_sem=recv_sem.at[40 + 2 * slot + part],
            device_id=device, device_id_type=MESH,
        )
        pl.when(role)(copy.start)
        passed.append((role, copy))

    def from_z(slot, part):
        return pltpu.make_async_remote_copy(
            src_ref=out3.at[0, :, parts[part]], dst_ref=in3.at[slot, :, parts[part]],
            send_sem=send_sem.at[40 + part], recv_sem=recv_sem.at[40 + 2 * slot + part],
            device_id=nbr, device_id_type=MESH,
        )

    def add_z(block, slot, part):
        p = parts[part]
        out3[block, :, p] = (out3[block, :, p].astype(F32) + in3[slot, :, p].astype(F32)).astype(BF16)

    def inward(i):
        k, part = i % 4, i // 4

        @pl.when(inner)
        def _():
            from_z(k, part).wait_recv()
            add_z(k, k, part)

        pass_z(3 + k, 3 + k, k, part, across, inner)

    def outward(part):
        @pl.when(inner)
        def _():
            from_z(4, part).wait_recv()
            add_z(2, 4, part)

        pass_z(5, 2, 2, part, nbr, inner)

    a_in, b_in, a_mid, b_mid = [], [], [], []
    size = 64
    tile = lambda i: pl.ds(pl.multiple_of(i * size, size), size)
    parts = (pl.ds(first_col, HD + width), pl.ds(0, first_col))

    def enter(i):
        k, p = i % 4, parts[i // 4]
        a_in.append(send(g_ref.at[:, 1 - x, order[k], low, p], in_a.at[k, :, :, p], xn))
        b_in.append(send(g_ref.at[1 - y, :, order[k], high, p], in_b.at[k, :, :, p], yn))

    def middle(i):
        k, p = i % 4, parts[i // 4]
        add = lambda p, q: (p.astype(F32) + q.astype(F32)).astype(BF16)
        a_in[i].wait_recv()
        mid_a[k, :, p] = add(g_ref[1 - y, x, order[k], 0:hr, p], in_a[k, 1 - y, :, p])
        a_mid.append(send(mid_a.at[k, :, p], got_a.at[k, :, p], yn))
        b_in[i].wait_recv()
        mid_b[k, :, p] = add(g_ref[y, 1 - x, order[k], hr:, p], in_b[k, 1 - x, :, p])
        b_mid.append(send(mid_b.at[k, :, p], got_b.at[k, :, p], xn))

    def leave(i):
        k, p = i % 4, parts[i // 4]
        add = lambda p, q, r: (p.astype(F32) + q.astype(F32) + r.astype(F32)).astype(BF16)
        a_mid[i].wait_recv()
        out3[k, 0:hr, p] = add(g_ref[y, x, order[k], 0:hr, p], in_a[k, y, :, p], got_a[k, :, p])
        b_mid[i].wait_recv()
        out3[k, hr:, p] = add(g_ref[y, x, order[k], hr:, p], in_b[k, x, :, p], got_b[k, :, p])
        if k < 3:
            pass_z(k, k, k, i // 4, nbr, outer)

    ready(3)
    enter(0)
    enter(1)
    enter(2)
    ready(1)
    cross.wait_recv()
    slots = ig_ref.shape[1]

    def give(i, _):
        rows = tile(i)
        give_ref[rows] = (mine_ref[1 - chip, rows].astype(F32) + sib_ref[1 - chip, rows].astype(F32)).astype(BF16)
        return 0

    def back(i, _):
        rows = tile(i)
        grad = mine_ref[chip, rows].astype(F32) + sib_ref[chip, rows].astype(F32) + nbr_ref[rows].astype(F32)
        through, _terms = norm_back(x_ref[rows, :].astype(F32), gain_ref[...], grad)
        back_ref[rows] = (ga_ref[rows, :].astype(F32) + through).astype(BF16)
        return 0

    swaps = []
    for first in (slots, 0):
        lax.fori_loop(first // size, (first + slots) // size, give, 0)
        rows = pl.ds(first, slots)
        swaps.append(send(give_ref.at[rows], nbr_ref.at[rows], nbr))
    ready(2)
    weigh(pl.ds(pl.multiple_of(chip * dq_ref.shape[0], dq_ref.shape[0]), dq_ref.shape[0]), dq_ref, 0)
    middle(0)
    enter(3)
    middle(1)
    middle(2)
    ready(2)
    weigh(slice(None), dk_ref, q_cols)
    weigh(slice(None), dv_ref, q_cols + kv_cols)
    enter(4)
    enter(5)
    leave(0)
    leave(1)
    middle(3)
    ready(2)
    swaps[0].wait_recv()
    lax.fori_loop(slots // size, 2 * slots // size, back, 0)
    home = send(back_ref.at[pl.ds(slots, slots)], ig_ref.at[which], far)
    leave(2)
    inward(0)
    inward(1)
    middle(4)
    enter(6)
    leave(3)
    middle(5)
    enter(7)
    leave(4)
    outward(0)
    swaps[1].wait_recv()
    lax.fori_loop(0, slots // size, back, 0)
    keep = pltpu.make_async_copy(back_ref.at[pl.ds(0, slots)], ig_ref.at[which], local_sem.at[0])
    keep.start()
    middle(6)
    leave(5)
    inward(4)
    middle(7)
    leave(6)
    inward(5)
    leave(7)
    outward(1)
    for part in range(2):
        from_z(2, part).wait_recv()

    @pl.when(inner)
    def _():
        for part in range(2):
            from_z(3, part).wait_recv()
            add_z(3, 3, part)

    total = out3[3].astype(F32) + in3[2].astype(F32)
    o_ref[...] = total[:, :near].astype(BF16)
    other = send(o_ref.at[pl.ds(pl.multiple_of((1 - c) * hr, hr), hr)], s_ref, sib)
    go_ref[...] = total[:, near:].astype(BF16)
    own = o_ref.at[pl.ds(pl.multiple_of(c * hr, hr), hr)]

    def place(source, core):
        at = 0
        for size in (q_cols, kv_cols, kv_cols):
            a_ref[:, pl.ds(pl.multiple_of(2 * at + core * size, HD), size)] = source[:, at : at + size]
            at += size

    place(own, c)
    other.wait_recv()
    place(s_ref, 1 - c)
    both = own[:, first_col:].astype(F32) + s_ref[:, first_col:].astype(F32)
    a_ref[:, 2 * first_col :] = both.astype(BF16)
    keep.wait()
    home.wait_recv()
    for copy in made:
        copy.wait_send()
    for role, copy in passed:
        pl.when(role)(copy.wait_send)


def reduce(hidden, dq, dk, dv, entries, out_own, out_sib, part, x_all, grad_middle, gain):
    seq, width = x_all.shape
    rows = width // 16
    near_cols = dq.shape[1] + dk.shape[1] + dv.shape[1] + HD
    cols = near_cols + width
    count = part.shape[0] // 4
    copies = 52
    anywhere = pl.BlockSpec(memory_space=pl.ANY)
    near = pl.BlockSpec(memory_space=pltpu.VMEM)
    return pl.pallas_call(
        reduce_kernel,
        out_shape=[
            jax.ShapeDtypeStruct((rows // 2, 2 * (near_cols - HD) + HD), BF16),
            jax.ShapeDtypeStruct((rows, width), BF16),
            jax.ShapeDtypeStruct((2, count // 2, width), BF16),
        ],
        in_specs=[anywhere] * 10 + [near],
        out_specs=[near] * 2 + [anywhere],
        scratch_shapes=[
            pltpu.VMEM((2, 2, 4, rows, cols), BF16),
            pltpu.VMEM((4, 2, rows // 2, cols), BF16),
            pltpu.VMEM((4, 2, rows // 2, cols), BF16),
        ]
        + [pltpu.VMEM((4, rows // 2, cols), BF16)] * 4
        + [
            pltpu.VMEM((4, rows, cols), BF16),
            pltpu.VMEM((5, rows, cols), BF16),
            pltpu.VMEM((2, count, width), BF16),
            pltpu.VMEM((2, count, width), BF16),
        ]
        + [pltpu.VMEM((count, width), BF16)] * 5
        + [pltpu.VMEM(v.shape, BF16) for v in (hidden, dq, dk, dv)]
        + [
            pltpu.VMEM((rows, near_cols), BF16),
            pltpu.VMEM((rows // 2, near_cols), BF16),
            pltpu.SemaphoreType.DMA((copies,)),
            pltpu.SemaphoreType.DMA((copies,)),
            pltpu.SemaphoreType.DMA((10,)),
        ],
        compiler_params=pltpu.CompilerParams(
            collective_id=1, has_side_effects=True, vmem_limit_bytes=48 * MIB
        ),
        cost_estimate=LINK_TIME,
        name="reduce",
    )(
        hidden, dq, dk, dv,
        entries.reshape(2, 2, 4, rows, HD),
        out_own.reshape(2, 4, 2, rows, width),
        out_sib.reshape(2, 4, rows, width),
        part.reshape(2, 2, count, width),
        x_all.reshape(4, count, width),
        grad_middle.reshape(2, count, width),
        gain,
    )


def by_core(c, own, other):
    return jnp.where(c == 0, jnp.stack([own, other]), jnp.stack([other, own]))


def layer(
    n_dp, n, tokens, positions, w_query, w_key, w_value, w_out, w_gate, w_up, w_down,
    attn_gain, mlp_gain, q_gain, k_gain, grad_out,
):
    axes = ("dp", "ctx")
    slots, width = tokens.shape[1:]
    seq = positions.shape[1]
    span = slots // 2
    half = n // 2
    chips = n_dp * half
    ctx = lax.axis_index("ctx")
    c = ctx % 2
    which = ctx // half
    r_in, r_out, r_down = w_query.shape[0], w_out.shape[0], w_down.shape[0]
    ff = w_gate.shape[1]
    ff_c = ff // 2
    q_c, kv_c = H * HD // 2, KV * HD // 2

    to_sibling = [(i, i ^ 1) for i in range(n)]
    to_partner = [(i, (i + half) % n) for i in range(n)]
    halves = [list(range(half)), list(range(half, n))]
    same_core = [list(range(0, n, 2)), list(range(1, n, 2))]
    sibling = lambda v: lax.ppermute(v, "ctx", to_sibling)
    partner = lambda v: lax.ppermute(v, "ctx", to_partner)

    def placed(values):
        mine = lax.dynamic_index_in_dim(values, which, 0, False)
        other = lax.dynamic_index_in_dim(values, 1 - which, 0, False)
        return jnp.concatenate([mine, partner(other)], axis=0)

    gains = jnp.concatenate(
        [
            attn_gain[:, None],
            mlp_gain[:, None],
            jnp.pad(q_gain, (0, r_in - q_gain.shape[0]))[:, None],
            jnp.pad(k_gain, (0, r_in - k_gain.shape[0]))[:, None],
            jnp.zeros((r_in, 124), BF16),
        ],
        axis=1,
    )
    tall = (n_dp, n) == (4, 8)
    qkv_halves = [
        jnp.concatenate(
            [
                w_query[:, i * q_c : (i + 1) * q_c],
                w_key[:, i * kv_c : (i + 1) * kv_c],
                w_value[:, i * kv_c : (i + 1) * kv_c],
            ],
            axis=1,
        )
        for i in range(2)
    ]

    def ff_order(shard):
        return shard.reshape(r_in, chips, 2, r_down).transpose(2, 0, 1, 3).reshape(2, r_in, ff_c)

    gate_order, up_order = ff_order(w_gate), ff_order(w_up)
    qkv_c = q_c + 2 * kv_c
    gu_c = 2 * ff_c
    all_c = gu_c + qkv_c
    by_tile = lambda v: v.reshape(2, r_in, ff_c // FF_TILE, FF_TILE)
    gu_shard = jnp.stack([by_tile(gate_order), by_tile(up_order)], axis=3).reshape(2, r_in, 2 * ff_c)
    packed = jnp.stack([jnp.concatenate([gu_shard[i], qkv_halves[i], gains], axis=1) for i in range(2)])
    if tall:
        w_all, x_all, go_chip = gather(packed, w_out, tokens, grad_out)
        out_rows = w_all[:, all_c + HD :].reshape(2, -1, r_out, width)
        out_keep = lax.dynamic_index_in_dim(out_rows, c, 0, False)
        out_give = lax.dynamic_index_in_dim(out_rows, 1 - c, 0, False)
        w_out_c = by_core(c, out_keep, sibling(out_give)).transpose(1, 0, 2, 3).reshape(q_c, width)
        w_down, w_all = lax.optimization_barrier((w_down, w_all))
    else:
        both = lax.all_gather(packed, axes, axis=1, tiled=True)
        w_all = lax.dynamic_index_in_dim(both, c, 0, False)
        out_all = lax.all_gather(w_out, axes, axis=0, tiled=True)
        w_out_c = lax.dynamic_slice_in_dim(out_all, c * q_c, q_c, 0)
        x_own = placed(tokens)
        x_all = lax.all_gather(x_own, "ctx", axis=0, tiled=True, axis_index_groups=halves)
        go_own = placed(grad_out)
        go_chip = by_core(c, go_own, sibling(go_own)).reshape(4 * slots, width)
    down_all = lax.all_gather(w_down, axes, axis=0, tiled=True).reshape(chips, 2, r_down, width)
    g_cols = w_all[:, all_c : all_c + HD].astype(F32)
    gain_attn = g_cols[:, 0][None]
    gain_mlp = g_cols[:, 1][None]
    per_head = g_cols.reshape(n_dp * n, r_in, HD)[:, : q_gain.shape[0]].reshape(HD, HD)
    gain_q = per_head[:, 2][None]
    gain_k = per_head[:, 3][None]

    chip = (ctx % half) // 2
    chip_rows = 4 * slots
    slot_ids = lax.dynamic_index_in_dim(positions, which, 0, False).reshape(2 * n, span)[:, 0] // span
    places = np.stack(
        [
            [s for d in side for k in (d, (d + half) % n) for s in (2 * k, 2 * k + 1)]
            for side in halves
        ]
    ).astype(np.int32)
    ids_all = slot_ids[lax.dynamic_index_in_dim(jnp.asarray(places), which, 0, False)]
    steps = jnp.arange(2 * n, dtype=jnp.int32)
    order = jnp.sum(jnp.where(ids_all[None, :] == steps[:, None], steps[None, :], 0), axis=1).astype(jnp.int32)
    ids = lax.dynamic_slice_in_dim(ids_all, chip * 8, 8, 0)
    cosine, sine = rope_tables(seq)

    chip_at = chip.astype(jnp.int32).reshape(1)
    hidden_all, q_raw, kv_raw = project(chip_at, x_all, gain_attn, w_all, gu_c, chip_rows)
    mixed, lse = attend(ids, order, q_raw, kv_raw, cosine, sine, gain_q, gain_k, span)
    proj = dot(mixed, w_out_c, NN, BF16)
    middle, second, activated, gate_up = feed(chip_at, x_all, proj, sibling(proj), gain_mlp, w_all, ff_c)
    grad_gu, w_down_c = feed_back(c.astype(jnp.int32).reshape(1), gate_up, go_chip, down_all)
    down = dot(activated, w_down_c, NN, BF16).reshape(2, 2 * slots, width)
    down_own = lax.dynamic_index_in_dim(down, c, 0, False)
    down_other = sibling(lax.dynamic_index_in_dim(down, 1 - c, 0, False))
    own_rows = lambda v: lax.dynamic_slice_in_dim(v, c * 2 * slots, 2 * slots, 0)
    result = (own_rows(middle) + (down_own.astype(F32) + down_other.astype(F32))).astype(BF16)

    def returned(rows):
        mine, back = rows[:slots], partner(rows[slots:])
        return jnp.where(which == 0, jnp.stack([mine, back]), jnp.stack([back, mine]))


    second_part = dot(grad_gu, w_all[:, :gu_c], NT, BF16)
    grad_gu_w = dot(second, grad_gu, TN, BF16)
    grad_down_w = dot(activated, go_chip, TN, BF16)
    grad_attn, grad_mixed, mlp_gain_sum = middle_back(
        middle, second_part, sibling(second_part), go_chip, gain_mlp, w_out_c
    )
    grad_mlp_gain = jnp.where(c == 0, mlp_gain_sum[0], 0.0)

    over_dp = lambda grad: lax.psum_scatter(grad, "dp", scatter_dimension=0, tiled=True)
    over_ctx = lambda part: lax.psum_scatter(
        part, "ctx", scatter_dimension=0, tiled=True, axis_index_groups=same_core
    )
    part_gu = over_dp(grad_gu_w)
    part_down = over_dp(grad_down_w)

    out_w = dot(mixed, grad_attn, TN, BF16).reshape(-1, 2, r_out, width)
    out_recv = sibling(lax.dynamic_index_in_dim(out_w, 1 - c, 1, False))
    out_recv, grad_mixed = lax.optimization_barrier((out_recv, grad_mixed))
    result, grad_mixed, part_down = lax.optimization_barrier((result, grad_mixed, part_down))
    if tall:
        pieces = part_down.reshape(half, r_down, width)
        place = ctx // 2
        down_own = lax.dynamic_index_in_dim(pieces, place, 0, False).astype(F32)
        down_got = [
            lax.ppermute(
                lax.dynamic_index_in_dim(pieces, jnp.bitwise_xor(place, k), 0, False),
                "ctx",
                [(i, i ^ (2 * k)) for i in range(n)],
            )
            for k in range(1, half)
        ]
    else:
        down_own, down_got = over_ctx(part_down).astype(F32), []
    output = returned(result)
    dq, dk, dv, dgq, dgk = attend_back(
        ids, order, q_raw, kv_raw, grad_mixed, mixed, lse, cosine, sine, gain_q, gain_k, span
    )
    output, dq, dk, dv, part_gu, down_got = lax.optimization_barrier((output, dq, dk, dv, part_gu, down_got))
    sum_gu = over_ctx(part_gu)
    sum_down = down_own
    for piece in down_got:
        sum_down = sum_down + piece.astype(F32)
    part_all, attn_gain_sum = project_back(chip_at, dq, dk, dv, x_all, w_all, gu_c)
    lot = lambda v: v.reshape(n_dp * n, -1)
    entries = jnp.concatenate([lot(attn_gain_sum), lot(grad_mlp_gain), lot(dgq), lot(dgk)], axis=1)
    entries = jnp.pad(entries[:, None], ((0, 0), (0, r_in - 1), (0, HD - entries.shape[1])))
    entries = entries.reshape(width, HD).astype(BF16)
    entries, sum_down = lax.optimization_barrier((entries, sum_down))
    near_c = qkv_c + HD
    beside = lambda v: v.transpose(1, 0, 2).reshape(r_in, -1)
    by_rows = lambda v: lax.dynamic_index_in_dim(v.reshape(2, r_in, -1), c, 0, False)

    def columns(sums):
        other = lax.dynamic_index_in_dim(sums.reshape(2, r_in, -1), 1 - c, 0, False)
        return by_core(c, by_rows(sums), sibling(other))

    if tall:
        sums, sum_out, input_grad = reduce(
            hidden_all, dq, dk, dv, entries, out_w, out_recv, part_all, x_all, grad_attn, gain_attn
        )
        grad_q, grad_k, grad_v = (
            sums[:, i:j].astype(F32) for i, j in ((0, 2 * q_c), (2 * q_c, 2 * q_c + 2 * kv_c), (2 * q_c + 2 * kv_c, 2 * qkv_c))
        )
        sum_out, gain_own = sum_out.astype(F32), sums[:, 2 * qkv_c :].astype(F32)
    else:
        hidden = lax.dynamic_slice_in_dim(hidden_all, chip * chip_rows, chip_rows, 0)
        grads = [dot(hidden, dq, TN, BF16), dot(hidden_all, dk, TN, BF16), dot(hidden_all, dv, TN, BF16), entries]
        qkv_own = columns(over_ctx(over_dp(jnp.concatenate(grads, axis=1)))).astype(F32)
        out_mine = lax.dynamic_index_in_dim(out_w, c, 1, False)
        sum_out = over_ctx(over_dp(by_core(c, out_mine, out_recv).reshape(chips * r_out, width))).astype(F32)
        grad_q = beside(qkv_own[:, :, :q_c])
        grad_k = beside(qkv_own[:, :, q_c : q_c + kv_c])
        grad_v = beside(qkv_own[:, :, q_c + kv_c : qkv_c])
        gain_own = jnp.sum(qkv_own[:, :, qkv_c:], axis=0)
        grad_hidden = lax.psum_scatter(
            part_all, "ctx", scatter_dimension=0, tiled=True, axis_index_groups=halves
        ).astype(F32)
        back, _terms = norm_back(x_own.astype(F32), gain_attn, grad_hidden)
        input_grad = returned((own_rows(grad_attn).astype(F32) + back).astype(BF16))
    sum_gu, gain_own = lax.optimization_barrier((sum_gu, gain_own))
    gain_row, r_head = gain_own[0], q_gain.shape[0]
    gu_own = columns(sum_gu).reshape(2, r_in, ff_c // FF_TILE, 2, FF_TILE)
    ff_back = lambda v: v.reshape(2, r_in, chips, r_down).transpose(1, 2, 0, 3).reshape(r_in, ff)
    return (
        output,
        input_grad,
        grad_q,
        grad_k,
        grad_v,
        sum_out,
        ff_back(gu_own[:, :, :, 0]).astype(F32),
        ff_back(gu_own[:, :, :, 1]).astype(F32),
        sum_down,
        gain_row[:r_in],
        gain_row[r_in : 2 * r_in],
        gain_row[2 * r_in : 2 * r_in + r_head],
        gain_row[2 * r_in + r_head : 2 * r_in + 2 * r_head],
    )


def solution(mesh):
    rows = P(("dp", "ctx"), None)
    gain = P(("dp", "ctx"))
    acts = P("dp", "ctx", None)
    return jax.shard_map(
        functools.partial(layer, mesh.shape["dp"], mesh.shape["ctx"]),
        mesh=mesh,
        in_specs=(acts, P("dp", None)) + (rows,) * 7 + (gain,) * 4 + (acts,),
        out_specs=(acts, acts) + (rows,) * 7 + (gain,) * 4,
        check_vma=False,
    )
```

```python
import functools

import jax
import jax.numpy as jnp
import numpy as np
from jax import lax
from jax.experimental import pallas as pl
from jax.experimental.pallas import tpu as pltpu
from jax.sharding import PartitionSpec as P

H = 16
KV = 8
HD = 128
GROUPS = H // KV
EPSILON = 1e-06
THETA = 1000000.0
LOG2E = 1.4426950408889634
KEY_TILE = 512
ROW_TILE = 256
TOKEN_TILE = 512
FF_TILE = 384
MIB = 1024 * 1024
MESH = pl.DeviceIdType.MESH
F32 = jnp.float32
BF16 = jnp.bfloat16


def normed(values, weights):
    return values * lax.rsqrt(jnp.mean(values * values, axis=-1, keepdims=True) + EPSILON) * weights


def norm_back(values, weights, grad):
    r = lax.rsqrt(jnp.mean(values * values, axis=-1, keepdims=True) + EPSILON)
    unit = values * r
    u = grad * weights
    return r * (u - unit * jnp.mean(u * unit, axis=-1, keepdims=True)), grad * unit


def rope_tables(seq):
    half = HD // 2
    inverse = (THETA ** (-(np.arange(half, dtype=np.float32) * np.float32(2.0) / np.float32(HD)))).astype(np.float32)
    angles = np.arange(seq, dtype=np.float32)[:, None] * inverse[None, :]
    cosine, sine = np.cos(angles), np.sin(angles)
    return (
        jnp.asarray(np.concatenate([cosine, cosine], axis=-1).astype(np.float32)),
        jnp.asarray(np.concatenate([-sine, sine], axis=-1).astype(np.float32)),
    )


def dot(a, b, dims, out=F32):
    return lax.dot_general(a, b, (dims, ((), ())), preferred_element_type=out)


NN = ((1,), (0,))
NT = ((1,), (1,))
TN = ((0,), (0,))


def row_mean(values):
    return dot(values.astype(BF16), jnp.full((HD, HD), 1.0 / HD, BF16), NN)


def row_sums(values):
    high = values.astype(BF16)
    ones = jnp.ones((8, HD), BF16)
    return (dot(ones, high, NT) + dot(ones, (values - high.astype(F32)).astype(BF16), NT))[0:1]


def unit_rows(raw):
    r = lax.rsqrt(row_mean(raw * raw) + EPSILON)
    return raw * r, r


def rope(values, cosine, sine):
    return values * cosine + pltpu.roll(values, HD // 2, 1) * sine


def rope_back(values, cosine, sine):
    return values * cosine - pltpu.roll(values, HD // 2, 1) * sine


def lanes(head, width=HD):
    return slice(head * width, (head + 1) * width)


def prepare_keys(span, order_ref, k_ref, v_ref, cos_ref, sin_ref, gk_ref, ks_ref, vs_ref):
    def body(i, _):
        rows = pl.ds(pl.multiple_of(i * span, span), span)
        source = pl.ds(pl.multiple_of(order_ref[i] * span, span), span)
        for p in range(k_ref.shape[1] // HD):
            unit, _r = unit_rows(k_ref[source, lanes(p)].astype(F32))
            ks_ref[rows, lanes(p)] = rope(unit * gk_ref[...], cos_ref[rows, :], sin_ref[rows, :]).astype(BF16)
        vs_ref[rows, :] = v_ref[source, :]
        return 0

    lax.fori_loop(0, k_ref.shape[0] // span, body, 0)


def query_block(q_ref, p, rows, places, cos_ref, sin_ref, gq_ref):
    units, scales, parts = [], [], []
    for g in range(GROUPS):
        unit, r = unit_rows(q_ref[rows, lanes(p * GROUPS + g)].astype(F32))
        turned = rope(unit * gq_ref[...], cos_ref[places, :], sin_ref[places, :])
        units.append(unit)
        scales.append(r)
        parts.append((turned * (LOG2E * HD**-0.5)).astype(BF16))
    return units, scales, jnp.concatenate(parts, axis=0)


def seen(shape, t, b, span, key_axis):
    at = t * KEY_TILE + lax.broadcasted_iota(jnp.int32, shape, key_axis)
    own = b * span + lax.broadcasted_iota(jnp.int32, shape, 1 - key_axis) % span
    return at <= own


def attend_kernel(
    span, ids_ref, order_ref, q_ref, k_ref, v_ref, cos_ref, sin_ref, gq_ref, gk_ref,
    o_ref, lse_ref, ks_ref, vs_ref, acc_ref, sum_ref,
):
    @pl.when(pl.program_id(0) == 0)
    def _():
        prepare_keys(span, order_ref, k_ref, v_ref, cos_ref, sin_ref, gk_ref, ks_ref, vs_ref)

    m = GROUPS * span
    heads = range(k_ref.shape[1] // HD)
    b = ids_ref[pl.program_id(0)]
    rows = slice(None)
    places = pl.ds(pl.multiple_of(b * span, span), span)
    q2 = [query_block(q_ref, p, rows, places, cos_ref, sin_ref, gq_ref)[2] for p in heads]
    acc_ref[...] = jnp.zeros_like(acc_ref)
    sum_ref[...] = jnp.zeros_like(sum_ref)

    def tile(t, masked):
        keys = pl.ds(pl.multiple_of(t * KEY_TILE, KEY_TILE), KEY_TILE)
        scores = [dot(q2[p], ks_ref[keys, lanes(p)], NT) for p in heads]
        keep = seen(scores[0].shape, t, b, span, 1) if masked else None
        for p in heads:
            e = jnp.exp2(scores[p])
            if masked:
                e = jnp.where(keep, e, 0.0)
            part = e[:, 0:HD]
            for i in range(1, KEY_TILE // HD):
                part = part + e[:, lanes(i)]
            sum_ref[p] += part
            acc_ref[p] += dot(e.astype(BF16), vs_ref[keys, lanes(p)], NN)

    last = (b * span) // KEY_TILE
    lax.fori_loop(0, last, lambda t, _: (tile(t, False), 0)[1], 0)
    tile(last, True)
    for p in heads:
        total = jnp.sum(sum_ref[p], axis=-1, keepdims=True)
        mixed = acc_ref[p] * (1.0 / total)
        for g in range(GROUPS):
            o_ref[rows, lanes(p * GROUPS + g)] = mixed[g * span : (g + 1) * span].astype(BF16)
        wide = jnp.broadcast_to(jnp.log2(total), (m, HD))
        lse_ref[p, 0] = jnp.transpose(wide)[0:1, :]


def attend(ids, order, q_raw, kv_raw, cosine, sine, gq, gk, span):
    rows = q_raw.shape[0]
    seq = kv_raw.shape[0]
    heads = q_raw.shape[1] // (GROUPS * HD)
    blocks, m = rows // span, GROUPS * span
    hp = heads
    whole = lambda k, ids, order: (0, 0)
    per_query = pl.BlockSpec((span, hp * GROUPS * HD), lambda j, ids, order: (j, 0))
    once = pl.Buffered(1)
    return pl.pallas_call(
        functools.partial(attend_kernel, span),
        out_shape=[
            jax.ShapeDtypeStruct((rows, heads * GROUPS * HD), BF16),
            jax.ShapeDtypeStruct((heads, blocks, 1, m), F32),
        ],
        grid_spec=pltpu.PrefetchScalarGridSpec(
            num_scalar_prefetch=2,
            grid=(blocks,),
            in_specs=[
                per_query,
                pl.BlockSpec((seq, hp * HD), whole, pipeline_mode=once),
                pl.BlockSpec((seq, hp * HD), lambda j, ids, order: (0, 1), pipeline_mode=once),
                pl.BlockSpec((seq, HD), whole, pipeline_mode=once),
                pl.BlockSpec((seq, HD), whole, pipeline_mode=once),
                pl.BlockSpec((1, HD), whole),
                pl.BlockSpec((1, HD), whole),
            ],
            out_specs=[
                per_query,
                pl.BlockSpec((hp, 1, 1, m), lambda j, ids, order: (0, j, 0, 0)),
            ],
            scratch_shapes=[
                pltpu.VMEM((seq, hp * HD), BF16),
                pltpu.VMEM((seq, hp * HD), BF16),
                pltpu.VMEM((hp, m, HD), F32),
                pltpu.VMEM((hp, m, HD), F32),
            ],
        ),
        compiler_params=pltpu.CompilerParams(vmem_limit_bytes=48 * MIB),
        cost_estimate=pl.CostEstimate(
            flops=2 * 2 * rows * seq * heads * GROUPS * HD,
            bytes_accessed=2 * (2 * rows * heads * GROUPS * HD + 2 * seq * heads * HD),
            transcendentals=rows * seq * heads * GROUPS // 2,
        ),
        name="attend",
    )(ids, order, q_raw, kv_raw, kv_raw, cosine, sine, gq, gk)


def attend_back_kernel(
    span, ids_ref, order_ref, q_ref, k_ref, v_ref, do_ref, o_ref, lse_ref, cos_ref, sin_ref, gq_ref, gk_ref,
    dq_ref, dk_ref, dv_ref, dgq_ref, dgk_ref, ks_ref, vs_ref, dka_ref, dva_ref, dqa_ref,
):
    heads = range(k_ref.shape[1] // HD)

    @pl.when(pl.program_id(0) == 0)
    def _():
        prepare_keys(span, order_ref, k_ref, v_ref, cos_ref, sin_ref, gk_ref, ks_ref, vs_ref)
        dka_ref[...] = jnp.zeros_like(dka_ref)
        dva_ref[...] = jnp.zeros_like(dva_ref)
        dgq_ref[...] = jnp.zeros_like(dgq_ref)
        dgk_ref[...] = jnp.zeros_like(dgk_ref)

    b = ids_ref[pl.program_id(0)]
    rows = slice(None)
    places = pl.ds(pl.multiple_of(b * span, span), span)
    q2, do2, delta, lse = [], [], [], []
    for p in heads:
        q2.append(query_block(q_ref, p, rows, places, cos_ref, sin_ref, gq_ref)[2])
        pick = lambda ref: jnp.concatenate([ref[rows, lanes(p * GROUPS + g)] for g in range(GROUPS)], axis=0)
        do2.append(pick(do_ref))
        delta.append(
            row_sums(do2[p].astype(F32) * pick(o_ref).astype(F32))
        )
        lse.append(lse_ref[p, 0])
    dqa_ref[...] = jnp.zeros_like(dqa_ref)

    def tile(t, masked):
        keys = pl.ds(pl.multiple_of(t * KEY_TILE, KEY_TILE), KEY_TILE)
        kt = [ks_ref[keys, lanes(p)] for p in heads]
        scores = [dot(kt[p], q2[p], NT) for p in heads]
        slopes = [dot(vs_ref[keys, lanes(p)], do2[p], NT) for p in heads]
        keep = seen(scores[0].shape, t, b, span, 0) if masked else None
        for p in heads:
            e = jnp.exp2(scores[p] - lse[p])
            if masked:
                e = jnp.where(keep, e, 0.0)
            ds = (e * (slopes[p] - delta[p])).astype(BF16)
            dva_ref[keys, lanes(p)] += dot(e.astype(BF16), do2[p], NN)
            dka_ref[keys, lanes(p)] += dot(ds, q2[p], NN)
            dqa_ref[p] += dot(ds, kt[p], TN)

    last = (b * span) // KEY_TILE
    lax.fori_loop(0, last, lambda t, _: (tile(t, False), 0)[1], 0)
    tile(last, True)
    for p in heads:
        units, scales, _q = query_block(q_ref, p, rows, places, cos_ref, sin_ref, gq_ref)
        dq = dqa_ref[p] * HD**-0.5
        for g in range(GROUPS):
            grad = rope_back(dq[g * span : (g + 1) * span], cos_ref[places, :], sin_ref[places, :])
            dgq_ref[...] += jnp.sum(grad * units[g], axis=0, keepdims=True)
            u = grad * gq_ref[...]
            back = scales[g] * (u - units[g] * row_mean(u * units[g]))
            dq_ref[rows, lanes(p * GROUPS + g)] = back.astype(BF16)

    def finish(i, _):
        rows = pl.ds(pl.multiple_of(i * span, span), span)
        source = pl.ds(pl.multiple_of(order_ref[i] * span, span), span)
        for p in heads:
            unit, r = unit_rows(k_ref[source, lanes(p)].astype(F32))
            grad = rope_back(dka_ref[rows, lanes(p)] * (1.0 / LOG2E), cos_ref[rows, :], sin_ref[rows, :])
            dgk_ref[...] += jnp.sum(grad * unit, axis=0, keepdims=True)
            u = grad * gk_ref[...]
            back = r * (u - unit * row_mean(u * unit))
            dk_ref[source, lanes(p)] = back.astype(BF16)
        dv_ref[source, :] = dva_ref[rows, :].astype(BF16)
        return 0

    @pl.when(pl.program_id(0) == pl.num_programs(0) - 1)
    def _():
        lax.fori_loop(0, k_ref.shape[0] // span, finish, 0)


def attend_back(ids, order, q_raw, kv_raw, grad_mixed, mixed, lse, cosine, sine, gq, gk, span):
    rows = q_raw.shape[0]
    seq = kv_raw.shape[0]
    heads = q_raw.shape[1] // (GROUPS * HD)
    blocks, m = rows // span, GROUPS * span
    hp = heads
    whole = lambda k, ids, order: (0, 0)
    once = pl.Buffered(1)
    per_query = pl.BlockSpec((span, hp * GROUPS * HD), lambda j, ids, order: (j, 0))
    per_key = pl.BlockSpec((seq, hp * HD), whole, pipeline_mode=once)
    gain = pl.BlockSpec((1, HD), whole)
    return pl.pallas_call(
        functools.partial(attend_back_kernel, span),
        out_shape=[
            jax.ShapeDtypeStruct((rows, heads * GROUPS * HD), BF16),
            jax.ShapeDtypeStruct((seq, heads * HD), BF16),
            jax.ShapeDtypeStruct((seq, heads * HD), BF16),
            jax.ShapeDtypeStruct((1, HD), F32),
            jax.ShapeDtypeStruct((1, HD), F32),
        ],
        grid_spec=pltpu.PrefetchScalarGridSpec(
            num_scalar_prefetch=2,
            grid=(blocks,),
            in_specs=[
                per_query,
                per_key,
                pl.BlockSpec((seq, hp * HD), lambda j, ids, order: (0, 1), pipeline_mode=once),
                per_query,
                per_query,
                pl.BlockSpec((hp, 1, 1, m), lambda j, ids, order: (0, j, 0, 0)),
                pl.BlockSpec((seq, HD), whole, pipeline_mode=once),
                pl.BlockSpec((seq, HD), whole, pipeline_mode=once),
                gain,
                gain,
            ],
            out_specs=[per_query] + [pl.BlockSpec((seq, hp * HD), whole)] * 2 + [gain, gain],
            scratch_shapes=[
                pltpu.VMEM((seq, hp * HD), BF16),
                pltpu.VMEM((seq, hp * HD), BF16),
                pltpu.VMEM((seq, hp * HD), F32),
                pltpu.VMEM((seq, hp * HD), F32),
                pltpu.VMEM((hp, m, HD), F32),
            ],
        ),
        compiler_params=pltpu.CompilerParams(vmem_limit_bytes=46 * MIB),
        cost_estimate=pl.CostEstimate(
            flops=5 * 2 * rows * seq * heads * GROUPS * HD // 2,
            bytes_accessed=2 * (4 * rows * heads * GROUPS * HD + 4 * seq * heads * HD),
            transcendentals=rows * seq * heads * GROUPS // 2,
        ),
        name="attend_back",
    )(ids, order, q_raw, kv_raw, kv_raw, grad_mixed, mixed, lse, cosine, sine, gq, gk)


def project_kernel(own, chip_ref, x_ref, gain_ref, wq_ref, wkv_ref, h_ref, q_ref, kv_ref):
    hidden = normed(x_ref[...].astype(F32), gain_ref[...]).astype(BF16)
    h_ref[...] = hidden
    kv_ref[...] = dot(hidden, wkv_ref[...], NN).astype(BF16)

    @pl.when(pl.program_id(0) < own)
    def _():
        q_ref[...] = dot(hidden, wq_ref[...], NN).astype(BF16)


def project(chip, x_all, gain, w_all, first, chip_rows):
    seq, width = x_all.shape
    size = min(TOKEN_TILE, chip_rows)
    own, tiles = chip_rows // size, seq // size
    at = lambda i, chip: ((i + chip[0] * own) % tiles, 0)
    weight = lambda col: pl.BlockSpec((width, width), lambda i, chip: (0, col), pipeline_mode=pl.Buffered(1))
    return pl.pallas_call(
        functools.partial(project_kernel, own),
        out_shape=[
            jax.ShapeDtypeStruct((seq, width), BF16),
            jax.ShapeDtypeStruct((chip_rows, width), BF16),
            jax.ShapeDtypeStruct((seq, width), BF16),
        ],
        grid_spec=pltpu.PrefetchScalarGridSpec(
            num_scalar_prefetch=1,
            grid=(tiles,),
            in_specs=[
                pl.BlockSpec((size, width), at),
                pl.BlockSpec((1, width), lambda i, chip: (0, 0)),
                weight(first // width),
                weight(first // width + 1),
            ],
            out_specs=[
                pl.BlockSpec((size, width), at),
                pl.BlockSpec((size, width), lambda i, chip: (jnp.minimum(i, own - 1), 0)),
                pl.BlockSpec((size, width), at),
            ],
        ),
        compiler_params=pltpu.CompilerParams(vmem_limit_bytes=48 * MIB),
        name="project",
    )(chip, x_all, gain, w_all, w_all)


def project_back_kernel(own, chip_ref, dq_ref, dk_ref, dv_ref, x_ref, wq_ref, wk_ref, wv_ref, p_ref, g_ref, acc_ref):
    i = pl.program_id(0)
    acc_ref[...] = dot(dk_ref[...], wk_ref[...], NT) + dot(dv_ref[...], wv_ref[...], NT)

    @pl.when(i < own)
    def _():
        acc_ref[...] += dot(dq_ref[...], wq_ref[...], NT)

    @pl.when(i == 0)
    def _():
        g_ref[...] = jnp.zeros_like(g_ref)

    part = acc_ref[...]
    p_ref[...] = part.astype(BF16)
    g_ref[...] += jnp.sum(part * normed(x_ref[...].astype(F32), 1.0), axis=0, keepdims=True)


def project_back(chip, dq, dk, dv, x_all, w_all, first):
    seq, width = x_all.shape
    chip_rows, kv = dq.shape[0], dk.shape[1]
    size = min(TOKEN_TILE, chip_rows)
    own, tiles = chip_rows // size, seq // size
    at = lambda i, chip: ((i + chip[0] * own) % tiles, 0)
    weight = lambda cols, col: pl.BlockSpec((width, cols), lambda i, chip: (0, col), pipeline_mode=pl.Buffered(1))
    return pl.pallas_call(
        functools.partial(project_back_kernel, own),
        out_shape=[jax.ShapeDtypeStruct((seq, width), BF16), jax.ShapeDtypeStruct((1, width), F32)],
        grid_spec=pltpu.PrefetchScalarGridSpec(
            num_scalar_prefetch=1,
            grid=(tiles,),
            in_specs=[
                pl.BlockSpec((size, width), lambda i, chip: (jnp.minimum(i, own - 1), 0)),
                pl.BlockSpec((size, kv), at),
                pl.BlockSpec((size, kv), at),
                pl.BlockSpec((size, width), at),
                weight(width, first // width),
                weight(kv, (first + width) // kv),
                weight(kv, (first + width) // kv + 1),
            ],
            out_specs=[
                pl.BlockSpec((size, width), at),
                pl.BlockSpec((1, width), lambda i, chip: (0, 0)),
            ],
            scratch_shapes=[pltpu.VMEM((size, width), F32)],
        ),
        compiler_params=pltpu.CompilerParams(vmem_limit_bytes=48 * MIB),
        name="project_back",
    )(chip, dq, dk, dv, x_all, w_all, w_all, w_all)


def feed_kernel(chip_ref, x_ref, p0_ref, p1_ref, gain_ref, w_ref, mid_ref, sec_ref, act_ref, gu_ref):
    count = x_ref.shape[0]
    size = min(ROW_TILE, count)
    tile = lambda i: pl.ds(pl.multiple_of(i * size, size), size)

    @pl.when(pl.program_id(0) == 0)
    def _():
        def start(i, _):
            rows = tile(i)
            middle = x_ref[rows, :].astype(F32) + (p0_ref[rows, :].astype(F32) + p1_ref[rows, :].astype(F32))
            mid_ref[rows, :] = middle
            sec_ref[rows, :] = normed(middle, gain_ref[...]).astype(BF16)
            return 0

        lax.fori_loop(0, count // size, start, 0)

    def body(i, _):
        rows = tile(i)
        both = dot(sec_ref[rows, :], w_ref[...], NN)
        gate, up = both[:, :FF_TILE], both[:, FF_TILE:]
        act_ref[rows, :] = (gate * jax.nn.sigmoid(gate) * up).astype(BF16)
        gu_ref[rows, :] = both.astype(BF16)
        return 0

    lax.fori_loop(0, count // size, body, 0)


def feed(chip, x_all, p0, p1, gain, w_all, ff):
    rows, width = p0.shape
    once = pl.Buffered(1)
    whole = lambda: pl.BlockSpec((rows, width), lambda j, chip: (0, 0), pipeline_mode=once)
    return pl.pallas_call(
        feed_kernel,
        out_shape=[
            jax.ShapeDtypeStruct((rows, width), F32),
            jax.ShapeDtypeStruct((rows, width), BF16),
            jax.ShapeDtypeStruct((rows, ff), BF16),
            jax.ShapeDtypeStruct((rows, 2 * ff), BF16),
        ],
        grid_spec=pltpu.PrefetchScalarGridSpec(
            num_scalar_prefetch=1,
            grid=(ff // FF_TILE,),
            in_specs=[
                pl.BlockSpec((rows, width), lambda j, chip: (chip[0], 0), pipeline_mode=once),
                whole(), whole(),
                pl.BlockSpec((1, width), lambda j, chip: (0, 0)),
                pl.BlockSpec((width, 2 * FF_TILE), lambda j, chip: (0, j)),
            ],
            out_specs=[
                pl.BlockSpec((rows, width), lambda j, chip: (0, 0)),
                pl.BlockSpec((rows, width), lambda j, chip: (0, 0)),
                pl.BlockSpec((rows, FF_TILE), lambda j, chip: (0, j)),
                pl.BlockSpec((rows, 2 * FF_TILE), lambda j, chip: (0, j)),
            ],
        ),
        compiler_params=pltpu.CompilerParams(vmem_limit_bytes=38 * MIB),
        name="feed",
    )(chip, x_all, p0, p1, gain, w_all)


def feed_back_kernel(core_ref, gu_ref, go_ref, wd_ref, gg_ref, d_ref):
    count = gu_ref.shape[0]
    size = min(ROW_TILE, count)
    unit = wd_ref.shape[2]
    for u in range(FF_TILE // unit):
        d_ref[u * unit : (u + 1) * unit, :] = wd_ref[u, 0]

    def body(i, _):
        rows = pl.ds(pl.multiple_of(i * size, size), size)
        grad = dot(go_ref[rows, :], d_ref[...], NT)
        gate, up = gu_ref[rows, :FF_TILE].astype(F32), gu_ref[rows, FF_TILE:].astype(F32)
        sig = jax.nn.sigmoid(gate)
        gg_ref[rows, :FF_TILE] = (grad * up * sig * (1.0 + gate * (1.0 - sig))).astype(BF16)
        gg_ref[rows, FF_TILE:] = (grad * (gate * sig)).astype(BF16)
        return 0

    lax.fori_loop(0, count // size, body, 0)


def feed_back(core, gate_up, go, w_down):
    rows, width = go.shape
    chips, _, unit, _ = w_down.shape
    ff = chips * unit
    return pl.pallas_call(
        feed_back_kernel,
        out_shape=[jax.ShapeDtypeStruct((rows, 2 * ff), BF16), jax.ShapeDtypeStruct((ff, width), BF16)],
        grid_spec=pltpu.PrefetchScalarGridSpec(
            num_scalar_prefetch=1,
            grid=(ff // FF_TILE,),
            in_specs=[
                pl.BlockSpec((rows, 2 * FF_TILE), lambda j, core: (0, j)),
                pl.BlockSpec((rows, width), lambda j, core: (0, 0), pipeline_mode=pl.Buffered(1)),
                pl.BlockSpec((FF_TILE // unit, 1, unit, width), lambda j, core: (j, core[0], 0, 0)),
            ],
            out_specs=[
                pl.BlockSpec((rows, 2 * FF_TILE), lambda j, core: (0, j)),
                pl.BlockSpec((FF_TILE, width), lambda j, core: (j, 0)),
            ],
        ),
        compiler_params=pltpu.CompilerParams(vmem_limit_bytes=48 * MIB),
        name="feed_back",
    )(core, gate_up, go, w_down)


def middle_back_kernel(mid_ref, s0_ref, s1_ref, go_ref, gain_ref, wo_ref, ga_ref, gm_ref, g_ref):
    back, terms = norm_back(mid_ref[...], gain_ref[...], s0_ref[...].astype(F32) + s1_ref[...].astype(F32))
    grad = (go_ref[...].astype(F32) + back).astype(BF16)
    ga_ref[...] = grad
    gm_ref[...] = dot(grad, wo_ref[...], NT).astype(BF16)

    @pl.when(pl.program_id(0) == 0)
    def _():
        g_ref[...] = jnp.zeros_like(g_ref)

    g_ref[...] += jnp.sum(terms, axis=0, keepdims=True)


def middle_back(middle, s0, s1, go, gain, w_out):
    rows, width = middle.shape
    size = min(ROW_TILE, rows)
    row = pl.BlockSpec((size, width), lambda i: (i, 0))
    line = pl.BlockSpec((1, width), lambda i: (0, 0))
    return pl.pallas_call(
        middle_back_kernel,
        out_shape=[
            jax.ShapeDtypeStruct((rows, width), BF16),
            jax.ShapeDtypeStruct((rows, w_out.shape[0]), BF16),
            jax.ShapeDtypeStruct((1, width), F32),
        ],
        grid=(rows // size,),
        in_specs=[row, row, row, row, line, pl.BlockSpec(w_out.shape, lambda i: (0, 0), pipeline_mode=pl.Buffered(1))],
        out_specs=[row, pl.BlockSpec((size, w_out.shape[0]), lambda i: (i, 0)), line],
        compiler_params=pltpu.CompilerParams(vmem_limit_bytes=22 * MIB),
        name="middle_back",
    )(middle, s0, s1, go, gain, w_out)


LINK_TIME = pl.CostEstimate(flops=0, bytes_accessed=300_000_000, transcendentals=0)


def peers():
    dp, ctx = lax.axis_index("dp"), lax.axis_index("ctx")
    to = lambda d, k: (jnp.bitwise_xor(dp, d), jnp.bitwise_xor(ctx, k))
    return dp, ctx, to


def greet(devices):
    barrier = pltpu.get_barrier_semaphore()
    for device in devices:
        pl.semaphore_signal(barrier, inc=1, device_id=device, device_id_type=MESH)
    pl.semaphore_wait(barrier, len(devices))


def sender(send_sem, recv_sem):
    made = []

    def send(src, dst, device):
        i = len(made)
        copy = pltpu.make_async_remote_copy(
            src_ref=src, dst_ref=dst, send_sem=send_sem.at[i], recv_sem=recv_sem.at[i],
            device_id=device, device_id_type=MESH,
        )
        copy.start()
        made.append(copy)
        return copy

    return send, made


def gather_kernel(pk_ref, wo_ref, tok_ref, go_ref, w_ref, x_ref, g_ref, send_sem, recv_sem, local_sem):
    dp, ctx, to = peers()
    c, z = ctx % 2, ctx // 2
    which, me = ctx // 4, ctx % 4
    inner = jnp.logical_or(z == 1, z == 2)
    greet([to(0, 1), to(0, 2), to(0, 4), to(0, 6), to(1, 0), to(2, 0)])
    send, made = sender(send_sem, recv_sem)
    sib, nbr, far, across, xn, yn = to(0, 1), to(0, 2), to(0, 4), to(0, 6), to(1, 0), to(2, 0)
    rows, cols = pk_ref.shape[1:]

    place = w_ref.at[dp, z, pl.ds(c * rows, rows), pl.ds(0, cols)]
    local = [
        pltpu.make_async_copy(pk_ref.at[c], place, local_sem.at[0]),
        pltpu.make_async_copy(wo_ref, w_ref.at[dp, z, :, pl.ds(cols, wo_ref.shape[1])], local_sem.at[1]),
        pltpu.make_async_copy(tok_ref.at[which], x_ref.at[me, 0], local_sem.at[2]),
        pltpu.make_async_copy(go_ref.at[which], g_ref.at[c, 0], local_sem.at[3]),
    ]
    for copy in local:
        copy.start()
    cross = send(pk_ref.at[1 - c], place, sib)
    for copy in local:
        copy.wait()
    cross.wait_recv()
    done = []

    def half(h, q, zz):
        return w_ref.at[q, zz, pl.ds(h * rows, rows)]

    first = []

    def spread(zz):
        low, high = half(0, dp, zz), half(1, dp, zz)
        first.append((send(low, low, yn), low, half(0, jnp.bitwise_xor(dp, 2), zz), xn))
        first.append((send(high, high, xn), high, half(1, jnp.bitwise_xor(dp, 1), zz), yn))

    def pass_on():
        for copy, own, part, device in first[:2]:
            done.append(send(own, own, device))
            copy.wait_recv()
            done.append(send(part, part, device))
        del first[:2]

    z_one = jnp.bitwise_xor(z, 1)
    z_near = jnp.bitwise_xor(z, jnp.where(inner, 3, 2))
    z_far = jnp.bitwise_xor(z, jnp.where(inner, 2, 3))
    relayed = []

    def relay(slot, source, device):
        copy = pltpu.make_async_remote_copy(
            src_ref=w_ref.at[dp, source], dst_ref=w_ref.at[dp, source],
            send_sem=send_sem.at[send_sem.shape[0] - 4 + len(relayed)],
            recv_sem=recv_sem.at[send_sem.shape[0] - 2 + slot],
            device_id=device, device_id_type=MESH,
        )
        relayed.append(copy)
        pl.when(inner)(copy.start)
        return copy

    step = send(w_ref.at[dp, z], w_ref.at[dp, z], nbr)
    near = relay(0, z, across)
    spread(z)
    pass_on()
    step.wait_recv()
    far_block = relay(1, z_one, across)
    spread(z_one)
    near.wait_recv()
    relay(0, z_near, nbr)
    spread(z_near)
    pass_on()
    far_block.wait_recv()
    relay(1, z_far, nbr)
    spread(z_far)
    swap = send(tok_ref.at[1 - which], x_ref.at[me, 1], far)
    mine_nbr = send(tok_ref.at[which], x_ref.at[me, 0], nbr)
    done += [send(tok_ref.at[which], x_ref.at[me, 0], sib), send(go_ref.at[which], g_ref.at[c, 0], sib)]
    pass_on()
    swap.wait_recv()
    done.append(send(x_ref.at[me, 1], x_ref.at[me, 1], sib))
    swap_nbr = send(x_ref.at[me, 1], x_ref.at[me, 1], nbr)
    go_swap = send(go_ref.at[1 - which], g_ref.at[c, 1], far)
    pass_on()
    other = jnp.bitwise_xor(me, 2)
    mine_nbr.wait_recv()
    done.append(send(x_ref.at[other, 0], x_ref.at[other, 0], sib))
    swap_nbr.wait_recv()
    done.append(send(x_ref.at[other, 1], x_ref.at[other, 1], sib))
    go_swap.wait_recv()
    done.append(send(g_ref.at[c, 1], g_ref.at[c, 1], sib))
    for copy in done:
        copy.wait_recv()
    for copy in made:
        copy.wait_send()

    @pl.when(inner)
    def _():
        for copy in relayed:
            copy.wait_send()


def gather(packed, w_out, tokens, grad_out):
    rows, cols = 2 * packed.shape[1], packed.shape[2] + w_out.shape[1]
    slots, width = tokens.shape[1:]
    copies = 36 + 4
    anywhere = pl.BlockSpec(memory_space=pl.ANY)
    near = pl.BlockSpec(memory_space=pltpu.VMEM)
    w, x, g = pl.pallas_call(
        gather_kernel,
        out_shape=[
            jax.ShapeDtypeStruct((4, 4, rows, cols), BF16),
            jax.ShapeDtypeStruct((4, 2, slots, width), BF16),
            jax.ShapeDtypeStruct((2, 2, slots, width), BF16),
        ],
        in_specs=[near] * 4,
        out_specs=[anywhere] * 3,
        scratch_shapes=[
            pltpu.SemaphoreType.DMA((copies,)),
            pltpu.SemaphoreType.DMA((copies,)),
            pltpu.SemaphoreType.DMA((4,)),
        ],
        compiler_params=pltpu.CompilerParams(
            collective_id=0, has_side_effects=True, vmem_limit_bytes=48 * MIB
        ),
        cost_estimate=LINK_TIME,
        name="gather",
    )(packed, w_out, tokens, grad_out)
    return w.reshape(16 * rows, cols), x.reshape(-1, width), g.reshape(-1, width)


def reduce_kernel(
    h_hbm, dq_hbm, dk_hbm, dv_hbm, e_hbm, ow_hbm, or_hbm, part_ref, xa_hbm, gm_hbm, gain_ref,
    a_ref, go_ref, ig_ref,
    g_ref, in_a, in_b, mid_a, mid_b, got_a, got_b, out3, in3, mine_ref, sib_ref, give_ref, nbr_ref, back_ref,
    x_ref, ga_ref, h_ref, dq_ref, dk_ref, dv_ref, o_ref, s_ref, send_sem, recv_sem, local_sem,
):
    dp, ctx, to = peers()
    c, z = ctx % 2, ctx // 2
    which, chip = ctx // 4, z % 2
    x, y = dp % 2, dp // 2
    hr = g_ref.shape[3] // 2
    count = mine_ref.shape[1]
    q_cols, kv_cols = dq_ref.shape[1], dk_ref.shape[1]
    near = s_ref.shape[1]
    first_col, width = near - HD, ow_hbm.shape[-1]
    local = []

    def fetch(src, dst):
        copy = pltpu.make_async_copy(src, dst, local_sem.at[len(local)])
        copy.start()
        local.append(copy)

    fetch(ow_hbm.at[:, :, c], g_ref.at[c, :, :, :, pl.ds(near, width)])
    fetch(or_hbm, g_ref.at[1 - c, :, :, :, pl.ds(near, width)])
    fetch(e_hbm, g_ref.at[:, :, :, :, pl.ds(first_col, HD)])
    fetch(part_ref.at[:, c], mine_ref)
    fetch(dq_hbm, dq_ref)
    fetch(h_hbm, h_ref)
    fetch(dk_hbm, dk_ref)
    fetch(dv_hbm, dv_ref)
    fetch(xa_hbm.at[ctx % 4], x_ref)
    fetch(gm_hbm.at[c], ga_ref)
    greet([to(0, 1), to(0, 2), to(0, 4), to(0, 6), to(1, 0), to(2, 0)])
    send, made = sender(send_sem, recv_sem)
    sib, nbr, far, across = to(0, 1), to(0, 2), to(0, 4), to(0, 6)
    xn, yn = to(1, 0), to(2, 0)
    cross = send(part_ref.at[:, 1 - c], sib_ref, sib)

    def ready(count):
        for copy in local[:count]:
            copy.wait()
        del local[:count]

    def weigh(rows, grad_ref, at):
        def body(i, _):
            some = h_ref[rows, pl.ds(pl.multiple_of(i * 4 * 2 * hr, 128), 4 * 2 * hr)]
            part = dot(some, grad_ref[...], TN).astype(BF16)
            g_ref[i // 2, i % 2, :, :, at : at + grad_ref.shape[1]] = part.reshape(4, 2 * hr, grad_ref.shape[1])
            return 0

        lax.fori_loop(0, 4, body, 0)

    low, high = pl.ds(0, hr), pl.ds(hr, hr)
    inner = jnp.logical_or(z == 1, z == 2)
    outer = jnp.logical_not(inner)
    order = [jnp.bitwise_xor(z, jnp.where(inner, 3, 2)), jnp.bitwise_xor(z, jnp.where(inner, 2, 3)), jnp.bitwise_xor(z, 1), z]
    passed = []

    def pass_z(kind, slot, source, part, device, role):
        copy = pltpu.make_async_remote_copy(
            src_ref=out3.at[source, :, parts[part]], dst_ref=in3.at[slot, :, parts[part]],
            send_sem=send_sem.at[40 + 2 * kind + part], recv_sem=recv_sem.at[40 + 2 * slot + part],
            device_id=device, device_id_type=MESH,
        )
        pl.when(role)(copy.start)
        passed.append((role, copy))

    def from_z(slot, part):
        return pltpu.make_async_remote_copy(
            src_ref=out3.at[0, :, parts[part]], dst_ref=in3.at[slot, :, parts[part]],
            send_sem=send_sem.at[40 + part], recv_sem=recv_sem.at[40 + 2 * slot + part],
            device_id=nbr, device_id_type=MESH,
        )

    def add_z(block, slot, part):
        p = parts[part]
        out3[block, :, p] = (out3[block, :, p].astype(F32) + in3[slot, :, p].astype(F32)).astype(BF16)

    def inward(i):
        k, part = i % 4, i // 4

        @pl.when(inner)
        def _():
            from_z(k, part).wait_recv()
            add_z(k, k, part)

        pass_z(3 + k, 3 + k, k, part, across, inner)

    def outward(part):
        @pl.when(inner)
        def _():
            from_z(4, part).wait_recv()
            add_z(2, 4, part)

        pass_z(5, 2, 2, part, nbr, inner)

    a_in, b_in, a_mid, b_mid = [], [], [], []
    size = 64
    tile = lambda i: pl.ds(pl.multiple_of(i * size, size), size)
    parts = (pl.ds(first_col, HD + width), pl.ds(0, first_col))

    def enter(i):
        k, p = i % 4, parts[i // 4]
        a_in.append(send(g_ref.at[:, 1 - x, order[k], low, p], in_a.at[k, :, :, p], xn))
        b_in.append(send(g_ref.at[1 - y, :, order[k], high, p], in_b.at[k, :, :, p], yn))

    def middle(i):
        k, p = i % 4, parts[i // 4]
        add = lambda p, q: (p.astype(F32) + q.astype(F32)).astype(BF16)
        a_in[i].wait_recv()
        mid_a[k, :, p] = add(g_ref[1 - y, x, order[k], 0:hr, p], in_a[k, 1 - y, :, p])
        a_mid.append(send(mid_a.at[k, :, p], got_a.at[k, :, p], yn))
        b_in[i].wait_recv()
        mid_b[k, :, p] = add(g_ref[y, 1 - x, order[k], hr:, p], in_b[k, 1 - x, :, p])
        b_mid.append(send(mid_b.at[k, :, p], got_b.at[k, :, p], xn))

    def leave(i):
        k, p = i % 4, parts[i // 4]
        add = lambda p, q, r: (p.astype(F32) + q.astype(F32) + r.astype(F32)).astype(BF16)
        a_mid[i].wait_recv()
        out3[k, 0:hr, p] = add(g_ref[y, x, order[k], 0:hr, p], in_a[k, y, :, p], got_a[k, :, p])
        b_mid[i].wait_recv()
        out3[k, hr:, p] = add(g_ref[y, x, order[k], hr:, p], in_b[k, x, :, p], got_b[k, :, p])
        if k < 3:
            pass_z(k, k, k, i // 4, nbr, outer)

    ready(3)
    enter(0)
    enter(1)
    enter(2)
    ready(1)
    cross.wait_recv()
    slots = ig_ref.shape[1]

    def give(i, _):
        rows = tile(i)
        give_ref[rows] = (mine_ref[1 - chip, rows].astype(F32) + sib_ref[1 - chip, rows].astype(F32)).astype(BF16)
        return 0

    def back(i, _):
        rows = tile(i)
        grad = mine_ref[chip, rows].astype(F32) + sib_ref[chip, rows].astype(F32) + nbr_ref[rows].astype(F32)
        through, _terms = norm_back(x_ref[rows, :].astype(F32), gain_ref[...], grad)
        back_ref[rows] = (ga_ref[rows, :].astype(F32) + through).astype(BF16)
        return 0

    swaps = []
    for first in (slots, 0):
        lax.fori_loop(first // size, (first + slots) // size, give, 0)
        rows = pl.ds(first, slots)
        swaps.append(send(give_ref.at[rows], nbr_ref.at[rows], nbr))
    ready(2)
    weigh(pl.ds(pl.multiple_of(chip * dq_ref.shape[0], dq_ref.shape[0]), dq_ref.shape[0]), dq_ref, 0)
    middle(0)
    enter(3)
    middle(1)
    middle(2)
    ready(2)
    weigh(slice(None), dk_ref, q_cols)
    weigh(slice(None), dv_ref, q_cols + kv_cols)
    enter(4)
    enter(5)
    leave(0)
    leave(1)
    middle(3)
    ready(2)
    swaps[0].wait_recv()
    lax.fori_loop(slots // size, 2 * slots // size, back, 0)
    home = send(back_ref.at[pl.ds(slots, slots)], ig_ref.at[which], far)
    leave(2)
    inward(0)
    inward(1)
    middle(4)
    enter(6)
    leave(3)
    middle(5)
    enter(7)
    leave(4)
    outward(0)
    swaps[1].wait_recv()
    lax.fori_loop(0, slots // size, back, 0)
    keep = pltpu.make_async_copy(back_ref.at[pl.ds(0, slots)], ig_ref.at[which], local_sem.at[0])
    keep.start()
    middle(6)
    leave(5)
    inward(4)
    middle(7)
    leave(6)
    inward(5)
    leave(7)
    outward(1)
    for part in range(2):
        from_z(2, part).wait_recv()

    @pl.when(inner)
    def _():
        for part in range(2):
            from_z(3, part).wait_recv()
            add_z(3, 3, part)

    total = out3[3].astype(F32) + in3[2].astype(F32)
    o_ref[...] = total[:, :near].astype(BF16)
    other = send(o_ref.at[pl.ds(pl.multiple_of((1 - c) * hr, hr), hr)], s_ref, sib)
    go_ref[...] = total[:, near:].astype(BF16)
    own = o_ref.at[pl.ds(pl.multiple_of(c * hr, hr), hr)]

    def place(source, core):
        at = 0
        for size in (q_cols, kv_cols, kv_cols):
            a_ref[:, pl.ds(pl.multiple_of(2 * at + core * size, HD), size)] = source[:, at : at + size]
            at += size

    place(own, c)
    other.wait_recv()
    place(s_ref, 1 - c)
    both = own[:, first_col:].astype(F32) + s_ref[:, first_col:].astype(F32)
    a_ref[:, 2 * first_col :] = both.astype(BF16)
    keep.wait()
    home.wait_recv()
    for copy in made:
        copy.wait_send()
    for role, copy in passed:
        pl.when(role)(copy.wait_send)


def reduce(hidden, dq, dk, dv, entries, out_own, out_sib, part, x_all, grad_middle, gain):
    seq, width = x_all.shape
    rows = width // 16
    near_cols = dq.shape[1] + dk.shape[1] + dv.shape[1] + HD
    cols = near_cols + width
    count = part.shape[0] // 4
    copies = 52
    anywhere = pl.BlockSpec(memory_space=pl.ANY)
    near = pl.BlockSpec(memory_space=pltpu.VMEM)
    return pl.pallas_call(
        reduce_kernel,
        out_shape=[
            jax.ShapeDtypeStruct((rows // 2, 2 * (near_cols - HD) + HD), BF16),
            jax.ShapeDtypeStruct((rows, width), BF16),
            jax.ShapeDtypeStruct((2, count // 2, width), BF16),
        ],
        in_specs=[anywhere] * 10 + [near],
        out_specs=[near] * 2 + [anywhere],
        scratch_shapes=[
            pltpu.VMEM((2, 2, 4, rows, cols), BF16),
            pltpu.VMEM((4, 2, rows // 2, cols), BF16),
            pltpu.VMEM((4, 2, rows // 2, cols), BF16),
        ]
        + [pltpu.VMEM((4, rows // 2, cols), BF16)] * 4
        + [
            pltpu.VMEM((4, rows, cols), BF16),
            pltpu.VMEM((5, rows, cols), BF16),
            pltpu.VMEM((2, count, width), BF16),
            pltpu.VMEM((2, count, width), BF16),
        ]
        + [pltpu.VMEM((count, width), BF16)] * 5
        + [pltpu.VMEM(v.shape, BF16) for v in (hidden, dq, dk, dv)]
        + [
            pltpu.VMEM((rows, near_cols), BF16),
            pltpu.VMEM((rows // 2, near_cols), BF16),
            pltpu.SemaphoreType.DMA((copies,)),
            pltpu.SemaphoreType.DMA((copies,)),
            pltpu.SemaphoreType.DMA((10,)),
        ],
        compiler_params=pltpu.CompilerParams(
            collective_id=1, has_side_effects=True, vmem_limit_bytes=48 * MIB
        ),
        cost_estimate=LINK_TIME,
        name="reduce",
    )(
        hidden, dq, dk, dv,
        entries.reshape(2, 2, 4, rows, HD),
        out_own.reshape(2, 4, 2, rows, width),
        out_sib.reshape(2, 4, rows, width),
        part.reshape(2, 2, count, width),
        x_all.reshape(4, count, width),
        grad_middle.reshape(2, count, width),
        gain,
    )


def by_core(c, own, other):
    return jnp.where(c == 0, jnp.stack([own, other]), jnp.stack([other, own]))


def layer(
    n_dp, n, tokens, positions, w_query, w_key, w_value, w_out, w_gate, w_up, w_down,
    attn_gain, mlp_gain, q_gain, k_gain, grad_out,
):
    axes = ("dp", "ctx")
    slots, width = tokens.shape[1:]
    seq = positions.shape[1]
    span = slots // 2
    half = n // 2
    chips = n_dp * half
    ctx = lax.axis_index("ctx")
    c = ctx % 2
    which = ctx // half
    r_in, r_out, r_down = w_query.shape[0], w_out.shape[0], w_down.shape[0]
    ff = w_gate.shape[1]
    ff_c = ff // 2
    q_c, kv_c = H * HD // 2, KV * HD // 2

    to_sibling = [(i, i ^ 1) for i in range(n)]
    to_partner = [(i, (i + half) % n) for i in range(n)]
    halves = [list(range(half)), list(range(half, n))]
    same_core = [list(range(0, n, 2)), list(range(1, n, 2))]
    sibling = lambda v: lax.ppermute(v, "ctx", to_sibling)
    partner = lambda v: lax.ppermute(v, "ctx", to_partner)

    def placed(values):
        mine = lax.dynamic_index_in_dim(values, which, 0, False)
        other = lax.dynamic_index_in_dim(values, 1 - which, 0, False)
        return jnp.concatenate([mine, partner(other)], axis=0)

    gains = jnp.concatenate(
        [
            attn_gain[:, None],
            mlp_gain[:, None],
            jnp.pad(q_gain, (0, r_in - q_gain.shape[0]))[:, None],
            jnp.pad(k_gain, (0, r_in - k_gain.shape[0]))[:, None],
            jnp.zeros((r_in, 124), BF16),
        ],
        axis=1,
    )
    tall = (n_dp, n) == (4, 8)
    qkv_halves = [
        jnp.concatenate(
            [
                w_query[:, i * q_c : (i + 1) * q_c],
                w_key[:, i * kv_c : (i + 1) * kv_c],
                w_value[:, i * kv_c : (i + 1) * kv_c],
            ],
            axis=1,
        )
        for i in range(2)
    ]

    def ff_order(shard):
        return shard.reshape(r_in, chips, 2, r_down).transpose(2, 0, 1, 3).reshape(2, r_in, ff_c)

    gate_order, up_order = ff_order(w_gate), ff_order(w_up)
    qkv_c = q_c + 2 * kv_c
    gu_c = 2 * ff_c
    all_c = gu_c + qkv_c
    by_tile = lambda v: v.reshape(2, r_in, ff_c // FF_TILE, FF_TILE)
    gu_shard = jnp.stack([by_tile(gate_order), by_tile(up_order)], axis=3).reshape(2, r_in, 2 * ff_c)
    packed = jnp.stack([jnp.concatenate([gu_shard[i], qkv_halves[i], gains], axis=1) for i in range(2)])
    if tall:
        w_all, x_all, go_chip = gather(packed, w_out, tokens, grad_out)
        out_rows = w_all[:, all_c + HD :].reshape(2, -1, r_out, width)
        out_keep = lax.dynamic_index_in_dim(out_rows, c, 0, False)
        out_give = lax.dynamic_index_in_dim(out_rows, 1 - c, 0, False)
        w_out_c = by_core(c, out_keep, sibling(out_give)).transpose(1, 0, 2, 3).reshape(q_c, width)
        w_down, w_all = lax.optimization_barrier((w_down, w_all))
    else:
        both = lax.all_gather(packed, axes, axis=1, tiled=True)
        w_all = lax.dynamic_index_in_dim(both, c, 0, False)
        out_all = lax.all_gather(w_out, axes, axis=0, tiled=True)
        w_out_c = lax.dynamic_slice_in_dim(out_all, c * q_c, q_c, 0)
        x_own = placed(tokens)
        x_all = lax.all_gather(x_own, "ctx", axis=0, tiled=True, axis_index_groups=halves)
        go_own = placed(grad_out)
        go_chip = by_core(c, go_own, sibling(go_own)).reshape(4 * slots, width)
    down_all = lax.all_gather(w_down, axes, axis=0, tiled=True).reshape(chips, 2, r_down, width)
    g_cols = w_all[:, all_c : all_c + HD].astype(F32)
    gain_attn = g_cols[:, 0][None]
    gain_mlp = g_cols[:, 1][None]
    per_head = g_cols.reshape(n_dp * n, r_in, HD)[:, : q_gain.shape[0]].reshape(HD, HD)
    gain_q = per_head[:, 2][None]
    gain_k = per_head[:, 3][None]

    chip = (ctx % half) // 2
    chip_rows = 4 * slots
    slot_ids = lax.dynamic_index_in_dim(positions, which, 0, False).reshape(2 * n, span)[:, 0] // span
    places = np.stack(
        [
            [s for d in side for k in (d, (d + half) % n) for s in (2 * k, 2 * k + 1)]
            for side in halves
        ]
    ).astype(np.int32)
    ids_all = slot_ids[lax.dynamic_index_in_dim(jnp.asarray(places), which, 0, False)]
    steps = jnp.arange(2 * n, dtype=jnp.int32)
    order = jnp.sum(jnp.where(ids_all[None, :] == steps[:, None], steps[None, :], 0), axis=1).astype(jnp.int32)
    ids = lax.dynamic_slice_in_dim(ids_all, chip * 8, 8, 0)
    cosine, sine = rope_tables(seq)

    chip_at = chip.astype(jnp.int32).reshape(1)
    hidden_all, q_raw, kv_raw = project(chip_at, x_all, gain_attn, w_all, gu_c, chip_rows)
    mixed, lse = attend(ids, order, q_raw, kv_raw, cosine, sine, gain_q, gain_k, span)
    proj = dot(mixed, w_out_c, NN, BF16)
    middle, second, activated, gate_up = feed(chip_at, x_all, proj, sibling(proj), gain_mlp, w_all, ff_c)
    grad_gu, w_down_c = feed_back(c.astype(jnp.int32).reshape(1), gate_up, go_chip, down_all)
    down = dot(activated, w_down_c, NN, BF16).reshape(2, 2 * slots, width)
    down_own = lax.dynamic_index_in_dim(down, c, 0, False)
    down_other = sibling(lax.dynamic_index_in_dim(down, 1 - c, 0, False))
    own_rows = lambda v: lax.dynamic_slice_in_dim(v, c * 2 * slots, 2 * slots, 0)
    result = (own_rows(middle) + (down_own.astype(F32) + down_other.astype(F32))).astype(BF16)

    def returned(rows):
        mine, back = rows[:slots], partner(rows[slots:])
        return jnp.where(which == 0, jnp.stack([mine, back]), jnp.stack([back, mine]))


    second_part = dot(grad_gu, w_all[:, :gu_c], NT, BF16)
    grad_gu_w = dot(second, grad_gu, TN, BF16)
    grad_down_w = dot(activated, go_chip, TN, BF16)
    grad_attn, grad_mixed, mlp_gain_sum = middle_back(
        middle, second_part, sibling(second_part), go_chip, gain_mlp, w_out_c
    )
    grad_mlp_gain = jnp.where(c == 0, mlp_gain_sum[0], 0.0)

    over_dp = lambda grad: lax.psum_scatter(grad, "dp", scatter_dimension=0, tiled=True)
    over_ctx = lambda part: lax.psum_scatter(
        part, "ctx", scatter_dimension=0, tiled=True, axis_index_groups=same_core
    )
    part_gu = over_dp(grad_gu_w)
    part_down = over_dp(grad_down_w)

    out_w = dot(mixed, grad_attn, TN, BF16).reshape(-1, 2, r_out, width)
    out_recv = sibling(lax.dynamic_index_in_dim(out_w, 1 - c, 1, False))
    out_recv, grad_mixed = lax.optimization_barrier((out_recv, grad_mixed))
    result, grad_mixed, part_down = lax.optimization_barrier((result, grad_mixed, part_down))
    if tall:
        pieces = part_down.reshape(half, r_down, width)
        place = ctx // 2
        down_own = lax.dynamic_index_in_dim(pieces, place, 0, False).astype(F32)
        down_got = [
            lax.ppermute(
                lax.dynamic_index_in_dim(pieces, jnp.bitwise_xor(place, k), 0, False),
                "ctx",
                [(i, i ^ (2 * k)) for i in range(n)],
            )
            for k in range(1, half)
        ]
    else:
        down_own, down_got = over_ctx(part_down).astype(F32), []
    output = returned(result)
    dq, dk, dv, dgq, dgk = attend_back(
        ids, order, q_raw, kv_raw, grad_mixed, mixed, lse, cosine, sine, gain_q, gain_k, span
    )
    output, dq, dk, dv, part_gu, down_got = lax.optimization_barrier((output, dq, dk, dv, part_gu, down_got))
    sum_gu = over_ctx(part_gu)
    sum_down = down_own
    for piece in down_got:
        sum_down = sum_down + piece.astype(F32)
    part_all, attn_gain_sum = project_back(chip_at, dq, dk, dv, x_all, w_all, gu_c)
    lot = lambda v: v.reshape(n_dp * n, -1)
    entries = jnp.concatenate([lot(attn_gain_sum), lot(grad_mlp_gain), lot(dgq), lot(dgk)], axis=1)
    entries = jnp.pad(entries[:, None], ((0, 0), (0, r_in - 1), (0, HD - entries.shape[1])))
    entries = entries.reshape(width, HD).astype(BF16)
    entries, sum_down = lax.optimization_barrier((entries, sum_down))
    near_c = qkv_c + HD
    beside = lambda v: v.transpose(1, 0, 2).reshape(r_in, -1)
    by_rows = lambda v: lax.dynamic_index_in_dim(v.reshape(2, r_in, -1), c, 0, False)

    def columns(sums):
        other = lax.dynamic_index_in_dim(sums.reshape(2, r_in, -1), 1 - c, 0, False)
        return by_core(c, by_rows(sums), sibling(other))

    if tall:
        sums, sum_out, input_grad = reduce(
            hidden_all, dq, dk, dv, entries, out_w, out_recv, part_all, x_all, grad_attn, gain_attn
        )
        grad_q, grad_k, grad_v = (
            sums[:, i:j].astype(F32) for i, j in ((0, 2 * q_c), (2 * q_c, 2 * q_c + 2 * kv_c), (2 * q_c + 2 * kv_c, 2 * qkv_c))
        )
        sum_out, gain_own = sum_out.astype(F32), sums[:, 2 * qkv_c :].astype(F32)
    else:
        hidden = lax.dynamic_slice_in_dim(hidden_all, chip * chip_rows, chip_rows, 0)
        grads = [dot(hidden, dq, TN, BF16), dot(hidden_all, dk, TN, BF16), dot(hidden_all, dv, TN, BF16), entries]
        qkv_own = columns(over_ctx(over_dp(jnp.concatenate(grads, axis=1)))).astype(F32)
        out_mine = lax.dynamic_index_in_dim(out_w, c, 1, False)
        sum_out = over_ctx(over_dp(by_core(c, out_mine, out_recv).reshape(chips * r_out, width))).astype(F32)
        grad_q = beside(qkv_own[:, :, :q_c])
        grad_k = beside(qkv_own[:, :, q_c : q_c + kv_c])
        grad_v = beside(qkv_own[:, :, q_c + kv_c : qkv_c])
        gain_own = jnp.sum(qkv_own[:, :, qkv_c:], axis=0)
        grad_hidden = lax.psum_scatter(
            part_all, "ctx", scatter_dimension=0, tiled=True, axis_index_groups=halves
        ).astype(F32)
        back, _terms = norm_back(x_own.astype(F32), gain_attn, grad_hidden)
        input_grad = returned((own_rows(grad_attn).astype(F32) + back).astype(BF16))
    sum_gu, gain_own = lax.optimization_barrier((sum_gu, gain_own))
    gain_row, r_head = gain_own[0], q_gain.shape[0]
    gu_own = columns(sum_gu).reshape(2, r_in, ff_c // FF_TILE, 2, FF_TILE)
    ff_back = lambda v: v.reshape(2, r_in, chips, r_down).transpose(1, 2, 0, 3).reshape(r_in, ff)
    return (
        output,
        input_grad,
        grad_q,
        grad_k,
        grad_v,
        sum_out,
        ff_back(gu_own[:, :, :, 0]).astype(F32),
        ff_back(gu_own[:, :, :, 1]).astype(F32),
        sum_down,
        gain_row[:r_in],
        gain_row[r_in : 2 * r_in],
        gain_row[2 * r_in : 2 * r_in + r_head],
        gain_row[2 * r_in + r_head : 2 * r_in + 2 * r_head],
    )


def solution(mesh):
    rows = P(("dp", "ctx"), None)
    gain = P(("dp", "ctx"))
    acts = P("dp", "ctx", None)
    return jax.shard_map(
        functools.partial(layer, mesh.shape["dp"], mesh.shape["ctx"]),
        mesh=mesh,
        in_specs=(acts, P("dp", None)) + (rows,) * 7 + (gain,) * 4 + (acts,),
        out_specs=(acts, acts) + (rows,) * 7 + (gain,) * 4,
        check_vma=False,
    )
```

```python
import functools

import jax
import jax.numpy as jnp
import numpy as np
from jax import lax
from jax.experimental import pallas as pl
from jax.experimental.pallas import tpu as pltpu
from jax.sharding import PartitionSpec as P

H = 16
KV = 8
HD = 128
GROUPS = H // KV
EPSILON = 1e-06
THETA = 1000000.0
LOG2E = 1.4426950408889634
KEY_TILE = 512
ROW_TILE = 256
TOKEN_TILE = 512
FF_TILE = 384
MIB = 1024 * 1024
MESH = pl.DeviceIdType.MESH
F32 = jnp.float32
BF16 = jnp.bfloat16


def normed(values, weights):
    return values * lax.rsqrt(jnp.mean(values * values, axis=-1, keepdims=True) + EPSILON) * weights


def norm_back(values, weights, grad):
    r = lax.rsqrt(jnp.mean(values * values, axis=-1, keepdims=True) + EPSILON)
    unit = values * r
    u = grad * weights
    return r * (u - unit * jnp.mean(u * unit, axis=-1, keepdims=True)), grad * unit


def rope_tables(seq):
    half = HD // 2
    inverse = (THETA ** (-(np.arange(half, dtype=np.float32) * np.float32(2.0) / np.float32(HD)))).astype(np.float32)
    angles = np.arange(seq, dtype=np.float32)[:, None] * inverse[None, :]
    cosine, sine = np.cos(angles), np.sin(angles)
    return (
        jnp.asarray(np.concatenate([cosine, cosine], axis=-1).astype(np.float32)),
        jnp.asarray(np.concatenate([-sine, sine], axis=-1).astype(np.float32)),
    )


def dot(a, b, dims, out=F32):
    return lax.dot_general(a, b, (dims, ((), ())), preferred_element_type=out)


NN = ((1,), (0,))
NT = ((1,), (1,))
TN = ((0,), (0,))


def row_mean(values):
    return dot(values.astype(BF16), jnp.full((HD, HD), 1.0 / HD, BF16), NN)


def row_sums(values):
    high = values.astype(BF16)
    ones = jnp.ones((8, HD), BF16)
    return (dot(ones, high, NT) + dot(ones, (values - high.astype(F32)).astype(BF16), NT))[0:1]


def unit_rows(raw):
    r = lax.rsqrt(row_mean(raw * raw) + EPSILON)
    return raw * r, r


def rope(values, cosine, sine):
    return values * cosine + pltpu.roll(values, HD // 2, 1) * sine


def rope_back(values, cosine, sine):
    return values * cosine - pltpu.roll(values, HD // 2, 1) * sine


def lanes(head, width=HD):
    return slice(head * width, (head + 1) * width)


def prepare_keys(span, order_ref, k_ref, v_ref, cos_ref, sin_ref, gk_ref, ks_ref, vs_ref):
    def body(i, _):
        rows = pl.ds(pl.multiple_of(i * span, span), span)
        source = pl.ds(pl.multiple_of(order_ref[i] * span, span), span)
        for p in range(k_ref.shape[1] // HD):
            unit, _r = unit_rows(k_ref[source, lanes(p)].astype(F32))
            ks_ref[rows, lanes(p)] = rope(unit * gk_ref[...], cos_ref[rows, :], sin_ref[rows, :]).astype(BF16)
        vs_ref[rows, :] = v_ref[source, :]
        return 0

    lax.fori_loop(0, k_ref.shape[0] // span, body, 0)


def query_block(q_ref, p, rows, places, cos_ref, sin_ref, gq_ref):
    units, scales, parts = [], [], []
    for g in range(GROUPS):
        unit, r = unit_rows(q_ref[rows, lanes(p * GROUPS + g)].astype(F32))
        turned = rope(unit * gq_ref[...], cos_ref[places, :], sin_ref[places, :])
        units.append(unit)
        scales.append(r)
        parts.append((turned * (LOG2E * HD**-0.5)).astype(BF16))
    return units, scales, jnp.concatenate(parts, axis=0)


def seen(shape, t, b, span, key_axis):
    at = t * KEY_TILE + lax.broadcasted_iota(jnp.int32, shape, key_axis)
    own = b * span + lax.broadcasted_iota(jnp.int32, shape, 1 - key_axis) % span
    return at <= own


def attend_kernel(
    span, ids_ref, order_ref, q_ref, k_ref, v_ref, cos_ref, sin_ref, gq_ref, gk_ref,
    o_ref, lse_ref, ks_ref, vs_ref, acc_ref, sum_ref,
):
    @pl.when(pl.program_id(0) == 0)
    def _():
        prepare_keys(span, order_ref, k_ref, v_ref, cos_ref, sin_ref, gk_ref, ks_ref, vs_ref)

    m = GROUPS * span
    heads = range(k_ref.shape[1] // HD)
    b = ids_ref[pl.program_id(0)]
    rows = slice(None)
    places = pl.ds(pl.multiple_of(b * span, span), span)
    q2 = [query_block(q_ref, p, rows, places, cos_ref, sin_ref, gq_ref)[2] for p in heads]
    acc_ref[...] = jnp.zeros_like(acc_ref)
    sum_ref[...] = jnp.zeros_like(sum_ref)

    def tile(t, masked):
        keys = pl.ds(pl.multiple_of(t * KEY_TILE, KEY_TILE), KEY_TILE)
        scores = [dot(q2[p], ks_ref[keys, lanes(p)], NT) for p in heads]
        keep = seen(scores[0].shape, t, b, span, 1) if masked else None
        for p in heads:
            e = jnp.exp2(scores[p])
            if masked:
                e = jnp.where(keep, e, 0.0)
            part = e[:, 0:HD]
            for i in range(1, KEY_TILE // HD):
                part = part + e[:, lanes(i)]
            sum_ref[p] += part
            acc_ref[p] += dot(e.astype(BF16), vs_ref[keys, lanes(p)], NN)

    last = (b * span) // KEY_TILE
    lax.fori_loop(0, last, lambda t, _: (tile(t, False), 0)[1], 0)
    tile(last, True)
    for p in heads:
        total = jnp.sum(sum_ref[p], axis=-1, keepdims=True)
        mixed = acc_ref[p] * (1.0 / total)
        for g in range(GROUPS):
            o_ref[rows, lanes(p * GROUPS + g)] = mixed[g * span : (g + 1) * span].astype(BF16)
        wide = jnp.broadcast_to(jnp.log2(total), (m, HD))
        lse_ref[p, 0] = jnp.transpose(wide)[0:1, :]


def attend(ids, order, q_raw, kv_raw, cosine, sine, gq, gk, span):
    rows = q_raw.shape[0]
    seq = kv_raw.shape[0]
    heads = q_raw.shape[1] // (GROUPS * HD)
    blocks, m = rows // span, GROUPS * span
    hp = heads
    whole = lambda k, ids, order: (0, 0)
    per_query = pl.BlockSpec((span, hp * GROUPS * HD), lambda j, ids, order: (j, 0))
    once = pl.Buffered(1)
    return pl.pallas_call(
        functools.partial(attend_kernel, span),
        out_shape=[
            jax.ShapeDtypeStruct((rows, heads * GROUPS * HD), BF16),
            jax.ShapeDtypeStruct((heads, blocks, 1, m), F32),
        ],
        grid_spec=pltpu.PrefetchScalarGridSpec(
            num_scalar_prefetch=2,
            grid=(blocks,),
            in_specs=[
                per_query,
                pl.BlockSpec((seq, hp * HD), whole, pipeline_mode=once),
                pl.BlockSpec((seq, hp * HD), lambda j, ids, order: (0, 1), pipeline_mode=once),
                pl.BlockSpec((seq, HD), whole, pipeline_mode=once),
                pl.BlockSpec((seq, HD), whole, pipeline_mode=once),
                pl.BlockSpec((1, HD), whole),
                pl.BlockSpec((1, HD), whole),
            ],
            out_specs=[
                per_query,
                pl.BlockSpec((hp, 1, 1, m), lambda j, ids, order: (0, j, 0, 0)),
            ],
            scratch_shapes=[
                pltpu.VMEM((seq, hp * HD), BF16),
                pltpu.VMEM((seq, hp * HD), BF16),
                pltpu.VMEM((hp, m, HD), F32),
                pltpu.VMEM((hp, m, HD), F32),
            ],
        ),
        compiler_params=pltpu.CompilerParams(vmem_limit_bytes=48 * MIB),
        cost_estimate=pl.CostEstimate(
            flops=2 * 2 * rows * seq * heads * GROUPS * HD,
            bytes_accessed=2 * (2 * rows * heads * GROUPS * HD + 2 * seq * heads * HD),
            transcendentals=rows * seq * heads * GROUPS // 2,
        ),
        name="attend",
    )(ids, order, q_raw, kv_raw, kv_raw, cosine, sine, gq, gk)


def attend_back_kernel(
    span, ids_ref, order_ref, q_ref, k_ref, v_ref, do_ref, o_ref, lse_ref, cos_ref, sin_ref, gq_ref, gk_ref,
    dq_ref, dk_ref, dv_ref, dgq_ref, dgk_ref, ks_ref, vs_ref, dka_ref, dva_ref, dqa_ref,
):
    heads = range(k_ref.shape[1] // HD)

    @pl.when(pl.program_id(0) == 0)
    def _():
        prepare_keys(span, order_ref, k_ref, v_ref, cos_ref, sin_ref, gk_ref, ks_ref, vs_ref)
        dka_ref[...] = jnp.zeros_like(dka_ref)
        dva_ref[...] = jnp.zeros_like(dva_ref)
        dgq_ref[...] = jnp.zeros_like(dgq_ref)
        dgk_ref[...] = jnp.zeros_like(dgk_ref)

    b = ids_ref[pl.program_id(0)]
    rows = slice(None)
    places = pl.ds(pl.multiple_of(b * span, span), span)
    q2, do2, delta, lse = [], [], [], []
    for p in heads:
        q2.append(query_block(q_ref, p, rows, places, cos_ref, sin_ref, gq_ref)[2])
        pick = lambda ref: jnp.concatenate([ref[rows, lanes(p * GROUPS + g)] for g in range(GROUPS)], axis=0)
        do2.append(pick(do_ref))
        delta.append(
            row_sums(do2[p].astype(F32) * pick(o_ref).astype(F32))
        )
        lse.append(lse_ref[p, 0])
    dqa_ref[...] = jnp.zeros_like(dqa_ref)

    def tile(t, masked):
        keys = pl.ds(pl.multiple_of(t * KEY_TILE, KEY_TILE), KEY_TILE)
        kt = [ks_ref[keys, lanes(p)] for p in heads]
        scores = [dot(kt[p], q2[p], NT) for p in heads]
        slopes = [dot(vs_ref[keys, lanes(p)], do2[p], NT) for p in heads]
        keep = seen(scores[0].shape, t, b, span, 0) if masked else None
        for p in heads:
            e = jnp.exp2(scores[p] - lse[p])
            if masked:
                e = jnp.where(keep, e, 0.0)
            ds = (e * (slopes[p] - delta[p])).astype(BF16)
            dva_ref[keys, lanes(p)] += dot(e.astype(BF16), do2[p], NN)
            dka_ref[keys, lanes(p)] += dot(ds, q2[p], NN)
            dqa_ref[p] += dot(ds, kt[p], TN)

    last = (b * span) // KEY_TILE
    lax.fori_loop(0, last, lambda t, _: (tile(t, False), 0)[1], 0)
    tile(last, True)
    for p in heads:
        units, scales, _q = query_block(q_ref, p, rows, places, cos_ref, sin_ref, gq_ref)
        dq = dqa_ref[p] * HD**-0.5
        for g in range(GROUPS):
            grad = rope_back(dq[g * span : (g + 1) * span], cos_ref[places, :], sin_ref[places, :])
            dgq_ref[...] += jnp.sum(grad * units[g], axis=0, keepdims=True)
            u = grad * gq_ref[...]
            back = scales[g] * (u - units[g] * row_mean(u * units[g]))
            dq_ref[rows, lanes(p * GROUPS + g)] = back.astype(BF16)

    def finish(i, _):
        rows = pl.ds(pl.multiple_of(i * span, span), span)
        source = pl.ds(pl.multiple_of(order_ref[i] * span, span), span)
        for p in heads:
            unit, r = unit_rows(k_ref[source, lanes(p)].astype(F32))
            grad = rope_back(dka_ref[rows, lanes(p)] * (1.0 / LOG2E), cos_ref[rows, :], sin_ref[rows, :])
            dgk_ref[...] += jnp.sum(grad * unit, axis=0, keepdims=True)
            u = grad * gk_ref[...]
            back = r * (u - unit * row_mean(u * unit))
            dk_ref[source, lanes(p)] = back.astype(BF16)
        dv_ref[source, :] = dva_ref[rows, :].astype(BF16)
        return 0

    @pl.when(pl.program_id(0) == pl.num_programs(0) - 1)
    def _():
        lax.fori_loop(0, k_ref.shape[0] // span, finish, 0)


def attend_back(ids, order, q_raw, kv_raw, grad_mixed, mixed, lse, cosine, sine, gq, gk, span):
    rows = q_raw.shape[0]
    seq = kv_raw.shape[0]
    heads = q_raw.shape[1] // (GROUPS * HD)
    blocks, m = rows // span, GROUPS * span
    hp = heads
    whole = lambda k, ids, order: (0, 0)
    once = pl.Buffered(1)
    per_query = pl.BlockSpec((span, hp * GROUPS * HD), lambda j, ids, order: (j, 0))
    per_key = pl.BlockSpec((seq, hp * HD), whole, pipeline_mode=once)
    gain = pl.BlockSpec((1, HD), whole)
    return pl.pallas_call(
        functools.partial(attend_back_kernel, span),
        out_shape=[
            jax.ShapeDtypeStruct((rows, heads * GROUPS * HD), BF16),
            jax.ShapeDtypeStruct((seq, heads * HD), BF16),
            jax.ShapeDtypeStruct((seq, heads * HD), BF16),
            jax.ShapeDtypeStruct((1, HD), F32),
            jax.ShapeDtypeStruct((1, HD), F32),
        ],
        grid_spec=pltpu.PrefetchScalarGridSpec(
            num_scalar_prefetch=2,
            grid=(blocks,),
            in_specs=[
                per_query,
                per_key,
                pl.BlockSpec((seq, hp * HD), lambda j, ids, order: (0, 1), pipeline_mode=once),
                per_query,
                per_query,
                pl.BlockSpec((hp, 1, 1, m), lambda j, ids, order: (0, j, 0, 0)),
                pl.BlockSpec((seq, HD), whole, pipeline_mode=once),
                pl.BlockSpec((seq, HD), whole, pipeline_mode=once),
                gain,
                gain,
            ],
            out_specs=[per_query] + [pl.BlockSpec((seq, hp * HD), whole)] * 2 + [gain, gain],
            scratch_shapes=[
                pltpu.VMEM((seq, hp * HD), BF16),
                pltpu.VMEM((seq, hp * HD), BF16),
                pltpu.VMEM((seq, hp * HD), F32),
                pltpu.VMEM((seq, hp * HD), F32),
                pltpu.VMEM((hp, m, HD), F32),
            ],
        ),
        compiler_params=pltpu.CompilerParams(vmem_limit_bytes=46 * MIB),
        cost_estimate=pl.CostEstimate(
            flops=5 * 2 * rows * seq * heads * GROUPS * HD // 2,
            bytes_accessed=2 * (4 * rows * heads * GROUPS * HD + 4 * seq * heads * HD),
            transcendentals=rows * seq * heads * GROUPS // 2,
        ),
        name="attend_back",
    )(ids, order, q_raw, kv_raw, kv_raw, grad_mixed, mixed, lse, cosine, sine, gq, gk)


def project_kernel(own, chip_ref, x_ref, gain_ref, wq_ref, wkv_ref, h_ref, q_ref, kv_ref):
    hidden = normed(x_ref[...].astype(F32), gain_ref[...]).astype(BF16)
    h_ref[...] = hidden
    kv_ref[...] = dot(hidden, wkv_ref[...], NN).astype(BF16)

    @pl.when(pl.program_id(0) < own)
    def _():
        q_ref[...] = dot(hidden, wq_ref[...], NN).astype(BF16)


def project(chip, x_all, gain, w_all, first, chip_rows):
    seq, width = x_all.shape
    size = min(TOKEN_TILE, chip_rows)
    own, tiles = chip_rows // size, seq // size
    at = lambda i, chip: ((i + chip[0] * own) % tiles, 0)
    weight = lambda col: pl.BlockSpec((width, width), lambda i, chip: (0, col), pipeline_mode=pl.Buffered(1))
    return pl.pallas_call(
        functools.partial(project_kernel, own),
        out_shape=[
            jax.ShapeDtypeStruct((seq, width), BF16),
            jax.ShapeDtypeStruct((chip_rows, width), BF16),
            jax.ShapeDtypeStruct((seq, width), BF16),
        ],
        grid_spec=pltpu.PrefetchScalarGridSpec(
            num_scalar_prefetch=1,
            grid=(tiles,),
            in_specs=[
                pl.BlockSpec((size, width), at),
                pl.BlockSpec((1, width), lambda i, chip: (0, 0)),
                weight(first // width),
                weight(first // width + 1),
            ],
            out_specs=[
                pl.BlockSpec((size, width), at),
                pl.BlockSpec((size, width), lambda i, chip: (jnp.minimum(i, own - 1), 0)),
                pl.BlockSpec((size, width), at),
            ],
        ),
        compiler_params=pltpu.CompilerParams(vmem_limit_bytes=48 * MIB),
        name="project",
    )(chip, x_all, gain, w_all, w_all)


def project_back_kernel(own, chip_ref, dq_ref, dk_ref, dv_ref, x_ref, wq_ref, wk_ref, wv_ref, p_ref, g_ref, acc_ref):
    i = pl.program_id(0)
    acc_ref[...] = dot(dk_ref[...], wk_ref[...], NT) + dot(dv_ref[...], wv_ref[...], NT)

    @pl.when(i < own)
    def _():
        acc_ref[...] += dot(dq_ref[...], wq_ref[...], NT)

    @pl.when(i == 0)
    def _():
        g_ref[...] = jnp.zeros_like(g_ref)

    part = acc_ref[...]
    p_ref[...] = part.astype(BF16)
    g_ref[...] += jnp.sum(part * normed(x_ref[...].astype(F32), 1.0), axis=0, keepdims=True)


def project_back(chip, dq, dk, dv, x_all, w_all, first):
    seq, width = x_all.shape
    chip_rows, kv = dq.shape[0], dk.shape[1]
    size = min(TOKEN_TILE, chip_rows)
    own, tiles = chip_rows // size, seq // size
    at = lambda i, chip: ((i + chip[0] * own) % tiles, 0)
    weight = lambda cols, col: pl.BlockSpec((width, cols), lambda i, chip: (0, col), pipeline_mode=pl.Buffered(1))
    return pl.pallas_call(
        functools.partial(project_back_kernel, own),
        out_shape=[jax.ShapeDtypeStruct((seq, width), BF16), jax.ShapeDtypeStruct((1, width), F32)],
        grid_spec=pltpu.PrefetchScalarGridSpec(
            num_scalar_prefetch=1,
            grid=(tiles,),
            in_specs=[
                pl.BlockSpec((size, width), lambda i, chip: (jnp.minimum(i, own - 1), 0)),
                pl.BlockSpec((size, kv), at),
                pl.BlockSpec((size, kv), at),
                pl.BlockSpec((size, width), at),
                weight(width, first // width),
                weight(kv, (first + width) // kv),
                weight(kv, (first + width) // kv + 1),
            ],
            out_specs=[
                pl.BlockSpec((size, width), at),
                pl.BlockSpec((1, width), lambda i, chip: (0, 0)),
            ],
            scratch_shapes=[pltpu.VMEM((size, width), F32)],
        ),
        compiler_params=pltpu.CompilerParams(vmem_limit_bytes=48 * MIB),
        name="project_back",
    )(chip, dq, dk, dv, x_all, w_all, w_all, w_all)


def feed_kernel(chip_ref, x_ref, p0_ref, p1_ref, gain_ref, w_ref, mid_ref, sec_ref, act_ref, gu_ref):
    count = x_ref.shape[0]
    size = min(TOKEN_TILE, count)
    tile = lambda i: pl.ds(pl.multiple_of(i * size, size), size)

    @pl.when(pl.program_id(0) == 0)
    def _():
        def start(i, _):
            rows = tile(i)
            middle = x_ref[rows, :].astype(F32) + (p0_ref[rows, :].astype(F32) + p1_ref[rows, :].astype(F32))
            mid_ref[rows, :] = middle
            sec_ref[rows, :] = normed(middle, gain_ref[...]).astype(BF16)
            return 0

        lax.fori_loop(0, count // size, start, 0)

    def body(i, _):
        rows = tile(i)
        both = dot(sec_ref[rows, :], w_ref[...], NN)
        gate, up = both[:, :FF_TILE], both[:, FF_TILE:]
        act_ref[rows, :] = (gate * jax.nn.sigmoid(gate) * up).astype(BF16)
        gu_ref[rows, :] = both.astype(BF16)
        return 0

    lax.fori_loop(0, count // size, body, 0)


def feed(chip, x_all, p0, p1, gain, w_all, ff):
    rows, width = p0.shape
    once = pl.Buffered(1)
    whole = lambda: pl.BlockSpec((rows, width), lambda j, chip: (0, 0), pipeline_mode=once)
    return pl.pallas_call(
        feed_kernel,
        out_shape=[
            jax.ShapeDtypeStruct((rows, width), F32),
            jax.ShapeDtypeStruct((rows, width), BF16),
            jax.ShapeDtypeStruct((rows, ff), BF16),
            jax.ShapeDtypeStruct((rows, 2 * ff), BF16),
        ],
        grid_spec=pltpu.PrefetchScalarGridSpec(
            num_scalar_prefetch=1,
            grid=(ff // FF_TILE,),
            in_specs=[
                pl.BlockSpec((rows, width), lambda j, chip: (chip[0], 0), pipeline_mode=once),
                whole(), whole(),
                pl.BlockSpec((1, width), lambda j, chip: (0, 0)),
                pl.BlockSpec((width, 2 * FF_TILE), lambda j, chip: (0, j)),
            ],
            out_specs=[
                pl.BlockSpec((rows, width), lambda j, chip: (0, 0)),
                pl.BlockSpec((rows, width), lambda j, chip: (0, 0)),
                pl.BlockSpec((rows, FF_TILE), lambda j, chip: (0, j)),
                pl.BlockSpec((rows, 2 * FF_TILE), lambda j, chip: (0, j)),
            ],
        ),
        compiler_params=pltpu.CompilerParams(vmem_limit_bytes=38 * MIB),
        name="feed",
    )(chip, x_all, p0, p1, gain, w_all)


def feed_back_kernel(core_ref, gu_ref, go_ref, wd_ref, gg_ref, d_ref):
    count = gu_ref.shape[0]
    size = min(TOKEN_TILE, count)
    unit = wd_ref.shape[2]
    for u in range(FF_TILE // unit):
        d_ref[u * unit : (u + 1) * unit, :] = wd_ref[u, 0]

    def body(i, _):
        rows = pl.ds(pl.multiple_of(i * size, size), size)
        grad = dot(go_ref[rows, :], d_ref[...], NT)
        gate, up = gu_ref[rows, :FF_TILE].astype(F32), gu_ref[rows, FF_TILE:].astype(F32)
        sig = jax.nn.sigmoid(gate)
        gg_ref[rows, :FF_TILE] = (grad * up * sig * (1.0 + gate * (1.0 - sig))).astype(BF16)
        gg_ref[rows, FF_TILE:] = (grad * (gate * sig)).astype(BF16)
        return 0

    lax.fori_loop(0, count // size, body, 0)


def feed_back(core, gate_up, go, w_down):
    rows, width = go.shape
    chips, _, unit, _ = w_down.shape
    ff = chips * unit
    return pl.pallas_call(
        feed_back_kernel,
        out_shape=[jax.ShapeDtypeStruct((rows, 2 * ff), BF16), jax.ShapeDtypeStruct((ff, width), BF16)],
        grid_spec=pltpu.PrefetchScalarGridSpec(
            num_scalar_prefetch=1,
            grid=(ff // FF_TILE,),
            in_specs=[
                pl.BlockSpec((rows, 2 * FF_TILE), lambda j, core: (0, j)),
                pl.BlockSpec((rows, width), lambda j, core: (0, 0), pipeline_mode=pl.Buffered(1)),
                pl.BlockSpec((FF_TILE // unit, 1, unit, width), lambda j, core: (j, core[0], 0, 0)),
            ],
            out_specs=[
                pl.BlockSpec((rows, 2 * FF_TILE), lambda j, core: (0, j)),
                pl.BlockSpec((FF_TILE, width), lambda j, core: (j, 0)),
            ],
        ),
        compiler_params=pltpu.CompilerParams(vmem_limit_bytes=48 * MIB),
        name="feed_back",
    )(core, gate_up, go, w_down)


def middle_back_kernel(mid_ref, s0_ref, s1_ref, go_ref, gain_ref, wo_ref, ga_ref, gm_ref, g_ref):
    back, terms = norm_back(mid_ref[...], gain_ref[...], s0_ref[...].astype(F32) + s1_ref[...].astype(F32))
    grad = (go_ref[...].astype(F32) + back).astype(BF16)
    ga_ref[...] = grad
    gm_ref[...] = dot(grad, wo_ref[...], NT).astype(BF16)

    @pl.when(pl.program_id(0) == 0)
    def _():
        g_ref[...] = jnp.zeros_like(g_ref)

    g_ref[...] += jnp.sum(terms, axis=0, keepdims=True)


def middle_back(middle, s0, s1, go, gain, w_out):
    rows, width = middle.shape
    size = min(ROW_TILE, rows)
    row = pl.BlockSpec((size, width), lambda i: (i, 0))
    line = pl.BlockSpec((1, width), lambda i: (0, 0))
    return pl.pallas_call(
        middle_back_kernel,
        out_shape=[
            jax.ShapeDtypeStruct((rows, width), BF16),
            jax.ShapeDtypeStruct((rows, w_out.shape[0]), BF16),
            jax.ShapeDtypeStruct((1, width), F32),
        ],
        grid=(rows // size,),
        in_specs=[row, row, row, row, line, pl.BlockSpec(w_out.shape, lambda i: (0, 0), pipeline_mode=pl.Buffered(1))],
        out_specs=[row, pl.BlockSpec((size, w_out.shape[0]), lambda i: (i, 0)), line],
        compiler_params=pltpu.CompilerParams(vmem_limit_bytes=22 * MIB),
        name="middle_back",
    )(middle, s0, s1, go, gain, w_out)


LINK_TIME = pl.CostEstimate(flops=0, bytes_accessed=300_000_000, transcendentals=0)


def peers():
    dp, ctx = lax.axis_index("dp"), lax.axis_index("ctx")
    to = lambda d, k: (jnp.bitwise_xor(dp, d), jnp.bitwise_xor(ctx, k))
    return dp, ctx, to


def greet(devices):
    barrier = pltpu.get_barrier_semaphore()
    for device in devices:
        pl.semaphore_signal(barrier, inc=1, device_id=device, device_id_type=MESH)
    pl.semaphore_wait(barrier, len(devices))


def sender(send_sem, recv_sem):
    made = []

    def send(src, dst, device):
        i = len(made)
        copy = pltpu.make_async_remote_copy(
            src_ref=src, dst_ref=dst, send_sem=send_sem.at[i], recv_sem=recv_sem.at[i],
            device_id=device, device_id_type=MESH,
        )
        copy.start()
        made.append(copy)
        return copy

    return send, made


def gather_kernel(pk_ref, wo_ref, tok_ref, go_ref, w_ref, x_ref, g_ref, send_sem, recv_sem, local_sem):
    dp, ctx, to = peers()
    c, z = ctx % 2, ctx // 2
    which, me = ctx // 4, ctx % 4
    inner = jnp.logical_or(z == 1, z == 2)
    greet([to(0, 1), to(0, 2), to(0, 4), to(0, 6), to(1, 0), to(2, 0)])
    send, made = sender(send_sem, recv_sem)
    sib, nbr, far, across, xn, yn = to(0, 1), to(0, 2), to(0, 4), to(0, 6), to(1, 0), to(2, 0)
    rows, cols = pk_ref.shape[1:]

    place = w_ref.at[dp, z, pl.ds(c * rows, rows), pl.ds(0, cols)]
    local = [
        pltpu.make_async_copy(pk_ref.at[c], place, local_sem.at[0]),
        pltpu.make_async_copy(wo_ref, w_ref.at[dp, z, :, pl.ds(cols, wo_ref.shape[1])], local_sem.at[1]),
        pltpu.make_async_copy(tok_ref.at[which], x_ref.at[me, 0], local_sem.at[2]),
        pltpu.make_async_copy(go_ref.at[which], g_ref.at[c, 0], local_sem.at[3]),
    ]
    for copy in local:
        copy.start()
    cross = send(pk_ref.at[1 - c], place, sib)
    for copy in local:
        copy.wait()
    cross.wait_recv()
    done = []

    def half(h, q, zz):
        return w_ref.at[q, zz, pl.ds(h * rows, rows)]

    first = []

    def spread(zz):
        low, high = half(0, dp, zz), half(1, dp, zz)
        first.append((send(low, low, yn), low, half(0, jnp.bitwise_xor(dp, 2), zz), xn))
        first.append((send(high, high, xn), high, half(1, jnp.bitwise_xor(dp, 1), zz), yn))

    def pass_on():
        for copy, own, part, device in first[:2]:
            done.append(send(own, own, device))
            copy.wait_recv()
            done.append(send(part, part, device))
        del first[:2]

    z_one = jnp.bitwise_xor(z, 1)
    z_near = jnp.bitwise_xor(z, jnp.where(inner, 3, 2))
    z_far = jnp.bitwise_xor(z, jnp.where(inner, 2, 3))
    relayed = []

    def relay(slot, source, device):
        copy = pltpu.make_async_remote_copy(
            src_ref=w_ref.at[dp, source], dst_ref=w_ref.at[dp, source],
            send_sem=send_sem.at[send_sem.shape[0] - 4 + len(relayed)],
            recv_sem=recv_sem.at[send_sem.shape[0] - 2 + slot],
            device_id=device, device_id_type=MESH,
        )
        relayed.append(copy)
        pl.when(inner)(copy.start)
        return copy

    step = send(w_ref.at[dp, z], w_ref.at[dp, z], nbr)
    near = relay(0, z, across)
    spread(z)
    pass_on()
    step.wait_recv()
    far_block = relay(1, z_one, across)
    spread(z_one)
    near.wait_recv()
    relay(0, z_near, nbr)
    spread(z_near)
    pass_on()
    far_block.wait_recv()
    relay(1, z_far, nbr)
    spread(z_far)
    swap = send(tok_ref.at[1 - which], x_ref.at[me, 1], far)
    mine_nbr = send(tok_ref.at[which], x_ref.at[me, 0], nbr)
    done += [send(tok_ref.at[which], x_ref.at[me, 0], sib), send(go_ref.at[which], g_ref.at[c, 0], sib)]
    pass_on()
    swap.wait_recv()
    done.append(send(x_ref.at[me, 1], x_ref.at[me, 1], sib))
    swap_nbr = send(x_ref.at[me, 1], x_ref.at[me, 1], nbr)
    go_swap = send(go_ref.at[1 - which], g_ref.at[c, 1], far)
    pass_on()
    other = jnp.bitwise_xor(me, 2)
    mine_nbr.wait_recv()
    done.append(send(x_ref.at[other, 0], x_ref.at[other, 0], sib))
    swap_nbr.wait_recv()
    done.append(send(x_ref.at[other, 1], x_ref.at[other, 1], sib))
    go_swap.wait_recv()
    done.append(send(g_ref.at[c, 1], g_ref.at[c, 1], sib))
    for copy in done:
        copy.wait_recv()
    for copy in made:
        copy.wait_send()

    @pl.when(inner)
    def _():
        for copy in relayed:
            copy.wait_send()


def gather(packed, w_out, tokens, grad_out):
    rows, cols = 2 * packed.shape[1], packed.shape[2] + w_out.shape[1]
    slots, width = tokens.shape[1:]
    copies = 36 + 4
    anywhere = pl.BlockSpec(memory_space=pl.ANY)
    near = pl.BlockSpec(memory_space=pltpu.VMEM)
    w, x, g = pl.pallas_call(
        gather_kernel,
        out_shape=[
            jax.ShapeDtypeStruct((4, 4, rows, cols), BF16),
            jax.ShapeDtypeStruct((4, 2, slots, width), BF16),
            jax.ShapeDtypeStruct((2, 2, slots, width), BF16),
        ],
        in_specs=[near] * 4,
        out_specs=[anywhere] * 3,
        scratch_shapes=[
            pltpu.SemaphoreType.DMA((copies,)),
            pltpu.SemaphoreType.DMA((copies,)),
            pltpu.SemaphoreType.DMA((4,)),
        ],
        compiler_params=pltpu.CompilerParams(
            collective_id=0, has_side_effects=True, vmem_limit_bytes=48 * MIB
        ),
        cost_estimate=LINK_TIME,
        name="gather",
    )(packed, w_out, tokens, grad_out)
    return w.reshape(16 * rows, cols), x.reshape(-1, width), g.reshape(-1, width)


def reduce_kernel(
    h_hbm, dq_hbm, dk_hbm, dv_hbm, e_hbm, ow_hbm, or_hbm, part_ref, xa_hbm, gm_hbm, gain_ref,
    a_ref, go_ref, ig_ref,
    g_ref, in_a, in_b, mid_a, mid_b, got_a, got_b, out3, in3, mine_ref, sib_ref, give_ref, nbr_ref, back_ref,
    x_ref, ga_ref, h_ref, dq_ref, dk_ref, dv_ref, o_ref, s_ref, send_sem, recv_sem, local_sem,
):
    dp, ctx, to = peers()
    c, z = ctx % 2, ctx // 2
    which, chip = ctx // 4, z % 2
    x, y = dp % 2, dp // 2
    hr = g_ref.shape[3] // 2
    count = mine_ref.shape[1]
    q_cols, kv_cols = dq_ref.shape[1], dk_ref.shape[1]
    near = s_ref.shape[1]
    first_col, width = near - HD, ow_hbm.shape[-1]
    local = []

    def fetch(src, dst):
        copy = pltpu.make_async_copy(src, dst, local_sem.at[len(local)])
        copy.start()
        local.append(copy)

    fetch(ow_hbm.at[:, :, c], g_ref.at[c, :, :, :, pl.ds(near, width)])
    fetch(or_hbm, g_ref.at[1 - c, :, :, :, pl.ds(near, width)])
    fetch(e_hbm, g_ref.at[:, :, :, :, pl.ds(first_col, HD)])
    fetch(part_ref.at[:, c], mine_ref)
    fetch(dq_hbm, dq_ref)
    fetch(h_hbm, h_ref)
    fetch(dk_hbm, dk_ref)
    fetch(dv_hbm, dv_ref)
    fetch(xa_hbm.at[ctx % 4], x_ref)
    fetch(gm_hbm.at[c], ga_ref)
    greet([to(0, 1), to(0, 2), to(0, 4), to(0, 6), to(1, 0), to(2, 0)])
    send, made = sender(send_sem, recv_sem)
    sib, nbr, far, across = to(0, 1), to(0, 2), to(0, 4), to(0, 6)
    xn, yn = to(1, 0), to(2, 0)
    cross = send(part_ref.at[:, 1 - c], sib_ref, sib)

    def ready(count):
        for copy in local[:count]:
            copy.wait()
        del local[:count]

    def weigh(rows, grad_ref, at):
        def body(i, _):
            some = h_ref[rows, pl.ds(pl.multiple_of(i * 4 * 2 * hr, 128), 4 * 2 * hr)]
            part = dot(some, grad_ref[...], TN).astype(BF16)
            g_ref[i // 2, i % 2, :, :, at : at + grad_ref.shape[1]] = part.reshape(4, 2 * hr, grad_ref.shape[1])
            return 0

        lax.fori_loop(0, 4, body, 0)

    low, high = pl.ds(0, hr), pl.ds(hr, hr)
    inner = jnp.logical_or(z == 1, z == 2)
    outer = jnp.logical_not(inner)
    order = [jnp.bitwise_xor(z, jnp.where(inner, 3, 2)), jnp.bitwise_xor(z, jnp.where(inner, 2, 3)), jnp.bitwise_xor(z, 1), z]
    passed = []

    def pass_z(kind, slot, source, part, device, role):
        copy = pltpu.make_async_remote_copy(
            src_ref=out3.at[source, :, parts[part]], dst_ref=in3.at[slot, :, parts[part]],
            send_sem=send_sem.at[40 + 2 * kind + part], recv_sem=recv_sem.at[40 + 2 * slot + part],
            device_id=device, device_id_type=MESH,
        )
        pl.when(role)(copy.start)
        passed.append((role, copy))

    def from_z(slot, part):
        return pltpu.make_async_remote_copy(
            src_ref=out3.at[0, :, parts[part]], dst_ref=in3.at[slot, :, parts[part]],
            send_sem=send_sem.at[40 + part], recv_sem=recv_sem.at[40 + 2 * slot + part],
            device_id=nbr, device_id_type=MESH,
        )

    def add_z(block, slot, part):
        p = parts[part]
        out3[block, :, p] = (out3[block, :, p].astype(F32) + in3[slot, :, p].astype(F32)).astype(BF16)

    def inward(i):
        k, part = i % 4, i // 4

        @pl.when(inner)
        def _():
            from_z(k, part).wait_recv()
            add_z(k, k, part)

        pass_z(3 + k, 3 + k, k, part, across, inner)

    def outward(part):
        @pl.when(inner)
        def _():
            from_z(4, part).wait_recv()
            add_z(2, 4, part)

        pass_z(5, 2, 2, part, nbr, inner)

    a_in, b_in, a_mid, b_mid = [], [], [], []
    size = 64
    tile = lambda i: pl.ds(pl.multiple_of(i * size, size), size)
    parts = (pl.ds(first_col, HD + width), pl.ds(0, first_col))

    def enter(i):
        k, p = i % 4, parts[i // 4]
        a_in.append(send(g_ref.at[:, 1 - x, order[k], low, p], in_a.at[k, :, :, p], xn))
        b_in.append(send(g_ref.at[1 - y, :, order[k], high, p], in_b.at[k, :, :, p], yn))

    def middle(i):
        k, p = i % 4, parts[i // 4]
        add = lambda p, q: (p.astype(F32) + q.astype(F32)).astype(BF16)
        a_in[i].wait_recv()
        mid_a[k, :, p] = add(g_ref[1 - y, x, order[k], 0:hr, p], in_a[k, 1 - y, :, p])
        a_mid.append(send(mid_a.at[k, :, p], got_a.at[k, :, p], yn))
        b_in[i].wait_recv()
        mid_b[k, :, p] = add(g_ref[y, 1 - x, order[k], hr:, p], in_b[k, 1 - x, :, p])
        b_mid.append(send(mid_b.at[k, :, p], got_b.at[k, :, p], xn))

    def leave(i):
        k, p = i % 4, parts[i // 4]
        add = lambda p, q, r: (p.astype(F32) + q.astype(F32) + r.astype(F32)).astype(BF16)
        a_mid[i].wait_recv()
        out3[k, 0:hr, p] = add(g_ref[y, x, order[k], 0:hr, p], in_a[k, y, :, p], got_a[k, :, p])
        b_mid[i].wait_recv()
        out3[k, hr:, p] = add(g_ref[y, x, order[k], hr:, p], in_b[k, x, :, p], got_b[k, :, p])
        if k < 3:
            pass_z(k, k, k, i // 4, nbr, outer)

    ready(3)
    enter(0)
    enter(1)
    enter(2)
    ready(1)
    cross.wait_recv()
    slots = ig_ref.shape[1]

    def give(i, _):
        rows = tile(i)
        give_ref[rows] = (mine_ref[1 - chip, rows].astype(F32) + sib_ref[1 - chip, rows].astype(F32)).astype(BF16)
        return 0

    def back(i, _):
        rows = tile(i)
        grad = mine_ref[chip, rows].astype(F32) + sib_ref[chip, rows].astype(F32) + nbr_ref[rows].astype(F32)
        through, _terms = norm_back(x_ref[rows, :].astype(F32), gain_ref[...], grad)
        back_ref[rows] = (ga_ref[rows, :].astype(F32) + through).astype(BF16)
        return 0

    swaps = []
    for first in (slots, 0):
        lax.fori_loop(first // size, (first + slots) // size, give, 0)
        rows = pl.ds(first, slots)
        swaps.append(send(give_ref.at[rows], nbr_ref.at[rows], nbr))
    ready(2)
    weigh(pl.ds(pl.multiple_of(chip * dq_ref.shape[0], dq_ref.shape[0]), dq_ref.shape[0]), dq_ref, 0)
    middle(0)
    enter(3)
    middle(1)
    middle(2)
    ready(2)
    weigh(slice(None), dk_ref, q_cols)
    weigh(slice(None), dv_ref, q_cols + kv_cols)
    enter(4)
    enter(5)
    leave(0)
    leave(1)
    middle(3)
    ready(2)
    swaps[0].wait_recv()
    lax.fori_loop(slots // size, 2 * slots // size, back, 0)
    home = send(back_ref.at[pl.ds(slots, slots)], ig_ref.at[which], far)
    leave(2)
    inward(0)
    inward(1)
    middle(4)
    enter(6)
    leave(3)
    middle(5)
    enter(7)
    leave(4)
    outward(0)
    swaps[1].wait_recv()
    lax.fori_loop(0, slots // size, back, 0)
    keep = pltpu.make_async_copy(back_ref.at[pl.ds(0, slots)], ig_ref.at[which], local_sem.at[0])
    keep.start()
    middle(6)
    leave(5)
    inward(4)
    middle(7)
    leave(6)
    inward(5)
    leave(7)
    outward(1)
    for part in range(2):
        from_z(2, part).wait_recv()

    @pl.when(inner)
    def _():
        for part in range(2):
            from_z(3, part).wait_recv()
            add_z(3, 3, part)

    total = out3[3].astype(F32) + in3[2].astype(F32)
    o_ref[...] = total[:, :near].astype(BF16)
    other = send(o_ref.at[pl.ds(pl.multiple_of((1 - c) * hr, hr), hr)], s_ref, sib)
    go_ref[...] = total[:, near:].astype(BF16)
    own = o_ref.at[pl.ds(pl.multiple_of(c * hr, hr), hr)]

    def place(source, core):
        at = 0
        for size in (q_cols, kv_cols, kv_cols):
            a_ref[:, pl.ds(pl.multiple_of(2 * at + core * size, HD), size)] = source[:, at : at + size]
            at += size

    place(own, c)
    other.wait_recv()
    place(s_ref, 1 - c)
    both = own[:, first_col:].astype(F32) + s_ref[:, first_col:].astype(F32)
    a_ref[:, 2 * first_col :] = both.astype(BF16)
    keep.wait()
    home.wait_recv()
    for copy in made:
        copy.wait_send()
    for role, copy in passed:
        pl.when(role)(copy.wait_send)


def reduce(hidden, dq, dk, dv, entries, out_own, out_sib, part, x_all, grad_middle, gain):
    seq, width = x_all.shape
    rows = width // 16
    near_cols = dq.shape[1] + dk.shape[1] + dv.shape[1] + HD
    cols = near_cols + width
    count = part.shape[0] // 4
    copies = 52
    anywhere = pl.BlockSpec(memory_space=pl.ANY)
    near = pl.BlockSpec(memory_space=pltpu.VMEM)
    return pl.pallas_call(
        reduce_kernel,
        out_shape=[
            jax.ShapeDtypeStruct((rows // 2, 2 * (near_cols - HD) + HD), BF16),
            jax.ShapeDtypeStruct((rows, width), BF16),
            jax.ShapeDtypeStruct((2, count // 2, width), BF16),
        ],
        in_specs=[anywhere] * 10 + [near],
        out_specs=[near] * 2 + [anywhere],
        scratch_shapes=[
            pltpu.VMEM((2, 2, 4, rows, cols), BF16),
            pltpu.VMEM((4, 2, rows // 2, cols), BF16),
            pltpu.VMEM((4, 2, rows // 2, cols), BF16),
        ]
        + [pltpu.VMEM((4, rows // 2, cols), BF16)] * 4
        + [
            pltpu.VMEM((4, rows, cols), BF16),
            pltpu.VMEM((5, rows, cols), BF16),
            pltpu.VMEM((2, count, width), BF16),
            pltpu.VMEM((2, count, width), BF16),
        ]
        + [pltpu.VMEM((count, width), BF16)] * 5
        + [pltpu.VMEM(v.shape, BF16) for v in (hidden, dq, dk, dv)]
        + [
            pltpu.VMEM((rows, near_cols), BF16),
            pltpu.VMEM((rows // 2, near_cols), BF16),
            pltpu.SemaphoreType.DMA((copies,)),
            pltpu.SemaphoreType.DMA((copies,)),
            pltpu.SemaphoreType.DMA((10,)),
        ],
        compiler_params=pltpu.CompilerParams(
            collective_id=1, has_side_effects=True, vmem_limit_bytes=48 * MIB
        ),
        cost_estimate=LINK_TIME,
        name="reduce",
    )(
        hidden, dq, dk, dv,
        entries.reshape(2, 2, 4, rows, HD),
        out_own.reshape(2, 4, 2, rows, width),
        out_sib.reshape(2, 4, rows, width),
        part.reshape(2, 2, count, width),
        x_all.reshape(4, count, width),
        grad_middle.reshape(2, count, width),
        gain,
    )


def by_core(c, own, other):
    return jnp.where(c == 0, jnp.stack([own, other]), jnp.stack([other, own]))


def layer(
    n_dp, n, tokens, positions, w_query, w_key, w_value, w_out, w_gate, w_up, w_down,
    attn_gain, mlp_gain, q_gain, k_gain, grad_out,
):
    axes = ("dp", "ctx")
    slots, width = tokens.shape[1:]
    seq = positions.shape[1]
    span = slots // 2
    half = n // 2
    chips = n_dp * half
    ctx = lax.axis_index("ctx")
    c = ctx % 2
    which = ctx // half
    r_in, r_out, r_down = w_query.shape[0], w_out.shape[0], w_down.shape[0]
    ff = w_gate.shape[1]
    ff_c = ff // 2
    q_c, kv_c = H * HD // 2, KV * HD // 2

    to_sibling = [(i, i ^ 1) for i in range(n)]
    to_partner = [(i, (i + half) % n) for i in range(n)]
    halves = [list(range(half)), list(range(half, n))]
    same_core = [list(range(0, n, 2)), list(range(1, n, 2))]
    sibling = lambda v: lax.ppermute(v, "ctx", to_sibling)
    partner = lambda v: lax.ppermute(v, "ctx", to_partner)

    def placed(values):
        mine = lax.dynamic_index_in_dim(values, which, 0, False)
        other = lax.dynamic_index_in_dim(values, 1 - which, 0, False)
        return jnp.concatenate([mine, partner(other)], axis=0)

    gains = jnp.concatenate(
        [
            attn_gain[:, None],
            mlp_gain[:, None],
            jnp.pad(q_gain, (0, r_in - q_gain.shape[0]))[:, None],
            jnp.pad(k_gain, (0, r_in - k_gain.shape[0]))[:, None],
            jnp.zeros((r_in, 124), BF16),
        ],
        axis=1,
    )
    tall = (n_dp, n) == (4, 8)
    qkv_halves = [
        jnp.concatenate(
            [
                w_query[:, i * q_c : (i + 1) * q_c],
                w_key[:, i * kv_c : (i + 1) * kv_c],
                w_value[:, i * kv_c : (i + 1) * kv_c],
            ],
            axis=1,
        )
        for i in range(2)
    ]

    def ff_order(shard):
        return shard.reshape(r_in, chips, 2, r_down).transpose(2, 0, 1, 3).reshape(2, r_in, ff_c)

    gate_order, up_order = ff_order(w_gate), ff_order(w_up)
    qkv_c = q_c + 2 * kv_c
    gu_c = 2 * ff_c
    all_c = gu_c + qkv_c
    by_tile = lambda v: v.reshape(2, r_in, ff_c // FF_TILE, FF_TILE)
    gu_shard = jnp.stack([by_tile(gate_order), by_tile(up_order)], axis=3).reshape(2, r_in, 2 * ff_c)
    packed = jnp.stack([jnp.concatenate([gu_shard[i], qkv_halves[i], gains], axis=1) for i in range(2)])
    if tall:
        w_all, x_all, go_chip = gather(packed, w_out, tokens, grad_out)
        out_rows = w_all[:, all_c + HD :].reshape(2, -1, r_out, width)
        out_keep = lax.dynamic_index_in_dim(out_rows, c, 0, False)
        out_give = lax.dynamic_index_in_dim(out_rows, 1 - c, 0, False)
        w_out_c = by_core(c, out_keep, sibling(out_give)).transpose(1, 0, 2, 3).reshape(q_c, width)
        w_down, w_all = lax.optimization_barrier((w_down, w_all))
    else:
        both = lax.all_gather(packed, axes, axis=1, tiled=True)
        w_all = lax.dynamic_index_in_dim(both, c, 0, False)
        out_all = lax.all_gather(w_out, axes, axis=0, tiled=True)
        w_out_c = lax.dynamic_slice_in_dim(out_all, c * q_c, q_c, 0)
        x_own = placed(tokens)
        x_all = lax.all_gather(x_own, "ctx", axis=0, tiled=True, axis_index_groups=halves)
        go_own = placed(grad_out)
        go_chip = by_core(c, go_own, sibling(go_own)).reshape(4 * slots, width)
    down_all = lax.all_gather(w_down, axes, axis=0, tiled=True).reshape(chips, 2, r_down, width)
    g_cols = w_all[:, all_c : all_c + HD].astype(F32)
    gain_attn = g_cols[:, 0][None]
    gain_mlp = g_cols[:, 1][None]
    per_head = g_cols.reshape(n_dp * n, r_in, HD)[:, : q_gain.shape[0]].reshape(HD, HD)
    gain_q = per_head[:, 2][None]
    gain_k = per_head[:, 3][None]

    chip = (ctx % half) // 2
    chip_rows = 4 * slots
    slot_ids = lax.dynamic_index_in_dim(positions, which, 0, False).reshape(2 * n, span)[:, 0] // span
    places = np.stack(
        [
            [s for d in side for k in (d, (d + half) % n) for s in (2 * k, 2 * k + 1)]
            for side in halves
        ]
    ).astype(np.int32)
    ids_all = slot_ids[lax.dynamic_index_in_dim(jnp.asarray(places), which, 0, False)]
    steps = jnp.arange(2 * n, dtype=jnp.int32)
    order = jnp.sum(jnp.where(ids_all[None, :] == steps[:, None], steps[None, :], 0), axis=1).astype(jnp.int32)
    ids = lax.dynamic_slice_in_dim(ids_all, chip * 8, 8, 0)
    cosine, sine = rope_tables(seq)

    chip_at = chip.astype(jnp.int32).reshape(1)
    hidden_all, q_raw, kv_raw = project(chip_at, x_all, gain_attn, w_all, gu_c, chip_rows)
    mixed, lse = attend(ids, order, q_raw, kv_raw, cosine, sine, gain_q, gain_k, span)
    proj = dot(mixed, w_out_c, NN, BF16)
    middle, second, activated, gate_up = feed(chip_at, x_all, proj, sibling(proj), gain_mlp, w_all, ff_c)
    grad_gu, w_down_c = feed_back(c.astype(jnp.int32).reshape(1), gate_up, go_chip, down_all)
    down = dot(activated, w_down_c, NN, BF16).reshape(2, 2 * slots, width)
    down_own = lax.dynamic_index_in_dim(down, c, 0, False)
    down_other = sibling(lax.dynamic_index_in_dim(down, 1 - c, 0, False))
    own_rows = lambda v: lax.dynamic_slice_in_dim(v, c * 2 * slots, 2 * slots, 0)
    result = (own_rows(middle) + (down_own.astype(F32) + down_other.astype(F32))).astype(BF16)

    def returned(rows):
        mine, back = rows[:slots], partner(rows[slots:])
        return jnp.where(which == 0, jnp.stack([mine, back]), jnp.stack([back, mine]))


    second_part = dot(grad_gu, w_all[:, :gu_c], NT, BF16)
    grad_gu_w = dot(second, grad_gu, TN, BF16)
    grad_down_w = dot(activated, go_chip, TN, BF16)
    grad_attn, grad_mixed, mlp_gain_sum = middle_back(
        middle, second_part, sibling(second_part), go_chip, gain_mlp, w_out_c
    )
    grad_mlp_gain = jnp.where(c == 0, mlp_gain_sum[0], 0.0)

    over_dp = lambda grad: lax.psum_scatter(grad, "dp", scatter_dimension=0, tiled=True)
    over_ctx = lambda part: lax.psum_scatter(
        part, "ctx", scatter_dimension=0, tiled=True, axis_index_groups=same_core
    )
    part_gu = over_dp(grad_gu_w)
    part_down = over_dp(grad_down_w)

    out_w = dot(mixed, grad_attn, TN, BF16).reshape(-1, 2, r_out, width)
    out_recv = sibling(lax.dynamic_index_in_dim(out_w, 1 - c, 1, False))
    out_recv, grad_mixed = lax.optimization_barrier((out_recv, grad_mixed))
    result, grad_mixed, part_down = lax.optimization_barrier((result, grad_mixed, part_down))
    if tall:
        pieces = part_down.reshape(half, r_down, width)
        place = ctx // 2
        down_own = lax.dynamic_index_in_dim(pieces, place, 0, False).astype(F32)
        down_got = [
            lax.ppermute(
                lax.dynamic_index_in_dim(pieces, jnp.bitwise_xor(place, k), 0, False),
                "ctx",
                [(i, i ^ (2 * k)) for i in range(n)],
            )
            for k in range(1, half)
        ]
    else:
        down_own, down_got = over_ctx(part_down).astype(F32), []
    output = returned(result)
    dq, dk, dv, dgq, dgk = attend_back(
        ids, order, q_raw, kv_raw, grad_mixed, mixed, lse, cosine, sine, gain_q, gain_k, span
    )
    output, dq, dk, dv, part_gu, down_got = lax.optimization_barrier((output, dq, dk, dv, part_gu, down_got))
    sum_gu = over_ctx(part_gu)
    sum_down = down_own
    for piece in down_got:
        sum_down = sum_down + piece.astype(F32)
    part_all, attn_gain_sum = project_back(chip_at, dq, dk, dv, x_all, w_all, gu_c)
    lot = lambda v: v.reshape(n_dp * n, -1)
    entries = jnp.concatenate([lot(attn_gain_sum), lot(grad_mlp_gain), lot(dgq), lot(dgk)], axis=1)
    entries = jnp.pad(entries[:, None], ((0, 0), (0, r_in - 1), (0, HD - entries.shape[1])))
    entries = entries.reshape(width, HD).astype(BF16)
    entries, sum_down = lax.optimization_barrier((entries, sum_down))
    near_c = qkv_c + HD
    beside = lambda v: v.transpose(1, 0, 2).reshape(r_in, -1)
    by_rows = lambda v: lax.dynamic_index_in_dim(v.reshape(2, r_in, -1), c, 0, False)

    def columns(sums):
        other = lax.dynamic_index_in_dim(sums.reshape(2, r_in, -1), 1 - c, 0, False)
        return by_core(c, by_rows(sums), sibling(other))

    if tall:
        sums, sum_out, input_grad = reduce(
            hidden_all, dq, dk, dv, entries, out_w, out_recv, part_all, x_all, grad_attn, gain_attn
        )
        grad_q, grad_k, grad_v = (
            sums[:, i:j].astype(F32) for i, j in ((0, 2 * q_c), (2 * q_c, 2 * q_c + 2 * kv_c), (2 * q_c + 2 * kv_c, 2 * qkv_c))
        )
        sum_out, gain_own = sum_out.astype(F32), sums[:, 2 * qkv_c :].astype(F32)
    else:
        hidden = lax.dynamic_slice_in_dim(hidden_all, chip * chip_rows, chip_rows, 0)
        grads = [dot(hidden, dq, TN, BF16), dot(hidden_all, dk, TN, BF16), dot(hidden_all, dv, TN, BF16), entries]
        qkv_own = columns(over_ctx(over_dp(jnp.concatenate(grads, axis=1)))).astype(F32)
        out_mine = lax.dynamic_index_in_dim(out_w, c, 1, False)
        sum_out = over_ctx(over_dp(by_core(c, out_mine, out_recv).reshape(chips * r_out, width))).astype(F32)
        grad_q = beside(qkv_own[:, :, :q_c])
        grad_k = beside(qkv_own[:, :, q_c : q_c + kv_c])
        grad_v = beside(qkv_own[:, :, q_c + kv_c : qkv_c])
        gain_own = jnp.sum(qkv_own[:, :, qkv_c:], axis=0)
        grad_hidden = lax.psum_scatter(
            part_all, "ctx", scatter_dimension=0, tiled=True, axis_index_groups=halves
        ).astype(F32)
        back, _terms = norm_back(x_own.astype(F32), gain_attn, grad_hidden)
        input_grad = returned((own_rows(grad_attn).astype(F32) + back).astype(BF16))
    sum_gu, gain_own = lax.optimization_barrier((sum_gu, gain_own))
    gain_row, r_head = gain_own[0], q_gain.shape[0]
    gu_own = columns(sum_gu).reshape(2, r_in, ff_c // FF_TILE, 2, FF_TILE)
    ff_back = lambda v: v.reshape(2, r_in, chips, r_down).transpose(1, 2, 0, 3).reshape(r_in, ff)
    return (
        output,
        input_grad,
        grad_q,
        grad_k,
        grad_v,
        sum_out,
        ff_back(gu_own[:, :, :, 0]).astype(F32),
        ff_back(gu_own[:, :, :, 1]).astype(F32),
        sum_down,
        gain_row[:r_in],
        gain_row[r_in : 2 * r_in],
        gain_row[2 * r_in : 2 * r_in + r_head],
        gain_row[2 * r_in + r_head : 2 * r_in + 2 * r_head],
    )


def solution(mesh):
    rows = P(("dp", "ctx"), None)
    gain = P(("dp", "ctx"))
    acts = P("dp", "ctx", None)
    return jax.shard_map(
        functools.partial(layer, mesh.shape["dp"], mesh.shape["ctx"]),
        mesh=mesh,
        in_specs=(acts, P("dp", None)) + (rows,) * 7 + (gain,) * 4 + (acts,),
        out_specs=(acts, acts) + (rows,) * 7 + (gain,) * 4,
        check_vma=False,
    )
```

```python
import functools

import jax
import jax.numpy as jnp
import numpy as np
from jax import lax
from jax.experimental import pallas as pl
from jax.experimental.pallas import tpu as pltpu
from jax.sharding import PartitionSpec as P

H = 16
KV = 8
HD = 128
GROUPS = H // KV
EPSILON = 1e-06
THETA = 1000000.0
LOG2E = 1.4426950408889634
KEY_TILE = 512
ROW_TILE = 256
TOKEN_TILE = 512
FF_TILE = 384
MIB = 1024 * 1024
MESH = pl.DeviceIdType.MESH
F32 = jnp.float32
BF16 = jnp.bfloat16


def normed(values, weights):
    return values * lax.rsqrt(jnp.mean(values * values, axis=-1, keepdims=True) + EPSILON) * weights


def norm_back(values, weights, grad):
    r = lax.rsqrt(jnp.mean(values * values, axis=-1, keepdims=True) + EPSILON)
    unit = values * r
    u = grad * weights
    return r * (u - unit * jnp.mean(u * unit, axis=-1, keepdims=True)), grad * unit


def rope_tables(seq):
    half = HD // 2
    inverse = (THETA ** (-(np.arange(half, dtype=np.float32) * np.float32(2.0) / np.float32(HD)))).astype(np.float32)
    angles = np.arange(seq, dtype=np.float32)[:, None] * inverse[None, :]
    cosine, sine = np.cos(angles), np.sin(angles)
    return (
        jnp.asarray(np.concatenate([cosine, cosine], axis=-1).astype(np.float32)),
        jnp.asarray(np.concatenate([-sine, sine], axis=-1).astype(np.float32)),
    )


def dot(a, b, dims, out=F32):
    return lax.dot_general(a, b, (dims, ((), ())), preferred_element_type=out)


NN = ((1,), (0,))
NT = ((1,), (1,))
TN = ((0,), (0,))


def row_mean(values):
    return dot(values.astype(BF16), jnp.full((HD, HD), 1.0 / HD, BF16), NN)


def row_sums(values):
    high = values.astype(BF16)
    ones = jnp.ones((8, HD), BF16)
    return (dot(ones, high, NT) + dot(ones, (values - high.astype(F32)).astype(BF16), NT))[0:1]


def unit_rows(raw):
    r = lax.rsqrt(row_mean(raw * raw) + EPSILON)
    return raw * r, r


def rope(values, cosine, sine):
    return values * cosine + pltpu.roll(values, HD // 2, 1) * sine


def rope_back(values, cosine, sine):
    return values * cosine - pltpu.roll(values, HD // 2, 1) * sine


def lanes(head, width=HD):
    return slice(head * width, (head + 1) * width)


def prepare_keys(span, order_ref, k_ref, v_ref, cos_ref, sin_ref, gk_ref, ks_ref, vs_ref):
    def body(i, _):
        rows = pl.ds(pl.multiple_of(i * span, span), span)
        source = pl.ds(pl.multiple_of(order_ref[i] * span, span), span)
        for p in range(k_ref.shape[1] // HD):
            unit, _r = unit_rows(k_ref[source, lanes(p)].astype(F32))
            ks_ref[rows, lanes(p)] = rope(unit * gk_ref[...], cos_ref[rows, :], sin_ref[rows, :]).astype(BF16)
        vs_ref[rows, :] = v_ref[source, :]
        return 0

    lax.fori_loop(0, k_ref.shape[0] // span, body, 0)


def query_block(q_ref, p, rows, places, cos_ref, sin_ref, gq_ref):
    units, scales, parts = [], [], []
    for g in range(GROUPS):
        unit, r = unit_rows(q_ref[rows, lanes(p * GROUPS + g)].astype(F32))
        turned = rope(unit * gq_ref[...], cos_ref[places, :], sin_ref[places, :])
        units.append(unit)
        scales.append(r)
        parts.append((turned * (LOG2E * HD**-0.5)).astype(BF16))
    return units, scales, jnp.concatenate(parts, axis=0)


def seen(shape, t, b, span, key_axis):
    at = t * KEY_TILE + lax.broadcasted_iota(jnp.int32, shape, key_axis)
    own = b * span + lax.broadcasted_iota(jnp.int32, shape, 1 - key_axis) % span
    return at <= own


def attend_kernel(
    span, ids_ref, order_ref, q_ref, k_ref, v_ref, cos_ref, sin_ref, gq_ref, gk_ref,
    o_ref, lse_ref, ks_ref, vs_ref, acc_ref, sum_ref,
):
    @pl.when(pl.program_id(0) == 0)
    def _():
        prepare_keys(span, order_ref, k_ref, v_ref, cos_ref, sin_ref, gk_ref, ks_ref, vs_ref)

    m = GROUPS * span
    heads = range(k_ref.shape[1] // HD)
    b = ids_ref[pl.program_id(0)]
    rows = slice(None)
    places = pl.ds(pl.multiple_of(b * span, span), span)
    q2 = [query_block(q_ref, p, rows, places, cos_ref, sin_ref, gq_ref)[2] for p in heads]
    acc_ref[...] = jnp.zeros_like(acc_ref)
    sum_ref[...] = jnp.zeros_like(sum_ref)

    def tile(t, masked):
        keys = pl.ds(pl.multiple_of(t * KEY_TILE, KEY_TILE), KEY_TILE)
        scores = [dot(q2[p], ks_ref[keys, lanes(p)], NT) for p in heads]
        keep = seen(scores[0].shape, t, b, span, 1) if masked else None
        for p in heads:
            e = jnp.exp2(scores[p])
            if masked:
                e = jnp.where(keep, e, 0.0)
            part = e[:, 0:HD]
            for i in range(1, KEY_TILE // HD):
                part = part + e[:, lanes(i)]
            sum_ref[p] += part
            acc_ref[p] += dot(e.astype(BF16), vs_ref[keys, lanes(p)], NN)

    last = (b * span) // KEY_TILE
    lax.fori_loop(0, last, lambda t, _: (tile(t, False), 0)[1], 0)
    tile(last, True)
    for p in heads:
        total = jnp.sum(sum_ref[p], axis=-1, keepdims=True)
        mixed = acc_ref[p] * (1.0 / total)
        for g in range(GROUPS):
            o_ref[rows, lanes(p * GROUPS + g)] = mixed[g * span : (g + 1) * span].astype(BF16)
        wide = jnp.broadcast_to(jnp.log2(total), (m, HD))
        lse_ref[p, 0] = jnp.transpose(wide)[0:1, :]


def attend(ids, order, q_raw, kv_raw, cosine, sine, gq, gk, span):
    rows = q_raw.shape[0]
    seq = kv_raw.shape[0]
    heads = q_raw.shape[1] // (GROUPS * HD)
    blocks, m = rows // span, GROUPS * span
    hp = heads
    whole = lambda k, ids, order: (0, 0)
    per_query = pl.BlockSpec((span, hp * GROUPS * HD), lambda j, ids, order: (j, 0))
    once = pl.Buffered(1)
    return pl.pallas_call(
        functools.partial(attend_kernel, span),
        out_shape=[
            jax.ShapeDtypeStruct((rows, heads * GROUPS * HD), BF16),
            jax.ShapeDtypeStruct((heads, blocks, 1, m), F32),
        ],
        grid_spec=pltpu.PrefetchScalarGridSpec(
            num_scalar_prefetch=2,
            grid=(blocks,),
            in_specs=[
                per_query,
                pl.BlockSpec((seq, hp * HD), whole, pipeline_mode=once),
                pl.BlockSpec((seq, hp * HD), lambda j, ids, order: (0, 1), pipeline_mode=once),
                pl.BlockSpec((seq, HD), whole, pipeline_mode=once),
                pl.BlockSpec((seq, HD), whole, pipeline_mode=once),
                pl.BlockSpec((1, HD), whole),
                pl.BlockSpec((1, HD), whole),
            ],
            out_specs=[
                per_query,
                pl.BlockSpec((hp, 1, 1, m), lambda j, ids, order: (0, j, 0, 0)),
            ],
            scratch_shapes=[
                pltpu.VMEM((seq, hp * HD), BF16),
                pltpu.VMEM((seq, hp * HD), BF16),
                pltpu.VMEM((hp, m, HD), F32),
                pltpu.VMEM((hp, m, HD), F32),
            ],
        ),
        compiler_params=pltpu.CompilerParams(vmem_limit_bytes=48 * MIB),
        cost_estimate=pl.CostEstimate(
            flops=2 * 2 * rows * seq * heads * GROUPS * HD,
            bytes_accessed=2 * (2 * rows * heads * GROUPS * HD + 2 * seq * heads * HD),
            transcendentals=rows * seq * heads * GROUPS // 2,
        ),
        name="attend",
    )(ids, order, q_raw, kv_raw, kv_raw, cosine, sine, gq, gk)


def attend_back_kernel(
    span, ids_ref, order_ref, q_ref, k_ref, v_ref, do_ref, o_ref, lse_ref, cos_ref, sin_ref, gq_ref, gk_ref,
    dq_ref, dk_ref, dv_ref, dgq_ref, dgk_ref, ks_ref, vs_ref, dka_ref, dva_ref, dqa_ref,
):
    heads = range(k_ref.shape[1] // HD)

    @pl.when(pl.program_id(0) == 0)
    def _():
        prepare_keys(span, order_ref, k_ref, v_ref, cos_ref, sin_ref, gk_ref, ks_ref, vs_ref)
        dka_ref[...] = jnp.zeros_like(dka_ref)
        dva_ref[...] = jnp.zeros_like(dva_ref)
        dgq_ref[...] = jnp.zeros_like(dgq_ref)
        dgk_ref[...] = jnp.zeros_like(dgk_ref)

    b = ids_ref[pl.program_id(0)]
    rows = slice(None)
    places = pl.ds(pl.multiple_of(b * span, span), span)
    q2, do2, delta, lse = [], [], [], []
    for p in heads:
        q2.append(query_block(q_ref, p, rows, places, cos_ref, sin_ref, gq_ref)[2])
        pick = lambda ref: jnp.concatenate([ref[rows, lanes(p * GROUPS + g)] for g in range(GROUPS)], axis=0)
        do2.append(pick(do_ref))
        delta.append(
            row_sums(do2[p].astype(F32) * pick(o_ref).astype(F32))
        )
        lse.append(lse_ref[p, 0])
    dqa_ref[...] = jnp.zeros_like(dqa_ref)

    def tile(t, masked):
        keys = pl.ds(pl.multiple_of(t * KEY_TILE, KEY_TILE), KEY_TILE)
        kt = [ks_ref[keys, lanes(p)] for p in heads]
        scores = [dot(kt[p], q2[p], NT) for p in heads]
        slopes = [dot(vs_ref[keys, lanes(p)], do2[p], NT) for p in heads]
        keep = seen(scores[0].shape, t, b, span, 0) if masked else None
        for p in heads:
            e = jnp.exp2(scores[p] - lse[p])
            if masked:
                e = jnp.where(keep, e, 0.0)
            ds = (e * (slopes[p] - delta[p])).astype(BF16)
            dva_ref[keys, lanes(p)] += dot(e.astype(BF16), do2[p], NN)
            dka_ref[keys, lanes(p)] += dot(ds, q2[p], NN)
            dqa_ref[p] += dot(ds, kt[p], TN)

    last = (b * span) // KEY_TILE
    lax.fori_loop(0, last, lambda t, _: (tile(t, False), 0)[1], 0)
    tile(last, True)
    for p in heads:
        units, scales, _q = query_block(q_ref, p, rows, places, cos_ref, sin_ref, gq_ref)
        dq = dqa_ref[p] * HD**-0.5
        for g in range(GROUPS):
            grad = rope_back(dq[g * span : (g + 1) * span], cos_ref[places, :], sin_ref[places, :])
            dgq_ref[...] += jnp.sum(grad * units[g], axis=0, keepdims=True)
            u = grad * gq_ref[...]
            back = scales[g] * (u - units[g] * row_mean(u * units[g]))
            dq_ref[rows, lanes(p * GROUPS + g)] = back.astype(BF16)

    def finish(i, _):
        rows = pl.ds(pl.multiple_of(i * span, span), span)
        source = pl.ds(pl.multiple_of(order_ref[i] * span, span), span)
        for p in heads:
            unit, r = unit_rows(k_ref[source, lanes(p)].astype(F32))
            grad = rope_back(dka_ref[rows, lanes(p)] * (1.0 / LOG2E), cos_ref[rows, :], sin_ref[rows, :])
            dgk_ref[...] += jnp.sum(grad * unit, axis=0, keepdims=True)
            u = grad * gk_ref[...]
            back = r * (u - unit * row_mean(u * unit))
            dk_ref[source, lanes(p)] = back.astype(BF16)
        dv_ref[source, :] = dva_ref[rows, :].astype(BF16)
        return 0

    @pl.when(pl.program_id(0) == pl.num_programs(0) - 1)
    def _():
        lax.fori_loop(0, k_ref.shape[0] // span, finish, 0)


def attend_back(ids, order, q_raw, kv_raw, grad_mixed, mixed, lse, cosine, sine, gq, gk, span):
    rows = q_raw.shape[0]
    seq = kv_raw.shape[0]
    heads = q_raw.shape[1] // (GROUPS * HD)
    blocks, m = rows // span, GROUPS * span
    hp = heads
    whole = lambda k, ids, order: (0, 0)
    once = pl.Buffered(1)
    per_query = pl.BlockSpec((span, hp * GROUPS * HD), lambda j, ids, order: (j, 0))
    per_key = pl.BlockSpec((seq, hp * HD), whole, pipeline_mode=once)
    gain = pl.BlockSpec((1, HD), whole)
    return pl.pallas_call(
        functools.partial(attend_back_kernel, span),
        out_shape=[
            jax.ShapeDtypeStruct((rows, heads * GROUPS * HD), BF16),
            jax.ShapeDtypeStruct((seq, heads * HD), BF16),
            jax.ShapeDtypeStruct((seq, heads * HD), BF16),
            jax.ShapeDtypeStruct((1, HD), F32),
            jax.ShapeDtypeStruct((1, HD), F32),
        ],
        grid_spec=pltpu.PrefetchScalarGridSpec(
            num_scalar_prefetch=2,
            grid=(blocks,),
            in_specs=[
                per_query,
                per_key,
                pl.BlockSpec((seq, hp * HD), lambda j, ids, order: (0, 1), pipeline_mode=once),
                per_query,
                per_query,
                pl.BlockSpec((hp, 1, 1, m), lambda j, ids, order: (0, j, 0, 0)),
                pl.BlockSpec((seq, HD), whole, pipeline_mode=once),
                pl.BlockSpec((seq, HD), whole, pipeline_mode=once),
                gain,
                gain,
            ],
            out_specs=[per_query] + [pl.BlockSpec((seq, hp * HD), whole)] * 2 + [gain, gain],
            scratch_shapes=[
                pltpu.VMEM((seq, hp * HD), BF16),
                pltpu.VMEM((seq, hp * HD), BF16),
                pltpu.VMEM((seq, hp * HD), F32),
                pltpu.VMEM((seq, hp * HD), F32),
                pltpu.VMEM((hp, m, HD), F32),
            ],
        ),
        compiler_params=pltpu.CompilerParams(vmem_limit_bytes=46 * MIB),
        cost_estimate=pl.CostEstimate(
            flops=5 * 2 * rows * seq * heads * GROUPS * HD // 2,
            bytes_accessed=2 * (4 * rows * heads * GROUPS * HD + 4 * seq * heads * HD),
            transcendentals=rows * seq * heads * GROUPS // 2,
        ),
        name="attend_back",
    )(ids, order, q_raw, kv_raw, kv_raw, grad_mixed, mixed, lse, cosine, sine, gq, gk)


def project_kernel(own, chip_ref, x_ref, gain_ref, wq_ref, wkv_ref, h_ref, q_ref, kv_ref):
    hidden = normed(x_ref[...].astype(F32), gain_ref[...]).astype(BF16)
    h_ref[...] = hidden
    kv_ref[...] = dot(hidden, wkv_ref[...], NN).astype(BF16)

    @pl.when(pl.program_id(0) < own)
    def _():
        q_ref[...] = dot(hidden, wq_ref[...], NN).astype(BF16)


def project(chip, x_all, gain, w_all, first, chip_rows):
    seq, width = x_all.shape
    size = min(TOKEN_TILE, chip_rows)
    own, tiles = chip_rows // size, seq // size
    at = lambda i, chip: ((i + chip[0] * own) % tiles, 0)
    weight = lambda col: pl.BlockSpec((width, width), lambda i, chip: (0, col), pipeline_mode=pl.Buffered(1))
    return pl.pallas_call(
        functools.partial(project_kernel, own),
        out_shape=[
            jax.ShapeDtypeStruct((seq, width), BF16),
            jax.ShapeDtypeStruct((chip_rows, width), BF16),
            jax.ShapeDtypeStruct((seq, width), BF16),
        ],
        grid_spec=pltpu.PrefetchScalarGridSpec(
            num_scalar_prefetch=1,
            grid=(tiles,),
            in_specs=[
                pl.BlockSpec((size, width), at),
                pl.BlockSpec((1, width), lambda i, chip: (0, 0)),
                weight(first // width),
                weight(first // width + 1),
            ],
            out_specs=[
                pl.BlockSpec((size, width), at),
                pl.BlockSpec((size, width), lambda i, chip: (jnp.minimum(i, own - 1), 0)),
                pl.BlockSpec((size, width), at),
            ],
        ),
        compiler_params=pltpu.CompilerParams(vmem_limit_bytes=48 * MIB),
        name="project",
    )(chip, x_all, gain, w_all, w_all)


def project_back_kernel(own, chip_ref, dq_ref, dk_ref, dv_ref, x_ref, wq_ref, wk_ref, wv_ref, p_ref, g_ref, acc_ref):
    i = pl.program_id(0)
    acc_ref[...] = dot(dk_ref[...], wk_ref[...], NT) + dot(dv_ref[...], wv_ref[...], NT)

    @pl.when(i < own)
    def _():
        acc_ref[...] += dot(dq_ref[...], wq_ref[...], NT)

    @pl.when(i == 0)
    def _():
        g_ref[...] = jnp.zeros_like(g_ref)

    part = acc_ref[...]
    p_ref[...] = part.astype(BF16)
    g_ref[...] += jnp.sum(part * normed(x_ref[...].astype(F32), 1.0), axis=0, keepdims=True)


def project_back(chip, dq, dk, dv, x_all, w_all, first):
    seq, width = x_all.shape
    chip_rows, kv = dq.shape[0], dk.shape[1]
    size = min(TOKEN_TILE, chip_rows)
    own, tiles = chip_rows // size, seq // size
    at = lambda i, chip: ((i + chip[0] * own) % tiles, 0)
    weight = lambda cols, col: pl.BlockSpec((width, cols), lambda i, chip: (0, col), pipeline_mode=pl.Buffered(1))
    return pl.pallas_call(
        functools.partial(project_back_kernel, own),
        out_shape=[jax.ShapeDtypeStruct((seq, width), BF16), jax.ShapeDtypeStruct((1, width), F32)],
        grid_spec=pltpu.PrefetchScalarGridSpec(
            num_scalar_prefetch=1,
            grid=(tiles,),
            in_specs=[
                pl.BlockSpec((size, width), lambda i, chip: (jnp.minimum(i, own - 1), 0)),
                pl.BlockSpec((size, kv), at),
                pl.BlockSpec((size, kv), at),
                pl.BlockSpec((size, width), at),
                weight(width, first // width),
                weight(kv, (first + width) // kv),
                weight(kv, (first + width) // kv + 1),
            ],
            out_specs=[
                pl.BlockSpec((size, width), at),
                pl.BlockSpec((1, width), lambda i, chip: (0, 0)),
            ],
            scratch_shapes=[pltpu.VMEM((size, width), F32)],
        ),
        compiler_params=pltpu.CompilerParams(vmem_limit_bytes=48 * MIB),
        name="project_back",
    )(chip, dq, dk, dv, x_all, w_all, w_all, w_all)


def feed_kernel(chip_ref, x_ref, p0_ref, p1_ref, gain_ref, w_ref, mid_ref, sec_ref, act_ref, gu_ref):
    count = x_ref.shape[0]
    size = min(TOKEN_TILE, count)
    tile = lambda i: pl.ds(pl.multiple_of(i * size, size), size)

    @pl.when(pl.program_id(0) == 0)
    def _():
        def start(i, _):
            rows = tile(i)
            middle = x_ref[rows, :].astype(F32) + (p0_ref[rows, :].astype(F32) + p1_ref[rows, :].astype(F32))
            mid_ref[rows, :] = middle
            sec_ref[rows, :] = normed(middle, gain_ref[...]).astype(BF16)
            return 0

        lax.fori_loop(0, count // size, start, 0)

    def body(i, _):
        rows = tile(i)
        both = dot(sec_ref[rows, :], w_ref[...], NN)
        gate, up = both[:, :FF_TILE], both[:, FF_TILE:]
        act_ref[rows, :] = (gate * jax.nn.sigmoid(gate) * up).astype(BF16)
        gu_ref[rows, :] = both.astype(BF16)
        return 0

    lax.fori_loop(0, count // size, body, 0)


def feed(chip, x_all, p0, p1, gain, w_all, ff):
    rows, width = p0.shape
    once = pl.Buffered(1)
    whole = lambda: pl.BlockSpec((rows, width), lambda j, chip: (0, 0), pipeline_mode=once)
    return pl.pallas_call(
        feed_kernel,
        out_shape=[
            jax.ShapeDtypeStruct((rows, width), F32),
            jax.ShapeDtypeStruct((rows, width), BF16),
            jax.ShapeDtypeStruct((rows, ff), BF16),
            jax.ShapeDtypeStruct((rows, 2 * ff), BF16),
        ],
        grid_spec=pltpu.PrefetchScalarGridSpec(
            num_scalar_prefetch=1,
            grid=(ff // FF_TILE,),
            in_specs=[
                pl.BlockSpec((rows, width), lambda j, chip: (chip[0], 0), pipeline_mode=once),
                whole(), whole(),
                pl.BlockSpec((1, width), lambda j, chip: (0, 0)),
                pl.BlockSpec((width, 2 * FF_TILE), lambda j, chip: (0, j)),
            ],
            out_specs=[
                pl.BlockSpec((rows, width), lambda j, chip: (0, 0)),
                pl.BlockSpec((rows, width), lambda j, chip: (0, 0)),
                pl.BlockSpec((rows, FF_TILE), lambda j, chip: (0, j)),
                pl.BlockSpec((rows, 2 * FF_TILE), lambda j, chip: (0, j)),
            ],
        ),
        compiler_params=pltpu.CompilerParams(vmem_limit_bytes=38 * MIB),
        name="feed",
    )(chip, x_all, p0, p1, gain, w_all)


def feed_back_kernel(core_ref, gu_ref, go_ref, wd_ref, gg_ref, d_ref):
    count = gu_ref.shape[0]
    size = min(2 * TOKEN_TILE, count)
    unit = wd_ref.shape[2]
    for u in range(FF_TILE // unit):
        d_ref[u * unit : (u + 1) * unit, :] = wd_ref[u, 0]

    def body(i, _):
        rows = pl.ds(pl.multiple_of(i * size, size), size)
        grad = dot(go_ref[rows, :], d_ref[...], NT)
        gate, up = gu_ref[rows, :FF_TILE].astype(F32), gu_ref[rows, FF_TILE:].astype(F32)
        sig = jax.nn.sigmoid(gate)
        gg_ref[rows, :FF_TILE] = (grad * up * sig * (1.0 + gate * (1.0 - sig))).astype(BF16)
        gg_ref[rows, FF_TILE:] = (grad * (gate * sig)).astype(BF16)
        return 0

    lax.fori_loop(0, count // size, body, 0)


def feed_back(core, gate_up, go, w_down):
    rows, width = go.shape
    chips, _, unit, _ = w_down.shape
    ff = chips * unit
    return pl.pallas_call(
        feed_back_kernel,
        out_shape=[jax.ShapeDtypeStruct((rows, 2 * ff), BF16), jax.ShapeDtypeStruct((ff, width), BF16)],
        grid_spec=pltpu.PrefetchScalarGridSpec(
            num_scalar_prefetch=1,
            grid=(ff // FF_TILE,),
            in_specs=[
                pl.BlockSpec((rows, 2 * FF_TILE), lambda j, core: (0, j)),
                pl.BlockSpec((rows, width), lambda j, core: (0, 0), pipeline_mode=pl.Buffered(1)),
                pl.BlockSpec((FF_TILE // unit, 1, unit, width), lambda j, core: (j, core[0], 0, 0)),
            ],
            out_specs=[
                pl.BlockSpec((rows, 2 * FF_TILE), lambda j, core: (0, j)),
                pl.BlockSpec((FF_TILE, width), lambda j, core: (j, 0)),
            ],
        ),
        compiler_params=pltpu.CompilerParams(vmem_limit_bytes=48 * MIB),
        name="feed_back",
    )(core, gate_up, go, w_down)


def middle_back_kernel(mid_ref, s0_ref, s1_ref, go_ref, gain_ref, wo_ref, ga_ref, gm_ref, g_ref):
    back, terms = norm_back(mid_ref[...], gain_ref[...], s0_ref[...].astype(F32) + s1_ref[...].astype(F32))
    grad = (go_ref[...].astype(F32) + back).astype(BF16)
    ga_ref[...] = grad
    gm_ref[...] = dot(grad, wo_ref[...], NT).astype(BF16)

    @pl.when(pl.program_id(0) == 0)
    def _():
        g_ref[...] = jnp.zeros_like(g_ref)

    g_ref[...] += jnp.sum(terms, axis=0, keepdims=True)


def middle_back(middle, s0, s1, go, gain, w_out):
    rows, width = middle.shape
    size = min(ROW_TILE, rows)
    row = pl.BlockSpec((size, width), lambda i: (i, 0))
    line = pl.BlockSpec((1, width), lambda i: (0, 0))
    return pl.pallas_call(
        middle_back_kernel,
        out_shape=[
            jax.ShapeDtypeStruct((rows, width), BF16),
            jax.ShapeDtypeStruct((rows, w_out.shape[0]), BF16),
            jax.ShapeDtypeStruct((1, width), F32),
        ],
        grid=(rows // size,),
        in_specs=[row, row, row, row, line, pl.BlockSpec(w_out.shape, lambda i: (0, 0), pipeline_mode=pl.Buffered(1))],
        out_specs=[row, pl.BlockSpec((size, w_out.shape[0]), lambda i: (i, 0)), line],
        compiler_params=pltpu.CompilerParams(vmem_limit_bytes=22 * MIB),
        name="middle_back",
    )(middle, s0, s1, go, gain, w_out)


LINK_TIME = pl.CostEstimate(flops=0, bytes_accessed=300_000_000, transcendentals=0)


def peers():
    dp, ctx = lax.axis_index("dp"), lax.axis_index("ctx")
    to = lambda d, k: (jnp.bitwise_xor(dp, d), jnp.bitwise_xor(ctx, k))
    return dp, ctx, to


def greet(devices):
    barrier = pltpu.get_barrier_semaphore()
    for device in devices:
        pl.semaphore_signal(barrier, inc=1, device_id=device, device_id_type=MESH)
    pl.semaphore_wait(barrier, len(devices))


def sender(send_sem, recv_sem):
    made = []

    def send(src, dst, device):
        i = len(made)
        copy = pltpu.make_async_remote_copy(
            src_ref=src, dst_ref=dst, send_sem=send_sem.at[i], recv_sem=recv_sem.at[i],
            device_id=device, device_id_type=MESH,
        )
        copy.start()
        made.append(copy)
        return copy

    return send, made


def gather_kernel(pk_ref, wo_ref, tok_ref, go_ref, w_ref, x_ref, g_ref, send_sem, recv_sem, local_sem):
    dp, ctx, to = peers()
    c, z = ctx % 2, ctx // 2
    which, me = ctx // 4, ctx % 4
    inner = jnp.logical_or(z == 1, z == 2)
    greet([to(0, 1), to(0, 2), to(0, 4), to(0, 6), to(1, 0), to(2, 0)])
    send, made = sender(send_sem, recv_sem)
    sib, nbr, far, across, xn, yn = to(0, 1), to(0, 2), to(0, 4), to(0, 6), to(1, 0), to(2, 0)
    rows, cols = pk_ref.shape[1:]

    place = w_ref.at[dp, z, pl.ds(c * rows, rows), pl.ds(0, cols)]
    local = [
        pltpu.make_async_copy(pk_ref.at[c], place, local_sem.at[0]),
        pltpu.make_async_copy(wo_ref, w_ref.at[dp, z, :, pl.ds(cols, wo_ref.shape[1])], local_sem.at[1]),
        pltpu.make_async_copy(tok_ref.at[which], x_ref.at[me, 0], local_sem.at[2]),
        pltpu.make_async_copy(go_ref.at[which], g_ref.at[c, 0], local_sem.at[3]),
    ]
    for copy in local:
        copy.start()
    cross = send(pk_ref.at[1 - c], place, sib)
    for copy in local:
        copy.wait()
    cross.wait_recv()
    done = []

    def half(h, q, zz):
        return w_ref.at[q, zz, pl.ds(h * rows, rows)]

    first = []

    def spread(zz):
        low, high = half(0, dp, zz), half(1, dp, zz)
        first.append((send(low, low, yn), low, half(0, jnp.bitwise_xor(dp, 2), zz), xn))
        first.append((send(high, high, xn), high, half(1, jnp.bitwise_xor(dp, 1), zz), yn))

    def pass_on():
        for copy, own, part, device in first[:2]:
            done.append(send(own, own, device))
            copy.wait_recv()
            done.append(send(part, part, device))
        del first[:2]

    z_one = jnp.bitwise_xor(z, 1)
    z_near = jnp.bitwise_xor(z, jnp.where(inner, 3, 2))
    z_far = jnp.bitwise_xor(z, jnp.where(inner, 2, 3))
    relayed = []

    def relay(slot, source, device):
        copy = pltpu.make_async_remote_copy(
            src_ref=w_ref.at[dp, source], dst_ref=w_ref.at[dp, source],
            send_sem=send_sem.at[send_sem.shape[0] - 4 + len(relayed)],
            recv_sem=recv_sem.at[send_sem.shape[0] - 2 + slot],
            device_id=device, device_id_type=MESH,
        )
        relayed.append(copy)
        pl.when(inner)(copy.start)
        return copy

    step = send(w_ref.at[dp, z], w_ref.at[dp, z], nbr)
    near = relay(0, z, across)
    spread(z)
    pass_on()
    step.wait_recv()
    far_block = relay(1, z_one, across)
    spread(z_one)
    near.wait_recv()
    relay(0, z_near, nbr)
    spread(z_near)
    pass_on()
    far_block.wait_recv()
    relay(1, z_far, nbr)
    spread(z_far)
    swap = send(tok_ref.at[1 - which], x_ref.at[me, 1], far)
    mine_nbr = send(tok_ref.at[which], x_ref.at[me, 0], nbr)
    done += [send(tok_ref.at[which], x_ref.at[me, 0], sib), send(go_ref.at[which], g_ref.at[c, 0], sib)]
    pass_on()
    swap.wait_recv()
    done.append(send(x_ref.at[me, 1], x_ref.at[me, 1], sib))
    swap_nbr = send(x_ref.at[me, 1], x_ref.at[me, 1], nbr)
    go_swap = send(go_ref.at[1 - which], g_ref.at[c, 1], far)
    pass_on()
    other = jnp.bitwise_xor(me, 2)
    mine_nbr.wait_recv()
    done.append(send(x_ref.at[other, 0], x_ref.at[other, 0], sib))
    swap_nbr.wait_recv()
    done.append(send(x_ref.at[other, 1], x_ref.at[other, 1], sib))
    go_swap.wait_recv()
    done.append(send(g_ref.at[c, 1], g_ref.at[c, 1], sib))
    for copy in done:
        copy.wait_recv()
    for copy in made:
        copy.wait_send()

    @pl.when(inner)
    def _():
        for copy in relayed:
            copy.wait_send()


def gather(packed, w_out, tokens, grad_out):
    rows, cols = 2 * packed.shape[1], packed.shape[2] + w_out.shape[1]
    slots, width = tokens.shape[1:]
    copies = 36 + 4
    anywhere = pl.BlockSpec(memory_space=pl.ANY)
    near = pl.BlockSpec(memory_space=pltpu.VMEM)
    w, x, g = pl.pallas_call(
        gather_kernel,
        out_shape=[
            jax.ShapeDtypeStruct((4, 4, rows, cols), BF16),
            jax.ShapeDtypeStruct((4, 2, slots, width), BF16),
            jax.ShapeDtypeStruct((2, 2, slots, width), BF16),
        ],
        in_specs=[near] * 4,
        out_specs=[anywhere] * 3,
        scratch_shapes=[
            pltpu.SemaphoreType.DMA((copies,)),
            pltpu.SemaphoreType.DMA((copies,)),
            pltpu.SemaphoreType.DMA((4,)),
        ],
        compiler_params=pltpu.CompilerParams(
            collective_id=0, has_side_effects=True, vmem_limit_bytes=48 * MIB
        ),
        cost_estimate=LINK_TIME,
        name="gather",
    )(packed, w_out, tokens, grad_out)
    return w.reshape(16 * rows, cols), x.reshape(-1, width), g.reshape(-1, width)


def reduce_kernel(
    h_hbm, dq_hbm, dk_hbm, dv_hbm, e_hbm, ow_hbm, or_hbm, part_ref, xa_hbm, gm_hbm, gain_ref,
    a_ref, go_ref, ig_ref,
    g_ref, in_a, in_b, mid_a, mid_b, got_a, got_b, out3, in3, mine_ref, sib_ref, give_ref, nbr_ref, back_ref,
    x_ref, ga_ref, h_ref, dq_ref, dk_ref, dv_ref, o_ref, s_ref, send_sem, recv_sem, local_sem,
):
    dp, ctx, to = peers()
    c, z = ctx % 2, ctx // 2
    which, chip = ctx // 4, z % 2
    x, y = dp % 2, dp // 2
    hr = g_ref.shape[3] // 2
    count = mine_ref.shape[1]
    q_cols, kv_cols = dq_ref.shape[1], dk_ref.shape[1]
    near = s_ref.shape[1]
    first_col, width = near - HD, ow_hbm.shape[-1]
    local = []

    def fetch(src, dst):
        copy = pltpu.make_async_copy(src, dst, local_sem.at[len(local)])
        copy.start()
        local.append(copy)

    fetch(ow_hbm.at[:, :, c], g_ref.at[c, :, :, :, pl.ds(near, width)])
    fetch(or_hbm, g_ref.at[1 - c, :, :, :, pl.ds(near, width)])
    fetch(e_hbm, g_ref.at[:, :, :, :, pl.ds(first_col, HD)])
    fetch(part_ref.at[:, c], mine_ref)
    fetch(dq_hbm, dq_ref)
    fetch(h_hbm, h_ref)
    fetch(dk_hbm, dk_ref)
    fetch(dv_hbm, dv_ref)
    fetch(xa_hbm.at[ctx % 4], x_ref)
    fetch(gm_hbm.at[c], ga_ref)
    greet([to(0, 1), to(0, 2), to(0, 4), to(0, 6), to(1, 0), to(2, 0)])
    send, made = sender(send_sem, recv_sem)
    sib, nbr, far, across = to(0, 1), to(0, 2), to(0, 4), to(0, 6)
    xn, yn = to(1, 0), to(2, 0)
    cross = send(part_ref.at[:, 1 - c], sib_ref, sib)

    def ready(count):
        for copy in local[:count]:
            copy.wait()
        del local[:count]

    def weigh(rows, grad_ref, at):
        def body(i, _):
            some = h_ref[rows, pl.ds(pl.multiple_of(i * 4 * 2 * hr, 128), 4 * 2 * hr)]
            part = dot(some, grad_ref[...], TN).astype(BF16)
            g_ref[i // 2, i % 2, :, :, at : at + grad_ref.shape[1]] = part.reshape(4, 2 * hr, grad_ref.shape[1])
            return 0

        lax.fori_loop(0, 4, body, 0)

    low, high = pl.ds(0, hr), pl.ds(hr, hr)
    inner = jnp.logical_or(z == 1, z == 2)
    outer = jnp.logical_not(inner)
    order = [jnp.bitwise_xor(z, jnp.where(inner, 3, 2)), jnp.bitwise_xor(z, jnp.where(inner, 2, 3)), jnp.bitwise_xor(z, 1), z]
    passed = []

    def pass_z(kind, slot, source, part, device, role):
        copy = pltpu.make_async_remote_copy(
            src_ref=out3.at[source, :, parts[part]], dst_ref=in3.at[slot, :, parts[part]],
            send_sem=send_sem.at[40 + 2 * kind + part], recv_sem=recv_sem.at[40 + 2 * slot + part],
            device_id=device, device_id_type=MESH,
        )
        pl.when(role)(copy.start)
        passed.append((role, copy))

    def from_z(slot, part):
        return pltpu.make_async_remote_copy(
            src_ref=out3.at[0, :, parts[part]], dst_ref=in3.at[slot, :, parts[part]],
            send_sem=send_sem.at[40 + part], recv_sem=recv_sem.at[40 + 2 * slot + part],
            device_id=nbr, device_id_type=MESH,
        )

    def add_z(block, slot, part):
        p = parts[part]
        out3[block, :, p] = (out3[block, :, p].astype(F32) + in3[slot, :, p].astype(F32)).astype(BF16)

    def inward(i):
        k, part = i % 4, i // 4

        @pl.when(inner)
        def _():
            from_z(k, part).wait_recv()
            add_z(k, k, part)

        pass_z(3 + k, 3 + k, k, part, across, inner)

    def outward(part):
        @pl.when(inner)
        def _():
            from_z(4, part).wait_recv()
            add_z(2, 4, part)

        pass_z(5, 2, 2, part, nbr, inner)

    a_in, b_in, a_mid, b_mid = [], [], [], []
    size = 64
    tile = lambda i: pl.ds(pl.multiple_of(i * size, size), size)
    parts = (pl.ds(first_col, HD + width), pl.ds(0, first_col))

    def enter(i):
        k, p = i % 4, parts[i // 4]
        a_in.append(send(g_ref.at[:, 1 - x, order[k], low, p], in_a.at[k, :, :, p], xn))
        b_in.append(send(g_ref.at[1 - y, :, order[k], high, p], in_b.at[k, :, :, p], yn))

    def middle(i):
        k, p = i % 4, parts[i // 4]
        add = lambda p, q: (p.astype(F32) + q.astype(F32)).astype(BF16)
        a_in[i].wait_recv()
        mid_a[k, :, p] = add(g_ref[1 - y, x, order[k], 0:hr, p], in_a[k, 1 - y, :, p])
        a_mid.append(send(mid_a.at[k, :, p], got_a.at[k, :, p], yn))
        b_in[i].wait_recv()
        mid_b[k, :, p] = add(g_ref[y, 1 - x, order[k], hr:, p], in_b[k, 1 - x, :, p])
        b_mid.append(send(mid_b.at[k, :, p], got_b.at[k, :, p], xn))

    def leave(i):
        k, p = i % 4, parts[i // 4]
        add = lambda p, q, r: (p.astype(F32) + q.astype(F32) + r.astype(F32)).astype(BF16)
        a_mid[i].wait_recv()
        out3[k, 0:hr, p] = add(g_ref[y, x, order[k], 0:hr, p], in_a[k, y, :, p], got_a[k, :, p])
        b_mid[i].wait_recv()
        out3[k, hr:, p] = add(g_ref[y, x, order[k], hr:, p], in_b[k, x, :, p], got_b[k, :, p])
        if k < 3:
            pass_z(k, k, k, i // 4, nbr, outer)

    ready(3)
    enter(0)
    enter(1)
    enter(2)
    ready(1)
    cross.wait_recv()
    slots = ig_ref.shape[1]

    def give(i, _):
        rows = tile(i)
        give_ref[rows] = (mine_ref[1 - chip, rows].astype(F32) + sib_ref[1 - chip, rows].astype(F32)).astype(BF16)
        return 0

    def back(i, _):
        rows = tile(i)
        grad = mine_ref[chip, rows].astype(F32) + sib_ref[chip, rows].astype(F32) + nbr_ref[rows].astype(F32)
        through, _terms = norm_back(x_ref[rows, :].astype(F32), gain_ref[...], grad)
        back_ref[rows] = (ga_ref[rows, :].astype(F32) + through).astype(BF16)
        return 0

    swaps = []
    for first in (slots, 0):
        lax.fori_loop(first // size, (first + slots) // size, give, 0)
        rows = pl.ds(first, slots)
        swaps.append(send(give_ref.at[rows], nbr_ref.at[rows], nbr))
    ready(2)
    weigh(pl.ds(pl.multiple_of(chip * dq_ref.shape[0], dq_ref.shape[0]), dq_ref.shape[0]), dq_ref, 0)
    middle(0)
    enter(3)
    middle(1)
    middle(2)
    ready(2)
    weigh(slice(None), dk_ref, q_cols)
    weigh(slice(None), dv_ref, q_cols + kv_cols)
    enter(4)
    enter(5)
    leave(0)
    leave(1)
    middle(3)
    ready(2)
    swaps[0].wait_recv()
    lax.fori_loop(slots // size, 2 * slots // size, back, 0)
    home = send(back_ref.at[pl.ds(slots, slots)], ig_ref.at[which], far)
    leave(2)
    inward(0)
    inward(1)
    middle(4)
    enter(6)
    leave(3)
    middle(5)
    enter(7)
    leave(4)
    outward(0)
    swaps[1].wait_recv()
    lax.fori_loop(0, slots // size, back, 0)
    keep = pltpu.make_async_copy(back_ref.at[pl.ds(0, slots)], ig_ref.at[which], local_sem.at[0])
    keep.start()
    middle(6)
    leave(5)
    inward(4)
    middle(7)
    leave(6)
    inward(5)
    leave(7)
    outward(1)
    for part in range(2):
        from_z(2, part).wait_recv()

    @pl.when(inner)
    def _():
        for part in range(2):
            from_z(3, part).wait_recv()
            add_z(3, 3, part)

    total = out3[3].astype(F32) + in3[2].astype(F32)
    o_ref[...] = total[:, :near].astype(BF16)
    other = send(o_ref.at[pl.ds(pl.multiple_of((1 - c) * hr, hr), hr)], s_ref, sib)
    go_ref[...] = total[:, near:].astype(BF16)
    own = o_ref.at[pl.ds(pl.multiple_of(c * hr, hr), hr)]

    def place(source, core):
        at = 0
        for size in (q_cols, kv_cols, kv_cols):
            a_ref[:, pl.ds(pl.multiple_of(2 * at + core * size, HD), size)] = source[:, at : at + size]
            at += size

    place(own, c)
    other.wait_recv()
    place(s_ref, 1 - c)
    both = own[:, first_col:].astype(F32) + s_ref[:, first_col:].astype(F32)
    a_ref[:, 2 * first_col :] = both.astype(BF16)
    keep.wait()
    home.wait_recv()
    for copy in made:
        copy.wait_send()
    for role, copy in passed:
        pl.when(role)(copy.wait_send)


def reduce(hidden, dq, dk, dv, entries, out_own, out_sib, part, x_all, grad_middle, gain):
    seq, width = x_all.shape
    rows = width // 16
    near_cols = dq.shape[1] + dk.shape[1] + dv.shape[1] + HD
    cols = near_cols + width
    count = part.shape[0] // 4
    copies = 52
    anywhere = pl.BlockSpec(memory_space=pl.ANY)
    near = pl.BlockSpec(memory_space=pltpu.VMEM)
    return pl.pallas_call(
        reduce_kernel,
        out_shape=[
            jax.ShapeDtypeStruct((rows // 2, 2 * (near_cols - HD) + HD), BF16),
            jax.ShapeDtypeStruct((rows, width), BF16),
            jax.ShapeDtypeStruct((2, count // 2, width), BF16),
        ],
        in_specs=[anywhere] * 10 + [near],
        out_specs=[near] * 2 + [anywhere],
        scratch_shapes=[
            pltpu.VMEM((2, 2, 4, rows, cols), BF16),
            pltpu.VMEM((4, 2, rows // 2, cols), BF16),
            pltpu.VMEM((4, 2, rows // 2, cols), BF16),
        ]
        + [pltpu.VMEM((4, rows // 2, cols), BF16)] * 4
        + [
            pltpu.VMEM((4, rows, cols), BF16),
            pltpu.VMEM((5, rows, cols), BF16),
            pltpu.VMEM((2, count, width), BF16),
            pltpu.VMEM((2, count, width), BF16),
        ]
        + [pltpu.VMEM((count, width), BF16)] * 5
        + [pltpu.VMEM(v.shape, BF16) for v in (hidden, dq, dk, dv)]
        + [
            pltpu.VMEM((rows, near_cols), BF16),
            pltpu.VMEM((rows // 2, near_cols), BF16),
            pltpu.SemaphoreType.DMA((copies,)),
            pltpu.SemaphoreType.DMA((copies,)),
            pltpu.SemaphoreType.DMA((10,)),
        ],
        compiler_params=pltpu.CompilerParams(
            collective_id=1, has_side_effects=True, vmem_limit_bytes=48 * MIB
        ),
        cost_estimate=LINK_TIME,
        name="reduce",
    )(
        hidden, dq, dk, dv,
        entries.reshape(2, 2, 4, rows, HD),
        out_own.reshape(2, 4, 2, rows, width),
        out_sib.reshape(2, 4, rows, width),
        part.reshape(2, 2, count, width),
        x_all.reshape(4, count, width),
        grad_middle.reshape(2, count, width),
        gain,
    )


def by_core(c, own, other):
    return jnp.where(c == 0, jnp.stack([own, other]), jnp.stack([other, own]))


def layer(
    n_dp, n, tokens, positions, w_query, w_key, w_value, w_out, w_gate, w_up, w_down,
    attn_gain, mlp_gain, q_gain, k_gain, grad_out,
):
    axes = ("dp", "ctx")
    slots, width = tokens.shape[1:]
    seq = positions.shape[1]
    span = slots // 2
    half = n // 2
    chips = n_dp * half
    ctx = lax.axis_index("ctx")
    c = ctx % 2
    which = ctx // half
    r_in, r_out, r_down = w_query.shape[0], w_out.shape[0], w_down.shape[0]
    ff = w_gate.shape[1]
    ff_c = ff // 2
    q_c, kv_c = H * HD // 2, KV * HD // 2

    to_sibling = [(i, i ^ 1) for i in range(n)]
    to_partner = [(i, (i + half) % n) for i in range(n)]
    halves = [list(range(half)), list(range(half, n))]
    same_core = [list(range(0, n, 2)), list(range(1, n, 2))]
    sibling = lambda v: lax.ppermute(v, "ctx", to_sibling)
    partner = lambda v: lax.ppermute(v, "ctx", to_partner)

    def placed(values):
        mine = lax.dynamic_index_in_dim(values, which, 0, False)
        other = lax.dynamic_index_in_dim(values, 1 - which, 0, False)
        return jnp.concatenate([mine, partner(other)], axis=0)

    gains = jnp.concatenate(
        [
            attn_gain[:, None],
            mlp_gain[:, None],
            jnp.pad(q_gain, (0, r_in - q_gain.shape[0]))[:, None],
            jnp.pad(k_gain, (0, r_in - k_gain.shape[0]))[:, None],
            jnp.zeros((r_in, 124), BF16),
        ],
        axis=1,
    )
    tall = (n_dp, n) == (4, 8)
    qkv_halves = [
        jnp.concatenate(
            [
                w_query[:, i * q_c : (i + 1) * q_c],
                w_key[:, i * kv_c : (i + 1) * kv_c],
                w_value[:, i * kv_c : (i + 1) * kv_c],
            ],
            axis=1,
        )
        for i in range(2)
    ]

    def ff_order(shard):
        return shard.reshape(r_in, chips, 2, r_down).transpose(2, 0, 1, 3).reshape(2, r_in, ff_c)

    gate_order, up_order = ff_order(w_gate), ff_order(w_up)
    qkv_c = q_c + 2 * kv_c
    gu_c = 2 * ff_c
    all_c = gu_c + qkv_c
    by_tile = lambda v: v.reshape(2, r_in, ff_c // FF_TILE, FF_TILE)
    gu_shard = jnp.stack([by_tile(gate_order), by_tile(up_order)], axis=3).reshape(2, r_in, 2 * ff_c)
    packed = jnp.stack([jnp.concatenate([gu_shard[i], qkv_halves[i], gains], axis=1) for i in range(2)])
    if tall:
        w_all, x_all, go_chip = gather(packed, w_out, tokens, grad_out)
        out_rows = w_all[:, all_c + HD :].reshape(2, -1, r_out, width)
        out_keep = lax.dynamic_index_in_dim(out_rows, c, 0, False)
        out_give = lax.dynamic_index_in_dim(out_rows, 1 - c, 0, False)
        w_out_c = by_core(c, out_keep, sibling(out_give)).transpose(1, 0, 2, 3).reshape(q_c, width)
        w_down, w_all = lax.optimization_barrier((w_down, w_all))
    else:
        both = lax.all_gather(packed, axes, axis=1, tiled=True)
        w_all = lax.dynamic_index_in_dim(both, c, 0, False)
        out_all = lax.all_gather(w_out, axes, axis=0, tiled=True)
        w_out_c = lax.dynamic_slice_in_dim(out_all, c * q_c, q_c, 0)
        x_own = placed(tokens)
        x_all = lax.all_gather(x_own, "ctx", axis=0, tiled=True, axis_index_groups=halves)
        go_own = placed(grad_out)
        go_chip = by_core(c, go_own, sibling(go_own)).reshape(4 * slots, width)
    down_all = lax.all_gather(w_down, axes, axis=0, tiled=True).reshape(chips, 2, r_down, width)
    g_cols = w_all[:, all_c : all_c + HD].astype(F32)
    gain_attn = g_cols[:, 0][None]
    gain_mlp = g_cols[:, 1][None]
    per_head = g_cols.reshape(n_dp * n, r_in, HD)[:, : q_gain.shape[0]].reshape(HD, HD)
    gain_q = per_head[:, 2][None]
    gain_k = per_head[:, 3][None]

    chip = (ctx % half) // 2
    chip_rows = 4 * slots
    slot_ids = lax.dynamic_index_in_dim(positions, which, 0, False).reshape(2 * n, span)[:, 0] // span
    places = np.stack(
        [
            [s for d in side for k in (d, (d + half) % n) for s in (2 * k, 2 * k + 1)]
            for side in halves
        ]
    ).astype(np.int32)
    ids_all = slot_ids[lax.dynamic_index_in_dim(jnp.asarray(places), which, 0, False)]
    steps = jnp.arange(2 * n, dtype=jnp.int32)
    order = jnp.sum(jnp.where(ids_all[None, :] == steps[:, None], steps[None, :], 0), axis=1).astype(jnp.int32)
    ids = lax.dynamic_slice_in_dim(ids_all, chip * 8, 8, 0)
    cosine, sine = rope_tables(seq)

    chip_at = chip.astype(jnp.int32).reshape(1)
    hidden_all, q_raw, kv_raw = project(chip_at, x_all, gain_attn, w_all, gu_c, chip_rows)
    mixed, lse = attend(ids, order, q_raw, kv_raw, cosine, sine, gain_q, gain_k, span)
    proj = dot(mixed, w_out_c, NN, BF16)
    middle, second, activated, gate_up = feed(chip_at, x_all, proj, sibling(proj), gain_mlp, w_all, ff_c)
    grad_gu, w_down_c = feed_back(c.astype(jnp.int32).reshape(1), gate_up, go_chip, down_all)
    down = dot(activated, w_down_c, NN, BF16).reshape(2, 2 * slots, width)
    down_own = lax.dynamic_index_in_dim(down, c, 0, False)
    down_other = sibling(lax.dynamic_index_in_dim(down, 1 - c, 0, False))
    own_rows = lambda v: lax.dynamic_slice_in_dim(v, c * 2 * slots, 2 * slots, 0)
    result = (own_rows(middle) + (down_own.astype(F32) + down_other.astype(F32))).astype(BF16)

    def returned(rows):
        mine, back = rows[:slots], partner(rows[slots:])
        return jnp.where(which == 0, jnp.stack([mine, back]), jnp.stack([back, mine]))


    second_part = dot(grad_gu, w_all[:, :gu_c], NT, BF16)
    grad_gu_w = dot(second, grad_gu, TN, BF16)
    grad_down_w = dot(activated, go_chip, TN, BF16)
    grad_attn, grad_mixed, mlp_gain_sum = middle_back(
        middle, second_part, sibling(second_part), go_chip, gain_mlp, w_out_c
    )
    grad_mlp_gain = jnp.where(c == 0, mlp_gain_sum[0], 0.0)

    over_dp = lambda grad: lax.psum_scatter(grad, "dp", scatter_dimension=0, tiled=True)
    over_ctx = lambda part: lax.psum_scatter(
        part, "ctx", scatter_dimension=0, tiled=True, axis_index_groups=same_core
    )
    part_gu = over_dp(grad_gu_w)
    part_down = over_dp(grad_down_w)

    out_w = dot(mixed, grad_attn, TN, BF16).reshape(-1, 2, r_out, width)
    out_recv = sibling(lax.dynamic_index_in_dim(out_w, 1 - c, 1, False))
    out_recv, grad_mixed = lax.optimization_barrier((out_recv, grad_mixed))
    result, grad_mixed, part_down = lax.optimization_barrier((result, grad_mixed, part_down))
    if tall:
        pieces = part_down.reshape(half, r_down, width)
        place = ctx // 2
        down_own = lax.dynamic_index_in_dim(pieces, place, 0, False).astype(F32)
        down_got = [
            lax.ppermute(
                lax.dynamic_index_in_dim(pieces, jnp.bitwise_xor(place, k), 0, False),
                "ctx",
                [(i, i ^ (2 * k)) for i in range(n)],
            )
            for k in range(1, half)
        ]
    else:
        down_own, down_got = over_ctx(part_down).astype(F32), []
    output = returned(result)
    dq, dk, dv, dgq, dgk = attend_back(
        ids, order, q_raw, kv_raw, grad_mixed, mixed, lse, cosine, sine, gain_q, gain_k, span
    )
    output, dq, dk, dv, part_gu, down_got = lax.optimization_barrier((output, dq, dk, dv, part_gu, down_got))
    sum_gu = over_ctx(part_gu)
    sum_down = down_own
    for piece in down_got:
        sum_down = sum_down + piece.astype(F32)
    part_all, attn_gain_sum = project_back(chip_at, dq, dk, dv, x_all, w_all, gu_c)
    lot = lambda v: v.reshape(n_dp * n, -1)
    entries = jnp.concatenate([lot(attn_gain_sum), lot(grad_mlp_gain), lot(dgq), lot(dgk)], axis=1)
    entries = jnp.pad(entries[:, None], ((0, 0), (0, r_in - 1), (0, HD - entries.shape[1])))
    entries = entries.reshape(width, HD).astype(BF16)
    entries, sum_down = lax.optimization_barrier((entries, sum_down))
    near_c = qkv_c + HD
    beside = lambda v: v.transpose(1, 0, 2).reshape(r_in, -1)
    by_rows = lambda v: lax.dynamic_index_in_dim(v.reshape(2, r_in, -1), c, 0, False)

    def columns(sums):
        other = lax.dynamic_index_in_dim(sums.reshape(2, r_in, -1), 1 - c, 0, False)
        return by_core(c, by_rows(sums), sibling(other))

    if tall:
        sums, sum_out, input_grad = reduce(
            hidden_all, dq, dk, dv, entries, out_w, out_recv, part_all, x_all, grad_attn, gain_attn
        )
        grad_q, grad_k, grad_v = (
            sums[:, i:j].astype(F32) for i, j in ((0, 2 * q_c), (2 * q_c, 2 * q_c + 2 * kv_c), (2 * q_c + 2 * kv_c, 2 * qkv_c))
        )
        sum_out, gain_own = sum_out.astype(F32), sums[:, 2 * qkv_c :].astype(F32)
    else:
        hidden = lax.dynamic_slice_in_dim(hidden_all, chip * chip_rows, chip_rows, 0)
        grads = [dot(hidden, dq, TN, BF16), dot(hidden_all, dk, TN, BF16), dot(hidden_all, dv, TN, BF16), entries]
        qkv_own = columns(over_ctx(over_dp(jnp.concatenate(grads, axis=1)))).astype(F32)
        out_mine = lax.dynamic_index_in_dim(out_w, c, 1, False)
        sum_out = over_ctx(over_dp(by_core(c, out_mine, out_recv).reshape(chips * r_out, width))).astype(F32)
        grad_q = beside(qkv_own[:, :, :q_c])
        grad_k = beside(qkv_own[:, :, q_c : q_c + kv_c])
        grad_v = beside(qkv_own[:, :, q_c + kv_c : qkv_c])
        gain_own = jnp.sum(qkv_own[:, :, qkv_c:], axis=0)
        grad_hidden = lax.psum_scatter(
            part_all, "ctx", scatter_dimension=0, tiled=True, axis_index_groups=halves
        ).astype(F32)
        back, _terms = norm_back(x_own.astype(F32), gain_attn, grad_hidden)
        input_grad = returned((own_rows(grad_attn).astype(F32) + back).astype(BF16))
    sum_gu, gain_own = lax.optimization_barrier((sum_gu, gain_own))
    gain_row, r_head = gain_own[0], q_gain.shape[0]
    gu_own = columns(sum_gu).reshape(2, r_in, ff_c // FF_TILE, 2, FF_TILE)
    ff_back = lambda v: v.reshape(2, r_in, chips, r_down).transpose(1, 2, 0, 3).reshape(r_in, ff)
    return (
        output,
        input_grad,
        grad_q,
        grad_k,
        grad_v,
        sum_out,
        ff_back(gu_own[:, :, :, 0]).astype(F32),
        ff_back(gu_own[:, :, :, 1]).astype(F32),
        sum_down,
        gain_row[:r_in],
        gain_row[r_in : 2 * r_in],
        gain_row[2 * r_in : 2 * r_in + r_head],
        gain_row[2 * r_in + r_head : 2 * r_in + 2 * r_head],
    )


def solution(mesh):
    rows = P(("dp", "ctx"), None)
    gain = P(("dp", "ctx"))
    acts = P("dp", "ctx", None)
    return jax.shard_map(
        functools.partial(layer, mesh.shape["dp"], mesh.shape["ctx"]),
        mesh=mesh,
        in_specs=(acts, P("dp", None)) + (rows,) * 7 + (gain,) * 4 + (acts,),
        out_specs=(acts, acts) + (rows,) * 7 + (gain,) * 4,
        check_vma=False,
    )
```
